32 devices in a mesh: dp: 8 (over y, x, core), mp: 4 (over z).
Axes of the slice: x: 2, y: 2, z: 4, core: 2. Of those that a mesh axis runs over, the one named last changes fastest.
Arguments:
- activations: bfloat16 [16384, 1024], P('dp'), may hold values from -6 to 6
- cotangent: bfloat16 [16384, 1024], P('dp'), may hold values from -6 to 6
- level_table: bfloat16 [1024, 1024], P('dp'), may hold values from -6 to 6
- true_frames: int32 [16], P('dp'), may hold values from 4 to 16
- group_pattern: int32 [16], P('dp'), may hold values from 0 to 3
- noise_levels: int32 [4, 16], replicated, may hold values from 1 to 1023
- context_flags: int32 [16, 16], P('dp'), may hold values 0 or 1
- owner_list: int32 [288], replicated, may hold values from 0 to 287, as said below
- masters: float32 [4, 288, 128, 128], P('mp', 'dp')
- moment_one: float32 [4, 288, 128, 128], P('mp', 'dp')
- moment_two: float32 [4, 288, 128, 128], P('mp', 'dp')
- basis_left: float32 [4, 288, 128, 128], P('mp', 'dp'), as said below
- basis_right: float32 [4, 288, 128, 128], P('mp', 'dp'), as said below
Outputs:
- block_output: bfloat16 [16384, 1024], P('dp')
- input_grad: float32 [16384, 1024], P('dp')
- table_grad: float32 [1024, 1024], P(('dp', 'mp'))
- new_masters: float32 [4, 288, 128, 128], P('mp', 'dp')
- new_moment_one: float32 [4, 288, 128, 128], P('mp', 'dp')
- new_moment_two: float32 [4, 288, 128, 128], P('mp', 'dp')
- new_weights: bfloat16 [4, 288, 128, 128], P('mp', 'dp')
The draws below stay inside these ranges and needn't reach their ends.
Inputs may be any that keep to these rules, and one draw needn't show every extreme that they name: `owner_list`: each tile number appears once; position p belongs to the dp index p // 36. `basis_left`: every tile is an orthogonal matrix. `basis_right`: every tile is an orthogonal matrix.
All inputs are finite; a program needn't handle non-finite values. No bound on the sum of `context_flags` on one device may be relied on, other than what follows from the above.
Results may differ from the reference program's by a relative error of at most 0.02.
Values may be sent and summed in bfloat16 or wider, within the bound.
A program may use at most 256 MiB of HBM per device.

```python
import math
import jax
import jax.numpy as jnp
from jax import lax

D = 1024
H = 16
HD = 64
FF = 4096
FRAMES = 16
FRAME_TOK = 64
LEVELS = 1024
PATTERNS = 4
TILE = 128
CLIP_TOK = 1024
TOKENS = 16384
CLIPS = 16
TILES = 288
N_MP = 4


def tile_counts():
    local_width = H // N_MP * HD
    shapes = [(D, 3 * local_width), (local_width, D), (D, FF // N_MP), (FF // N_MP, D), (D, 6 * D // N_MP)]
    return [height // TILE * (breadth // TILE) for height, breadth in shapes]


def category_values(tile_ids, listed):
    result = jnp.full(tile_ids.shape, listed[0], jnp.float32)
    boundary = 0
    counts = tile_counts()
    for category in range(1, 5):
        boundary = boundary + counts[category - 1]
        result = jnp.where(tile_ids >= boundary, jnp.float32(listed[category]), result)
    return result


def owner_order(key):
    return jax.random.permutation(jax.random.fold_in(key, 11), TILES).astype(jnp.int32)


def weight_scales():
    return [0.7 * D ** (-0.5), 3.0 * (H * HD) ** (-0.5), D ** (-0.5), FF ** (-0.5), D ** (-0.5)]


def grad_sizes():
    root_tokens = math.sqrt(TOKENS)
    return [0.3 * root_tokens, root_tokens, 0.5 * root_tokens, 0.5 * root_tokens, root_tokens]


def draw_owner_list(key, part):
    return owner_order(key)


def draw_masters(key, part):
    tile_ids = owner_order(key)
    noise = jax.random.normal(jax.random.fold_in(key, 21), (N_MP, TILES, TILE, TILE), jnp.float32)
    return noise * category_values(tile_ids, weight_scales())[None, :, None, None]


def draw_moment_one(key, part):
    tile_ids = owner_order(key)
    noise = jax.random.normal(jax.random.fold_in(key, 22), (N_MP, TILES, TILE, TILE), jnp.float32)
    return noise * category_values(tile_ids, grad_sizes())[None, :, None, None]


def draw_moment_two(key, part):
    tile_ids = owner_order(key)
    spread = jax.random.uniform(jax.random.fold_in(key, 23), (N_MP, TILES, TILE, TILE), jnp.float32, 0.0, math.log(4.0))
    sizes_here = category_values(tile_ids, grad_sizes())
    return (sizes_here * sizes_here / 3.0)[None, :, None, None] * jnp.exp(spread)


def reflections(key):
    basis = jnp.broadcast_to(jnp.eye(TILE, dtype=jnp.float32), (N_MP, TILES, TILE, TILE))
    for repeat in range(16):
        reflector = jax.random.normal(jax.random.fold_in(key, repeat), (N_MP, TILES, TILE), jnp.float32)
        reflector = reflector * lax.rsqrt(jnp.sum(reflector * reflector, axis=-1, keepdims=True))
        image = jnp.sum(basis * reflector[:, :, None, :], axis=-1)
        basis = basis - 2.0 * image[..., None] * reflector[:, :, None, :]
    return basis


def draw_basis_left(key, part):
    return reflections(jax.random.fold_in(key, 31))


def draw_basis_right(key, part):
    return reflections(jax.random.fold_in(key, 32))


def place_ends(array, stream_key, smallest, largest):
    longest = array.shape.index(max(array.shape))
    spots = []
    for shift in (0, 1):
        where = [jax.random.randint(jax.random.fold_in(stream_key, axis), (), 0, length) for axis, length in enumerate(array.shape)]
        where[longest] = (where[longest] + shift) % array.shape[longest]
        spots.append(tuple(where))
    return array.at[spots[0]].set(smallest).at[spots[1]].set(largest)


def block_scale(key, extent, pieces, low, top_value):
    factor_of = 1.0
    for axis_at, shards_of in pieces:
        heights = jax.random.uniform(jax.random.fold_in(jax.random.fold_in(key, 6), axis_at), (shards_of,), jnp.float32, low / len(pieces), top_value / len(pieces))
        factor_of = factor_of * jnp.repeat(jnp.exp(heights), extent[axis_at] // shards_of).reshape((-1,) + (1,) * (len(extent) - 1 - axis_at))
    return factor_of


def bell_draw(stream_key, shape, width, reach, shards=(), held_as=jnp.bfloat16):
    values = width * jax.random.normal(stream_key, shape, jnp.float32)
    if shards:
        values = values * block_scale(stream_key, shape, shards, -0.22, 0.18)
    return jnp.clip(values, -reach, reach).astype(held_as)


def setup_inputs(seed: int = 0) -> dict:
    seeds = jax.random.split(jax.random.key(seed), 14)
    activations = bell_draw(seeds[0], (TOKENS, D), 1.0, 6.0, ((0, 8),))
    cotangent = bell_draw(seeds[1], (TOKENS, D), 1.0, 6.0, ((0, 8),))
    level_table = bell_draw(seeds[2], (LEVELS, D), 1.0, 6.0, ((0, 8),))
    true_frames = place_ends(jax.random.randint(seeds[3], (CLIPS,), FRAMES // 4, FRAMES + 1), jax.random.fold_in(seeds[3], 1), FRAMES // 4, FRAMES).astype(jnp.int32)
    group_pattern = place_ends(jax.random.randint(seeds[4], (CLIPS,), 0, PATTERNS), jax.random.fold_in(seeds[4], 1), 0, PATTERNS - 1).astype(jnp.int32)
    noise_levels = place_ends(jax.random.randint(seeds[5], (PATTERNS, FRAMES), 1, LEVELS), jax.random.fold_in(seeds[5], 1), 1, LEVELS - 1).astype(jnp.int32)
    context_flags = place_ends((jax.random.randint(seeds[6], (CLIPS, FRAMES), 0, 3) < 1).astype(jnp.int32), jax.random.fold_in(seeds[6], 1), 0, 1)
    owner_list = draw_owner_list(jax.random.fold_in(seeds[13], 71), 0)
    masters = draw_masters(jax.random.fold_in(seeds[13], 71), 0)
    moment_one = draw_moment_one(jax.random.fold_in(seeds[13], 71), 0)
    moment_two = draw_moment_two(jax.random.fold_in(seeds[13], 71), 0)
    basis_left = draw_basis_left(jax.random.fold_in(seeds[13], 71), 0)
    basis_right = draw_basis_right(jax.random.fold_in(seeds[13], 71), 0)
    return {"activations": activations, "cotangent": cotangent, "level_table": level_table, "true_frames": true_frames, "group_pattern": group_pattern, "noise_levels": noise_levels, "context_flags": context_flags, "owner_list": owner_list, "masters": masters, "moment_one": moment_one, "moment_two": moment_two, "basis_left": basis_left, "basis_right": basis_right}


@jax.custom_vjp
def low(v):
    return lax.optimization_barrier(v.astype(jnp.bfloat16)).astype(jnp.float32)

@jax.custom_vjp
def low_back(v):
    return v

def low_keep(v):
    return (low(v), None)

def low_pass(kept, grad):
    return (grad,)

def back_keep(v):
    return (v, None)

def back_low(kept, grad):
    return (low(grad),)
low.defvjp(low_keep, low_pass)
low_back.defvjp(back_keep, back_low)
HIGHEST = lax.Precision.HIGHEST
EPS_NORM = 1e-06
BETA_ONE = 0.5
BETA_TWO = 0.75
EPS_ADAM = 1e-08
DECAY = 0.01

def tile_layout(model_width, heads, head_dim, hidden, groups, tile_size):
    local_width = heads // groups * head_dim
    shapes = [(model_width, 3 * local_width), (local_width, model_width), (model_width, hidden // groups), (hidden // groups, model_width), (model_width, 6 * model_width // groups)]
    counts = [height // tile_size * (breadth // tile_size) for height, breadth in shapes]
    return (shapes, counts)

def unpack(tile_stack, shapes, counts, tile_size):
    matrices = []
    offset = 0
    for (height, breadth), amount in zip(shapes, counts):
        stacked = tile_stack[offset:offset + amount].reshape(height // tile_size, breadth // tile_size, tile_size, tile_size)
        matrices.append(stacked.transpose(0, 2, 1, 3).reshape(height, breadth))
        offset = offset + amount
    return matrices

def kind_rates(tile_ids, counts):
    scales = [0.35 * D ** (-0.5), 1.5 * (H * HD) ** (-0.5), 0.5 * D ** (-0.5), 0.5 * FF ** (-0.5), 0.5 * D ** (-0.5)]
    tile_rates = jnp.full(tile_ids.shape, scales[0], jnp.float32)
    boundary = 0
    for category in range(1, 5):
        boundary = boundary + counts[category - 1]
        tile_rates = jnp.where(tile_ids >= boundary, jnp.float32(scales[category]), tile_rates)
    return tile_rates

def layer_norm(stream):
    centered = stream - lax.optimization_barrier(jnp.mean(stream, axis=-1, keepdims=True))
    inverse_std = lax.rsqrt(lax.optimization_barrier(jnp.mean(centered * centered, axis=-1, keepdims=True)) + EPS_NORM)
    return centered * inverse_std

def clip_forward(weights, embedded, clip_input, frame_mask):
    w_query, w_key, w_value, w_out, w_up, w_down, w_mod = weights
    modulation = low_back(jnp.dot(embedded, w_mod, precision=HIGHEST)).reshape(FRAMES, 6, D)
    stream = clip_input.reshape(FRAMES, FRAME_TOK, D)
    normed = layer_norm(stream)
    hidden_one = low((normed * (1.0 + modulation[:, 1, None, :]) + modulation[:, 0, None, :]).reshape(CLIP_TOK, D))
    queries = low(low_back(jnp.dot(hidden_one, w_query, precision=HIGHEST))).reshape(CLIP_TOK, H, HD)
    key_rows = low(low_back(jnp.dot(hidden_one, w_key, precision=HIGHEST))).reshape(CLIP_TOK, H, HD)
    values = low(low_back(jnp.dot(hidden_one, w_value, precision=HIGHEST))).reshape(CLIP_TOK, H, HD)
    token_mask = jnp.repeat(jnp.repeat(frame_mask, FRAME_TOK, axis=0), FRAME_TOK, axis=1)
    scores = low_back(jnp.einsum('qhd,khd->hqk', queries, key_rows, precision=HIGHEST) * HD ** (-0.5))
    scores = jnp.where(token_mask[None], scores, -1e+30)
    soft_rows = low(jax.nn.softmax(scores, axis=-1))
    attended = low(low_back(jnp.einsum('hqk,khd->qhd', soft_rows, values, precision=HIGHEST).reshape(CLIP_TOK, H * HD)))
    branch = low_back(jnp.dot(attended, w_out, precision=HIGHEST))
    middle = stream + modulation[:, 2, None, :] * branch.reshape(FRAMES, FRAME_TOK, D)
    normed_two = layer_norm(middle)
    hidden_two = low((normed_two * (1.0 + modulation[:, 4, None, :]) + modulation[:, 3, None, :]).reshape(CLIP_TOK, D))
    pre_act = low_back(jnp.dot(hidden_two, w_up, precision=HIGHEST))
    activated = low(low_back(jax.nn.gelu(pre_act, approximate=True)))
    feed_out = low_back(jnp.dot(activated, w_down, precision=HIGHEST))
    result = middle + modulation[:, 5, None, :] * feed_out.reshape(FRAMES, FRAME_TOK, D)
    return result.reshape(CLIP_TOK, D)

def reference(activations, cotangent, level_table, true_frames, group_pattern, noise_levels, context_flags, owner_list, masters, moment_one, moment_two, basis_left, basis_right):
    shapes, counts = tile_layout(D, H, HD, FF, N_MP, TILE)
    inverse = jnp.argsort(owner_list).astype(jnp.int32)
    tile_order = masters.astype(jnp.bfloat16).astype(jnp.float32)[:, inverse]
    frame_index = jnp.arange(FRAMES, dtype=jnp.int32)
    valid_frame = frame_index[None, :] < true_frames[:, None]
    flagged = context_flags == 1
    in_context = flagged & valid_frame
    visible = valid_frame[:, None, :] & (jnp.logical_not(in_context)[:, :, None] | in_context[:, None, :])
    levels = jnp.where(flagged, 0, noise_levels[group_pattern]).astype(jnp.int32)
    level_hot = (levels.reshape(-1)[:, None] == jnp.arange(LEVELS, dtype=jnp.int32)[None, :]).astype(jnp.float32)
    local_width = H // N_MP * HD

    def forward(tile_stack, table, inputs):
        shard_mats = [unpack(tile_stack[member], shapes, counts, TILE) for member in range(N_MP)]
        w_query = jnp.concatenate([mats[0][:, :local_width] for mats in shard_mats], axis=1)
        w_key = jnp.concatenate([mats[0][:, local_width:2 * local_width] for mats in shard_mats], axis=1)
        w_value = jnp.concatenate([mats[0][:, 2 * local_width:] for mats in shard_mats], axis=1)
        w_out = jnp.concatenate([mats[1] for mats in shard_mats], axis=0)
        w_up = jnp.concatenate([mats[2] for mats in shard_mats], axis=1)
        w_down = jnp.concatenate([mats[3] for mats in shard_mats], axis=0)
        w_mod = jnp.concatenate([mats[4].reshape(D, 6, D // N_MP) for mats in shard_mats], axis=2).reshape(D, 6 * D)
        weights = (w_query, w_key, w_value, w_out, w_up, w_down, w_mod)
        embedded = jnp.dot(level_hot, table, precision=HIGHEST).reshape(CLIPS, FRAMES, D)

        def one_clip(bundle):
            return clip_forward(weights, bundle[0], bundle[1], bundle[2])
        outputs = lax.map(jax.checkpoint(one_clip), (embedded, inputs.reshape(CLIPS, CLIP_TOK, D), visible))
        return outputs.reshape(TOKENS, D)
    output, pullback = jax.vjp(forward, tile_order, level_table.astype(jnp.float32), activations.astype(jnp.float32))
    tile_grad, table_grad, input_grad = pullback(cotangent.astype(jnp.float32))
    owner_grad = tile_grad[:, owner_list]
    rotated = jnp.einsum('mpji,mpjk->mpik', basis_left, owner_grad, precision=HIGHEST)
    rotated = jnp.einsum('mpik,mpkl->mpil', rotated, basis_right, precision=HIGHEST)
    new_one = BETA_ONE * moment_one + (1.0 - BETA_ONE) * rotated
    new_two = BETA_TWO * moment_two + (1.0 - BETA_TWO) * rotated * rotated
    direction = new_one / (jnp.sqrt(new_two) + EPS_ADAM)
    turned = jnp.einsum('mpij,mpjk->mpik', basis_left, direction, precision=HIGHEST)
    turned = jnp.einsum('mpik,mplk->mpil', turned, basis_right, precision=HIGHEST)
    tile_rates = kind_rates(owner_list, counts)
    new_masters = masters - tile_rates[None, :, None, None] * (turned + DECAY * masters)
    return (output.astype(jnp.bfloat16), input_grad, table_grad, new_masters, new_one, new_two, new_masters.astype(jnp.bfloat16))
```

```python
import functools

import jax
import jax.numpy as jnp
from jax import lax
from jax.experimental import pallas as pl
from jax.experimental.pallas import tpu as pltpu
from jax.sharding import PartitionSpec as P

D = 1024
H = 16
HD = 64
FF = 4096
FRAMES = 16
FRAME_TOK = 64
LEVELS = 1024
PATTERNS = 4
TILE = 128
CLIP = FRAMES * FRAME_TOK

EPS_NORM = 1e-06
BETA_ONE = 0.5
BETA_TWO = 0.75
EPS_ADAM = 1e-08
DECAY = 0.01
LOG2E = 1.4426950408889634
GELU_A = 0.7978845608028654
GELU_B = 0.044715

BF = jnp.bfloat16
F32 = jnp.float32
VMEM_BYTES = 60 * 1024 * 1024


def params(**kw):
    return pltpu.CompilerParams(vmem_limit_bytes=VMEM_BYTES, **kw)


def cost(flops, nbytes, trans=0):
    return pl.CostEstimate(flops=int(flops), bytes_accessed=int(nbytes), transcendentals=int(trans))


def dot(left, right, dims):
    return lax.dot_general(left, right, (dims, ((), ())), preferred_element_type=F32)


NN = ((1,), (0,))
NT = ((1,), (1,))
TN = ((0,), (0,))


def tile_layout(groups):
    local_width = H // groups * HD
    shapes = [
        (D, 3 * local_width),
        (local_width, D),
        (D, FF // groups),
        (FF // groups, D),
        (D, 6 * D // groups),
    ]
    counts = [height // TILE * (breadth // TILE) for height, breadth in shapes]
    return (shapes, counts)


def kind_rates(tile_ids, counts):
    scales = [
        0.35 * D ** (-0.5),
        1.5 * (H * HD) ** (-0.5),
        0.5 * D ** (-0.5),
        0.5 * FF ** (-0.5),
        0.5 * D ** (-0.5),
    ]
    tile_rates = jnp.full(tile_ids.shape, scales[0], F32)
    boundary = 0
    for category in range(1, 5):
        boundary = boundary + counts[category - 1]
        tile_rates = jnp.where(tile_ids >= boundary, jnp.float32(scales[category]), tile_rates)
    return tile_rates


def unpack(tile_stack, shapes, counts):
    matrices = []
    offset = 0
    for (height, breadth), amount in zip(shapes, counts):
        stacked = tile_stack[offset : offset + amount].reshape(
            height // TILE, breadth // TILE, TILE, TILE
        )
        matrices.append(stacked.transpose(0, 2, 1, 3).reshape(height, breadth))
        offset = offset + amount
    return matrices


def pack(matrices):
    stacked = []
    for matrix in matrices:
        height, breadth = matrix.shape
        stacked.append(
            matrix.reshape(height // TILE, TILE, breadth // TILE, TILE)
            .transpose(0, 2, 1, 3)
            .reshape(-1, TILE, TILE)
        )
    return jnp.concatenate(stacked, axis=0)


def pick_kernel(inv_ref, q_ref, k_ref, v_ref, o_ref, up_ref, down_ref, *rest):
    mod_refs, (attn_out, up_out, down_out, mod_out) = rest[:-4], rest[-4:]
    part = inv_ref[inv_ref.shape[0] - 1]
    del part
    for role, ref in enumerate((q_ref, k_ref, v_ref)):
        attn_out[role] = ref[0].T
    attn_out[3] = o_ref[0]
    up_out[...] = up_ref[0].T
    down_out[...] = down_ref[0]
    for col, ref in enumerate(mod_refs):
        mod_out[:, col * TILE : (col + 1) * TILE] = ref[0]


def pick_chunk(gathered, inverse, chip, core):
    table = jnp.concatenate([inverse, jnp.stack([chip, core]).astype(jnp.int32)])
    base = inverse.shape[0]

    def at(fn):
        def index_map(j, tab):
            return (tab[fn(j, tab[base], tab[base + 1])], 0, 0)

        return pl.BlockSpec((1, TILE, TILE), index_map)

    specs = [
        at(lambda j, c, k: j * 6 + k),
        at(lambda j, c, k: j * 6 + 2 + k),
        at(lambda j, c, k: j * 6 + 4 + k),
        at(lambda j, c, k: 48 + k * 8 + j),
        at(lambda j, c, k: 64 + j * 8 + 4 * k + c),
        at(lambda j, c, k: 128 + (4 * k + c) * 8 + j),
    ] + [at(lambda j, c, k, col=col: 192 + j * 12 + col) for col in range(12)]
    attn, up, down, mod = pl.pallas_call(
        pick_kernel,
        grid_spec=pltpu.PrefetchScalarGridSpec(
            num_scalar_prefetch=1,
            grid=(8,),
            in_specs=specs,
            out_specs=[
                pl.BlockSpec((4, TILE, TILE), lambda j, tab: (0, 0, j)),
                pl.BlockSpec((TILE, TILE), lambda j, tab: (0, j)),
                pl.BlockSpec((TILE, TILE), lambda j, tab: (0, j)),
                pl.BlockSpec((TILE, 12 * TILE), lambda j, tab: (j, 0)),
            ],
        ),
        out_shape=[
            jax.ShapeDtypeStruct((4, TILE, D), BF),
            jax.ShapeDtypeStruct((TILE, D), BF),
            jax.ShapeDtypeStruct((TILE, D), BF),
            jax.ShapeDtypeStruct((D, 12 * TILE), BF),
        ],
        compiler_params=params(),
        cost_estimate=cost(0, 2 * 144 * 32768),
        name="pick",
    )(table, *([gathered] * len(specs)))
    rows = TILE // 4
    attn = lax.dynamic_slice_in_dim(attn, chip * rows, rows, axis=1)
    return attn.reshape(4 * rows, D), up, down, mod


def pick_chunk_plain(gathered, inverse, chip, core, chips, shapes, counts):
    w_qkv, w_out, w_up, w_down, w_mod = unpack(jnp.take(gathered, inverse, axis=0), shapes, counts)
    width = w_out.shape[0]
    half = width // 2
    ffn = w_up.shape[1] // 2
    rows, ffn_rows = half // chips, ffn // chips
    parts = []
    for role in range(3):
        parts.append(w_qkv[:, role * width : (role + 1) * width].T)
    parts.append(w_out)
    start = core * half + chip * rows
    attn = jnp.concatenate([lax.dynamic_slice_in_dim(p, start, rows, axis=0) for p in parts], axis=0)
    ffn_start = core * ffn + chip * ffn_rows
    up = lax.dynamic_slice_in_dim(w_up.T, ffn_start, ffn_rows, axis=0)
    down = lax.dynamic_slice_in_dim(w_down, ffn_start, ffn_rows, axis=0)
    return attn, up, down, w_mod


def norm_rows(values):
    centered = values - jnp.mean(values, axis=-1, keepdims=True)
    inverse_std = lax.rsqrt(jnp.mean(centered * centered, axis=-1, keepdims=True) + EPS_NORM)
    return centered * inverse_std, inverse_std


def norm_back(grad_normed, normed, inverse_std):
    centered = grad_normed - jnp.mean(grad_normed, axis=-1, keepdims=True)
    return inverse_std * (centered - normed * jnp.mean(grad_normed * normed, axis=-1, keepdims=True))


def frames_of(rows):
    return rows.reshape(-1, FRAME_TOK, D)


def flat(framed):
    return framed.reshape(-1, D)


BLK = 256
FBLK = BLK // FRAME_TOK


def row_spec():
    return pl.BlockSpec((BLK, D), lambda i: (i, 0))


def mod_spec(parts):
    return pl.BlockSpec((FBLK, parts, D), lambda i: (i, 0, 0))


def row_call(kernel, name, row_ins, mods, row_outs, mod_outs, nbytes):
    outs = [jax.ShapeDtypeStruct((CLIP, D), t) for t in row_outs]
    outs += [jax.ShapeDtypeStruct((FRAMES, n, D), F32) for n in mod_outs]
    return pl.pallas_call(
        kernel,
        grid=(CLIP // BLK,),
        in_specs=[row_spec() for _ in row_ins] + [mod_spec(6)],
        out_specs=[row_spec() for _ in row_outs] + [mod_spec(n) for n in mod_outs],
        out_shape=outs,
        compiler_params=params(),
        cost_estimate=cost(30 * CLIP * D, nbytes),
        name=name,
    )(*row_ins, mods)


def first_norm_kernel(x_ref, mod_ref, h_ref):
    normed, _ = norm_rows(x_ref[...].astype(F32))
    mods = mod_ref[...]
    h_ref[...] = flat(
        frames_of(normed) * (1.0 + mods[:, 1:2]) + mods[:, 0:1]
    ).astype(BF)


def middle_kernel(x_ref, a_ref, b_ref, dy_ref, mod_ref, y_ref, s_ref, h_ref, de_ref):
    mods = mod_ref[...]
    branch = (a_ref[...].astype(F32) + b_ref[...].astype(F32)).astype(BF)
    s_ref[...] = branch
    mid = frames_of(x_ref[...].astype(F32)) + mods[:, 2:3] * frames_of(branch.astype(F32))
    y_ref[...] = flat(mid)
    normed, _ = norm_rows(flat(mid))
    h_ref[...] = flat(
        frames_of(normed) * (1.0 + mods[:, 4:5]) + mods[:, 3:4]
    ).astype(BF)
    de_ref[...] = flat(mods[:, 5:6] * frames_of(dy_ref[...].astype(F32))).astype(BF)


def back_kernel(y_ref, g_ref, gp_ref, dy_ref, s_ref, e_ref, ep_ref, mod_ref, out_ref, dy1_ref, da_ref, dm_ref):
    mods = mod_ref[...]
    mid = y_ref[...]
    feed = e_ref[...].astype(F32) + ep_ref[...].astype(F32)
    dy = dy_ref[...].astype(F32)
    out_ref[...] = (mid + flat(mods[:, 5:6] * frames_of(feed))).astype(BF)
    normed, inverse_std = norm_rows(mid)
    grad = g_ref[...].astype(F32) + gp_ref[...].astype(F32)
    dm_ref[:, 0] = jnp.sum(frames_of(grad), axis=1)
    dm_ref[:, 1] = jnp.sum(frames_of(grad * normed), axis=1)
    scaled = flat(frames_of(grad) * (1.0 + mods[:, 4:5]))
    dy1 = dy + norm_back(scaled, normed, inverse_std)
    dy1_ref[...] = dy1
    dm_ref[:, 2] = jnp.sum(frames_of(dy1 * s_ref[...].astype(F32)), axis=1)
    dm_ref[:, 3] = jnp.sum(frames_of(dy * feed), axis=1)
    da_ref[...] = flat(mods[:, 2:3] * frames_of(dy1)).astype(BF)


def last_kernel(x_ref, g_ref, gp_ref, dy1_ref, mod_ref, out_ref, dm_ref):
    mods = mod_ref[...]
    normed, inverse_std = norm_rows(x_ref[...].astype(F32))
    grad = g_ref[...].astype(F32) + gp_ref[...].astype(F32)
    dm_ref[:, 0] = jnp.sum(frames_of(grad), axis=1)
    dm_ref[:, 1] = jnp.sum(frames_of(grad * normed), axis=1)
    scaled = flat(frames_of(grad) * (1.0 + mods[:, 1:2]))
    out_ref[...] = (dy1_ref[...] + norm_back(scaled, normed, inverse_std)).astype(BF)


QBLK = 256
SCALE2 = HD ** (-0.5) * LOG2E


def attend_kernel(qkv_ref, bias_ref, o_ref, lse_ref):
    for head in range(2):
        lanes = slice(head * HD, (head + 1) * HD)
        keys = qkv_ref[:, TILE + head * HD : TILE + (head + 1) * HD]
        values = qkv_ref[:, 2 * TILE + head * HD : 2 * TILE + (head + 1) * HD]

        def step(i, _, lanes=lanes, keys=keys, values=values, head=head):
            start = pl.multiple_of(i * QBLK, QBLK)
            queries = qkv_ref[pl.ds(start, QBLK), lanes]
            scores = dot(keys, queries, NT).reshape(FRAMES, FRAME_TOK, QBLK)
            scores = scores * SCALE2 + bias_ref[:, pl.ds(start, QBLK)][:, None, :]
            peak = jnp.max(jnp.max(scores, axis=0), axis=0, keepdims=True)
            weights = jnp.exp2(scores - peak[None])
            total = jnp.sum(jnp.sum(weights, axis=0), axis=0, keepdims=True)
            mixed = dot(values, weights.reshape(CLIP, QBLK).astype(BF), TN)
            o_ref[lanes, pl.ds(start, QBLK)] = (mixed / total).astype(BF)
            lse_ref[0, head : head + 1, pl.ds(start, QBLK)] = peak + jnp.log2(total)
            return 0

        lax.fori_loop(0, CLIP // QBLK, step, 0)


def attend(qkv, bias):
    groups = qkv.shape[1] // (3 * TILE)
    return pl.pallas_call(
        attend_kernel,
        grid=(groups,),
        in_specs=[
            pl.BlockSpec((CLIP, 3 * TILE), lambda m: (0, m)),
            pl.BlockSpec((FRAMES, CLIP), lambda m: (0, 0)),
        ],
        out_specs=[
            pl.BlockSpec((TILE, CLIP), lambda m: (m, 0)),
            pl.BlockSpec((1, 2, CLIP), lambda m: (m, 0, 0)),
        ],
        out_shape=[
            jax.ShapeDtypeStruct((groups * TILE, CLIP), BF),
            jax.ShapeDtypeStruct((groups, 2, CLIP), F32),
        ],
        compiler_params=params(),
        cost_estimate=cost(groups * 2 * 4 * CLIP * CLIP * HD * 3, 2 * qkv.size, groups * 2 * CLIP * CLIP),
        name="attend",
    )(qkv, bias)


def attend_back_kernel(qkv_ref, o_ref, do_ref, lse_ref, bias_ref, out_ref, dk_ref, dv_ref):
    for head in range(2):
        lanes = slice(head * HD, (head + 1) * HD)
        keys = qkv_ref[:, TILE + head * HD : TILE + (head + 1) * HD]
        values = qkv_ref[:, 2 * TILE + head * HD : 2 * TILE + (head + 1) * HD]
        dk_ref[...] = jnp.zeros_like(dk_ref)
        dv_ref[...] = jnp.zeros_like(dv_ref)

        def step(i, _, lanes=lanes, keys=keys, values=values, head=head):
            start = pl.multiple_of(i * QBLK, QBLK)
            across = pl.ds(start, QBLK)
            queries = qkv_ref[across, lanes]
            grad = do_ref[lanes, across]
            shift = bias_ref[:, across] - lse_ref[0, head : head + 1, across]
            scores = dot(keys, queries, NT).reshape(FRAMES, FRAME_TOK, QBLK)
            soft = jnp.exp2(scores * SCALE2 + shift[:, None, :]).reshape(CLIP, QBLK)
            delta = jnp.sum(
                grad.astype(F32) * o_ref[lanes, across].astype(F32), axis=0, keepdims=True
            )
            grad_soft = dot(values, grad, NN)
            grad_scores = (soft * (grad_soft - delta)).astype(BF)
            dv_ref[...] += dot(soft.astype(BF), grad, NT)
            dk_ref[...] += dot(grad_scores, queries, NN)
            grad_query = dot(keys, grad_scores, TN) * HD ** (-0.5)
            out_ref[across, lanes] = grad_query.T.astype(BF)
            return 0

        lax.fori_loop(0, CLIP // QBLK, step, 0)
        out_ref[:, TILE + head * HD : TILE + (head + 1) * HD] = (dk_ref[...] * HD ** (-0.5)).astype(BF)
        out_ref[:, 2 * TILE + head * HD : 2 * TILE + (head + 1) * HD] = dv_ref[...].astype(BF)


def attend_back(qkv, o_rows, do_rows, lse, bias):
    groups = qkv.shape[1] // (3 * TILE)
    return pl.pallas_call(
        attend_back_kernel,
        grid=(groups,),
        in_specs=[
            pl.BlockSpec((CLIP, 3 * TILE), lambda m: (0, m)),
            pl.BlockSpec((TILE, CLIP), lambda m: (m, 0)),
            pl.BlockSpec((TILE, CLIP), lambda m: (m, 0)),
            pl.BlockSpec((1, 2, CLIP), lambda m: (m, 0, 0)),
            pl.BlockSpec((FRAMES, CLIP), lambda m: (0, 0)),
        ],
        out_specs=pl.BlockSpec((CLIP, 3 * TILE), lambda m: (0, m)),
        out_shape=jax.ShapeDtypeStruct(qkv.shape, BF),
        scratch_shapes=[pltpu.VMEM((CLIP, HD), F32), pltpu.VMEM((CLIP, HD), F32)],
        compiler_params=params(),
        cost_estimate=cost(groups * 2 * 10 * CLIP * CLIP * HD * 3, 4 * qkv.size, groups * 2 * CLIP * CLIP),
        name="attend_back",
    )(qkv, o_rows, do_rows, lse, bias)


UNITS = 256
ROWS = 512


def feed_kernel(h_ref, de_ref, up_ref, down_ref, e_ref, dh_ref, dup_ref, ddown_ref, e_acc, dh_acc, up_acc, down_acc):
    block = pl.program_id(0)
    last = pl.num_programs(0) - 1
    up = up_ref[...]
    down = down_ref[...]
    for part in range(CLIP // ROWS):
        rows = slice(part * ROWS, (part + 1) * ROWS)
        hidden = h_ref[rows]
        grad = de_ref[rows]
        pre = dot(hidden, up, NT)
        square = pre * pre
        tanh = jnp.tanh(GELU_A * pre * (1.0 + GELU_B * square))
        act = (0.5 * pre * (1.0 + tanh)).astype(BF)
        slope = 0.5 * (1.0 + tanh) + 0.5 * pre * (1.0 - tanh * tanh) * (
            GELU_A * (1.0 + 3.0 * GELU_B * square)
        )
        grad_act = dot(grad, down, NT).astype(BF).astype(F32)
        grad_pre = (grad_act * slope).astype(BF)
        feed = dot(act, down, NN)
        back = dot(grad_pre, up, NN)

        @pl.when(block == 0)
        def _():
            e_acc[rows] = feed
            dh_acc[rows] = back

        @pl.when(block > 0)
        def _():
            e_acc[rows] += feed
            dh_acc[rows] += back

        if part == 0:
            down_acc[...] = dot(act, grad, TN)
            up_acc[...] = dot(grad_pre, hidden, TN)
        else:
            ddown_ref[...] = (down_acc[...] + dot(act, grad, TN)).astype(BF)
            dup_ref[...] = (up_acc[...] + dot(grad_pre, hidden, TN)).astype(BF)

    @pl.when(block == last)
    def _():
        e_ref[...] = e_acc[...].astype(BF)
        dh_ref[...] = dh_acc[...].astype(BF)


def feed_both(hidden, grad, up, down):
    units = up.shape[0]
    whole = pl.BlockSpec((CLIP, D), lambda i: (0, 0))
    strip = pl.BlockSpec((UNITS, D), lambda i: (i, 0))
    return pl.pallas_call(
        feed_kernel,
        grid=(units // UNITS,),
        in_specs=[whole, whole, strip, strip],
        out_specs=[whole, whole, strip, strip],
        out_shape=[jax.ShapeDtypeStruct((CLIP, D), BF)] * 2 + [jax.ShapeDtypeStruct((units, D), BF)] * 2,
        scratch_shapes=[
            pltpu.VMEM((CLIP, D), F32),
            pltpu.VMEM((CLIP, D), F32),
            pltpu.VMEM((UNITS, D), F32),
            pltpu.VMEM((UNITS, D), F32),
        ],
        compiler_params=params(),
        cost_estimate=cost(12 * CLIP * D * units, 8 * CLIP * D + 8 * units * D, CLIP * units),
        name="feed_both",
    )(hidden, grad, up, down)


def adam_step(grad, left, right, one, two, master, rate):
    low_left, low_right = left.astype(BF), right.astype(BF)
    turned = dot(low_left, grad.astype(BF), TN)
    rotated = dot(turned.astype(BF), low_right, NN)
    new_one = BETA_ONE * one + (1.0 - BETA_ONE) * rotated
    new_two = BETA_TWO * two + (1.0 - BETA_TWO) * rotated * rotated
    direction = new_one / (jnp.sqrt(new_two) + EPS_ADAM)
    back = dot(low_left, direction.astype(BF), NN)
    back = dot(back.astype(BF), low_right, NT)
    return master - rate * (back + DECAY * master), new_one, new_two


def adam_kernel(tab_ref, rate_ref, *refs, picked, batch):
    if picked:
        red_ref, mod_ref = refs[:2]
        refs = refs[2:]
    else:
        grad_ref = refs[0]
        refs = refs[1:]
    master_ref, one_ref, two_ref, left_ref, right_ref, nm_ref, n1_ref, n2_ref, nw_ref = refs
    for slot in range(batch):
        tile = pl.program_id(0) * batch + slot
        if picked:
            col = pl.multiple_of(tab_ref[tile, 8] * TILE, TILE)
            pieces = [
                red_ref[
                    tab_ref[tile, i],
                    pl.ds(pl.multiple_of(tab_ref[tile, 4 + i] * 32, 32), 32),
                    pl.ds(col, TILE),
                ]
                for i in range(4)
            ]
            grad = jnp.concatenate(pieces, axis=0).astype(F32)
            mod_row = pl.multiple_of(tab_ref[tile, 9] * TILE, TILE)
            mod_col = pl.multiple_of(tab_ref[tile, 10] * TILE, TILE)
            mod_grad = mod_ref[pl.ds(mod_row, TILE), pl.ds(mod_col, TILE)].astype(F32)
            kind = tab_ref[tile, 11]
            grad = jnp.where(kind == 1, grad.T, jnp.where(kind == 2, mod_grad, grad))
        else:
            grad = grad_ref[slot].astype(F32)
        master, one, two = adam_step(
            grad, left_ref[slot], right_ref[slot], one_ref[slot], two_ref[slot], master_ref[slot], rate_ref[tile]
        )
        nm_ref[slot] = master
        n1_ref[slot] = one
        n2_ref[slot] = two
        nw_ref[slot] = master.astype(BF)


def pick_table(tiles, device):
    table = []
    piece = jnp.arange(4, dtype=jnp.int32)[None, :]
    t = tiles[:, None]
    is_in = t < 48
    is_out = (t >= 48) & (t < 64)
    is_up = (t >= 64) & (t < 128)
    is_down = (t >= 128) & (t < 192)
    is_mod = t >= 192
    q0, q1, q2, q3, q4 = t, t - 48, t - 64, t - 128, t - 192
    core = jnp.where(is_in, (q0 % 6) % 2, jnp.where(is_out, q1 // 8, jnp.where(is_up, (q2 % 8) // 4, (q3 // 8) // 4)))
    chip = jnp.where(is_up, q2 % 4, (q3 // 8) % 4)
    chip = jnp.where(is_in | is_out, piece, chip)
    source = jnp.where(is_mod, 0, jnp.bitwise_xor(2 * chip + core, device))
    row = jnp.where(is_in, (q0 % 6) // 2, jnp.where(is_out, 3, jnp.where(is_up, 4 + piece, 8 + piece)))
    row = jnp.where(is_mod, 0, row + jnp.zeros_like(piece))
    col = jnp.where(is_in, q0 // 6, jnp.where(is_out, q1 % 8, jnp.where(is_up, q2 // 8, q3 % 8)))
    col = jnp.where(is_mod, 0, col)
    mod_row = jnp.where(is_mod, q4 // 12, 0)
    mod_col = jnp.where(is_mod, q4 % 12, 0)
    kind = jnp.where(is_mod, 2, jnp.where(is_in | is_up, 1, 0))
    return jnp.concatenate([source, row, col, mod_row, mod_col, kind], axis=1).astype(jnp.int32)


def adam(table, rates, sources, master, one, two, left, right):
    slots = master.shape[0]
    batch = max(b for b in (4, 3, 2, 1) if slots % b == 0)
    picked = len(sources) == 2
    tiles = pl.BlockSpec((batch, TILE, TILE), lambda i, *_: (i, 0, 0))
    if picked:
        source_specs = [
            pl.BlockSpec(sources[0].shape, lambda i, *_: (0, 0, 0)),
            pl.BlockSpec(sources[1].shape, lambda i, *_: (0, 0)),
        ]
    else:
        source_specs = [tiles]
    return pl.pallas_call(
        functools.partial(adam_kernel, picked=picked, batch=batch),
        grid_spec=pltpu.PrefetchScalarGridSpec(
            num_scalar_prefetch=2,
            grid=(slots // batch,),
            in_specs=source_specs + [tiles] * 5,
            out_specs=[tiles] * 4,
        ),
        out_shape=[jax.ShapeDtypeStruct(master.shape, F32)] * 3 + [jax.ShapeDtypeStruct(master.shape, BF)],
        compiler_params=params(),
        cost_estimate=cost(slots * 8 * TILE**3, slots * TILE * TILE * 36),
        name="adam",
    )(table, rates, *sources, master, one, two, left, right)


def body(
    activations,
    cotangent,
    level_table,
    true_frames,
    group_pattern,
    noise_levels,
    context_flags,
    owner_list,
    masters,
    moment_one,
    moment_two,
    basis_left,
    basis_right,
):
    groups = lax.axis_size("mp")
    owners = lax.axis_size("dp")
    chips = owners // 2
    bits = chips.bit_length() - 1
    z = lax.axis_index("mp")
    device = lax.axis_index("dp")
    core = device % 2
    chip = device // 2
    local_clips = true_frames.shape[0]
    column_clips = 2 * local_clips
    assert column_clips == groups and chips == 1 << bits
    shapes, counts = tile_layout(groups)
    slots = masters.shape[1]
    fast = chips == 4 and groups == 4

    def swap(v, step):
        return lax.ppermute(v, "dp", [(i, i ^ step) for i in range(owners)])

    def across(v):
        return swap(v, 1)

    def plane(v, bit):
        return swap(v, 2 << bit)

    def z_get(v, s):
        return lax.ppermute(v, "mp", [((i + s) % groups, i) for i in range(groups)])

    def z_put(v, s):
        return lax.ppermute(v, "mp", [(i, (i + s) % groups) for i in range(groups)])

    def plane_double(v):
        held = v[None]
        for bit in range(bits):
            held = jnp.concatenate([held, plane(held, bit)], axis=0)
        return held

    def plane_gather(v):
        if chips != 4:
            return plane_double(v)
        half = v.shape[0] // 2
        by_x, by_y = plane(v, 0), plane(v, 1)
        low, high = plane(by_x[:half], 1), plane(by_y[half:], 0)
        return jnp.stack([v, by_x, by_y, jnp.concatenate([low, high], axis=0)])

    def add(a, b):
        return (a.astype(F32) + b.astype(F32)).astype(BF)

    def plane_reduce(v):
        if chips != 4:
            held = v
            for bit in reversed(range(bits)):
                half = 1 << bit
                held = add(held[:half], plane(held[half:], bit))
            return held[0]
        half = v.shape[1] // 2
        got_low = [plane(v[1, :half], 0), plane(v[3, :half], 0)]
        got_high = [plane(v[2, half:], 1), plane(v[3, half:], 1)]
        pass_low = plane(add(v[2, :half], got_low[1]), 1)
        pass_high = plane(add(v[1, half:], got_high[1]), 0)
        low = v[0, :half].astype(F32) + got_low[0].astype(F32) + pass_low.astype(F32)
        high = v[0, half:].astype(F32) + got_high[0].astype(F32) + pass_high.astype(F32)
        return jnp.concatenate([low, high], axis=0).astype(BF)

    def z_gather(v):
        return jnp.stack([v] + [z_get(v, s) for s in range(1, groups)])

    def z_reduce(v):
        total = v[0].astype(F32)
        for s in range(1, groups):
            total = total + z_put(v[s], s).astype(F32)
        return total

    with jax.named_scope("entry"):
        holds = (z // local_clips) == core
        local = (z % local_clips) * CLIP
        pair = jnp.stack(
            [
                lax.dynamic_slice_in_dim(activations, local, CLIP, axis=0),
                lax.dynamic_slice_in_dim(cotangent, local, CLIP, axis=0),
            ]
        )
        pair = jnp.where(holds, pair, across(pair))
        x, dy = pair[0], pair[1]
        facts = jnp.concatenate(
            [context_flags, true_frames[:, None], group_pattern[:, None]], axis=1
        ).astype(jnp.int32)
        other = across(facts)
        facts = jnp.where(
            core == 0, jnp.concatenate([facts, other]), jnp.concatenate([other, facts])
        )
        flagged = facts[:, :FRAMES] == 1
        frame_index = jnp.arange(FRAMES, dtype=jnp.int32)
        valid = frame_index[None, :] < facts[:, FRAMES][:, None]
        pattern_hot = (
            facts[:, FRAMES + 1][:, None] == jnp.arange(PATTERNS, dtype=jnp.int32)[None, :]
        ).astype(jnp.int32)
        levels = jnp.where(
            flagged, 0, jnp.sum(pattern_hot[:, :, None] * noise_levels[None, :, :], axis=1)
        )
        in_context = flagged & valid
        visible = valid[:, :, None] & (
            jnp.logical_not(in_context)[:, None, :] | in_context[:, :, None]
        )
        visible = lax.dynamic_index_in_dim(visible, z, axis=0, keepdims=False)
        bias = jnp.repeat(jnp.where(visible, 0.0, -1e30).astype(F32), FRAME_TOK, axis=1)
        all_levels = plane_double(levels)

    with jax.named_scope("owner_gather"):
        gathered = lax.all_gather(masters[0].astype(BF), "dp", axis=0, tiled=True)
        table = lax.all_gather(level_table, "dp", axis=0, tiled=True)
        position = jnp.arange(owner_list.shape[0], dtype=jnp.int32)
        inverse = jnp.sum(
            jnp.where(owner_list[None, :] == position[:, None], position[None, :], 0), axis=1
        ).astype(jnp.int32)
        if fast:
            chunk_attn, chunk_up, chunk_down, w_mod = pick_chunk(gathered, inverse, chip, core)
        else:
            chunk_attn, chunk_up, chunk_down, w_mod = pick_chunk_plain(
                gathered, inverse, chip, core, chips, shapes, counts
            )

    with jax.named_scope("weights"):
        rows = chunk_attn.shape[0] // 4
        got = plane_gather(z_gather(chunk_attn)).reshape(chips, groups, 4, rows, D)
        w_in = got[:, :, :3].transpose(1, 2, 0, 3, 4).reshape(-1, D)
        w_out = got[:, :, 3].transpose(1, 0, 2, 3).reshape(-1, D)
        w_up = plane_gather(z_gather(chunk_up)).reshape(-1, D)
        w_down = plane_gather(z_gather(chunk_down)).reshape(-1, D)

    with jax.named_scope("modulation"):
        level_ids = jnp.arange(LEVELS, dtype=jnp.int32)[None, :]
        hot = (levels.reshape(-1)[:, None] == level_ids).astype(BF)
        embedded = dot(hot, table, NN).astype(BF)
        mod_part = dot(embedded, w_mod, NN).reshape(column_clips, FRAMES, -1)
        pieces = [lax.dynamic_index_in_dim(mod_part, z, axis=0, keepdims=False)]
        for s in range(1, groups):
            piece = lax.dynamic_index_in_dim(mod_part, (z + groups - s) % groups, axis=0, keepdims=False)
            pieces.append(z_get(piece, s))
        mods = lax.dynamic_slice_in_dim(jnp.stack(pieces + pieces), (groups - z) % groups, groups, axis=0)
        mods = mods.reshape(groups, FRAMES, 6, D // groups).transpose(1, 2, 0, 3).reshape(FRAMES, 6, D)

    mb = CLIP * D
    with jax.named_scope("attention"):
        (h1,) = row_call(first_norm_kernel, "first_norm", [x], mods, [BF], [], 4 * mb)
        qkv = dot(h1, w_in, NT).astype(BF)
        o_rows, lse = attend(qkv, bias)
        part = dot(o_rows, w_out, TN).astype(BF)
        y1, branch, h2, de = row_call(
            middle_kernel, "middle", [x, part, across(part), dy], mods, [F32, BF, BF, BF], [], 18 * mb
        )

    with jax.named_scope("feed"):
        e_part, dh2_part, d_up, d_down = feed_both(h2, de, w_up, w_down)
        out, dy1, da, dm_mid = row_call(
            back_kernel,
            "back",
            [y1, dh2_part, across(dh2_part), dy, branch, e_part, across(e_part)],
            mods,
            [BF, F32, BF],
            [4],
            24 * mb,
        )
        shape = (chips, groups, -1, D)
        red_up = z_reduce(plane_reduce(d_up.reshape(shape))).astype(BF)
        red_down = z_reduce(plane_reduce(d_down.reshape(shape))).astype(BF)

    def to_column(rows_here):
        half = CLIP // 2
        mine = lax.dynamic_slice_in_dim(rows_here, core * half, half, axis=0)
        by_clip = [mine] + [z_get(mine, s) for s in range(1, groups)]
        by_clip = lax.dynamic_slice_in_dim(jnp.stack(by_clip + by_clip), (groups - z) % groups, groups, axis=0)
        keep = lax.dynamic_slice_in_dim(by_clip, core * local_clips, local_clips, axis=0)
        send = lax.dynamic_slice_in_dim(by_clip, (1 - core) * local_clips, local_clips, axis=0)
        got_half = across(send)
        both = jnp.where(
            core == 0, jnp.stack([keep, got_half], axis=1), jnp.stack([got_half, keep], axis=1)
        )
        return both.reshape(local_clips * CLIP, D)

    with jax.named_scope("block_output"):
        block_output = to_column(out)

    with jax.named_scope("attention_back"):
        do_rows = dot(w_out, da, NT).astype(BF)
        d_out = dot(o_rows, da, NN).astype(BF)
        d_qkv = attend_back(qkv, o_rows, do_rows, lse, bias)
        dh1_part = dot(d_qkv, w_in, NN).astype(BF)
        d_in = dot(d_qkv, h1, TN).astype(BF)
        in_grad, dm_last = row_call(
            last_kernel, "last", [x, dh1_part, across(dh1_part), dy1], mods, [BF], [2], 12 * mb
        )
        d_in = d_in.reshape(groups, 3, chips, rows, D).transpose(2, 0, 1, 3, 4)
        d_out = d_out.reshape(groups, 1, chips, rows, D).transpose(2, 0, 1, 3, 4)
        d_attn = jnp.concatenate([d_in, d_out], axis=2).reshape(chips, groups, 4 * rows, D)
        red_attn = z_reduce(plane_reduce(d_attn)).astype(BF)

    with jax.named_scope("input_grad"):
        input_grad = to_column(in_grad).astype(F32)

    with jax.named_scope("modulation_back"):
        d_mod = jnp.stack(
            [dm_last[:, 0], dm_last[:, 1], dm_mid[:, 2], dm_mid[:, 0], dm_mid[:, 1], dm_mid[:, 3]], axis=1
        ).astype(BF)
        d_mod = (
            d_mod.reshape(FRAMES, 6, groups, D // groups).transpose(2, 0, 1, 3).reshape(groups, FRAMES, -1)
        )
        pieces = [lax.dynamic_index_in_dim(d_mod, z, axis=0, keepdims=False)]
        for s in range(1, groups):
            pieces.append(z_put(lax.dynamic_index_in_dim(d_mod, (z + s) % groups, axis=0, keepdims=False), s))
        d_mod = plane_double(jnp.stack(pieces)).reshape(chips * groups * FRAMES, -1)
        back_clip = (z + groups - jnp.arange(groups, dtype=jnp.int32)) % groups
        clip_hot = (back_clip[:, None] == jnp.arange(groups, dtype=jnp.int32)[None, :]).astype(jnp.int32)
        order = jnp.sum(clip_hot[None, :, :, None] * all_levels[:, None, :, :], axis=2).reshape(-1)
        all_embedded = dot((order[:, None] == level_ids).astype(BF), table, NN).astype(BF)
        d_w_mod = dot(all_embedded, d_mod, TN).astype(BF)
        own_levels = level_table.shape[0]
        own_hot = (
            order[:, None] == device * own_levels + jnp.arange(own_levels, dtype=jnp.int32)[None, :]
        ).astype(BF)
        own_rows = dot(dot(own_hot, d_mod, TN).astype(BF), w_mod, NT)
        own_rows = own_rows.reshape(groups, own_levels // groups, D)
        table_grad = lax.dynamic_index_in_dim(own_rows, z, axis=0, keepdims=False)
        for s in range(1, groups):
            table_grad = table_grad + z_put(
                lax.dynamic_index_in_dim(own_rows, (z + s) % groups, axis=0, keepdims=False), s
            )

    with jax.named_scope("owners"):
        reduced = jnp.concatenate([red_attn, red_up, red_down], axis=0)
        if chips == 4:
            height = reduced.shape[0]
            plane_parts = plane_gather(reduced.reshape(2, height // 2, D)).reshape(chips, height, D)
        else:
            plane_parts = plane_double(reduced)
        everyone = jnp.stack([plane_parts, across(plane_parts)], axis=1).reshape(owners, -1, D)
        tile_ids = lax.dynamic_slice_in_dim(owner_list, device * slots, slots)
        rates = kind_rates(tile_ids, counts)
        if fast:
            picks = pick_table(tile_ids, device)
            sources = [everyone, d_w_mod]
        else:
            picks = jnp.zeros((slots, 12), jnp.int32)
            absolute = jnp.take(
                everyone, jnp.bitwise_xor(jnp.arange(owners, dtype=jnp.int32), device), axis=0
            ).reshape(chips, 2, -1, D)
            attn = absolute[:, :, : 4 * rows].reshape(chips, 2, 4, rows, D)
            attn = attn.transpose(2, 1, 0, 3, 4).reshape(4, -1, D)
            ffn_rows = (absolute.shape[2] - 4 * rows) // 2
            up = absolute[:, :, 4 * rows : 4 * rows + ffn_rows].transpose(1, 0, 2, 3).reshape(-1, D)
            down = absolute[:, :, 4 * rows + ffn_rows :].transpose(1, 0, 2, 3).reshape(-1, D)
            g_in = jnp.concatenate([attn[0].T, attn[1].T, attn[2].T], axis=1)
            packed = pack([g_in, attn[3], up.T, down, d_w_mod])
            sources = [jnp.take(packed, tile_ids, axis=0)]
        new_masters, new_one, new_two, new_weights = adam(
            picks, rates, sources, masters[0], moment_one[0], moment_two[0], basis_left[0], basis_right[0]
        )
    return (
        block_output,
        input_grad,
        table_grad,
        new_masters[None],
        new_one[None],
        new_two[None],
        new_weights[None],
    )


def solution(mesh):
    tiles = P("mp", "dp", None, None)
    in_specs = (
        P("dp", None),
        P("dp", None),
        P("dp", None),
        P("dp"),
        P("dp"),
        P(),
        P("dp", None),
        P(),
        tiles,
        tiles,
        tiles,
        tiles,
        tiles,
    )
    out_specs = (P("dp", None), P("dp", None), P(("dp", "mp"), None), tiles, tiles, tiles, tiles)
    return jax.shard_map(body, mesh=mesh, in_specs=in_specs, out_specs=out_specs, check_vma=False)
```

```python
import functools

import jax
import jax.numpy as jnp
from jax import lax
from jax.experimental import pallas as pl
from jax.experimental.pallas import tpu as pltpu
from jax.sharding import PartitionSpec as P

D = 1024
H = 16
HD = 64
FF = 4096
FRAMES = 16
FRAME_TOK = 64
LEVELS = 1024
PATTERNS = 4
TILE = 128
CLIP = FRAMES * FRAME_TOK

EPS_NORM = 1e-06
BETA_ONE = 0.5
BETA_TWO = 0.75
EPS_ADAM = 1e-08
DECAY = 0.01
LOG2E = 1.4426950408889634
GELU_A = 0.7978845608028654
GELU_B = 0.044715

BF = jnp.bfloat16
F32 = jnp.float32
VMEM_BYTES = 60 * 1024 * 1024


def params(**kw):
    return pltpu.CompilerParams(vmem_limit_bytes=VMEM_BYTES, **kw)


def cost(flops, nbytes, trans=0):
    return pl.CostEstimate(flops=int(flops), bytes_accessed=int(nbytes), transcendentals=int(trans))


def dot(left, right, dims):
    return lax.dot_general(left, right, (dims, ((), ())), preferred_element_type=F32)


NN = ((1,), (0,))
NT = ((1,), (1,))
TN = ((0,), (0,))


def tile_layout(groups):
    local_width = H // groups * HD
    shapes = [
        (D, 3 * local_width),
        (local_width, D),
        (D, FF // groups),
        (FF // groups, D),
        (D, 6 * D // groups),
    ]
    counts = [height // TILE * (breadth // TILE) for height, breadth in shapes]
    return (shapes, counts)


def kind_rates(tile_ids, counts):
    scales = [
        0.35 * D ** (-0.5),
        1.5 * (H * HD) ** (-0.5),
        0.5 * D ** (-0.5),
        0.5 * FF ** (-0.5),
        0.5 * D ** (-0.5),
    ]
    tile_rates = jnp.full(tile_ids.shape, scales[0], F32)
    boundary = 0
    for category in range(1, 5):
        boundary = boundary + counts[category - 1]
        tile_rates = jnp.where(tile_ids >= boundary, jnp.float32(scales[category]), tile_rates)
    return tile_rates


def unpack(tile_stack, shapes, counts):
    matrices = []
    offset = 0
    for (height, breadth), amount in zip(shapes, counts):
        stacked = tile_stack[offset : offset + amount].reshape(
            height // TILE, breadth // TILE, TILE, TILE
        )
        matrices.append(stacked.transpose(0, 2, 1, 3).reshape(height, breadth))
        offset = offset + amount
    return matrices


def pack(matrices):
    stacked = []
    for matrix in matrices:
        height, breadth = matrix.shape
        stacked.append(
            matrix.reshape(height // TILE, TILE, breadth // TILE, TILE)
            .transpose(0, 2, 1, 3)
            .reshape(-1, TILE, TILE)
        )
    return jnp.concatenate(stacked, axis=0)


def pick_chunk_plain(gathered, inverse, chip, core, chips, shapes, counts):
    w_qkv, w_out, w_up, w_down, w_mod = unpack(jnp.take(gathered, inverse, axis=0), shapes, counts)
    width = w_out.shape[0]
    half = width // 2
    ffn = w_up.shape[1] // 2
    rows, ffn_rows = half // chips, ffn // chips
    parts = []
    for role in range(3):
        parts.append(w_qkv[:, role * width : (role + 1) * width].T)
    parts.append(w_out)
    start = core * half + chip * rows
    attn = jnp.concatenate([lax.dynamic_slice_in_dim(p, start, rows, axis=0) for p in parts], axis=0)
    ffn_start = core * ffn + chip * ffn_rows
    up = lax.dynamic_slice_in_dim(w_up.T, ffn_start, ffn_rows, axis=0)
    down = lax.dynamic_slice_in_dim(w_down, ffn_start, ffn_rows, axis=0)
    return attn, up, down, w_mod


def norm_rows(values):
    centered = values - jnp.mean(values, axis=-1, keepdims=True)
    inverse_std = lax.rsqrt(jnp.mean(centered * centered, axis=-1, keepdims=True) + EPS_NORM)
    return centered * inverse_std, inverse_std


def norm_back(grad_normed, normed, inverse_std):
    centered = grad_normed - jnp.mean(grad_normed, axis=-1, keepdims=True)
    return inverse_std * (centered - normed * jnp.mean(grad_normed * normed, axis=-1, keepdims=True))


def frames_of(rows):
    return rows.reshape(-1, FRAME_TOK, D)


def flat(framed):
    return framed.reshape(-1, D)


BLK = 256
FBLK = BLK // FRAME_TOK


def row_spec():
    return pl.BlockSpec((BLK, D), lambda i: (i, 0))


def mod_spec(parts):
    return pl.BlockSpec((FBLK, parts, D), lambda i: (i, 0, 0))


def row_call(kernel, name, row_ins, mods, row_outs, mod_outs, nbytes):
    outs = [jax.ShapeDtypeStruct((CLIP, D), t) for t in row_outs]
    outs += [jax.ShapeDtypeStruct((FRAMES, n, D), F32) for n in mod_outs]
    return pl.pallas_call(
        kernel,
        grid=(CLIP // BLK,),
        in_specs=[row_spec() for _ in row_ins] + [mod_spec(6)],
        out_specs=[row_spec() for _ in row_outs] + [mod_spec(n) for n in mod_outs],
        out_shape=outs,
        compiler_params=params(),
        cost_estimate=cost(30 * CLIP * D, nbytes),
        name=name,
    )(*row_ins, mods)


def first_norm_kernel(x_ref, mod_ref, h_ref):
    normed, _ = norm_rows(x_ref[...].astype(F32))
    mods = mod_ref[...]
    h_ref[...] = flat(
        frames_of(normed) * (1.0 + mods[:, 1:2]) + mods[:, 0:1]
    ).astype(BF)


def middle_kernel(x_ref, a_ref, b_ref, dy_ref, mod_ref, y_ref, s_ref, h_ref, de_ref):
    mods = mod_ref[...]
    branch = (a_ref[...].astype(F32) + b_ref[...].astype(F32)).astype(BF)
    s_ref[...] = branch
    mid = frames_of(x_ref[...].astype(F32)) + mods[:, 2:3] * frames_of(branch.astype(F32))
    y_ref[...] = flat(mid)
    normed, _ = norm_rows(flat(mid))
    h_ref[...] = flat(
        frames_of(normed) * (1.0 + mods[:, 4:5]) + mods[:, 3:4]
    ).astype(BF)
    de_ref[...] = flat(mods[:, 5:6] * frames_of(dy_ref[...].astype(F32))).astype(BF)


def back_kernel(y_ref, g_ref, gp_ref, dy_ref, s_ref, e_ref, ep_ref, mod_ref, out_ref, dy1_ref, da_ref, dm_ref):
    mods = mod_ref[...]
    mid = y_ref[...]
    feed = e_ref[...].astype(F32) + ep_ref[...].astype(F32)
    dy = dy_ref[...].astype(F32)
    out_ref[...] = (mid + flat(mods[:, 5:6] * frames_of(feed))).astype(BF)
    normed, inverse_std = norm_rows(mid)
    grad = g_ref[...].astype(F32) + gp_ref[...].astype(F32)
    dm_ref[:, 0] = jnp.sum(frames_of(grad), axis=1)
    dm_ref[:, 1] = jnp.sum(frames_of(grad * normed), axis=1)
    scaled = flat(frames_of(grad) * (1.0 + mods[:, 4:5]))
    dy1 = dy + norm_back(scaled, normed, inverse_std)
    dy1_ref[...] = dy1
    dm_ref[:, 2] = jnp.sum(frames_of(dy1 * s_ref[...].astype(F32)), axis=1)
    dm_ref[:, 3] = jnp.sum(frames_of(dy * feed), axis=1)
    da_ref[...] = flat(mods[:, 2:3] * frames_of(dy1)).astype(BF)


def last_kernel(x_ref, g_ref, gp_ref, dy1_ref, mod_ref, out_ref, dm_ref):
    mods = mod_ref[...]
    normed, inverse_std = norm_rows(x_ref[...].astype(F32))
    grad = g_ref[...].astype(F32) + gp_ref[...].astype(F32)
    dm_ref[:, 0] = jnp.sum(frames_of(grad), axis=1)
    dm_ref[:, 1] = jnp.sum(frames_of(grad * normed), axis=1)
    scaled = flat(frames_of(grad) * (1.0 + mods[:, 1:2]))
    out_ref[...] = (dy1_ref[...] + norm_back(scaled, normed, inverse_std)).astype(BF)


MESH = pl.DeviceIdType.MESH
HEAD_TILES = 36
TABLE_TILES = 8
PAYLOAD = 46
LEVEL_TILE = HEAD_TILES + TABLE_TILES


class Link:
    def __init__(self, sends, recvs):
        self.sends, self.recvs, self.used, self.pending = sends, recvs, 0, []

    def make(self, src, dst, dp, mp):
        copy = pltpu.make_async_remote_copy(
            src_ref=src,
            dst_ref=dst,
            send_sem=self.sends.at[self.used],
            recv_sem=self.recvs.at[self.used],
            device_id=(dp, mp),
            device_id_type=MESH,
        )
        self.used += 1
        return copy

    def send(self, src, dst, dp, mp):
        copy = self.make(src, dst, dp, mp)
        copy.start()
        self.pending.append(copy)
        return copy

    def drain(self):
        for copy in self.pending:
            copy.wait_send()
        self.pending = []


def greet(d, z):
    barrier = pltpu.get_barrier_semaphore()
    for step in (1, 2, 4):
        pl.semaphore_signal(barrier, inc=1, device_id=(jnp.bitwise_xor(d, step), z), device_id_type=MESH)
    for s in (1, 2, 3):
        pl.semaphore_signal(barrier, inc=1, device_id=(d, lax.rem(z + s, 4)), device_id_type=MESH)
    pl.semaphore_wait(barrier, 6)


ENTRY_COPIES = 8 + 45 + 3


def entry_kernel(
    idx_ref,
    pay_ref,
    act_ref,
    cot_ref,
    bias_ref,
    w_ref,
    wmod_ref,
    x_ref,
    dy_ref,
    h_ref,
    mods_ref,
    bias_out,
    emb_ref,
    own_hot_ref,
    gath,
    own,
    turn,
    xs,
    dys,
    bs,
    part,
    modbuf,
    hots,
    sends,
    recvs,
    swap_sends,
    swap_recvs,
    local_sems,
):
    d, z = lax.axis_index("dp"), lax.axis_index("mp")
    core, chip = lax.rem(d, 2), d // 2
    dk, dx, dy = jnp.bitwise_xor(d, 1), jnp.bitwise_xor(d, 2), jnp.bitwise_xor(d, 4)
    dxy = jnp.bitwise_xor(d, 6)
    link = Link(sends, recvs)
    greet(d, z)

    def slot(owner, first=0, count=PAYLOAD):
        return gath.at[pl.ds(owner * PAYLOAD + first, count)]

    half = PAYLOAD // 2
    home = pltpu.make_async_copy(pay_ref, slot(d), local_sems.at[0])
    home.start()
    to_x = link.send(pay_ref, slot(d), dx, z)
    to_y = link.send(pay_ref, slot(d), dy, z)
    to_k = link.send(pay_ref, slot(d), dk, z)

    holds = (z // 2) == core
    rows = pl.ds(lax.rem(z, 2) * CLIP, CLIP)
    picks = [
        (act_ref.at[rows], xs),
        (cot_ref.at[rows], dys),
        (bias_ref.at[lax.rem(z, 2)], bs),
    ]

    def swaps():
        return [
            pltpu.make_async_remote_copy(
                src_ref=src,
                dst_ref=dst,
                send_sem=swap_sends.at[i],
                recv_sem=swap_recvs.at[i],
                device_id=(dk, z),
                device_id_type=MESH,
            )
            for i, (src, dst) in enumerate(picks)
        ]

    def keeps():
        return [pltpu.make_async_copy(src, dst, local_sems.at[1 + i]) for i, (src, dst) in enumerate(picks)]

    @pl.when(holds)
    def _():
        for copy in swaps() + keeps():
            copy.start()

    to_x.wait_recv()
    x_to_y = link.send(slot(dx, 0, half), slot(dx, 0, half), dy, z)
    x_to_k = link.send(slot(dx), slot(dx), dk, z)
    to_y.wait_recv()
    y_to_x = link.send(slot(dy, half, half), slot(dy, half, half), dx, z)
    y_to_k = link.send(slot(dy), slot(dy), dk, z)

    @pl.when(holds)
    def _():
        for copy in swaps():
            copy.wait_send()
        for copy in keeps():
            copy.wait()

    @pl.when(jnp.logical_not(holds))
    def _():
        for copy in swaps():
            copy.wait_recv()

    x_ref[...] = xs[...]
    dy_ref[...] = dys[...]
    bias_out[...] = bs[...]

    x_to_y.wait_recv()
    y_to_x.wait_recv()
    xy_to_k = link.send(slot(dxy), slot(dxy), dk, z)
    home.wait()
    to_k.wait_recv()
    x_to_k.wait_recv()
    y_to_k.wait_recv()
    xy_to_k.wait_recv()

    def tile(number):
        return gath[idx_ref[number]]

    def pick_attn(j, _):
        lanes = pl.ds(pl.multiple_of(j * TILE, TILE), TILE)
        for role in range(3):
            turn[role] = tile(j * 6 + 2 * role + core).T
        turn[3] = tile(48 + core * 8 + j)
        for role in range(4):
            own[0, role * 32 : (role + 1) * 32, lanes] = turn[role, pl.ds(pl.multiple_of(chip * 32, 32), 32), :]
        return 0

    def pick_feed(j, _):
        lanes = pl.ds(pl.multiple_of(j * TILE, TILE), TILE)
        own[1, :, lanes] = tile(64 + j * 8 + 4 * core + chip).T
        own[2, :, lanes] = tile(128 + (4 * core + chip) * 8 + j)
        return 0

    def pick_mod(j, _):
        strip = pl.ds(pl.multiple_of(j * TILE, TILE), TILE)
        for col in range(12):
            wmod_ref[strip, col * TILE : (col + 1) * TILE] = tile(192 + j * 12 + col)
        return 0

    along, by_x, by_y, diag, homes = {}, {}, {}, {}, []

    def send_along(g):
        for s in (1, 3, 2):
            along[g, s] = link.send(own.at[g], w_ref.at[g, 0, z], d, lax.rem(z + s, 4))

    def send_plane(g, s):
        m = lax.rem(z + 4 - s, 4)
        src = own.at[g] if s == 0 else w_ref.at[g, 0, m]
        by_x[g, s] = link.send(src, w_ref.at[g, 1, m], dx, z)
        by_y[g, s] = link.send(src, w_ref.at[g, 2, m], dy, z)

    def send_diag(g, s):
        m = lax.rem(z + 4 - s, 4)
        if s < 2:
            by_x[g, s].wait_recv()
            diag[g, s] = link.send(w_ref.at[g, 1, m], w_ref.at[g, 3, m], dy, z)
        else:
            by_y[g, s].wait_recv()
            diag[g, s] = link.send(w_ref.at[g, 2, m], w_ref.at[g, 3, m], dx, z)

    def keep_home(g):
        copy = pltpu.make_async_copy(own.at[g], w_ref.at[g, 0, z], local_sems.at[4 + g])
        copy.start()
        homes.append(copy)

    lax.fori_loop(0, 8, pick_attn, 0)
    lax.fori_loop(0, 8, pick_feed, 0)
    send_along(0)
    send_plane(0, 0)
    keep_home(0)
    send_along(1)
    send_along(2)
    send_plane(1, 0)
    keep_home(1)
    keep_home(2)

    lax.fori_loop(0, 8, pick_mod, 0)
    places = lax.broadcasted_iota(jnp.int32, (32, LEVELS), 1).astype(F32)
    for owner in range(8):
        codes = gath[owner * PAYLOAD + LEVEL_TILE][:32].astype(F32)
        level = codes[:, 0:1] * 32.0 + codes[:, 64:65]
        hots[owner * 32 : (owner + 1) * 32] = jnp.where(level == places, 1.0, 0.0).astype(BF)
    own_hot_ref[...] = hots[:, pl.ds(pl.multiple_of(d * TILE, TILE), TILE)]
    for j in range(TABLE_TILES):
        strip = jnp.concatenate([gath[owner * PAYLOAD + HEAD_TILES + j] for owner in range(8)], axis=0)
        emb_ref[:, j * TILE : (j + 1) * TILE] = dot(hots[...], strip, NN).astype(BF)
    embedded = emb_ref[pl.ds(pl.multiple_of(chip * 64, 64), 64), :]
    part[...] = dot(embedded, wmod_ref[...], NN).reshape(4, FRAMES, 12 * TILE)
    modbuf[z] = part[z]
    shared = {}
    for s in (1, 3, 2):
        shared[s] = link.send(part.at[lax.rem(z + s, 4)], modbuf.at[z], d, lax.rem(z + s, 4))

    for s in (1, 3, 2):
        along[0, s].wait_recv()
        send_plane(0, s)
    send_plane(2, 0)
    for s in (0, 1, 3, 2):
        send_diag(0, s)

    for s in (1, 3, 2):
        shared[s].wait_recv()
    for m in range(4):
        for c in range(6):
            mods_ref[:, c, m * 256 : (m + 1) * 256] = modbuf[m, :, c * 256 : (c + 1) * 256]

    def norm_strip(i, _):
        strip = pl.ds(pl.multiple_of(i * BLK, BLK), BLK)
        normed, _ = norm_rows(xs[strip].astype(F32))
        mods = mods_ref[pl.ds(i * FBLK, FBLK)]
        h_ref[strip] = flat(frames_of(normed) * (1.0 + mods[:, 1:2]) + mods[:, 0:1]).astype(BF)
        return 0

    lax.fori_loop(0, CLIP // BLK, norm_strip, 0)

    for s in (1, 3, 2):
        along[1, s].wait_recv()
        send_plane(1, s)
    for s in (1, 3, 2):
        along[2, s].wait_recv()
        send_plane(2, s)
    for g in (1, 2):
        for s in (0, 1, 3, 2):
            send_diag(g, s)
    for g in range(3):
        for s in range(4):
            (by_y if s < 2 else by_x)[g, s].wait_recv()
            diag[g, s].wait_recv()
    for copy in homes:
        copy.wait()
    link.drain()


def entry(masters, level_table, levels, bias_pair, activations, cotangent, owner_list):
    slots = masters.shape[0]
    codes = jnp.stack([levels.reshape(-1) // 32, levels.reshape(-1) % 32], axis=1).astype(BF)
    codes = jnp.pad(jnp.repeat(codes, 64, axis=1), ((0, TILE - codes.shape[0]), (0, 0)))
    payload = jnp.concatenate(
        [
            masters.astype(BF),
            level_table.reshape(TILE, TABLE_TILES, TILE).transpose(1, 0, 2),
            codes[None],
            jnp.zeros((1, TILE, TILE), BF),
        ]
    )
    position = jnp.arange(owner_list.shape[0], dtype=jnp.int32)
    place = (position // slots) * PAYLOAD + position % slots
    index = jnp.sum(
        jnp.where(owner_list[None, :] == position[:, None], place[None, :], 0), axis=1
    ).astype(jnp.int32)
    vmem = pl.BlockSpec(memory_space=pltpu.VMEM)
    hbm = pl.BlockSpec(memory_space=pl.ANY)
    return pl.pallas_call(
        entry_kernel,
        in_specs=[pl.BlockSpec(memory_space=pltpu.SMEM), hbm, hbm, hbm, hbm],
        out_specs=[hbm] + [vmem] * 8,
        out_shape=[
            jax.ShapeDtypeStruct((3, 4, 4, TILE, D), BF),
            jax.ShapeDtypeStruct((D, 12 * TILE), BF),
            jax.ShapeDtypeStruct((CLIP, D), BF),
            jax.ShapeDtypeStruct((CLIP, D), BF),
            jax.ShapeDtypeStruct((CLIP, D), BF),
            jax.ShapeDtypeStruct((FRAMES, 6, D), F32),
            jax.ShapeDtypeStruct((FRAMES, CLIP), F32),
            jax.ShapeDtypeStruct((256, D), BF),
            jax.ShapeDtypeStruct((256, TILE), BF),
        ],
        scratch_shapes=[
            pltpu.VMEM((8 * PAYLOAD, TILE, TILE), BF),
            pltpu.VMEM((3, TILE, D), BF),
            pltpu.VMEM((4, TILE, TILE), BF),
            pltpu.VMEM((CLIP, D), BF),
            pltpu.VMEM((CLIP, D), BF),
            pltpu.VMEM((FRAMES, CLIP), F32),
            pltpu.VMEM((4, FRAMES, 12 * TILE), F32),
            pltpu.VMEM((4, FRAMES, 12 * TILE), F32),
            pltpu.VMEM((256, LEVELS), BF),
            pltpu.SemaphoreType.DMA((ENTRY_COPIES,)),
            pltpu.SemaphoreType.DMA((ENTRY_COPIES,)),
            pltpu.SemaphoreType.DMA((3,)),
            pltpu.SemaphoreType.DMA((3,)),
            pltpu.SemaphoreType.DMA((7,)),
        ],
        compiler_params=params(collective_id=0, has_side_effects=True),
        cost_estimate=cost(1e9, 40e6),
        name="entry",
    )(index, payload, activations, cotangent, bias_pair)


QBLK = 256
SCALE2 = HD ** (-0.5) * LOG2E


def attend_kernel(qkv_ref, bias_ref, o_ref, lse_ref):
    for head in range(2):
        lanes = slice(head * HD, (head + 1) * HD)
        keys = qkv_ref[:, TILE + head * HD : TILE + (head + 1) * HD]
        values = qkv_ref[:, 2 * TILE + head * HD : 2 * TILE + (head + 1) * HD]

        def step(i, _, lanes=lanes, keys=keys, values=values, head=head):
            start = pl.multiple_of(i * QBLK, QBLK)
            queries = qkv_ref[pl.ds(start, QBLK), lanes]
            scores = dot(keys, queries, NT).reshape(FRAMES, FRAME_TOK, QBLK)
            scores = scores * SCALE2 + bias_ref[:, pl.ds(start, QBLK)][:, None, :]
            peak = jnp.max(jnp.max(scores, axis=0), axis=0, keepdims=True)
            weights = jnp.exp2(scores - peak[None])
            total = jnp.sum(jnp.sum(weights, axis=0), axis=0, keepdims=True)
            mixed = dot(values, weights.reshape(CLIP, QBLK).astype(BF), TN)
            o_ref[lanes, pl.ds(start, QBLK)] = (mixed / total).astype(BF)
            lse_ref[0, head : head + 1, pl.ds(start, QBLK)] = peak + jnp.log2(total)
            return 0

        lax.fori_loop(0, CLIP // QBLK, step, 0)


def attend(qkv, bias):
    groups = qkv.shape[1] // (3 * TILE)
    return pl.pallas_call(
        attend_kernel,
        grid=(groups,),
        in_specs=[
            pl.BlockSpec((CLIP, 3 * TILE), lambda m: (0, m)),
            pl.BlockSpec((FRAMES, CLIP), lambda m: (0, 0)),
        ],
        out_specs=[
            pl.BlockSpec((TILE, CLIP), lambda m: (m, 0)),
            pl.BlockSpec((1, 2, CLIP), lambda m: (m, 0, 0)),
        ],
        out_shape=[
            jax.ShapeDtypeStruct((groups * TILE, CLIP), BF),
            jax.ShapeDtypeStruct((groups, 2, CLIP), F32),
        ],
        compiler_params=params(),
        cost_estimate=cost(groups * 2 * 4 * CLIP * CLIP * HD * 3, 2 * qkv.size, groups * 2 * CLIP * CLIP),
        name="attend",
    )(qkv, bias)


def attend_back_kernel(qkv_ref, o_ref, do_ref, lse_ref, bias_ref, out_ref, dk_ref, dv_ref):
    for head in range(2):
        lanes = slice(head * HD, (head + 1) * HD)
        keys = qkv_ref[:, TILE + head * HD : TILE + (head + 1) * HD]
        values = qkv_ref[:, 2 * TILE + head * HD : 2 * TILE + (head + 1) * HD]
        dk_ref[...] = jnp.zeros_like(dk_ref)
        dv_ref[...] = jnp.zeros_like(dv_ref)

        def step(i, _, lanes=lanes, keys=keys, values=values, head=head):
            start = pl.multiple_of(i * QBLK, QBLK)
            across = pl.ds(start, QBLK)
            queries = qkv_ref[across, lanes]
            grad = do_ref[lanes, across]
            shift = bias_ref[:, across] - lse_ref[0, head : head + 1, across]
            scores = dot(keys, queries, NT).reshape(FRAMES, FRAME_TOK, QBLK)
            soft = jnp.exp2(scores * SCALE2 + shift[:, None, :]).reshape(CLIP, QBLK)
            delta = jnp.sum(
                grad.astype(F32) * o_ref[lanes, across].astype(F32), axis=0, keepdims=True
            )
            grad_soft = dot(values, grad, NN)
            grad_scores = (soft * (grad_soft - delta)).astype(BF)
            dv_ref[...] += dot(soft.astype(BF), grad, NT)
            dk_ref[...] += dot(grad_scores, queries, NN)
            grad_query = dot(keys, grad_scores, TN) * HD ** (-0.5)
            out_ref[across, lanes] = grad_query.T.astype(BF)
            return 0

        lax.fori_loop(0, CLIP // QBLK, step, 0)
        out_ref[:, TILE + head * HD : TILE + (head + 1) * HD] = (dk_ref[...] * HD ** (-0.5)).astype(BF)
        out_ref[:, 2 * TILE + head * HD : 2 * TILE + (head + 1) * HD] = dv_ref[...].astype(BF)


def attend_back(qkv, o_rows, do_rows, lse, bias):
    groups = qkv.shape[1] // (3 * TILE)
    return pl.pallas_call(
        attend_back_kernel,
        grid=(groups,),
        in_specs=[
            pl.BlockSpec((CLIP, 3 * TILE), lambda m: (0, m)),
            pl.BlockSpec((TILE, CLIP), lambda m: (m, 0)),
            pl.BlockSpec((TILE, CLIP), lambda m: (m, 0)),
            pl.BlockSpec((1, 2, CLIP), lambda m: (m, 0, 0)),
            pl.BlockSpec((FRAMES, CLIP), lambda m: (0, 0)),
        ],
        out_specs=pl.BlockSpec((CLIP, 3 * TILE), lambda m: (0, m)),
        out_shape=jax.ShapeDtypeStruct(qkv.shape, BF),
        scratch_shapes=[pltpu.VMEM((CLIP, HD), F32), pltpu.VMEM((CLIP, HD), F32)],
        compiler_params=params(),
        cost_estimate=cost(groups * 2 * 10 * CLIP * CLIP * HD * 3, 4 * qkv.size, groups * 2 * CLIP * CLIP),
        name="attend_back",
    )(qkv, o_rows, do_rows, lse, bias)


UNITS = 256
ROWS = 512


def feed_kernel(h_ref, de_ref, up_ref, down_ref, e_ref, dh_ref, dup_ref, ddown_ref, e_acc, dh_acc, up_acc, down_acc):
    block = pl.program_id(0)
    last = pl.num_programs(0) - 1
    up = up_ref[...]
    down = down_ref[...]
    for part in range(CLIP // ROWS):
        rows = slice(part * ROWS, (part + 1) * ROWS)
        hidden = h_ref[rows]
        grad = de_ref[rows]
        pre = dot(hidden, up, NT)
        square = pre * pre
        tanh = jnp.tanh(GELU_A * pre * (1.0 + GELU_B * square))
        act = (0.5 * pre * (1.0 + tanh)).astype(BF)
        slope = 0.5 * (1.0 + tanh) + 0.5 * pre * (1.0 - tanh * tanh) * (
            GELU_A * (1.0 + 3.0 * GELU_B * square)
        )
        grad_act = dot(grad, down, NT).astype(BF).astype(F32)
        grad_pre = (grad_act * slope).astype(BF)
        feed = dot(act, down, NN)
        back = dot(grad_pre, up, NN)

        @pl.when(block == 0)
        def _():
            e_acc[rows] = feed
            dh_acc[rows] = back

        @pl.when(block > 0)
        def _():
            e_acc[rows] += feed
            dh_acc[rows] += back

        if part == 0:
            down_acc[...] = dot(act, grad, TN)
            up_acc[...] = dot(grad_pre, hidden, TN)
        else:
            ddown_ref[...] = (down_acc[...] + dot(act, grad, TN)).astype(BF)
            dup_ref[...] = (up_acc[...] + dot(grad_pre, hidden, TN)).astype(BF)

    @pl.when(block == last)
    def _():
        e_ref[...] = e_acc[...].astype(BF)
        dh_ref[...] = dh_acc[...].astype(BF)


def feed_both(hidden, grad, up, down):
    units = up.shape[0]
    whole = pl.BlockSpec((CLIP, D), lambda i: (0, 0))
    strip = pl.BlockSpec((UNITS, D), lambda i: (i, 0))
    return pl.pallas_call(
        feed_kernel,
        grid=(units // UNITS,),
        in_specs=[whole, whole, strip, strip],
        out_specs=[whole, whole, strip, strip],
        out_shape=[jax.ShapeDtypeStruct((CLIP, D), BF)] * 2 + [jax.ShapeDtypeStruct((units, D), BF)] * 2,
        scratch_shapes=[
            pltpu.VMEM((CLIP, D), F32),
            pltpu.VMEM((CLIP, D), F32),
            pltpu.VMEM((UNITS, D), F32),
            pltpu.VMEM((UNITS, D), F32),
        ],
        compiler_params=params(),
        cost_estimate=cost(12 * CLIP * D * units, 8 * CLIP * D + 8 * units * D, CLIP * units),
        name="feed_both",
    )(hidden, grad, up, down)


def adam_step(grad, left, right, one, two, master, rate):
    low_left, low_right = left.astype(BF), right.astype(BF)
    turned = dot(low_left, grad.astype(BF), TN)
    rotated = dot(turned.astype(BF), low_right, NN)
    new_one = BETA_ONE * one + (1.0 - BETA_ONE) * rotated
    new_two = BETA_TWO * two + (1.0 - BETA_TWO) * rotated * rotated
    direction = new_one / (jnp.sqrt(new_two) + EPS_ADAM)
    back = dot(low_left, direction.astype(BF), NN)
    back = dot(back.astype(BF), low_right, NT)
    return master - rate * (back + DECAY * master), new_one, new_two


def adam_kernel(tab_ref, rate_ref, *refs, picked, batch):
    if picked:
        red_ref, mod_ref = refs[:2]
        refs = refs[2:]
    else:
        grad_ref = refs[0]
        refs = refs[1:]
    master_ref, one_ref, two_ref, left_ref, right_ref, nm_ref, n1_ref, n2_ref, nw_ref = refs
    for slot in range(batch):
        tile = pl.program_id(0) * batch + slot
        if picked:
            col = pl.multiple_of(tab_ref[tile, 8] * TILE, TILE)
            pieces = [
                red_ref[
                    tab_ref[tile, i],
                    pl.ds(pl.multiple_of(tab_ref[tile, 4 + i] * 32, 32), 32),
                    pl.ds(col, TILE),
                ]
                for i in range(4)
            ]
            grad = jnp.concatenate(pieces, axis=0).astype(F32)
            mod_row = pl.multiple_of(tab_ref[tile, 9] * TILE, TILE)
            mod_col = pl.multiple_of(tab_ref[tile, 10] * TILE, TILE)
            mod_grad = mod_ref[pl.ds(mod_row, TILE), pl.ds(mod_col, TILE)].astype(F32)
            kind = tab_ref[tile, 11]
            grad = jnp.where(kind == 1, grad.T, jnp.where(kind == 2, mod_grad, grad))
        else:
            grad = grad_ref[slot].astype(F32)
        master, one, two = adam_step(
            grad, left_ref[slot], right_ref[slot], one_ref[slot], two_ref[slot], master_ref[slot], rate_ref[tile]
        )
        nm_ref[slot] = master
        n1_ref[slot] = one
        n2_ref[slot] = two
        nw_ref[slot] = master.astype(BF)


def pick_table(tiles, device):
    table = []
    piece = jnp.arange(4, dtype=jnp.int32)[None, :]
    t = tiles[:, None]
    is_in = t < 48
    is_out = (t >= 48) & (t < 64)
    is_up = (t >= 64) & (t < 128)
    is_down = (t >= 128) & (t < 192)
    is_mod = t >= 192
    q0, q1, q2, q3, q4 = t, t - 48, t - 64, t - 128, t - 192
    core = jnp.where(is_in, (q0 % 6) % 2, jnp.where(is_out, q1 // 8, jnp.where(is_up, (q2 % 8) // 4, (q3 // 8) // 4)))
    chip = jnp.where(is_up, q2 % 4, (q3 // 8) % 4)
    chip = jnp.where(is_in | is_out, piece, chip)
    source = jnp.where(is_mod, 0, jnp.bitwise_xor(2 * chip + core, device))
    row = jnp.where(is_in, (q0 % 6) // 2, jnp.where(is_out, 3, jnp.where(is_up, 4 + piece, 8 + piece)))
    row = jnp.where(is_mod, 0, row + jnp.zeros_like(piece))
    col = jnp.where(is_in, q0 // 6, jnp.where(is_out, q1 % 8, jnp.where(is_up, q2 // 8, q3 % 8)))
    col = jnp.where(is_mod, 0, col)
    mod_row = jnp.where(is_mod, q4 // 12, 0)
    mod_col = jnp.where(is_mod, q4 % 12, 0)
    kind = jnp.where(is_mod, 2, jnp.where(is_in | is_up, 1, 0))
    return jnp.concatenate([source, row, col, mod_row, mod_col, kind], axis=1).astype(jnp.int32)


def adam(table, rates, sources, master, one, two, left, right):
    slots = master.shape[0]
    batch = max(b for b in (4, 3, 2, 1) if slots % b == 0)
    picked = len(sources) == 2
    tiles = pl.BlockSpec((batch, TILE, TILE), lambda i, *_: (i, 0, 0))
    if picked:
        source_specs = [
            pl.BlockSpec(sources[0].shape, lambda i, *_: (0, 0, 0)),
            pl.BlockSpec(sources[1].shape, lambda i, *_: (0, 0)),
        ]
    else:
        source_specs = [tiles]
    return pl.pallas_call(
        functools.partial(adam_kernel, picked=picked, batch=batch),
        grid_spec=pltpu.PrefetchScalarGridSpec(
            num_scalar_prefetch=2,
            grid=(slots // batch,),
            in_specs=source_specs + [tiles] * 5,
            out_specs=[tiles] * 4,
        ),
        out_shape=[jax.ShapeDtypeStruct(master.shape, F32)] * 3 + [jax.ShapeDtypeStruct(master.shape, BF)],
        compiler_params=params(),
        cost_estimate=cost(slots * 8 * TILE**3, slots * TILE * TILE * 36),
        name="adam",
    )(table, rates, *sources, master, one, two, left, right)


def body(
    activations,
    cotangent,
    level_table,
    true_frames,
    group_pattern,
    noise_levels,
    context_flags,
    owner_list,
    masters,
    moment_one,
    moment_two,
    basis_left,
    basis_right,
):
    groups = lax.axis_size("mp")
    owners = lax.axis_size("dp")
    chips = owners // 2
    bits = chips.bit_length() - 1
    z = lax.axis_index("mp")
    device = lax.axis_index("dp")
    core = device % 2
    chip = device // 2
    local_clips = true_frames.shape[0]
    column_clips = 2 * local_clips
    assert column_clips == groups and chips == 1 << bits
    shapes, counts = tile_layout(groups)
    slots = masters.shape[1]
    fast = chips == 4 and groups == 4

    def swap(v, step):
        return lax.ppermute(v, "dp", [(i, i ^ step) for i in range(owners)])

    def across(v):
        return swap(v, 1)

    def plane(v, bit):
        return swap(v, 2 << bit)

    def z_get(v, s):
        return lax.ppermute(v, "mp", [((i + s) % groups, i) for i in range(groups)])

    def z_put(v, s):
        return lax.ppermute(v, "mp", [(i, (i + s) % groups) for i in range(groups)])

    def plane_double(v):
        held = v[None]
        for bit in range(bits):
            held = jnp.concatenate([held, plane(held, bit)], axis=0)
        return held

    def plane_gather(v):
        if chips != 4:
            return plane_double(v)
        half = v.shape[0] // 2
        by_x, by_y = plane(v, 0), plane(v, 1)
        low, high = plane(by_x[:half], 1), plane(by_y[half:], 0)
        return jnp.stack([v, by_x, by_y, jnp.concatenate([low, high], axis=0)])

    def add(a, b):
        return (a.astype(F32) + b.astype(F32)).astype(BF)

    def plane_reduce(v):
        if chips != 4:
            held = v
            for bit in reversed(range(bits)):
                half = 1 << bit
                held = add(held[:half], plane(held[half:], bit))
            return held[0]
        half = v.shape[1] // 2
        got_low = [plane(v[1, :half], 0), plane(v[3, :half], 0)]
        got_high = [plane(v[2, half:], 1), plane(v[3, half:], 1)]
        pass_low = plane(add(v[2, :half], got_low[1]), 1)
        pass_high = plane(add(v[1, half:], got_high[1]), 0)
        low = v[0, :half].astype(F32) + got_low[0].astype(F32) + pass_low.astype(F32)
        high = v[0, half:].astype(F32) + got_high[0].astype(F32) + pass_high.astype(F32)
        return jnp.concatenate([low, high], axis=0).astype(BF)

    def z_gather(v):
        return jnp.stack([v] + [z_get(v, s) for s in range(1, groups)])

    def z_reduce(v):
        if fast:
            v = lax.dynamic_slice_in_dim(jnp.concatenate([v, v]), z, groups, axis=0)
        total = v[0].astype(F32)
        for s in range(1, groups):
            total = total + z_put(v[s], s).astype(F32)
        return total

    frame_index = jnp.arange(FRAMES, dtype=jnp.int32)

    def mask_rows(flagged, lengths):
        valid = frame_index[None, :] < lengths[:, None]
        in_context = flagged & valid
        visible = valid[:, :, None] & (
            jnp.logical_not(in_context)[:, None, :] | in_context[:, :, None]
        )
        return jnp.repeat(jnp.where(visible, 0.0, -1e30).astype(F32), FRAME_TOK, axis=2)

    def level_rows(flagged, patterns):
        pattern_hot = (patterns[:, None] == jnp.arange(PATTERNS, dtype=jnp.int32)[None, :]).astype(
            jnp.int32
        )
        return jnp.where(
            flagged, 0, jnp.sum(pattern_hot[:, :, None] * noise_levels[None, :, :], axis=1)
        )

    rows = TILE // chips
    level_ids = jnp.arange(LEVELS, dtype=jnp.int32)[None, :]
    if fast:
        with jax.named_scope("entry"):
            flagged = context_flags == 1
            weights, w_mod, x, dy, h1, mods, bias, all_embedded, own_hot = entry(
                masters[0],
                level_table,
                level_rows(flagged, group_pattern),
                mask_rows(flagged, true_frames),
                activations,
                cotangent,
                owner_list,
            )
            got = weights[0].reshape(chips, groups, 4, rows, D)
            w_up = weights[1].reshape(-1, D)
            w_down = weights[2].reshape(-1, D)
    else:
        with jax.named_scope("entry"):
            holds = (z // local_clips) == core
            local = (z % local_clips) * CLIP
            pair = jnp.stack(
                [
                    lax.dynamic_slice_in_dim(activations, local, CLIP, axis=0),
                    lax.dynamic_slice_in_dim(cotangent, local, CLIP, axis=0),
                ]
            )
            pair = jnp.where(holds, pair, across(pair))
            x, dy = pair[0], pair[1]
            facts = jnp.concatenate(
                [context_flags, true_frames[:, None], group_pattern[:, None]], axis=1
            ).astype(jnp.int32)
            other = across(facts)
            facts = jnp.where(
                core == 0, jnp.concatenate([facts, other]), jnp.concatenate([other, facts])
            )
            flagged = facts[:, :FRAMES] == 1
            levels = level_rows(flagged, facts[:, FRAMES + 1])
            bias = lax.dynamic_index_in_dim(
                mask_rows(flagged, facts[:, FRAMES]), z, axis=0, keepdims=False
            )
            all_levels = plane_double(levels)

        with jax.named_scope("owner_gather"):
            gathered = lax.all_gather(masters[0].astype(BF), "dp", axis=0, tiled=True)
            table = lax.all_gather(level_table, "dp", axis=0, tiled=True)
            position = jnp.arange(owner_list.shape[0], dtype=jnp.int32)
            inverse = jnp.sum(
                jnp.where(owner_list[None, :] == position[:, None], position[None, :], 0), axis=1
            ).astype(jnp.int32)
            chunk_attn, chunk_up, chunk_down, w_mod = pick_chunk_plain(
                gathered, inverse, chip, core, chips, shapes, counts
            )

        with jax.named_scope("weights"):
            got = plane_gather(z_gather(chunk_attn)).reshape(chips, groups, 4, rows, D)
            w_up = plane_gather(z_gather(chunk_up)).reshape(-1, D)
            w_down = plane_gather(z_gather(chunk_down)).reshape(-1, D)

        with jax.named_scope("modulation"):
            hot = (levels.reshape(-1)[:, None] == level_ids).astype(BF)
            embedded = dot(hot, table, NN).astype(BF)
            mod_part = dot(embedded, w_mod, NN).reshape(column_clips, FRAMES, -1)
            pieces = [lax.dynamic_index_in_dim(mod_part, z, axis=0, keepdims=False)]
            for s in range(1, groups):
                piece = lax.dynamic_index_in_dim(
                    mod_part, (z + groups - s) % groups, axis=0, keepdims=False
                )
                pieces.append(z_get(piece, s))
            mods = lax.dynamic_slice_in_dim(
                jnp.stack(pieces + pieces), (groups - z) % groups, groups, axis=0
            )
            mods = (
                mods.reshape(groups, FRAMES, 6, D // groups).transpose(1, 2, 0, 3).reshape(FRAMES, 6, D)
            )
            (h1,) = row_call(first_norm_kernel, "first_norm", [x], mods, [BF], [], 4 * CLIP * D)

    w_in = got[:, :, :3].transpose(1, 2, 0, 3, 4).reshape(-1, D)
    w_out = got[:, :, 3].transpose(1, 0, 2, 3).reshape(-1, D)

    mb = CLIP * D
    with jax.named_scope("attention"):
        qkv = dot(h1, w_in, NT).astype(BF)
        o_rows, lse = attend(qkv, bias)
        part = dot(o_rows, w_out, TN).astype(BF)
        y1, branch, h2, de = row_call(
            middle_kernel, "middle", [x, part, across(part), dy], mods, [F32, BF, BF, BF], [], 18 * mb
        )

    with jax.named_scope("feed"):
        e_part, dh2_part, d_up, d_down = feed_both(h2, de, w_up, w_down)
        out, dy1, da, dm_mid = row_call(
            back_kernel,
            "back",
            [y1, dh2_part, across(dh2_part), dy, branch, e_part, across(e_part)],
            mods,
            [BF, F32, BF],
            [4],
            24 * mb,
        )
        shape = (chips, groups, -1, D)
        red_up = z_reduce(plane_reduce(d_up.reshape(shape))).astype(BF)
        red_down = z_reduce(plane_reduce(d_down.reshape(shape))).astype(BF)

    def to_column(rows_here):
        half = CLIP // 2
        mine = lax.dynamic_slice_in_dim(rows_here, core * half, half, axis=0)
        by_clip = [mine] + [z_get(mine, s) for s in range(1, groups)]
        by_clip = lax.dynamic_slice_in_dim(jnp.stack(by_clip + by_clip), (groups - z) % groups, groups, axis=0)
        keep = lax.dynamic_slice_in_dim(by_clip, core * local_clips, local_clips, axis=0)
        send = lax.dynamic_slice_in_dim(by_clip, (1 - core) * local_clips, local_clips, axis=0)
        got_half = across(send)
        both = jnp.where(
            core == 0, jnp.stack([keep, got_half], axis=1), jnp.stack([got_half, keep], axis=1)
        )
        return both.reshape(local_clips * CLIP, D)

    with jax.named_scope("block_output"):
        block_output = to_column(out)

    with jax.named_scope("attention_back"):
        do_rows = dot(w_out, da, NT).astype(BF)
        d_out = dot(o_rows, da, NN).astype(BF)
        d_qkv = attend_back(qkv, o_rows, do_rows, lse, bias)
        dh1_part = dot(d_qkv, w_in, NN).astype(BF)
        d_in = dot(d_qkv, h1, TN).astype(BF)
        in_grad, dm_last = row_call(
            last_kernel, "last", [x, dh1_part, across(dh1_part), dy1], mods, [BF], [2], 12 * mb
        )
        d_in = d_in.reshape(groups, 3, chips, rows, D).transpose(2, 0, 1, 3, 4)
        d_out = d_out.reshape(groups, 1, chips, rows, D).transpose(2, 0, 1, 3, 4)
        d_attn = jnp.concatenate([d_in, d_out], axis=2).reshape(chips, groups, 4 * rows, D)
        red_attn = z_reduce(plane_reduce(d_attn)).astype(BF)

    with jax.named_scope("input_grad"):
        input_grad = to_column(in_grad).astype(F32)

    with jax.named_scope("modulation_back"):
        d_mod = jnp.stack(
            [dm_last[:, 0], dm_last[:, 1], dm_mid[:, 2], dm_mid[:, 0], dm_mid[:, 1], dm_mid[:, 3]], axis=1
        ).astype(BF)
        d_mod = (
            d_mod.reshape(FRAMES, 6, groups, D // groups).transpose(2, 0, 1, 3).reshape(groups, FRAMES, -1)
        )
        pieces = [lax.dynamic_index_in_dim(d_mod, z, axis=0, keepdims=False)]
        for s in range(1, groups):
            pieces.append(z_put(lax.dynamic_index_in_dim(d_mod, (z + s) % groups, axis=0, keepdims=False), s))
        d_mod = jnp.stack(pieces)
        if fast:
            d_mod = lax.dynamic_slice_in_dim(
                jnp.concatenate([d_mod, d_mod])[::-1], groups - 1 - z, groups, axis=0
            )
            d_mod = jnp.take(plane_double(d_mod), jnp.bitwise_xor(jnp.arange(chips), chip), axis=0)
            d_mod = d_mod.reshape(chips * groups * FRAMES, -1)
        else:
            d_mod = plane_double(d_mod).reshape(chips * groups * FRAMES, -1)
            back_clip = (z + groups - jnp.arange(groups, dtype=jnp.int32)) % groups
            clip_hot = (back_clip[:, None] == jnp.arange(groups, dtype=jnp.int32)[None, :]).astype(
                jnp.int32
            )
            order = jnp.sum(clip_hot[None, :, :, None] * all_levels[:, None, :, :], axis=2).reshape(-1)
            all_embedded = dot((order[:, None] == level_ids).astype(BF), table, NN).astype(BF)
            own_levels = level_table.shape[0]
            own_ids = device * own_levels + jnp.arange(own_levels, dtype=jnp.int32)[None, :]
            own_hot = (order[:, None] == own_ids).astype(BF)
        d_w_mod = dot(all_embedded, d_mod, TN).astype(BF)
        own_levels = level_table.shape[0]
        own_rows = dot(dot(own_hot, d_mod, TN).astype(BF), w_mod, NT)
        own_rows = own_rows.reshape(groups, own_levels // groups, D)
        table_grad = lax.dynamic_index_in_dim(own_rows, z, axis=0, keepdims=False)
        for s in range(1, groups):
            table_grad = table_grad + z_put(
                lax.dynamic_index_in_dim(own_rows, (z + s) % groups, axis=0, keepdims=False), s
            )

    with jax.named_scope("owners"):
        reduced = jnp.concatenate([red_attn, red_up, red_down], axis=0)
        if chips == 4:
            height = reduced.shape[0]
            plane_parts = plane_gather(reduced.reshape(2, height // 2, D)).reshape(chips, height, D)
        else:
            plane_parts = plane_double(reduced)
        everyone = jnp.stack([plane_parts, across(plane_parts)], axis=1).reshape(owners, -1, D)
        tile_ids = lax.dynamic_slice_in_dim(owner_list, device * slots, slots)
        rates = kind_rates(tile_ids, counts)
        if fast:
            picks = pick_table(tile_ids, device)
            sources = [everyone, d_w_mod]
        else:
            picks = jnp.zeros((slots, 12), jnp.int32)
            absolute = jnp.take(
                everyone, jnp.bitwise_xor(jnp.arange(owners, dtype=jnp.int32), device), axis=0
            ).reshape(chips, 2, -1, D)
            attn = absolute[:, :, : 4 * rows].reshape(chips, 2, 4, rows, D)
            attn = attn.transpose(2, 1, 0, 3, 4).reshape(4, -1, D)
            ffn_rows = (absolute.shape[2] - 4 * rows) // 2
            up = absolute[:, :, 4 * rows : 4 * rows + ffn_rows].transpose(1, 0, 2, 3).reshape(-1, D)
            down = absolute[:, :, 4 * rows + ffn_rows :].transpose(1, 0, 2, 3).reshape(-1, D)
            g_in = jnp.concatenate([attn[0].T, attn[1].T, attn[2].T], axis=1)
            packed = pack([g_in, attn[3], up.T, down, d_w_mod])
            sources = [jnp.take(packed, tile_ids, axis=0)]
        new_masters, new_one, new_two, new_weights = adam(
            picks, rates, sources, masters[0], moment_one[0], moment_two[0], basis_left[0], basis_right[0]
        )
    return (
        block_output,
        input_grad,
        table_grad,
        new_masters[None],
        new_one[None],
        new_two[None],
        new_weights[None],
    )


def solution(mesh):
    tiles = P("mp", "dp", None, None)
    in_specs = (
        P("dp", None),
        P("dp", None),
        P("dp", None),
        P("dp"),
        P("dp"),
        P(),
        P("dp", None),
        P(),
        tiles,
        tiles,
        tiles,
        tiles,
        tiles,
    )
    out_specs = (P("dp", None), P("dp", None), P(("dp", "mp"), None), tiles, tiles, tiles, tiles)
    return jax.shard_map(body, mesh=mesh, in_specs=in_specs, out_specs=out_specs, check_vma=False)
```

```python
import functools

import jax
import jax.numpy as jnp
from jax import lax
from jax.experimental import pallas as pl
from jax.experimental.pallas import tpu as pltpu
from jax.sharding import PartitionSpec as P

D = 1024
H = 16
HD = 64
FF = 4096
FRAMES = 16
FRAME_TOK = 64
LEVELS = 1024
PATTERNS = 4
TILE = 128
CLIP = FRAMES * FRAME_TOK

EPS_NORM = 1e-06
BETA_ONE = 0.5
BETA_TWO = 0.75
EPS_ADAM = 1e-08
DECAY = 0.01
LOG2E = 1.4426950408889634
GELU_A = 0.7978845608028654
GELU_B = 0.044715

BF = jnp.bfloat16
F32 = jnp.float32
VMEM_BYTES = 60 * 1024 * 1024


def params(**kw):
    return pltpu.CompilerParams(vmem_limit_bytes=VMEM_BYTES, **kw)


def cost(flops, nbytes, trans=0):
    return pl.CostEstimate(flops=int(flops), bytes_accessed=int(nbytes), transcendentals=int(trans))


def dot(left, right, dims):
    return lax.dot_general(left, right, (dims, ((), ())), preferred_element_type=F32)


NN = ((1,), (0,))
NT = ((1,), (1,))
TN = ((0,), (0,))


def tile_layout(groups):
    local_width = H // groups * HD
    shapes = [
        (D, 3 * local_width),
        (local_width, D),
        (D, FF // groups),
        (FF // groups, D),
        (D, 6 * D // groups),
    ]
    counts = [height // TILE * (breadth // TILE) for height, breadth in shapes]
    return (shapes, counts)


def kind_rates(tile_ids, counts):
    scales = [
        0.35 * D ** (-0.5),
        1.5 * (H * HD) ** (-0.5),
        0.5 * D ** (-0.5),
        0.5 * FF ** (-0.5),
        0.5 * D ** (-0.5),
    ]
    tile_rates = jnp.full(tile_ids.shape, scales[0], F32)
    boundary = 0
    for category in range(1, 5):
        boundary = boundary + counts[category - 1]
        tile_rates = jnp.where(tile_ids >= boundary, jnp.float32(scales[category]), tile_rates)
    return tile_rates


def unpack(tile_stack, shapes, counts):
    matrices = []
    offset = 0
    for (height, breadth), amount in zip(shapes, counts):
        stacked = tile_stack[offset : offset + amount].reshape(
            height // TILE, breadth // TILE, TILE, TILE
        )
        matrices.append(stacked.transpose(0, 2, 1, 3).reshape(height, breadth))
        offset = offset + amount
    return matrices


def pack(matrices):
    stacked = []
    for matrix in matrices:
        height, breadth = matrix.shape
        stacked.append(
            matrix.reshape(height // TILE, TILE, breadth // TILE, TILE)
            .transpose(0, 2, 1, 3)
            .reshape(-1, TILE, TILE)
        )
    return jnp.concatenate(stacked, axis=0)


def pick_chunk_plain(gathered, inverse, chip, core, chips, shapes, counts):
    w_qkv, w_out, w_up, w_down, w_mod = unpack(jnp.take(gathered, inverse, axis=0), shapes, counts)
    width = w_out.shape[0]
    half = width // 2
    ffn = w_up.shape[1] // 2
    rows, ffn_rows = half // chips, ffn // chips
    parts = []
    for role in range(3):
        parts.append(w_qkv[:, role * width : (role + 1) * width].T)
    parts.append(w_out)
    start = core * half + chip * rows
    attn = jnp.concatenate([lax.dynamic_slice_in_dim(p, start, rows, axis=0) for p in parts], axis=0)
    ffn_start = core * ffn + chip * ffn_rows
    up = lax.dynamic_slice_in_dim(w_up.T, ffn_start, ffn_rows, axis=0)
    down = lax.dynamic_slice_in_dim(w_down, ffn_start, ffn_rows, axis=0)
    return attn, up, down, w_mod


def norm_rows(values):
    centered = values - jnp.mean(values, axis=-1, keepdims=True)
    inverse_std = lax.rsqrt(jnp.mean(centered * centered, axis=-1, keepdims=True) + EPS_NORM)
    return centered * inverse_std, inverse_std


def norm_back(grad_normed, normed, inverse_std):
    centered = grad_normed - jnp.mean(grad_normed, axis=-1, keepdims=True)
    return inverse_std * (centered - normed * jnp.mean(grad_normed * normed, axis=-1, keepdims=True))


def frames_of(rows):
    return rows.reshape(-1, FRAME_TOK, D)


def flat(framed):
    return framed.reshape(-1, D)


BLK = 256
FBLK = BLK // FRAME_TOK


def row_spec():
    return pl.BlockSpec((BLK, D), lambda i: (i, 0))


def mod_spec(parts):
    return pl.BlockSpec((FBLK, parts, D), lambda i: (i, 0, 0))


def row_call(kernel, name, row_ins, mods, row_outs, mod_outs, nbytes):
    outs = [jax.ShapeDtypeStruct((CLIP, D), t) for t in row_outs]
    outs += [jax.ShapeDtypeStruct((FRAMES, n, D), F32) for n in mod_outs]
    return pl.pallas_call(
        kernel,
        grid=(CLIP // BLK,),
        in_specs=[row_spec() for _ in row_ins] + [mod_spec(6)],
        out_specs=[row_spec() for _ in row_outs] + [mod_spec(n) for n in mod_outs],
        out_shape=outs,
        compiler_params=params(),
        cost_estimate=cost(30 * CLIP * D, nbytes),
        name=name,
    )(*row_ins, mods)


def first_norm_kernel(x_ref, mod_ref, h_ref):
    normed, _ = norm_rows(x_ref[...].astype(F32))
    mods = mod_ref[...]
    h_ref[...] = flat(
        frames_of(normed) * (1.0 + mods[:, 1:2]) + mods[:, 0:1]
    ).astype(BF)


def middle_kernel(x_ref, a_ref, b_ref, dy_ref, mod_ref, y_ref, s_ref, h_ref, de_ref):
    mods = mod_ref[...]
    branch = (a_ref[...].astype(F32) + b_ref[...].astype(F32)).astype(BF)
    s_ref[...] = branch
    mid = frames_of(x_ref[...].astype(F32)) + mods[:, 2:3] * frames_of(branch.astype(F32))
    y_ref[...] = flat(mid)
    normed, _ = norm_rows(flat(mid))
    h_ref[...] = flat(
        frames_of(normed) * (1.0 + mods[:, 4:5]) + mods[:, 3:4]
    ).astype(BF)
    de_ref[...] = flat(mods[:, 5:6] * frames_of(dy_ref[...].astype(F32))).astype(BF)


def back_kernel(y_ref, g_ref, gp_ref, dy_ref, s_ref, e_ref, ep_ref, mod_ref, out_ref, dy1_ref, da_ref, dm_ref):
    mods = mod_ref[...]
    mid = y_ref[...]
    feed = e_ref[...].astype(F32) + ep_ref[...].astype(F32)
    dy = dy_ref[...].astype(F32)
    out_ref[...] = (mid + flat(mods[:, 5:6] * frames_of(feed))).astype(BF)
    normed, inverse_std = norm_rows(mid)
    grad = g_ref[...].astype(F32) + gp_ref[...].astype(F32)
    dm_ref[:, 0] = jnp.sum(frames_of(grad), axis=1)
    dm_ref[:, 1] = jnp.sum(frames_of(grad * normed), axis=1)
    scaled = flat(frames_of(grad) * (1.0 + mods[:, 4:5]))
    dy1 = dy + norm_back(scaled, normed, inverse_std)
    dy1_ref[...] = dy1
    dm_ref[:, 2] = jnp.sum(frames_of(dy1 * s_ref[...].astype(F32)), axis=1)
    dm_ref[:, 3] = jnp.sum(frames_of(dy * feed), axis=1)
    da_ref[...] = flat(mods[:, 2:3] * frames_of(dy1)).astype(BF)


def last_kernel(x_ref, g_ref, gp_ref, dy1_ref, mod_ref, out_ref, dm_ref):
    mods = mod_ref[...]
    normed, inverse_std = norm_rows(x_ref[...].astype(F32))
    grad = g_ref[...].astype(F32) + gp_ref[...].astype(F32)
    dm_ref[:, 0] = jnp.sum(frames_of(grad), axis=1)
    dm_ref[:, 1] = jnp.sum(frames_of(grad * normed), axis=1)
    scaled = flat(frames_of(grad) * (1.0 + mods[:, 1:2]))
    out_ref[...] = (dy1_ref[...] + norm_back(scaled, normed, inverse_std)).astype(BF)


MESH = pl.DeviceIdType.MESH
HEAD_TILES = 36
TABLE_TILES = 8
PAYLOAD = 46
LEVEL_TILE = HEAD_TILES + TABLE_TILES


class Link:
    def __init__(self, sends, recvs):
        self.sends, self.recvs, self.used, self.pending = sends, recvs, 0, []

    def make(self, src, dst, dp, mp):
        copy = pltpu.make_async_remote_copy(
            src_ref=src,
            dst_ref=dst,
            send_sem=self.sends.at[self.used],
            recv_sem=self.recvs.at[self.used],
            device_id=(dp, mp),
            device_id_type=MESH,
        )
        self.used += 1
        return copy

    def send(self, src, dst, dp, mp):
        copy = self.make(src, dst, dp, mp)
        copy.start()
        self.pending.append(copy)
        return copy

    def drain(self):
        for copy in self.pending:
            copy.wait_send()
        self.pending = []


def greet(d, z):
    barrier = pltpu.get_barrier_semaphore()
    for step in (1, 2, 4):
        pl.semaphore_signal(barrier, inc=1, device_id=(jnp.bitwise_xor(d, step), z), device_id_type=MESH)
    for s in (1, 2, 3):
        pl.semaphore_signal(barrier, inc=1, device_id=(d, lax.rem(z + s, 4)), device_id_type=MESH)
    pl.semaphore_wait(barrier, 6)


ENTRY_COPIES = 8 + 45 + 3


def entry_kernel(
    idx_ref,
    pay_ref,
    act_ref,
    cot_ref,
    bias_ref,
    w_ref,
    wmod_ref,
    x_ref,
    dy_ref,
    h_ref,
    mods_ref,
    bias_out,
    emb_ref,
    own_hot_ref,
    gath,
    own,
    turn,
    xs,
    dys,
    bs,
    part,
    modbuf,
    hots,
    sends,
    recvs,
    swap_sends,
    swap_recvs,
    local_sems,
):
    d, z = lax.axis_index("dp"), lax.axis_index("mp")
    core, chip = lax.rem(d, 2), d // 2
    dk, dx, dy = jnp.bitwise_xor(d, 1), jnp.bitwise_xor(d, 2), jnp.bitwise_xor(d, 4)
    dxy = jnp.bitwise_xor(d, 6)
    link = Link(sends, recvs)
    greet(d, z)

    def slot(owner, first=0, count=PAYLOAD):
        return gath.at[pl.ds(owner * PAYLOAD + first, count)]

    half = PAYLOAD // 2
    home = pltpu.make_async_copy(pay_ref, slot(d), local_sems.at[0])
    home.start()
    to_x = link.send(pay_ref, slot(d), dx, z)
    to_y = link.send(pay_ref, slot(d), dy, z)
    to_k = link.send(pay_ref, slot(d), dk, z)

    holds = (z // 2) == core
    rows = pl.ds(lax.rem(z, 2) * CLIP, CLIP)
    picks = [
        (act_ref.at[rows], xs),
        (cot_ref.at[rows], dys),
        (bias_ref.at[lax.rem(z, 2)], bs),
    ]

    def swaps():
        return [
            pltpu.make_async_remote_copy(
                src_ref=src,
                dst_ref=dst,
                send_sem=swap_sends.at[i],
                recv_sem=swap_recvs.at[i],
                device_id=(dk, z),
                device_id_type=MESH,
            )
            for i, (src, dst) in enumerate(picks)
        ]

    def keeps():
        return [pltpu.make_async_copy(src, dst, local_sems.at[1 + i]) for i, (src, dst) in enumerate(picks)]

    @pl.when(holds)
    def _():
        for copy in swaps() + keeps():
            copy.start()

    to_x.wait_recv()
    x_to_y = link.send(slot(dx, 0, half), slot(dx, 0, half), dy, z)
    x_to_k = link.send(slot(dx), slot(dx), dk, z)
    to_y.wait_recv()
    y_to_x = link.send(slot(dy, half, half), slot(dy, half, half), dx, z)
    y_to_k = link.send(slot(dy), slot(dy), dk, z)

    @pl.when(holds)
    def _():
        for copy in swaps():
            copy.wait_send()
        for copy in keeps():
            copy.wait()

    @pl.when(jnp.logical_not(holds))
    def _():
        for copy in swaps():
            copy.wait_recv()

    x_ref[...] = xs[...]
    dy_ref[...] = dys[...]
    bias_out[...] = bs[...]

    x_to_y.wait_recv()
    y_to_x.wait_recv()
    xy_to_k = link.send(slot(dxy), slot(dxy), dk, z)
    home.wait()
    to_k.wait_recv()
    x_to_k.wait_recv()
    y_to_k.wait_recv()
    xy_to_k.wait_recv()

    def tile(number):
        return gath[idx_ref[number]]

    def pick_attn(j, _):
        lanes = pl.ds(pl.multiple_of(j * TILE, TILE), TILE)
        for role in range(3):
            turn[role] = tile(j * 6 + 2 * role + core).T
        turn[3] = tile(48 + core * 8 + j)
        for role in range(4):
            own[0, role * 32 : (role + 1) * 32, lanes] = turn[role, pl.ds(pl.multiple_of(chip * 32, 32), 32), :]
        return 0

    def pick_feed(j, _):
        lanes = pl.ds(pl.multiple_of(j * TILE, TILE), TILE)
        own[1, :, lanes] = tile(64 + j * 8 + 4 * core + chip).T
        own[2, :, lanes] = tile(128 + (4 * core + chip) * 8 + j)
        return 0

    def pick_mod(j, _):
        strip = pl.ds(pl.multiple_of(j * TILE, TILE), TILE)
        for col in range(12):
            wmod_ref[strip, col * TILE : (col + 1) * TILE] = tile(192 + j * 12 + col)
        return 0

    along, by_x, by_y, diag, homes = {}, {}, {}, {}, []

    def send_along(g):
        for s in (1, 3, 2):
            along[g, s] = link.send(own.at[g], w_ref.at[g, 0, z], d, lax.rem(z + s, 4))

    def send_plane(g, s):
        m = lax.rem(z + 4 - s, 4)
        src = own.at[g] if s == 0 else w_ref.at[g, 0, m]
        by_x[g, s] = link.send(src, w_ref.at[g, 1, m], dx, z)
        by_y[g, s] = link.send(src, w_ref.at[g, 2, m], dy, z)

    def send_diag(g, s):
        m = lax.rem(z + 4 - s, 4)
        if s < 2:
            by_x[g, s].wait_recv()
            diag[g, s] = link.send(w_ref.at[g, 1, m], w_ref.at[g, 3, m], dy, z)
        else:
            by_y[g, s].wait_recv()
            diag[g, s] = link.send(w_ref.at[g, 2, m], w_ref.at[g, 3, m], dx, z)

    def keep_home(g):
        copy = pltpu.make_async_copy(own.at[g], w_ref.at[g, 0, z], local_sems.at[4 + g])
        copy.start()
        homes.append(copy)

    lax.fori_loop(0, 8, pick_attn, 0)
    lax.fori_loop(0, 8, pick_feed, 0)
    send_along(0)
    send_plane(0, 0)
    keep_home(0)
    send_along(1)
    send_along(2)
    send_plane(1, 0)
    keep_home(1)
    keep_home(2)

    lax.fori_loop(0, 8, pick_mod, 0)
    places = lax.broadcasted_iota(jnp.int32, (32, LEVELS), 1).astype(F32)
    for owner in range(8):
        codes = gath[owner * PAYLOAD + LEVEL_TILE][:32].astype(F32)
        level = codes[:, 0:1] * 32.0 + codes[:, 64:65]
        hots[owner * 32 : (owner + 1) * 32] = jnp.where(level == places, 1.0, 0.0).astype(BF)
    own_hot_ref[...] = hots[:, pl.ds(pl.multiple_of(d * TILE, TILE), TILE)]
    for j in range(TABLE_TILES):
        strip = jnp.concatenate([gath[owner * PAYLOAD + HEAD_TILES + j] for owner in range(8)], axis=0)
        emb_ref[:, j * TILE : (j + 1) * TILE] = dot(hots[...], strip, NN).astype(BF)
    embedded = emb_ref[pl.ds(pl.multiple_of(chip * 64, 64), 64), :]
    part[...] = dot(embedded, wmod_ref[...], NN).reshape(4, FRAMES, 12 * TILE)
    modbuf[z] = part[z]
    shared = {}
    for s in (1, 3, 2):
        shared[s] = link.send(part.at[lax.rem(z + s, 4)], modbuf.at[z], d, lax.rem(z + s, 4))

    for s in (1, 3, 2):
        along[0, s].wait_recv()
        send_plane(0, s)
    send_plane(2, 0)
    for s in (0, 1, 3, 2):
        send_diag(0, s)

    for s in (1, 3, 2):
        shared[s].wait_recv()
    for m in range(4):
        for c in range(6):
            mods_ref[:, c, m * 256 : (m + 1) * 256] = modbuf[m, :, c * 256 : (c + 1) * 256]

    def norm_strip(i, _):
        strip = pl.ds(pl.multiple_of(i * BLK, BLK), BLK)
        normed, _ = norm_rows(xs[strip].astype(F32))
        mods = mods_ref[pl.ds(i * FBLK, FBLK)]
        h_ref[strip] = flat(frames_of(normed) * (1.0 + mods[:, 1:2]) + mods[:, 0:1]).astype(BF)
        return 0

    lax.fori_loop(0, CLIP // BLK, norm_strip, 0)

    for s in (1, 3, 2):
        along[1, s].wait_recv()
        send_plane(1, s)
    for s in (1, 3, 2):
        along[2, s].wait_recv()
        send_plane(2, s)
    for g in (1, 2):
        for s in (0, 1, 3, 2):
            send_diag(g, s)
    for g in range(3):
        for s in range(4):
            (by_y if s < 2 else by_x)[g, s].wait_recv()
            diag[g, s].wait_recv()
    for copy in homes:
        copy.wait()
    link.drain()


def entry(masters, level_table, levels, bias_pair, activations, cotangent, owner_list):
    slots = masters.shape[0]
    codes = jnp.stack([levels.reshape(-1) // 32, levels.reshape(-1) % 32], axis=1).astype(BF)
    codes = jnp.pad(jnp.repeat(codes, 64, axis=1), ((0, TILE - codes.shape[0]), (0, 0)))
    payload = jnp.concatenate(
        [
            masters.astype(BF),
            level_table.reshape(TILE, TABLE_TILES, TILE).transpose(1, 0, 2),
            codes[None],
            jnp.zeros((1, TILE, TILE), BF),
        ]
    )
    position = jnp.arange(owner_list.shape[0], dtype=jnp.int32)
    place = (position // slots) * PAYLOAD + position % slots
    index = jnp.sum(
        jnp.where(owner_list[None, :] == position[:, None], place[None, :], 0), axis=1
    ).astype(jnp.int32)
    vmem = pl.BlockSpec(memory_space=pltpu.VMEM)
    hbm = pl.BlockSpec(memory_space=pl.ANY)
    return pl.pallas_call(
        entry_kernel,
        in_specs=[pl.BlockSpec(memory_space=pltpu.SMEM), hbm, hbm, hbm, hbm],
        out_specs=[hbm] + [vmem] * 8,
        out_shape=[
            jax.ShapeDtypeStruct((3, 4, 4, TILE, D), BF),
            jax.ShapeDtypeStruct((D, 12 * TILE), BF),
            jax.ShapeDtypeStruct((CLIP, D), BF),
            jax.ShapeDtypeStruct((CLIP, D), BF),
            jax.ShapeDtypeStruct((CLIP, D), BF),
            jax.ShapeDtypeStruct((FRAMES, 6, D), F32),
            jax.ShapeDtypeStruct((FRAMES, CLIP), F32),
            jax.ShapeDtypeStruct((256, D), BF),
            jax.ShapeDtypeStruct((256, TILE), BF),
        ],
        scratch_shapes=[
            pltpu.VMEM((8 * PAYLOAD, TILE, TILE), BF),
            pltpu.VMEM((3, TILE, D), BF),
            pltpu.VMEM((4, TILE, TILE), BF),
            pltpu.VMEM((CLIP, D), BF),
            pltpu.VMEM((CLIP, D), BF),
            pltpu.VMEM((FRAMES, CLIP), F32),
            pltpu.VMEM((4, FRAMES, 12 * TILE), F32),
            pltpu.VMEM((4, FRAMES, 12 * TILE), F32),
            pltpu.VMEM((256, LEVELS), BF),
            pltpu.SemaphoreType.DMA((ENTRY_COPIES,)),
            pltpu.SemaphoreType.DMA((ENTRY_COPIES,)),
            pltpu.SemaphoreType.DMA((3,)),
            pltpu.SemaphoreType.DMA((3,)),
            pltpu.SemaphoreType.DMA((7,)),
        ],
        compiler_params=params(collective_id=0, has_side_effects=True),
        cost_estimate=cost(1e9, 40e6),
        name="entry",
    )(index, payload, activations, cotangent, bias_pair)


QBLK = 256
SCALE2 = HD ** (-0.5) * LOG2E


def attend_kernel(qkv_ref, bias_ref, o_ref, lse_ref):
    for head in range(2):
        lanes = slice(head * HD, (head + 1) * HD)
        keys = qkv_ref[:, TILE + head * HD : TILE + (head + 1) * HD]
        values = qkv_ref[:, 2 * TILE + head * HD : 2 * TILE + (head + 1) * HD]

        def step(i, _, lanes=lanes, keys=keys, values=values, head=head):
            start = pl.multiple_of(i * QBLK, QBLK)
            queries = qkv_ref[pl.ds(start, QBLK), lanes]
            scores = dot(keys, queries, NT).reshape(FRAMES, FRAME_TOK, QBLK)
            scores = scores * SCALE2 + bias_ref[:, pl.ds(start, QBLK)][:, None, :]
            peak = jnp.max(jnp.max(scores, axis=0), axis=0, keepdims=True)
            weights = jnp.exp2(scores - peak[None])
            total = jnp.sum(jnp.sum(weights, axis=0), axis=0, keepdims=True)
            mixed = dot(values, weights.reshape(CLIP, QBLK).astype(BF), TN)
            o_ref[lanes, pl.ds(start, QBLK)] = (mixed / total).astype(BF)
            lse_ref[0, head : head + 1, pl.ds(start, QBLK)] = peak + jnp.log2(total)
            return 0

        lax.fori_loop(0, CLIP // QBLK, step, 0)


def attend(qkv, bias):
    groups = qkv.shape[1] // (3 * TILE)
    return pl.pallas_call(
        attend_kernel,
        grid=(groups,),
        in_specs=[
            pl.BlockSpec((CLIP, 3 * TILE), lambda m: (0, m)),
            pl.BlockSpec((FRAMES, CLIP), lambda m: (0, 0)),
        ],
        out_specs=[
            pl.BlockSpec((TILE, CLIP), lambda m: (m, 0)),
            pl.BlockSpec((1, 2, CLIP), lambda m: (m, 0, 0)),
        ],
        out_shape=[
            jax.ShapeDtypeStruct((groups * TILE, CLIP), BF),
            jax.ShapeDtypeStruct((groups, 2, CLIP), F32),
        ],
        compiler_params=params(),
        cost_estimate=cost(groups * 2 * 4 * CLIP * CLIP * HD * 3, 2 * qkv.size, groups * 2 * CLIP * CLIP),
        name="attend",
    )(qkv, bias)


def attend_back_kernel(qkv_ref, o_ref, do_ref, lse_ref, bias_ref, out_ref, dk_ref, dv_ref):
    for head in range(2):
        lanes = slice(head * HD, (head + 1) * HD)
        keys = qkv_ref[:, TILE + head * HD : TILE + (head + 1) * HD]
        values = qkv_ref[:, 2 * TILE + head * HD : 2 * TILE + (head + 1) * HD]
        dk_ref[...] = jnp.zeros_like(dk_ref)
        dv_ref[...] = jnp.zeros_like(dv_ref)

        def step(i, _, lanes=lanes, keys=keys, values=values, head=head):
            start = pl.multiple_of(i * QBLK, QBLK)
            across = pl.ds(start, QBLK)
            queries = qkv_ref[across, lanes]
            grad = do_ref[lanes, across]
            shift = bias_ref[:, across] - lse_ref[0, head : head + 1, across]
            scores = dot(keys, queries, NT).reshape(FRAMES, FRAME_TOK, QBLK)
            soft = jnp.exp2(scores * SCALE2 + shift[:, None, :]).reshape(CLIP, QBLK)
            delta = jnp.sum(
                grad.astype(F32) * o_ref[lanes, across].astype(F32), axis=0, keepdims=True
            )
            grad_soft = dot(values, grad, NN)
            grad_scores = (soft * (grad_soft - delta)).astype(BF)
            dv_ref[...] += dot(soft.astype(BF), grad, NT)
            dk_ref[...] += dot(grad_scores, queries, NN)
            grad_query = dot(keys, grad_scores, TN) * HD ** (-0.5)
            out_ref[across, lanes] = grad_query.T.astype(BF)
            return 0

        lax.fori_loop(0, CLIP // QBLK, step, 0)
        out_ref[:, TILE + head * HD : TILE + (head + 1) * HD] = (dk_ref[...] * HD ** (-0.5)).astype(BF)
        out_ref[:, 2 * TILE + head * HD : 2 * TILE + (head + 1) * HD] = dv_ref[...].astype(BF)


def attend_back(qkv, o_rows, do_rows, lse, bias):
    groups = qkv.shape[1] // (3 * TILE)
    return pl.pallas_call(
        attend_back_kernel,
        grid=(groups,),
        in_specs=[
            pl.BlockSpec((CLIP, 3 * TILE), lambda m: (0, m)),
            pl.BlockSpec((TILE, CLIP), lambda m: (m, 0)),
            pl.BlockSpec((TILE, CLIP), lambda m: (m, 0)),
            pl.BlockSpec((1, 2, CLIP), lambda m: (m, 0, 0)),
            pl.BlockSpec((FRAMES, CLIP), lambda m: (0, 0)),
        ],
        out_specs=pl.BlockSpec((CLIP, 3 * TILE), lambda m: (0, m)),
        out_shape=jax.ShapeDtypeStruct(qkv.shape, BF),
        scratch_shapes=[pltpu.VMEM((CLIP, HD), F32), pltpu.VMEM((CLIP, HD), F32)],
        compiler_params=params(),
        cost_estimate=cost(groups * 2 * 10 * CLIP * CLIP * HD * 3, 4 * qkv.size, groups * 2 * CLIP * CLIP),
        name="attend_back",
    )(qkv, o_rows, do_rows, lse, bias)


UNITS = 256
ROWS = 512


def feed_kernel(h_ref, de_ref, up_ref, down_ref, e_ref, dh_ref, dup_ref, ddown_ref, e_acc, dh_acc, up_acc, down_acc):
    block = pl.program_id(0)
    last = pl.num_programs(0) - 1
    up = up_ref[...]
    down = down_ref[...]
    for part in range(CLIP // ROWS):
        rows = slice(part * ROWS, (part + 1) * ROWS)
        hidden = h_ref[rows]
        grad = de_ref[rows]
        pre = dot(hidden, up, NT)
        square = pre * pre
        tanh = jnp.tanh(GELU_A * pre * (1.0 + GELU_B * square))
        act = (0.5 * pre * (1.0 + tanh)).astype(BF)
        slope = 0.5 * (1.0 + tanh) + 0.5 * pre * (1.0 - tanh * tanh) * (
            GELU_A * (1.0 + 3.0 * GELU_B * square)
        )
        grad_act = dot(grad, down, NT).astype(BF).astype(F32)
        grad_pre = (grad_act * slope).astype(BF)
        feed = dot(act, down, NN)
        back = dot(grad_pre, up, NN)

        @pl.when(block == 0)
        def _():
            e_acc[rows] = feed
            dh_acc[rows] = back

        @pl.when(block > 0)
        def _():
            e_acc[rows] += feed
            dh_acc[rows] += back

        if part == 0:
            down_acc[...] = dot(act, grad, TN)
            up_acc[...] = dot(grad_pre, hidden, TN)
        else:
            ddown_ref[...] = (down_acc[...] + dot(act, grad, TN)).astype(BF)
            dup_ref[...] = (up_acc[...] + dot(grad_pre, hidden, TN)).astype(BF)

    @pl.when(block == last)
    def _():
        e_ref[...] = e_acc[...].astype(BF)
        dh_ref[...] = dh_acc[...].astype(BF)


def feed_both(hidden, grad, up, down):
    units = up.shape[0]
    whole = pl.BlockSpec((CLIP, D), lambda i: (0, 0))
    strip = pl.BlockSpec((UNITS, D), lambda i: (i, 0))
    return pl.pallas_call(
        feed_kernel,
        grid=(units // UNITS,),
        in_specs=[whole, whole, strip, strip],
        out_specs=[whole, whole, strip, strip],
        out_shape=[jax.ShapeDtypeStruct((CLIP, D), BF)] * 2 + [jax.ShapeDtypeStruct((units, D), BF)] * 2,
        scratch_shapes=[
            pltpu.VMEM((CLIP, D), F32),
            pltpu.VMEM((CLIP, D), F32),
            pltpu.VMEM((UNITS, D), F32),
            pltpu.VMEM((UNITS, D), F32),
        ],
        compiler_params=params(),
        cost_estimate=cost(12 * CLIP * D * units, 8 * CLIP * D + 8 * units * D, CLIP * units),
        name="feed_both",
    )(hidden, grad, up, down)


HALF = CLIP // 2
EXIT_COPIES = 8 + 1 + 18 + 9 + 24 + 12 + 6 + 14
EXIT_LOCAL = 32


class Relay:
    def __init__(self, sends, recvs, local, src, full, d, z):
        self.sends, self.recvs, self.local = sends, recvs, local
        self.src, self.full, self.d, self.z = src, full, d, z
        self.core = lax.rem(d, 2)

    def place(self, clip, first, count):
        start = pl.multiple_of(lax.rem(clip, 2) * CLIP + first * HALF, HALF)
        return self.full.at[pl.ds(start, count)]

    def copy(self, src, clip, half, way, hop):
        index = way * 6 + (hop - 1) * 2 + half
        return pltpu.make_async_remote_copy(
            src_ref=src,
            dst_ref=self.place(clip, half, HALF),
            send_sem=self.sends.at[index],
            recv_sem=self.recvs.at[index],
            device_id=(self.d - self.core + clip // 2, lax.rem(self.z + (1 if way == 0 else 3), 4)),
            device_id_type=MESH,
        )

    def more(self, way):
        return self.z < 3 if way == 0 else self.z > 0

    def own(self, way):
        part = self.src.at[pl.ds(pl.multiple_of(self.core * HALF, HALF), HALF)]
        return self.copy(part, self.z, self.core, way, 1)

    def home(self):
        return pltpu.make_async_copy(self.src, self.place(self.z, 0, CLIP), self.local)

    def first(self):
        for way in range(2):

            @pl.when(self.more(way))
            def _(way=way):
                self.own(way).start()

        @pl.when(self.z // 2 == self.core)
        def _():
            self.home().start()

    def arriving(self, way, hop):
        clip = lax.rem(self.z + (4 - hop if way == 0 else hop), 4)
        there = self.z >= hop if way == 0 else self.z + hop <= 3
        return clip, jnp.logical_and(there, clip // 2 == self.core)

    def hop(self, hop):
        for way in range(2):
            clip, here = self.arriving(way, hop)

            @pl.when(here)
            def _(way=way, clip=clip):
                for half in range(2):
                    part = self.place(clip, half, HALF)
                    self.copy(part, clip, half, way, hop).wait_recv()
                    if hop < 3:

                        @pl.when(self.more(way))
                        def _(part=part, half=half):
                            self.copy(part, clip, half, way, hop + 1).start()

    def finish(self):
        for way in range(2):

            @pl.when(self.more(way))
            def _(way=way):
                self.own(way).wait_send()

            for hop in (1, 2):
                clip, here = self.arriving(way, hop)

                @pl.when(jnp.logical_and(here, self.more(way)))
                def _(way=way, clip=clip, hop=hop):
                    for half in range(2):
                        self.copy(self.place(clip, half, HALF), clip, half, way, hop + 1).wait_send()

        @pl.when(self.z // 2 == self.core)
        def _():
            self.home().wait()


def exit_kernel(
    y_hbm,
    g_hbm,
    e_hbm,
    dy_hbm,
    br_hbm,
    x_hbm,
    h_hbm,
    qkv_hbm,
    o_hbm,
    win_hbm,
    wout_hbm,
    wmod_hbm,
    up_hbm,
    down_hbm,
    mods_ref,
    bias_ref,
    lse_ref,
    emb_ref,
    hot_ref,
    out_all,
    in_all,
    everyone,
    dwm_out,
    table_ref,
    ys,
    gs,
    es,
    dys,
    brs,
    gp,
    ep,
    qs,
    os_,
    dos,
    win,
    wout,
    dhp,
    dattn,
    got,
    loc,
    zbuf,
    red,
    dm,
    dms,
    dmall,
    trow,
    tbuf,
    dk_ref,
    dv_ref,
    sends,
    recvs,
    strip_sends,
    strip_recvs,
    out_sends,
    out_recvs,
    in_sends,
    in_recvs,
    local_sems,
):
    d, z = lax.axis_index("dp"), lax.axis_index("mp")
    core, chip = lax.rem(d, 2), d // 2
    dk, dx, dyd = jnp.bitwise_xor(d, 1), jnp.bitwise_xor(d, 2), jnp.bitwise_xor(d, 4)
    link = Link(sends, recvs)
    locals_used = [0]

    def load(src, dst):
        copy = pltpu.make_async_copy(src, dst, local_sems.at[locals_used[0]])
        locals_used[0] += 1
        copy.start()
        return copy

    barrier = pltpu.get_barrier_semaphore()
    for step in (1, 2, 4):
        pl.semaphore_signal(barrier, inc=1, device_id=(jnp.bitwise_xor(d, step), z), device_id_type=MESH)
    for s in (1, 2, 3):
        pl.semaphore_signal(barrier, inc=1, device_id=(d, lax.rem(z + s, 4)), device_id_type=MESH)
        pl.semaphore_signal(barrier, inc=1, device_id=(dk, lax.rem(z + s, 4)), device_id_type=MESH)

    first_loads = [load(a, b) for a, b in ((g_hbm, gs), (e_hbm, es), (y_hbm, ys), (dy_hbm, dys), (br_hbm, brs))]
    loads = [load(a, b) for a, b in ((o_hbm, os_), (wout_hbm, wout), (win_hbm, win))]
    loads += [load(qkv_hbm.at[:, m * 384 : (m + 1) * 384], qs.at[m]) for m in range(4)]
    feed_loads = []
    for g, src in enumerate((up_hbm, down_hbm)):
        feed_loads.append(load(src.at[0], loc.at[g, 0:4]))
        feed_loads.append(load(src.at[2, 0:2], loc.at[g, 4:6]))
        feed_loads.append(load(src.at[1, 2:4], loc.at[g, 6:8]))
    pl.semaphore_wait(barrier, 9)

    def strip_of(i):
        return pl.ds(pl.multiple_of(i * BLK, BLK), BLK)

    def swaps(i):
        return [
            pltpu.make_async_remote_copy(
                src_ref=src.at[strip_of(i)],
                dst_ref=dst.at[strip_of(i)],
                send_sem=strip_sends.at[2 * i + k],
                recv_sem=strip_recvs.at[2 * i + k],
                device_id=(dk, z),
                device_id_type=MESH,
            )
            for k, (src, dst) in enumerate(((g_hbm, gp), (e_hbm, ep)))
        ]

    def swap_start(i, _):
        for copy in swaps(i):
            copy.start()
        return 0

    lax.fori_loop(0, CLIP // BLK, swap_start, 0)

    plane = {}

    def plane_first(g, src):
        plane[g, 0] = link.send(src.at[3, 0:2], got.at[g, 0], dx, z)
        plane[g, 1] = link.send(src.at[3, 2:4], got.at[g, 1], dyd, z)
        plane[g, 2] = link.send(src.at[1, 0:2], got.at[g, 2], dx, z)
        plane[g, 3] = link.send(src.at[2, 2:4], got.at[g, 3], dyd, z)

    def add_into(dst, first, count, parts):
        def step(i, _):
            k = i // 4
            rows = pl.ds(pl.multiple_of(lax.rem(i, 4) * 32, 32), 32)
            total = dst[first + k, rows].astype(F32)
            for g, slot in parts:
                total = total + got[g, slot, k, rows].astype(F32)
            dst[first + k, rows] = total.astype(BF)
            return 0

        lax.fori_loop(0, count * 4, step, 0)

    def places(g):
        if g == 0:
            return (dattn.at[0], 0), (dattn.at[2], 0), (dattn.at[1], 2)
        return (loc.at[g - 1], 0), (loc.at[g - 1], 4), (loc.at[g - 1], 6)

    def plane_pass(g):
        _, (low, low_at), (high, high_at) = places(g)
        plane[g, 0].wait_recv()
        add_into(low, low_at, 2, [(g, 0)])
        plane[g, 4] = link.send(low.at[pl.ds(low_at, 2)], got.at[g, 4], dyd, z)
        plane[g, 1].wait_recv()
        add_into(high, high_at, 2, [(g, 1)])
        plane[g, 5] = link.send(high.at[pl.ds(high_at, 2)], got.at[g, 5], dx, z)

    column = {}

    def plane_final(g):
        (own, _), _, _ = places(g)
        for slot in (2, 3, 4, 5):
            plane[g, slot].wait_recv()
        add_into(own, 0, 2, [(g, 2), (g, 4)])
        add_into(own, 2, 2, [(g, 3), (g, 5)])
        for s in (1, 3, 2):
            to = lax.rem(z + s, 4)
            column[g, s] = link.send(own.at[to], zbuf.at[g, s - 1], d, to)

    spread = {}
    homes = []

    def column_final(g):
        (own, _), _, _ = places(g)
        for s in (1, 3, 2):
            column[g, s].wait_recv()

        def step(i, _):
            rows = pl.ds(pl.multiple_of(i * 32, 32), 32)
            total = own[z, rows].astype(F32)
            for s in range(3):
                total = total + zbuf[g, s, rows].astype(F32)
            red[g, rows] = total.astype(BF)
            return 0

        lax.fori_loop(0, 4, step, 0)
        rows = pl.ds(g * TILE, TILE)
        spread[g, 2] = link.send(red.at[g], everyone.at[2, rows], dx, z)
        spread[g, 4] = link.send(red.at[g], everyone.at[4, rows], dyd, z)
        spread[g, 1] = link.send(red.at[g], everyone.at[1, rows], dk, z)
        homes.append(load(red.at[g], everyone.at[0, rows]))

    def spread_on(g):
        rows = pl.ds(g * TILE, TILE)
        low, high = pl.ds(g * TILE, TILE // 2), pl.ds(g * TILE + TILE // 2, TILE // 2)
        spread[g, 2].wait_recv()
        spread[g, 6] = link.send(everyone.at[2, low], everyone.at[6, low], dyd, z)
        spread[g, 3] = link.send(everyone.at[2, rows], everyone.at[3, rows], dk, z)
        spread[g, 4].wait_recv()
        spread[g, 7] = link.send(everyone.at[4, high], everyone.at[6, high], dx, z)
        spread[g, 5] = link.send(everyone.at[4, rows], everyone.at[5, rows], dk, z)

    def spread_diag(g):
        rows = pl.ds(g * TILE, TILE)
        spread[g, 6].wait_recv()
        spread[g, 7].wait_recv()
        spread[g, 8] = link.send(everyone.at[6, rows], everyone.at[7, rows], dk, z)

    plane_first(1, up_hbm)
    plane_first(2, down_hbm)
    for copy in first_loads:
        copy.wait()

    def back_strip(i, _):
        strip, frames = strip_of(i), pl.ds(i * FBLK, FBLK)
        for copy in swaps(i):
            copy.wait_recv()
        mods = mods_ref[frames]
        mid = ys[strip]
        feed = es[strip].astype(F32) + ep[strip].astype(F32)
        dy = dys[strip].astype(F32)
        ep[strip] = (mid + flat(mods[:, 5:6] * frames_of(feed))).astype(BF)
        normed, inverse_std = norm_rows(mid)
        grad = gs[strip].astype(F32) + gp[strip].astype(F32)
        dm[frames, 3] = jnp.sum(frames_of(grad), axis=1)
        dm[frames, 4] = jnp.sum(frames_of(grad * normed), axis=1)
        dm[frames, 5] = jnp.sum(frames_of(dy * feed), axis=1)
        scaled = flat(frames_of(grad) * (1.0 + mods[:, 4:5]))
        dy1 = dy + norm_back(scaled, normed, inverse_std)
        ys[strip] = dy1
        dm[frames, 2] = jnp.sum(frames_of(dy1 * brs[strip].astype(F32)), axis=1)
        gp[strip] = flat(mods[:, 2:3] * frames_of(dy1)).astype(BF)
        return 0

    lax.fori_loop(0, CLIP // BLK, back_strip, 0)

    def swap_done(i, _):
        for copy in swaps(i):
            copy.wait_send()
        return 0

    lax.fori_loop(0, CLIP // BLK, swap_done, 0)
    x_load = load(x_hbm, gs)
    h_load = load(h_hbm, es)
    output = Relay(out_sends, out_recvs, local_sems.at[EXIT_LOCAL - 1], ep, out_all, d, z)
    output.first()
    for copy in loads:
        copy.wait()

    def project(m, _):
        dos[m] = dot(wout[m], gp[...], NT).astype(BF)
        grad = dot(os_[m], gp[...], NN).astype(BF)
        for c in range(4):
            dattn[c, m, 96:128] = grad[c * 32 : (c + 1) * 32]
        return 0

    lax.fori_loop(0, 4, project, 0)

    def attend_group(m, _):
        for head in range(2):
            lanes = slice(head * HD, (head + 1) * HD)
            keys = qs[m, :, TILE + head * HD : TILE + (head + 1) * HD]
            values = qs[m, :, 2 * TILE + head * HD : 2 * TILE + (head + 1) * HD]
            dk_ref[...] = jnp.zeros_like(dk_ref)
            dv_ref[...] = jnp.zeros_like(dv_ref)

            def step(i, _, lanes=lanes, keys=keys, values=values, head=head):
                across = pl.ds(pl.multiple_of(i * QBLK, QBLK), QBLK)
                queries = qs[m, across, lanes]
                grad = dos[m, lanes, across]
                shift = bias_ref[:, across] - lse_ref[m, head : head + 1, across]
                scores = dot(keys, queries, NT).reshape(FRAMES, FRAME_TOK, QBLK)
                soft = jnp.exp2(scores * SCALE2 + shift[:, None, :]).reshape(CLIP, QBLK)
                delta = jnp.sum(
                    grad.astype(F32) * os_[m, lanes, across].astype(F32), axis=0, keepdims=True
                )
                grad_soft = dot(values, grad, NN)
                grad_scores = (soft * (grad_soft - delta)).astype(BF)
                dv_ref[...] += dot(soft.astype(BF), grad, NT)
                dk_ref[...] += dot(grad_scores, queries, NN)
                grad_query = dot(keys, grad_scores, TN) * HD ** (-0.5)
                qs[m, across, lanes] = grad_query.T.astype(BF)
                return 0

            lax.fori_loop(0, CLIP // QBLK, step, 0)
            qs[m, :, TILE + head * HD : TILE + (head + 1) * HD] = (dk_ref[...] * HD ** (-0.5)).astype(BF)
            qs[m, :, 2 * TILE + head * HD : 2 * TILE + (head + 1) * HD] = dv_ref[...].astype(BF)
        return 0

    lax.fori_loop(0, 2, attend_group, 0)
    for copy in feed_loads:
        copy.wait()
    plane_pass(1)
    lax.fori_loop(2, 4, attend_group, 0)
    plane_pass(2)
    output.hop(1)

    def hidden_strip(i, _):
        strip = strip_of(i)
        total = dot(qs[0, strip], win[0:384], NN)
        for m in range(1, 4):
            total = total + dot(qs[m, strip], win[m * 384 : (m + 1) * 384], NN)
        brs[strip] = total.astype(BF)
        return 0

    lax.fori_loop(0, CLIP // BLK, hidden_strip, 0)
    hidden_swap = link.send(brs, dhp, dk, z)
    h_load.wait()
    x_load.wait()

    def input_weights(m, _):
        grad = dot(qs[m], es[...], TN).astype(BF)
        for role in range(3):
            for c in range(4):
                first = role * TILE + c * 32
                dattn[c, m, role * 32 : (role + 1) * 32] = grad[first : first + 32]
        return 0

    lax.fori_loop(0, 4, input_weights, 0)
    plane_first(0, dattn)
    mod_loads = [load(wmod_hbm.at[:, m * 384 : (m + 1) * 384], qs.at[m]) for m in range(4)]
    plane_final(1)
    plane_final(2)

    hidden_swap.wait_recv()

    def last_strip(i, _):
        strip, frames = strip_of(i), pl.ds(i * FBLK, FBLK)
        mods = mods_ref[frames]
        normed, inverse_std = norm_rows(gs[strip].astype(F32))
        grad = brs[strip].astype(F32) + dhp[strip].astype(F32)
        dm[frames, 0] = jnp.sum(frames_of(grad), axis=1)
        dm[frames, 1] = jnp.sum(frames_of(grad * normed), axis=1)
        scaled = flat(frames_of(grad) * (1.0 + mods[:, 1:2]))
        dys[strip] = (ys[strip] + norm_back(scaled, normed, inverse_std)).astype(BF)
        return 0

    lax.fori_loop(0, CLIP // BLK, last_strip, 0)
    for m in range(4):
        for c in range(6):
            dms[m, :, c * 256 : (c + 1) * 256] = dm[:, c, m * 256 : (m + 1) * 256].astype(BF)
    mod_column = {}
    clip = chip * 4 + z
    for s in (1, 3, 2):
        to = lax.rem(z + s, 4)
        mod_column[s] = link.send(dms.at[to], dmall.at[clip], d, to)
    dmall[clip] = dms[z]
    inner = Relay(in_sends, in_recvs, local_sems.at[EXIT_LOCAL - 2], dys, in_all, d, z)
    inner.first()
    output.hop(2)

    for s in (1, 3, 2):
        mod_column[s].wait_recv()

    def clips_of(which):
        return dmall.at[pl.ds(which * 4, 4)]

    mod_x = link.send(clips_of(chip), clips_of(chip), dx, z)
    mod_y = link.send(clips_of(chip), clips_of(chip), dyd, z)
    plane_pass(0)
    column_final(1)
    column_final(2)
    mod_x.wait_recv()
    over_x = jnp.bitwise_xor(chip, 1)
    mod_xy = link.send(clips_of(over_x), clips_of(over_x), dyd, z)
    spread_on(1)
    spread_on(2)
    plane_final(0)
    inner.hop(1)
    output.hop(3)

    mod_y.wait_recv()
    mod_xy.wait_recv()
    for copy in mod_loads:
        copy.wait()
    grads = dmall[...].reshape(256, 12 * TILE)

    level_grads = dot(hot_ref[...], grads, TN).astype(BF)
    rows = dot(level_grads[:, 0:384], qs[0], NT)
    for m in range(1, 4):
        rows = rows + dot(level_grads[:, m * 384 : (m + 1) * 384], qs[m], NT)
    trow[...] = rows.reshape(4, 32, D)
    table = {}
    for s in (1, 3, 2):
        to = lax.rem(z + s, 4)
        table[s] = link.send(trow.at[to], tbuf.at[s - 1], d, to)

    for part in range(6):
        win[part * 256 : (part + 1) * 256] = dot(
            grads[:, part * 256 : (part + 1) * 256], emb_ref[...], TN
        ).astype(BF)
    homes.append(load(win, dwm_out))
    spread_diag(1)
    spread_diag(2)
    column_final(0)
    inner.hop(2)
    spread_on(0)
    for s in (1, 3, 2):
        table[s].wait_recv()
    table_ref[...] = trow[z] + tbuf[0] + tbuf[1] + tbuf[2]
    spread_diag(0)
    inner.hop(3)
    for g in range(3):
        for slot in (1, 3, 5, 8):
            spread[g, slot].wait_recv()
    for copy in homes:
        copy.wait()
    output.finish()
    inner.finish()
    link.drain()


def exit_call(y1, dh2, e, dy, branch, x, h1, qkv, o_rows, w_in, w_out, w_mod, d_up, d_down, mods, bias, lse, emb, hot):
    vmem = pl.BlockSpec(memory_space=pltpu.VMEM)
    hbm = pl.BlockSpec(memory_space=pl.ANY)
    chunks = (4, 4, TILE, D)
    heads = (4, TILE, D)
    return pl.pallas_call(
        exit_kernel,
        in_specs=[hbm] * 14 + [vmem] * 5,
        out_specs=[hbm] * 4 + [vmem],
        out_shape=[
            jax.ShapeDtypeStruct((2 * CLIP, D), BF),
            jax.ShapeDtypeStruct((2 * CLIP, D), BF),
            jax.ShapeDtypeStruct((8, 3 * TILE, D), BF),
            jax.ShapeDtypeStruct((12 * TILE, D), BF),
            jax.ShapeDtypeStruct((32, D), F32),
        ],
        scratch_shapes=[
            pltpu.VMEM((CLIP, D), F32),
            pltpu.VMEM((CLIP, D), BF),
            pltpu.VMEM((CLIP, D), BF),
            pltpu.VMEM((CLIP, D), BF),
            pltpu.VMEM((CLIP, D), BF),
            pltpu.VMEM((CLIP, D), BF),
            pltpu.VMEM((CLIP, D), BF),
            pltpu.VMEM((4, CLIP, 3 * TILE), BF),
            pltpu.VMEM(heads, BF),
            pltpu.VMEM(heads, BF),
            pltpu.VMEM((12 * TILE, D), BF),
            pltpu.VMEM(heads, BF),
            pltpu.VMEM((CLIP, D), BF),
            pltpu.VMEM(chunks, BF),
            pltpu.VMEM((3, 6, 2, TILE, D), BF),
            pltpu.VMEM((2, 8, TILE, D), BF),
            pltpu.VMEM((3, 3, TILE, D), BF),
            pltpu.VMEM((3, TILE, D), BF),
            pltpu.VMEM((FRAMES, 6, D), F32),
            pltpu.VMEM((4, FRAMES, 12 * TILE), BF),
            pltpu.VMEM((16, FRAMES, 12 * TILE), BF),
            pltpu.VMEM((4, 32, D), F32),
            pltpu.VMEM((3, 32, D), F32),
            pltpu.VMEM((CLIP, HD), F32),
            pltpu.VMEM((CLIP, HD), F32),
            pltpu.SemaphoreType.DMA((EXIT_COPIES,)),
            pltpu.SemaphoreType.DMA((EXIT_COPIES,)),
            pltpu.SemaphoreType.DMA((8,)),
            pltpu.SemaphoreType.DMA((8,)),
            pltpu.SemaphoreType.DMA((12,)),
            pltpu.SemaphoreType.DMA((12,)),
            pltpu.SemaphoreType.DMA((12,)),
            pltpu.SemaphoreType.DMA((12,)),
            pltpu.SemaphoreType.DMA((EXIT_LOCAL,)),
        ],
        compiler_params=pltpu.CompilerParams(
            vmem_limit_bytes=63 * 1024 * 1024, collective_id=1, has_side_effects=True
        ),
        cost_estimate=cost(1e11, 60e6),
        name="exit",
    )(
        y1,
        dh2,
        e,
        dy,
        branch,
        x,
        h1,
        qkv,
        o_rows.reshape(heads),
        w_in,
        w_out.reshape(heads),
        w_mod,
        d_up.reshape(chunks),
        d_down.reshape(chunks),
        mods,
        bias,
        lse,
        emb,
        hot,
    )


def adam_step(grad, left, right, one, two, master, rate):
    low_left, low_right = left.astype(BF), right.astype(BF)
    turned = dot(low_left, grad.astype(BF), TN)
    rotated = dot(turned.astype(BF), low_right, NN)
    new_one = BETA_ONE * one + (1.0 - BETA_ONE) * rotated
    new_two = BETA_TWO * two + (1.0 - BETA_TWO) * rotated * rotated
    direction = new_one / (jnp.sqrt(new_two) + EPS_ADAM)
    back = dot(low_left, direction.astype(BF), NN)
    back = dot(back.astype(BF), low_right, NT)
    return master - rate * (back + DECAY * master), new_one, new_two


def adam_kernel(tab_ref, rate_ref, *refs, picked, batch):
    if picked:
        red_ref, mod_ref = refs[:2]
        refs = refs[2:]
    else:
        grad_ref = refs[0]
        refs = refs[1:]
    master_ref, one_ref, two_ref, left_ref, right_ref, nm_ref, n1_ref, n2_ref, nw_ref = refs
    for slot in range(batch):
        tile = pl.program_id(0) * batch + slot
        if picked:
            col = pl.multiple_of(tab_ref[tile, 8] * TILE, TILE)
            pieces = [
                red_ref[
                    tab_ref[tile, i],
                    pl.ds(pl.multiple_of(tab_ref[tile, 4 + i] * 32, 32), 32),
                    pl.ds(col, TILE),
                ]
                for i in range(4)
            ]
            grad = jnp.concatenate(pieces, axis=0).astype(F32)
            mod_row = pl.multiple_of(tab_ref[tile, 9] * TILE, TILE)
            mod_col = pl.multiple_of(tab_ref[tile, 10] * TILE, TILE)
            mod_grad = mod_ref[pl.ds(mod_col, TILE), pl.ds(mod_row, TILE)].astype(F32)
            kind = tab_ref[tile, 11]
            grad = jnp.where(kind == 0, grad, jnp.where(kind == 2, mod_grad, grad).T)
        else:
            grad = grad_ref[slot].astype(F32)
        master, one, two = adam_step(
            grad, left_ref[slot], right_ref[slot], one_ref[slot], two_ref[slot], master_ref[slot], rate_ref[tile]
        )
        nm_ref[slot] = master
        n1_ref[slot] = one
        n2_ref[slot] = two
        nw_ref[slot] = master.astype(BF)


def pick_table(tiles, device):
    table = []
    piece = jnp.arange(4, dtype=jnp.int32)[None, :]
    t = tiles[:, None]
    is_in = t < 48
    is_out = (t >= 48) & (t < 64)
    is_up = (t >= 64) & (t < 128)
    is_down = (t >= 128) & (t < 192)
    is_mod = t >= 192
    q0, q1, q2, q3, q4 = t, t - 48, t - 64, t - 128, t - 192
    core = jnp.where(is_in, (q0 % 6) % 2, jnp.where(is_out, q1 // 8, jnp.where(is_up, (q2 % 8) // 4, (q3 // 8) // 4)))
    chip = jnp.where(is_up, q2 % 4, (q3 // 8) % 4)
    chip = jnp.where(is_in | is_out, piece, chip)
    source = jnp.where(is_mod, 0, jnp.bitwise_xor(2 * chip + core, device))
    row = jnp.where(is_in, (q0 % 6) // 2, jnp.where(is_out, 3, jnp.where(is_up, 4 + piece, 8 + piece)))
    row = jnp.where(is_mod, 0, row + jnp.zeros_like(piece))
    col = jnp.where(is_in, q0 // 6, jnp.where(is_out, q1 % 8, jnp.where(is_up, q2 // 8, q3 % 8)))
    col = jnp.where(is_mod, 0, col)
    mod_row = jnp.where(is_mod, q4 // 12, 0)
    mod_col = jnp.where(is_mod, q4 % 12, 0)
    kind = jnp.where(is_mod, 2, jnp.where(is_in | is_up, 1, 0))
    return jnp.concatenate([source, row, col, mod_row, mod_col, kind], axis=1).astype(jnp.int32)


def adam(table, rates, sources, master, one, two, left, right):
    slots = master.shape[0]
    batch = max(b for b in (4, 3, 2, 1) if slots % b == 0)
    picked = len(sources) == 2
    tiles = pl.BlockSpec((batch, TILE, TILE), lambda i, *_: (i, 0, 0))
    if picked:
        source_specs = [
            pl.BlockSpec(sources[0].shape, lambda i, *_: (0, 0, 0)),
            pl.BlockSpec(sources[1].shape, lambda i, *_: (0, 0)),
        ]
    else:
        source_specs = [tiles]
    return pl.pallas_call(
        functools.partial(adam_kernel, picked=picked, batch=batch),
        grid_spec=pltpu.PrefetchScalarGridSpec(
            num_scalar_prefetch=2,
            grid=(slots // batch,),
            in_specs=source_specs + [tiles] * 5,
            out_specs=[tiles] * 4,
        ),
        out_shape=[jax.ShapeDtypeStruct(master.shape, F32)] * 3 + [jax.ShapeDtypeStruct(master.shape, BF)],
        compiler_params=params(),
        cost_estimate=cost(slots * 8 * TILE**3, slots * TILE * TILE * 36),
        name="adam",
    )(table, rates, *sources, master, one, two, left, right)


def body(
    activations,
    cotangent,
    level_table,
    true_frames,
    group_pattern,
    noise_levels,
    context_flags,
    owner_list,
    masters,
    moment_one,
    moment_two,
    basis_left,
    basis_right,
):
    groups = lax.axis_size("mp")
    owners = lax.axis_size("dp")
    chips = owners // 2
    bits = chips.bit_length() - 1
    z = lax.axis_index("mp")
    device = lax.axis_index("dp")
    core = device % 2
    chip = device // 2
    local_clips = true_frames.shape[0]
    column_clips = 2 * local_clips
    assert column_clips == groups and chips == 1 << bits
    shapes, counts = tile_layout(groups)
    slots = masters.shape[1]
    fast = chips == 4 and groups == 4

    def swap(v, step):
        return lax.ppermute(v, "dp", [(i, i ^ step) for i in range(owners)])

    def across(v):
        return swap(v, 1)

    def plane(v, bit):
        return swap(v, 2 << bit)

    def z_get(v, s):
        return lax.ppermute(v, "mp", [((i + s) % groups, i) for i in range(groups)])

    def z_put(v, s):
        return lax.ppermute(v, "mp", [(i, (i + s) % groups) for i in range(groups)])

    def plane_double(v):
        held = v[None]
        for bit in range(bits):
            held = jnp.concatenate([held, plane(held, bit)], axis=0)
        return held

    def plane_gather(v):
        if chips != 4:
            return plane_double(v)
        half = v.shape[0] // 2
        by_x, by_y = plane(v, 0), plane(v, 1)
        low, high = plane(by_x[:half], 1), plane(by_y[half:], 0)
        return jnp.stack([v, by_x, by_y, jnp.concatenate([low, high], axis=0)])

    def add(a, b):
        return (a.astype(F32) + b.astype(F32)).astype(BF)

    def plane_reduce(v):
        if chips != 4:
            held = v
            for bit in reversed(range(bits)):
                half = 1 << bit
                held = add(held[:half], plane(held[half:], bit))
            return held[0]
        half = v.shape[1] // 2
        got_low = [plane(v[1, :half], 0), plane(v[3, :half], 0)]
        got_high = [plane(v[2, half:], 1), plane(v[3, half:], 1)]
        pass_low = plane(add(v[2, :half], got_low[1]), 1)
        pass_high = plane(add(v[1, half:], got_high[1]), 0)
        low = v[0, :half].astype(F32) + got_low[0].astype(F32) + pass_low.astype(F32)
        high = v[0, half:].astype(F32) + got_high[0].astype(F32) + pass_high.astype(F32)
        return jnp.concatenate([low, high], axis=0).astype(BF)

    def z_gather(v):
        return jnp.stack([v] + [z_get(v, s) for s in range(1, groups)])

    def z_reduce(v):
        total = v[0].astype(F32)
        for s in range(1, groups):
            total = total + z_put(v[s], s).astype(F32)
        return total

    frame_index = jnp.arange(FRAMES, dtype=jnp.int32)

    def mask_rows(flagged, lengths):
        valid = frame_index[None, :] < lengths[:, None]
        in_context = flagged & valid
        visible = valid[:, :, None] & (
            jnp.logical_not(in_context)[:, None, :] | in_context[:, :, None]
        )
        return jnp.repeat(jnp.where(visible, 0.0, -1e30).astype(F32), FRAME_TOK, axis=2)

    def level_rows(flagged, patterns):
        pattern_hot = (patterns[:, None] == jnp.arange(PATTERNS, dtype=jnp.int32)[None, :]).astype(
            jnp.int32
        )
        return jnp.where(
            flagged, 0, jnp.sum(pattern_hot[:, :, None] * noise_levels[None, :, :], axis=1)
        )

    rows = TILE // chips
    level_ids = jnp.arange(LEVELS, dtype=jnp.int32)[None, :]
    if fast:
        with jax.named_scope("entry"):
            flagged = context_flags == 1
            weights, w_mod, x, dy, h1, mods, bias, all_embedded, own_hot = entry(
                masters[0],
                level_table,
                level_rows(flagged, group_pattern),
                mask_rows(flagged, true_frames),
                activations,
                cotangent,
                owner_list,
            )
            got = weights[0].reshape(chips, groups, 4, rows, D)
            w_up = weights[1].reshape(-1, D)
            w_down = weights[2].reshape(-1, D)
    else:
        with jax.named_scope("entry"):
            holds = (z // local_clips) == core
            local = (z % local_clips) * CLIP
            pair = jnp.stack(
                [
                    lax.dynamic_slice_in_dim(activations, local, CLIP, axis=0),
                    lax.dynamic_slice_in_dim(cotangent, local, CLIP, axis=0),
                ]
            )
            pair = jnp.where(holds, pair, across(pair))
            x, dy = pair[0], pair[1]
            facts = jnp.concatenate(
                [context_flags, true_frames[:, None], group_pattern[:, None]], axis=1
            ).astype(jnp.int32)
            other = across(facts)
            facts = jnp.where(
                core == 0, jnp.concatenate([facts, other]), jnp.concatenate([other, facts])
            )
            flagged = facts[:, :FRAMES] == 1
            levels = level_rows(flagged, facts[:, FRAMES + 1])
            bias = lax.dynamic_index_in_dim(
                mask_rows(flagged, facts[:, FRAMES]), z, axis=0, keepdims=False
            )
            all_levels = plane_double(levels)

        with jax.named_scope("owner_gather"):
            gathered = lax.all_gather(masters[0].astype(BF), "dp", axis=0, tiled=True)
            table = lax.all_gather(level_table, "dp", axis=0, tiled=True)
            position = jnp.arange(owner_list.shape[0], dtype=jnp.int32)
            inverse = jnp.sum(
                jnp.where(owner_list[None, :] == position[:, None], position[None, :], 0), axis=1
            ).astype(jnp.int32)
            chunk_attn, chunk_up, chunk_down, w_mod = pick_chunk_plain(
                gathered, inverse, chip, core, chips, shapes, counts
            )

        with jax.named_scope("weights"):
            got = plane_gather(z_gather(chunk_attn)).reshape(chips, groups, 4, rows, D)
            w_up = plane_gather(z_gather(chunk_up)).reshape(-1, D)
            w_down = plane_gather(z_gather(chunk_down)).reshape(-1, D)

        with jax.named_scope("modulation"):
            hot = (levels.reshape(-1)[:, None] == level_ids).astype(BF)
            embedded = dot(hot, table, NN).astype(BF)
            mod_part = dot(embedded, w_mod, NN).reshape(column_clips, FRAMES, -1)
            pieces = [lax.dynamic_index_in_dim(mod_part, z, axis=0, keepdims=False)]
            for s in range(1, groups):
                piece = lax.dynamic_index_in_dim(
                    mod_part, (z + groups - s) % groups, axis=0, keepdims=False
                )
                pieces.append(z_get(piece, s))
            mods = lax.dynamic_slice_in_dim(
                jnp.stack(pieces + pieces), (groups - z) % groups, groups, axis=0
            )
            mods = (
                mods.reshape(groups, FRAMES, 6, D // groups).transpose(1, 2, 0, 3).reshape(FRAMES, 6, D)
            )
            (h1,) = row_call(first_norm_kernel, "first_norm", [x], mods, [BF], [], 4 * CLIP * D)

    w_in = got[:, :, :3].transpose(1, 2, 0, 3, 4).reshape(-1, D)
    w_out = got[:, :, 3].transpose(1, 0, 2, 3).reshape(-1, D)

    mb = CLIP * D
    with jax.named_scope("attention"):
        qkv = dot(h1, w_in, NT).astype(BF)
        o_rows, lse = attend(qkv, bias)
        part = dot(o_rows, w_out, TN).astype(BF)
        y1, branch, h2, de = row_call(
            middle_kernel, "middle", [x, part, across(part), dy], mods, [F32, BF, BF, BF], [], 18 * mb
        )

    with jax.named_scope("feed"):
        e_part, dh2_part, d_up, d_down = feed_both(h2, de, w_up, w_down)
    if fast:
        with jax.named_scope("exit"):
            block_output, input_grad, everyone, d_w_mod, table_grad = exit_call(
                y1, dh2_part, e_part, dy, branch, x, h1, qkv, o_rows, w_in, w_out, w_mod,
                d_up, d_down, mods, bias, lse, all_embedded, own_hot,
            )
            input_grad = input_grad.astype(F32)
    else:
        with jax.named_scope("feed_back"):
            out, dy1, da, dm_mid = row_call(
                back_kernel,
                "back",
                [y1, dh2_part, across(dh2_part), dy, branch, e_part, across(e_part)],
                mods,
                [BF, F32, BF],
                [4],
                24 * mb,
            )
            shape = (chips, groups, -1, D)
            red_up = z_reduce(plane_reduce(d_up.reshape(shape))).astype(BF)
            red_down = z_reduce(plane_reduce(d_down.reshape(shape))).astype(BF)

        def to_column(rows_here):
            half = CLIP // 2
            mine = lax.dynamic_slice_in_dim(rows_here, core * half, half, axis=0)
            by_clip = [mine] + [z_get(mine, s) for s in range(1, groups)]
            by_clip = lax.dynamic_slice_in_dim(jnp.stack(by_clip + by_clip), (groups - z) % groups, groups, axis=0)
            keep = lax.dynamic_slice_in_dim(by_clip, core * local_clips, local_clips, axis=0)
            send = lax.dynamic_slice_in_dim(by_clip, (1 - core) * local_clips, local_clips, axis=0)
            got_half = across(send)
            both = jnp.where(
                core == 0, jnp.stack([keep, got_half], axis=1), jnp.stack([got_half, keep], axis=1)
            )
            return both.reshape(local_clips * CLIP, D)

        with jax.named_scope("block_output"):
            block_output = to_column(out)

        with jax.named_scope("attention_back"):
            do_rows = dot(w_out, da, NT).astype(BF)
            d_out = dot(o_rows, da, NN).astype(BF)
            d_qkv = attend_back(qkv, o_rows, do_rows, lse, bias)
            dh1_part = dot(d_qkv, w_in, NN).astype(BF)
            d_in = dot(d_qkv, h1, TN).astype(BF)
            in_grad, dm_last = row_call(
                last_kernel, "last", [x, dh1_part, across(dh1_part), dy1], mods, [BF], [2], 12 * mb
            )
            d_in = d_in.reshape(groups, 3, chips, rows, D).transpose(2, 0, 1, 3, 4)
            d_out = d_out.reshape(groups, 1, chips, rows, D).transpose(2, 0, 1, 3, 4)
            d_attn = jnp.concatenate([d_in, d_out], axis=2).reshape(chips, groups, 4 * rows, D)
            red_attn = z_reduce(plane_reduce(d_attn)).astype(BF)

        with jax.named_scope("input_grad"):
            input_grad = to_column(in_grad).astype(F32)

        with jax.named_scope("modulation_back"):
            d_mod = jnp.stack(
                [dm_last[:, 0], dm_last[:, 1], dm_mid[:, 2], dm_mid[:, 0], dm_mid[:, 1], dm_mid[:, 3]], axis=1
            ).astype(BF)
            d_mod = (
                d_mod.reshape(FRAMES, 6, groups, D // groups).transpose(2, 0, 1, 3).reshape(groups, FRAMES, -1)
            )
            pieces = [lax.dynamic_index_in_dim(d_mod, z, axis=0, keepdims=False)]
            for s in range(1, groups):
                pieces.append(z_put(lax.dynamic_index_in_dim(d_mod, (z + s) % groups, axis=0, keepdims=False), s))
            d_mod = jnp.stack(pieces)
            d_mod = plane_double(d_mod).reshape(chips * groups * FRAMES, -1)
            back_clip = (z + groups - jnp.arange(groups, dtype=jnp.int32)) % groups
            clip_hot = (back_clip[:, None] == jnp.arange(groups, dtype=jnp.int32)[None, :]).astype(
                jnp.int32
            )
            order = jnp.sum(clip_hot[None, :, :, None] * all_levels[:, None, :, :], axis=2).reshape(-1)
            all_embedded = dot((order[:, None] == level_ids).astype(BF), table, NN).astype(BF)
            own_levels = level_table.shape[0]
            own_ids = device * own_levels + jnp.arange(own_levels, dtype=jnp.int32)[None, :]
            own_hot = (order[:, None] == own_ids).astype(BF)
            d_w_mod = dot(all_embedded, d_mod, TN).astype(BF)
            own_levels = level_table.shape[0]
            own_rows = dot(dot(own_hot, d_mod, TN).astype(BF), w_mod, NT)
            own_rows = own_rows.reshape(groups, own_levels // groups, D)
            table_grad = lax.dynamic_index_in_dim(own_rows, z, axis=0, keepdims=False)
            for s in range(1, groups):
                table_grad = table_grad + z_put(
                    lax.dynamic_index_in_dim(own_rows, (z + s) % groups, axis=0, keepdims=False), s
                )

    with jax.named_scope("owners"):
        if not fast:
            reduced = jnp.concatenate([red_attn, red_up, red_down], axis=0)
            if chips == 4:
                height = reduced.shape[0]
                plane_parts = plane_gather(reduced.reshape(2, height // 2, D)).reshape(chips, height, D)
            else:
                plane_parts = plane_double(reduced)
            everyone = jnp.stack([plane_parts, across(plane_parts)], axis=1).reshape(owners, -1, D)
        tile_ids = lax.dynamic_slice_in_dim(owner_list, device * slots, slots)
        rates = kind_rates(tile_ids, counts)
        if fast:
            picks = pick_table(tile_ids, device)
            sources = [everyone, d_w_mod]
        else:
            picks = jnp.zeros((slots, 12), jnp.int32)
            absolute = jnp.take(
                everyone, jnp.bitwise_xor(jnp.arange(owners, dtype=jnp.int32), device), axis=0
            ).reshape(chips, 2, -1, D)
            attn = absolute[:, :, : 4 * rows].reshape(chips, 2, 4, rows, D)
            attn = attn.transpose(2, 1, 0, 3, 4).reshape(4, -1, D)
            ffn_rows = (absolute.shape[2] - 4 * rows) // 2
            up = absolute[:, :, 4 * rows : 4 * rows + ffn_rows].transpose(1, 0, 2, 3).reshape(-1, D)
            down = absolute[:, :, 4 * rows + ffn_rows :].transpose(1, 0, 2, 3).reshape(-1, D)
            g_in = jnp.concatenate([attn[0].T, attn[1].T, attn[2].T], axis=1)
            packed = pack([g_in, attn[3], up.T, down, d_w_mod])
            sources = [jnp.take(packed, tile_ids, axis=0)]
        new_masters, new_one, new_two, new_weights = adam(
            picks, rates, sources, masters[0], moment_one[0], moment_two[0], basis_left[0], basis_right[0]
        )
    return (
        block_output,
        input_grad,
        table_grad,
        new_masters[None],
        new_one[None],
        new_two[None],
        new_weights[None],
    )


def solution(mesh):
    tiles = P("mp", "dp", None, None)
    in_specs = (
        P("dp", None),
        P("dp", None),
        P("dp", None),
        P("dp"),
        P("dp"),
        P(),
        P("dp", None),
        P(),
        tiles,
        tiles,
        tiles,
        tiles,
        tiles,
    )
    out_specs = (P("dp", None), P("dp", None), P(("dp", "mp"), None), tiles, tiles, tiles, tiles)
    return jax.shard_map(body, mesh=mesh, in_specs=in_specs, out_specs=out_specs, check_vma=False)
```

```python
import functools

import jax
import jax.numpy as jnp
from jax import lax
from jax.experimental import pallas as pl
from jax.experimental.pallas import tpu as pltpu
from jax.sharding import PartitionSpec as P

D = 1024
H = 16
HD = 64
FF = 4096
FRAMES = 16
FRAME_TOK = 64
LEVELS = 1024
PATTERNS = 4
TILE = 128
CLIP = FRAMES * FRAME_TOK

EPS_NORM = 1e-06
BETA_ONE = 0.5
BETA_TWO = 0.75
EPS_ADAM = 1e-08
DECAY = 0.01
LOG2E = 1.4426950408889634
GELU_A = 0.7978845608028654
GELU_B = 0.044715

BF = jnp.bfloat16
F32 = jnp.float32
VMEM_BYTES = 60 * 1024 * 1024


def params(**kw):
    return pltpu.CompilerParams(vmem_limit_bytes=VMEM_BYTES, **kw)


def cost(flops, nbytes, trans=0):
    return pl.CostEstimate(flops=int(flops), bytes_accessed=int(nbytes), transcendentals=int(trans))


def dot(left, right, dims):
    return lax.dot_general(left, right, (dims, ((), ())), preferred_element_type=F32)


NN = ((1,), (0,))
NT = ((1,), (1,))
TN = ((0,), (0,))


def tile_layout(groups):
    local_width = H // groups * HD
    shapes = [
        (D, 3 * local_width),
        (local_width, D),
        (D, FF // groups),
        (FF // groups, D),
        (D, 6 * D // groups),
    ]
    counts = [height // TILE * (breadth // TILE) for height, breadth in shapes]
    return (shapes, counts)


def kind_rates(tile_ids, counts):
    scales = [
        0.35 * D ** (-0.5),
        1.5 * (H * HD) ** (-0.5),
        0.5 * D ** (-0.5),
        0.5 * FF ** (-0.5),
        0.5 * D ** (-0.5),
    ]
    tile_rates = jnp.full(tile_ids.shape, scales[0], F32)
    boundary = 0
    for category in range(1, 5):
        boundary = boundary + counts[category - 1]
        tile_rates = jnp.where(tile_ids >= boundary, jnp.float32(scales[category]), tile_rates)
    return tile_rates


def unpack(tile_stack, shapes, counts):
    matrices = []
    offset = 0
    for (height, breadth), amount in zip(shapes, counts):
        stacked = tile_stack[offset : offset + amount].reshape(
            height // TILE, breadth // TILE, TILE, TILE
        )
        matrices.append(stacked.transpose(0, 2, 1, 3).reshape(height, breadth))
        offset = offset + amount
    return matrices


def pack(matrices):
    stacked = []
    for matrix in matrices:
        height, breadth = matrix.shape
        stacked.append(
            matrix.reshape(height // TILE, TILE, breadth // TILE, TILE)
            .transpose(0, 2, 1, 3)
            .reshape(-1, TILE, TILE)
        )
    return jnp.concatenate(stacked, axis=0)


def pick_chunk_plain(gathered, inverse, chip, core, chips, shapes, counts):
    w_qkv, w_out, w_up, w_down, w_mod = unpack(jnp.take(gathered, inverse, axis=0), shapes, counts)
    width = w_out.shape[0]
    half = width // 2
    ffn = w_up.shape[1] // 2
    rows, ffn_rows = half // chips, ffn // chips
    parts = []
    for role in range(3):
        parts.append(w_qkv[:, role * width : (role + 1) * width].T)
    parts.append(w_out)
    start = core * half + chip * rows
    attn = jnp.concatenate([lax.dynamic_slice_in_dim(p, start, rows, axis=0) for p in parts], axis=0)
    ffn_start = core * ffn + chip * ffn_rows
    up = lax.dynamic_slice_in_dim(w_up.T, ffn_start, ffn_rows, axis=0)
    down = lax.dynamic_slice_in_dim(w_down, ffn_start, ffn_rows, axis=0)
    return attn, up, down, w_mod


def norm_rows(values):
    centered = values - jnp.mean(values, axis=-1, keepdims=True)
    inverse_std = lax.rsqrt(jnp.mean(centered * centered, axis=-1, keepdims=True) + EPS_NORM)
    return centered * inverse_std, inverse_std


def norm_back(grad_normed, normed, inverse_std):
    centered = grad_normed - jnp.mean(grad_normed, axis=-1, keepdims=True)
    return inverse_std * (centered - normed * jnp.mean(grad_normed * normed, axis=-1, keepdims=True))


def frames_of(rows):
    return rows.reshape(-1, FRAME_TOK, D)


def flat(framed):
    return framed.reshape(-1, D)


BLK = 256
FBLK = BLK // FRAME_TOK


def row_spec():
    return pl.BlockSpec((BLK, D), lambda i: (i, 0))


def mod_spec(parts):
    return pl.BlockSpec((FBLK, parts, D), lambda i: (i, 0, 0))


def row_call(kernel, name, row_ins, mods, row_outs, mod_outs, nbytes):
    outs = [jax.ShapeDtypeStruct((CLIP, D), t) for t in row_outs]
    outs += [jax.ShapeDtypeStruct((FRAMES, n, D), F32) for n in mod_outs]
    return pl.pallas_call(
        kernel,
        grid=(CLIP // BLK,),
        in_specs=[row_spec() for _ in row_ins] + [mod_spec(6)],
        out_specs=[row_spec() for _ in row_outs] + [mod_spec(n) for n in mod_outs],
        out_shape=outs,
        compiler_params=params(),
        cost_estimate=cost(30 * CLIP * D, nbytes),
        name=name,
    )(*row_ins, mods)


def first_norm_kernel(x_ref, mod_ref, h_ref):
    normed, _ = norm_rows(x_ref[...].astype(F32))
    mods = mod_ref[...]
    h_ref[...] = flat(
        frames_of(normed) * (1.0 + mods[:, 1:2]) + mods[:, 0:1]
    ).astype(BF)


def middle_kernel(x_ref, a_ref, b_ref, dy_ref, mod_ref, y_ref, s_ref, h_ref, de_ref):
    mods = mod_ref[...]
    branch = (a_ref[...].astype(F32) + b_ref[...].astype(F32)).astype(BF)
    s_ref[...] = branch
    mid = frames_of(x_ref[...].astype(F32)) + mods[:, 2:3] * frames_of(branch.astype(F32))
    y_ref[...] = flat(mid)
    normed, _ = norm_rows(flat(mid))
    h_ref[...] = flat(
        frames_of(normed) * (1.0 + mods[:, 4:5]) + mods[:, 3:4]
    ).astype(BF)
    de_ref[...] = flat(mods[:, 5:6] * frames_of(dy_ref[...].astype(F32))).astype(BF)


def back_kernel(y_ref, g_ref, gp_ref, dy_ref, s_ref, e_ref, ep_ref, mod_ref, out_ref, dy1_ref, da_ref, dm_ref):
    mods = mod_ref[...]
    mid = y_ref[...]
    feed = e_ref[...].astype(F32) + ep_ref[...].astype(F32)
    dy = dy_ref[...].astype(F32)
    out_ref[...] = (mid + flat(mods[:, 5:6] * frames_of(feed))).astype(BF)
    normed, inverse_std = norm_rows(mid)
    grad = g_ref[...].astype(F32) + gp_ref[...].astype(F32)
    dm_ref[:, 0] = jnp.sum(frames_of(grad), axis=1)
    dm_ref[:, 1] = jnp.sum(frames_of(grad * normed), axis=1)
    scaled = flat(frames_of(grad) * (1.0 + mods[:, 4:5]))
    dy1 = dy + norm_back(scaled, normed, inverse_std)
    dy1_ref[...] = dy1
    dm_ref[:, 2] = jnp.sum(frames_of(dy1 * s_ref[...].astype(F32)), axis=1)
    dm_ref[:, 3] = jnp.sum(frames_of(dy * feed), axis=1)
    da_ref[...] = flat(mods[:, 2:3] * frames_of(dy1)).astype(BF)


def last_kernel(x_ref, g_ref, gp_ref, dy1_ref, mod_ref, out_ref, dm_ref):
    mods = mod_ref[...]
    normed, inverse_std = norm_rows(x_ref[...].astype(F32))
    grad = g_ref[...].astype(F32) + gp_ref[...].astype(F32)
    dm_ref[:, 0] = jnp.sum(frames_of(grad), axis=1)
    dm_ref[:, 1] = jnp.sum(frames_of(grad * normed), axis=1)
    scaled = flat(frames_of(grad) * (1.0 + mods[:, 1:2]))
    out_ref[...] = (dy1_ref[...] + norm_back(scaled, normed, inverse_std)).astype(BF)


MESH = pl.DeviceIdType.MESH
HEAD_TILES = 36
TABLE_TILES = 8
PAYLOAD = 46
LEVEL_TILE = HEAD_TILES + TABLE_TILES


class Link:
    def __init__(self, sends, recvs):
        self.sends, self.recvs, self.used, self.pending = sends, recvs, 0, []

    def make(self, src, dst, dp, mp):
        copy = pltpu.make_async_remote_copy(
            src_ref=src,
            dst_ref=dst,
            send_sem=self.sends.at[self.used],
            recv_sem=self.recvs.at[self.used],
            device_id=(dp, mp),
            device_id_type=MESH,
        )
        self.used += 1
        self.pending.append(copy)
        return copy

    def send(self, src, dst, dp, mp):
        copy = self.make(src, dst, dp, mp)
        copy.start()
        return copy

    def drain(self):
        for copy in self.pending:
            copy.wait_send()
        self.pending = []


def greet(d, z):
    barrier = pltpu.get_barrier_semaphore()
    for step in (1, 2, 4):
        pl.semaphore_signal(barrier, inc=1, device_id=(jnp.bitwise_xor(d, step), z), device_id_type=MESH)
    for s in (1, 2, 3):
        pl.semaphore_signal(barrier, inc=1, device_id=(d, lax.rem(z + s, 4)), device_id_type=MESH)
    pl.semaphore_wait(barrier, 6)


QBLK = 256
ROWS = 512
SCALE2 = HD ** (-0.5) * LOG2E


ENTRY_COPIES = 8 + 45 + 3


def front_kernel(
    idx_ref,
    pay_ref,
    act_ref,
    cot_ref,
    bias_ref,
    w_ref,
    wmod_out,
    x_out,
    dy_out,
    h_out,
    wpack_out,
    qkv_out,
    o_out,
    branch_out,
    y_out,
    e_out,
    dh_out,
    dup_out,
    ddown_out,
    mods_ref,
    bias_out,
    lse_ref,
    emb_ref,
    own_hot_ref,
    gath,
    own,
    turn,
    xs,
    dys,
    bs,
    part,
    modbuf,
    hots,
    hs,
    wpack,
    qs,
    os_,
    mine,
    peer,
    e_acc,
    dh_acc,
    wfeed,
    up_stage,
    down_stage,
    up_acc,
    down_acc,
    sends,
    recvs,
    swap_sends,
    swap_recvs,
    strip_sends,
    strip_recvs,
    local_sems,
    pack_sems,
    stage_sems,
):
    d, z = lax.axis_index("dp"), lax.axis_index("mp")
    core, chip = lax.rem(d, 2), d // 2
    dk, dx, dyd = jnp.bitwise_xor(d, 1), jnp.bitwise_xor(d, 2), jnp.bitwise_xor(d, 4)
    dxy = jnp.bitwise_xor(d, 6)
    link = Link(sends, recvs)
    greet(d, z)

    def slot(owner, first=0, count=PAYLOAD):
        return gath.at[pl.ds(owner * PAYLOAD + first, count)]

    half = PAYLOAD // 2
    home = pltpu.make_async_copy(pay_ref, slot(d), local_sems.at[0])
    home.start()
    to_x = link.send(pay_ref, slot(d), dx, z)
    to_y = link.send(pay_ref, slot(d), dyd, z)
    to_k = link.send(pay_ref, slot(d), dk, z)

    holds = (z // 2) == core
    rows = pl.ds(lax.rem(z, 2) * CLIP, CLIP)
    picks = [
        (act_ref.at[rows], xs),
        (cot_ref.at[rows], dys),
        (bias_ref.at[lax.rem(z, 2)], bs),
    ]

    def swaps():
        return [
            pltpu.make_async_remote_copy(
                src_ref=src,
                dst_ref=dst,
                send_sem=swap_sends.at[i],
                recv_sem=swap_recvs.at[i],
                device_id=(dk, z),
                device_id_type=MESH,
            )
            for i, (src, dst) in enumerate(picks)
        ]

    def keeps():
        return [pltpu.make_async_copy(src, dst, local_sems.at[1 + i]) for i, (src, dst) in enumerate(picks)]

    @pl.when(holds)
    def _():
        for copy in swaps() + keeps():
            copy.start()

    to_x.wait_recv()
    x_to_y = link.send(slot(dx, 0, half), slot(dx, 0, half), dyd, z)
    x_to_k = link.send(slot(dx), slot(dx), dk, z)
    to_y.wait_recv()
    y_to_x = link.send(slot(dyd, half, half), slot(dyd, half, half), dx, z)
    y_to_k = link.send(slot(dyd), slot(dyd), dk, z)

    @pl.when(holds)
    def _():
        for copy in swaps():
            copy.wait_send()
        for copy in keeps():
            copy.wait()

    @pl.when(jnp.logical_not(holds))
    def _():
        for copy in swaps():
            copy.wait_recv()

    bias_out[...] = bs[...]
    locals_used = [7]

    def save(src, dst):
        copy = pltpu.make_async_copy(src, dst, local_sems.at[locals_used[0]])
        locals_used[0] += 1
        copy.start()
        return copy

    x_saved = save(xs, x_out)
    dy_saved = save(dys, dy_out)

    x_to_y.wait_recv()
    y_to_x.wait_recv()
    xy_to_k = link.send(slot(dxy), slot(dxy), dk, z)
    home.wait()
    to_k.wait_recv()
    x_to_k.wait_recv()
    y_to_k.wait_recv()
    xy_to_k.wait_recv()

    def tile(number):
        return gath[idx_ref[number]]

    def pick_attn(j, _):
        lanes = pl.ds(pl.multiple_of(j * TILE, TILE), TILE)
        for role in range(3):
            turn[role] = tile(j * 6 + 2 * role + core).T
        turn[3] = tile(48 + core * 8 + j)
        for role in range(4):
            own[0, role * 32 : (role + 1) * 32, lanes] = turn[role, pl.ds(pl.multiple_of(chip * 32, 32), 32), :]
        return 0

    def pick_feed(j, _):
        lanes = pl.ds(pl.multiple_of(j * TILE, TILE), TILE)
        own[1, :, lanes] = tile(64 + j * 8 + 4 * core + chip).T
        own[2, :, lanes] = tile(128 + (4 * core + chip) * 8 + j)
        return 0

    def pick_mod(j, _):
        strip = pl.ds(pl.multiple_of(j * TILE, TILE), TILE)
        for col in range(12):
            qs[col // 3, strip, (col % 3) * TILE : (col % 3 + 1) * TILE] = tile(192 + j * 12 + col)
        return 0

    along, by_x, by_y, diag = {}, {}, {}, {}
    all_groups = [(g, s) for g in range(3) for s in (0, 1, 3, 2)]

    def landing(g, p, m):
        return w_ref.at[p, m] if g == 0 else wfeed.at[g - 1, p, m]

    for g, s in all_groups:
        m = lax.rem(z + 4 - s, 4)
        if s:
            along[g, s] = link.make(own.at[g], landing(g, 0, z), d, lax.rem(z + s, 4))
        src = own.at[g] if s == 0 else landing(g, 0, m)
        by_x[g, s] = link.make(src, landing(g, 1, m), dx, z)
        by_y[g, s] = link.make(src, landing(g, 2, m), dyd, z)
        if s < 2:
            diag[g, s] = link.make(landing(g, 1, m), landing(g, 3, m), dyd, z)
        else:
            diag[g, s] = link.make(landing(g, 2, m), landing(g, 3, m), dx, z)
    homes = [pltpu.make_async_copy(own.at[g], landing(g, 0, z), local_sems.at[4 + g]) for g in range(3)]

    def send_along(g):
        for s in (1, 3, 2):
            along[g, s].start()

    def send_plane(g, s):
        if s:
            along[g, s].wait_recv()
        by_x[g, s].start()
        by_y[g, s].start()

    def send_diag(g, s):
        (by_x if s < 2 else by_y)[g, s].wait_recv()
        diag[g, s].start()

    lax.fori_loop(0, 8, pick_attn, 0)
    send_along(0)
    send_plane(0, 0)
    homes[0].start()
    lax.fori_loop(0, 8, pick_feed, 0)
    send_along(1)
    send_along(2)
    send_plane(1, 0)
    homes[1].start()
    homes[2].start()

    lax.fori_loop(0, 8, pick_mod, 0)
    mod_saved = save(qs, wmod_out)
    places = lax.broadcasted_iota(jnp.int32, (32, LEVELS), 1).astype(F32)
    for owner in range(8):
        codes = gath[owner * PAYLOAD + LEVEL_TILE][:32].astype(F32)
        level = codes[:, 0:1] * 32.0 + codes[:, 64:65]
        hots[owner * 32 : (owner + 1) * 32] = jnp.where(level == places, 1.0, 0.0).astype(BF)
    own_hot_ref[...] = hots[:, pl.ds(pl.multiple_of(d * TILE, TILE), TILE)]
    for j in range(TABLE_TILES):
        strip = jnp.concatenate([gath[owner * PAYLOAD + HEAD_TILES + j] for owner in range(8)], axis=0)
        emb_ref[:, j * TILE : (j + 1) * TILE] = dot(hots[...], strip, NN).astype(BF)
    embedded = emb_ref[pl.ds(pl.multiple_of(chip * 64, 64), 64), :]
    for k in range(4):
        part[:, :, k * 384 : (k + 1) * 384] = dot(embedded, qs[k], NN).reshape(4, FRAMES, 384)
    modbuf[z] = part[z]
    shared = {}
    for s in (1, 3, 2):
        shared[s] = link.send(part.at[lax.rem(z + s, 4)], modbuf.at[z], d, lax.rem(z + s, 4))

    for s in (1, 3, 2):
        send_plane(0, s)
    send_plane(2, 0)
    for s in (0, 1, 3, 2):
        send_diag(0, s)

    for s in (1, 3, 2):
        shared[s].wait_recv()
    for m in range(4):
        for c in range(6):
            mods_ref[:, c, m * 256 : (m + 1) * 256] = modbuf[m, :, c * 256 : (c + 1) * 256]

    def norm_strip(i, _):
        strip = pl.ds(pl.multiple_of(i * BLK, BLK), BLK)
        normed, _ = norm_rows(xs[strip].astype(F32))
        mods = mods_ref[pl.ds(i * FBLK, FBLK)]
        hs[strip] = flat(frames_of(normed) * (1.0 + mods[:, 1:2]) + mods[:, 0:1]).astype(BF)
        return 0

    lax.fori_loop(0, CLIP // BLK, norm_strip, 0)
    h_saved = save(hs, h_out)

    def late(g, p):
        for s in (0, 1, 3, 2):
            if p == 3:
                diag[g, s].wait_recv()
            elif (p == 1) == (s >= 2):
                (by_x if p == 1 else by_y)[g, s].wait_recv()

    for p in (1, 2, 3):
        late(0, p)
    homes[0].wait()

    def packs(m):
        return [
            pltpu.make_async_copy(
                w_ref.at[p, m, pl.ds(role * 32, 32)],
                wpack.at[m, pl.ds(role * TILE + p * 32, 32)],
                pack_sems.at[m * 16 + p * 4 + role],
            )
            for p in range(4)
            for role in range(4)
        ]

    def pack_start(m, _):
        for copy in packs(m):
            copy.start()
        return 0

    lax.fori_loop(0, 4, pack_start, 0)
    mod_saved.wait()

    def project_in(m, _):
        for copy in packs(m):
            copy.wait()
        qs[m] = dot(hs[...], wpack[m, 0 : 3 * TILE], NT).astype(BF)
        return 0

    lax.fori_loop(0, 4, project_in, 0)
    pack_saved = save(wpack, wpack_out)
    qkv_saved = save(qs, qkv_out)

    def attend_group(m, _):
        @pl.when(m == 0)
        def _():
            for s in (1, 3, 2):
                send_plane(1, s)

        @pl.when(m == 1)
        def _():
            send_diag(1, 0)
            send_diag(1, 1)

        @pl.when(m == 2)
        def _():
            send_plane(2, 1)
            send_plane(2, 3)
            send_diag(1, 3)

        @pl.when(m == 3)
        def _():
            send_plane(2, 2)
            send_diag(1, 2)
            send_diag(2, 0)

        for head in range(2):
            lanes = slice(head * HD, (head + 1) * HD)
            keys = qs[m, :, TILE + head * HD : TILE + (head + 1) * HD]
            values = qs[m, :, 2 * TILE + head * HD : 2 * TILE + (head + 1) * HD]

            def step(i, _, lanes=lanes, keys=keys, values=values, head=head):
                across = pl.ds(pl.multiple_of(i * QBLK, QBLK), QBLK)
                queries = qs[m, across, lanes]
                scores = dot(keys, queries, NT).reshape(FRAMES, FRAME_TOK, QBLK)
                scores = scores * SCALE2 + bs[:, across][:, None, :]
                peak = jnp.max(jnp.max(scores, axis=0), axis=0, keepdims=True)
                weights = jnp.exp2(scores - peak[None])
                total = jnp.sum(jnp.sum(weights, axis=0), axis=0, keepdims=True)
                mixed = dot(values, weights.reshape(CLIP, QBLK).astype(BF), TN)
                os_[m, lanes, across] = (mixed / total).astype(BF)
                lse_ref[m, head : head + 1, across] = peak + jnp.log2(total)
                return 0

            lax.fori_loop(0, CLIP // QBLK, step, 0)
        return 0

    lax.fori_loop(0, 4, attend_group, 0)
    o_saved = save(os_, o_out)
    send_diag(2, 1)

    def swap_strip(i):
        strip = pl.ds(pl.multiple_of(i * BLK, BLK), BLK)
        return pltpu.make_async_remote_copy(
            src_ref=mine.at[strip],
            dst_ref=peer.at[strip],
            send_sem=strip_sends.at[i],
            recv_sem=strip_recvs.at[i],
            device_id=(dk, z),
            device_id_type=MESH,
        )

    def project_out(i, _):
        strip = pl.ds(pl.multiple_of(i * BLK, BLK), BLK)
        total = dot(os_[0, :, strip], wpack[0, 3 * TILE : 4 * TILE], TN)
        for m in range(1, 4):
            total = total + dot(os_[m, :, strip], wpack[m, 3 * TILE : 4 * TILE], TN)
        mine[strip] = total.astype(BF)
        swap_strip(i).start()
        return 0

    lax.fori_loop(0, CLIP // BLK, project_out, 0)
    h_saved.wait()
    dy_saved.wait()

    def middle_strip(i, _):
        strip = pl.ds(pl.multiple_of(i * BLK, BLK), BLK)
        swap_strip(i).wait_recv()
        mods = mods_ref[pl.ds(i * FBLK, FBLK)]
        branch = (mine[strip].astype(F32) + peer[strip].astype(F32)).astype(BF)
        peer[strip] = branch
        mid = frames_of(xs[strip].astype(F32)) + mods[:, 2:3] * frames_of(branch.astype(F32))
        dh_acc[strip] = flat(mid)
        normed, _ = norm_rows(flat(mid))
        hs[strip] = flat(frames_of(normed) * (1.0 + mods[:, 4:5]) + mods[:, 3:4]).astype(BF)
        dys[strip] = flat(mods[:, 5:6] * frames_of(dys[strip].astype(F32))).astype(BF)
        return 0

    lax.fori_loop(0, CLIP // BLK, middle_strip, 0)
    y_saved = save(dh_acc, y_out)
    branch_saved = save(peer, branch_out)
    send_diag(2, 3)
    send_diag(2, 2)
    e_acc[...] = jnp.zeros_like(e_acc)
    y_saved.wait()
    dh_acc[...] = jnp.zeros_like(dh_acc)
    homes[1].wait()
    homes[2].wait()

    def stages(block):
        buf, p, first = lax.rem(block, 2), block // 2, lax.rem(block, 2) * 2
        return [
            pltpu.make_async_copy(stage.at[buf], dst.at[p, pl.ds(first, 2)], stage_sems.at[2 * buf + k])
            for k, (stage, dst) in enumerate(((up_stage, dup_out), (down_stage, ddown_out)))
        ]

    def feed_block(block, _):
        for p in (1, 2, 3):

            @pl.when(block == 2 * p)
            def _(p=p):
                late(1, p)
                late(2, p)

        buf, p, first = lax.rem(block, 2), block // 2, lax.rem(block, 2) * 2
        up = wfeed[0, p, pl.ds(first, 2)].reshape(2 * TILE, D)
        down = wfeed[1, p, pl.ds(first, 2)].reshape(2 * TILE, D)

        @pl.when(block >= 2)
        def _():
            for copy in stages(block - 2):
                copy.wait()

        for piece in range(CLIP // ROWS):
            rows = slice(piece * ROWS, (piece + 1) * ROWS)
            hidden = hs[rows]
            grad = dys[rows]
            pre = dot(hidden, up, NT)
            square = pre * pre
            tanh = jnp.tanh(GELU_A * pre * (1.0 + GELU_B * square))
            act = (0.5 * pre * (1.0 + tanh)).astype(BF)
            slope = 0.5 * (1.0 + tanh) + 0.5 * pre * (1.0 - tanh * tanh) * (
                GELU_A * (1.0 + 3.0 * GELU_B * square)
            )
            grad_act = dot(grad, down, NT).astype(BF).astype(F32)
            grad_pre = (grad_act * slope).astype(BF)
            e_acc[rows] += dot(act, down, NN)
            dh_acc[rows] += dot(grad_pre, up, NN)
            if piece == 0:
                down_acc[...] = dot(act, grad, TN)
                up_acc[...] = dot(grad_pre, hidden, TN)
            else:
                down_stage[buf] = (down_acc[...] + dot(act, grad, TN)).astype(BF).reshape(2, TILE, D)
                up_stage[buf] = (up_acc[...] + dot(grad_pre, hidden, TN)).astype(BF).reshape(2, TILE, D)
        for copy in stages(block):
            copy.start()
        return 0

    lax.fori_loop(0, 8, feed_block, 0)
    branch_saved.wait()

    def swap_done(i, _):
        swap_strip(i).wait_send()
        return 0

    lax.fori_loop(0, CLIP // BLK, swap_done, 0)

    def cast_strip(i, _):
        strip = pl.ds(pl.multiple_of(i * BLK, BLK), BLK)
        mine[strip] = e_acc[strip].astype(BF)
        peer[strip] = dh_acc[strip].astype(BF)
        return 0

    lax.fori_loop(0, CLIP // BLK, cast_strip, 0)
    ends = [save(mine, e_out), save(peer, dh_out), x_saved, pack_saved, qkv_saved, o_saved]
    for block in (6, 7):
        for copy in stages(block):
            copy.wait()
    for copy in ends:
        copy.wait()
    link.drain()


def front(masters, level_table, levels, bias_pair, activations, cotangent, owner_list):
    slots = masters.shape[0]
    codes = jnp.stack([levels.reshape(-1) // 32, levels.reshape(-1) % 32], axis=1).astype(BF)
    codes = jnp.pad(jnp.repeat(codes, 64, axis=1), ((0, TILE - codes.shape[0]), (0, 0)))
    payload = jnp.concatenate(
        [
            masters.astype(BF),
            level_table.reshape(TILE, TABLE_TILES, TILE).transpose(1, 0, 2),
            codes[None],
            jnp.zeros((1, TILE, TILE), BF),
        ]
    )
    position = jnp.arange(owner_list.shape[0], dtype=jnp.int32)
    place = (position // slots) * PAYLOAD + position % slots
    index = jnp.sum(
        jnp.where(owner_list[None, :] == position[:, None], place[None, :], 0), axis=1
    ).astype(jnp.int32)
    vmem = pl.BlockSpec(memory_space=pltpu.VMEM)
    hbm = pl.BlockSpec(memory_space=pl.ANY)
    clip = jax.ShapeDtypeStruct((CLIP, D), BF)
    chunks = jax.ShapeDtypeStruct((4, 4, TILE, D), BF)
    thirds = jax.ShapeDtypeStruct((4, CLIP, 3 * TILE), BF)
    return pl.pallas_call(
        front_kernel,
        in_specs=[pl.BlockSpec(memory_space=pltpu.SMEM), hbm, hbm, hbm, hbm],
        out_specs=[hbm] * 14 + [vmem] * 5,
        out_shape=[
            chunks,
            thirds,
            clip,
            clip,
            clip,
            jax.ShapeDtypeStruct((4, 4 * TILE, D), BF),
            thirds,
            jax.ShapeDtypeStruct((4, TILE, CLIP), BF),
            clip,
            jax.ShapeDtypeStruct((CLIP, D), F32),
            clip,
            clip,
            chunks,
            chunks,
            jax.ShapeDtypeStruct((FRAMES, 6, D), F32),
            jax.ShapeDtypeStruct((FRAMES, CLIP), F32),
            jax.ShapeDtypeStruct((4, 2, CLIP), F32),
            jax.ShapeDtypeStruct((256, D), BF),
            jax.ShapeDtypeStruct((256, TILE), BF),
        ],
        scratch_shapes=[
            pltpu.VMEM((8 * PAYLOAD, TILE, TILE), BF),
            pltpu.VMEM((3, TILE, D), BF),
            pltpu.VMEM((4, TILE, TILE), BF),
            pltpu.VMEM((CLIP, D), BF),
            pltpu.VMEM((CLIP, D), BF),
            pltpu.VMEM((FRAMES, CLIP), F32),
            pltpu.VMEM((4, FRAMES, 12 * TILE), F32),
            pltpu.VMEM((4, FRAMES, 12 * TILE), F32),
            pltpu.VMEM((256, LEVELS), BF),
            pltpu.VMEM((CLIP, D), BF),
            pltpu.VMEM((4, 4 * TILE, D), BF),
            pltpu.VMEM((4, CLIP, 3 * TILE), BF),
            pltpu.VMEM((4, TILE, CLIP), BF),
            pltpu.VMEM((CLIP, D), BF),
            pltpu.VMEM((CLIP, D), BF),
            pltpu.VMEM((CLIP, D), F32),
            pltpu.VMEM((CLIP, D), F32),
            pltpu.VMEM((2, 4, 4, TILE, D), BF),
            pltpu.VMEM((2, 2, TILE, D), BF),
            pltpu.VMEM((2, 2, TILE, D), BF),
            pltpu.VMEM((2 * TILE, D), F32),
            pltpu.VMEM((2 * TILE, D), F32),
            pltpu.SemaphoreType.DMA((ENTRY_COPIES,)),
            pltpu.SemaphoreType.DMA((ENTRY_COPIES,)),
            pltpu.SemaphoreType.DMA((3,)),
            pltpu.SemaphoreType.DMA((3,)),
            pltpu.SemaphoreType.DMA((4,)),
            pltpu.SemaphoreType.DMA((4,)),
            pltpu.SemaphoreType.DMA((24,)),
            pltpu.SemaphoreType.DMA((64,)),
            pltpu.SemaphoreType.DMA((4,)),
        ],
        compiler_params=pltpu.CompilerParams(
            vmem_limit_bytes=63 * 1024 * 1024, collective_id=0, has_side_effects=True
        ),
        cost_estimate=cost(1e11, 60e6),
        name="front",
    )(index, payload, activations, cotangent, bias_pair)


def attend_kernel(qkv_ref, bias_ref, o_ref, lse_ref):
    for head in range(2):
        lanes = slice(head * HD, (head + 1) * HD)
        keys = qkv_ref[:, TILE + head * HD : TILE + (head + 1) * HD]
        values = qkv_ref[:, 2 * TILE + head * HD : 2 * TILE + (head + 1) * HD]

        def step(i, _, lanes=lanes, keys=keys, values=values, head=head):
            start = pl.multiple_of(i * QBLK, QBLK)
            queries = qkv_ref[pl.ds(start, QBLK), lanes]
            scores = dot(keys, queries, NT).reshape(FRAMES, FRAME_TOK, QBLK)
            scores = scores * SCALE2 + bias_ref[:, pl.ds(start, QBLK)][:, None, :]
            peak = jnp.max(jnp.max(scores, axis=0), axis=0, keepdims=True)
            weights = jnp.exp2(scores - peak[None])
            total = jnp.sum(jnp.sum(weights, axis=0), axis=0, keepdims=True)
            mixed = dot(values, weights.reshape(CLIP, QBLK).astype(BF), TN)
            o_ref[lanes, pl.ds(start, QBLK)] = (mixed / total).astype(BF)
            lse_ref[0, head : head + 1, pl.ds(start, QBLK)] = peak + jnp.log2(total)
            return 0

        lax.fori_loop(0, CLIP // QBLK, step, 0)


def attend(qkv, bias):
    groups = qkv.shape[1] // (3 * TILE)
    return pl.pallas_call(
        attend_kernel,
        grid=(groups,),
        in_specs=[
            pl.BlockSpec((CLIP, 3 * TILE), lambda m: (0, m)),
            pl.BlockSpec((FRAMES, CLIP), lambda m: (0, 0)),
        ],
        out_specs=[
            pl.BlockSpec((TILE, CLIP), lambda m: (m, 0)),
            pl.BlockSpec((1, 2, CLIP), lambda m: (m, 0, 0)),
        ],
        out_shape=[
            jax.ShapeDtypeStruct((groups * TILE, CLIP), BF),
            jax.ShapeDtypeStruct((groups, 2, CLIP), F32),
        ],
        compiler_params=params(),
        cost_estimate=cost(groups * 2 * 4 * CLIP * CLIP * HD * 3, 2 * qkv.size, groups * 2 * CLIP * CLIP),
        name="attend",
    )(qkv, bias)


def attend_back_kernel(qkv_ref, o_ref, do_ref, lse_ref, bias_ref, out_ref, dk_ref, dv_ref):
    for head in range(2):
        lanes = slice(head * HD, (head + 1) * HD)
        keys = qkv_ref[:, TILE + head * HD : TILE + (head + 1) * HD]
        values = qkv_ref[:, 2 * TILE + head * HD : 2 * TILE + (head + 1) * HD]
        dk_ref[...] = jnp.zeros_like(dk_ref)
        dv_ref[...] = jnp.zeros_like(dv_ref)

        def step(i, _, lanes=lanes, keys=keys, values=values, head=head):
            start = pl.multiple_of(i * QBLK, QBLK)
            across = pl.ds(start, QBLK)
            queries = qkv_ref[across, lanes]
            grad = do_ref[lanes, across]
            shift = bias_ref[:, across] - lse_ref[0, head : head + 1, across]
            scores = dot(keys, queries, NT).reshape(FRAMES, FRAME_TOK, QBLK)
            soft = jnp.exp2(scores * SCALE2 + shift[:, None, :]).reshape(CLIP, QBLK)
            delta = jnp.sum(
                grad.astype(F32) * o_ref[lanes, across].astype(F32), axis=0, keepdims=True
            )
            grad_soft = dot(values, grad, NN)
            grad_scores = (soft * (grad_soft - delta)).astype(BF)
            dv_ref[...] += dot(soft.astype(BF), grad, NT)
            dk_ref[...] += dot(grad_scores, queries, NN)
            grad_query = dot(keys, grad_scores, TN) * HD ** (-0.5)
            out_ref[across, lanes] = grad_query.T.astype(BF)
            return 0

        lax.fori_loop(0, CLIP // QBLK, step, 0)
        out_ref[:, TILE + head * HD : TILE + (head + 1) * HD] = (dk_ref[...] * HD ** (-0.5)).astype(BF)
        out_ref[:, 2 * TILE + head * HD : 2 * TILE + (head + 1) * HD] = dv_ref[...].astype(BF)


def attend_back(qkv, o_rows, do_rows, lse, bias):
    groups = qkv.shape[1] // (3 * TILE)
    return pl.pallas_call(
        attend_back_kernel,
        grid=(groups,),
        in_specs=[
            pl.BlockSpec((CLIP, 3 * TILE), lambda m: (0, m)),
            pl.BlockSpec((TILE, CLIP), lambda m: (m, 0)),
            pl.BlockSpec((TILE, CLIP), lambda m: (m, 0)),
            pl.BlockSpec((1, 2, CLIP), lambda m: (m, 0, 0)),
            pl.BlockSpec((FRAMES, CLIP), lambda m: (0, 0)),
        ],
        out_specs=pl.BlockSpec((CLIP, 3 * TILE), lambda m: (0, m)),
        out_shape=jax.ShapeDtypeStruct(qkv.shape, BF),
        scratch_shapes=[pltpu.VMEM((CLIP, HD), F32), pltpu.VMEM((CLIP, HD), F32)],
        compiler_params=params(),
        cost_estimate=cost(groups * 2 * 10 * CLIP * CLIP * HD * 3, 4 * qkv.size, groups * 2 * CLIP * CLIP),
        name="attend_back",
    )(qkv, o_rows, do_rows, lse, bias)


UNITS = 256


def feed_kernel(h_ref, de_ref, up_ref, down_ref, e_ref, dh_ref, dup_ref, ddown_ref, e_acc, dh_acc, up_acc, down_acc):
    block = pl.program_id(0)
    last = pl.num_programs(0) - 1
    up = up_ref[...]
    down = down_ref[...]
    for part in range(CLIP // ROWS):
        rows = slice(part * ROWS, (part + 1) * ROWS)
        hidden = h_ref[rows]
        grad = de_ref[rows]
        pre = dot(hidden, up, NT)
        square = pre * pre
        tanh = jnp.tanh(GELU_A * pre * (1.0 + GELU_B * square))
        act = (0.5 * pre * (1.0 + tanh)).astype(BF)
        slope = 0.5 * (1.0 + tanh) + 0.5 * pre * (1.0 - tanh * tanh) * (
            GELU_A * (1.0 + 3.0 * GELU_B * square)
        )
        grad_act = dot(grad, down, NT).astype(BF).astype(F32)
        grad_pre = (grad_act * slope).astype(BF)
        feed = dot(act, down, NN)
        back = dot(grad_pre, up, NN)

        @pl.when(block == 0)
        def _():
            e_acc[rows] = feed
            dh_acc[rows] = back

        @pl.when(block > 0)
        def _():
            e_acc[rows] += feed
            dh_acc[rows] += back

        if part == 0:
            down_acc[...] = dot(act, grad, TN)
            up_acc[...] = dot(grad_pre, hidden, TN)
        else:
            ddown_ref[...] = (down_acc[...] + dot(act, grad, TN)).astype(BF)
            dup_ref[...] = (up_acc[...] + dot(grad_pre, hidden, TN)).astype(BF)

    @pl.when(block == last)
    def _():
        e_ref[...] = e_acc[...].astype(BF)
        dh_ref[...] = dh_acc[...].astype(BF)


def feed_both(hidden, grad, up, down):
    units = up.shape[0]
    whole = pl.BlockSpec((CLIP, D), lambda i: (0, 0))
    strip = pl.BlockSpec((UNITS, D), lambda i: (i, 0))
    return pl.pallas_call(
        feed_kernel,
        grid=(units // UNITS,),
        in_specs=[whole, whole, strip, strip],
        out_specs=[whole, whole, strip, strip],
        out_shape=[jax.ShapeDtypeStruct((CLIP, D), BF)] * 2 + [jax.ShapeDtypeStruct((units, D), BF)] * 2,
        scratch_shapes=[
            pltpu.VMEM((CLIP, D), F32),
            pltpu.VMEM((CLIP, D), F32),
            pltpu.VMEM((UNITS, D), F32),
            pltpu.VMEM((UNITS, D), F32),
        ],
        compiler_params=params(),
        cost_estimate=cost(12 * CLIP * D * units, 8 * CLIP * D + 8 * units * D, CLIP * units),
        name="feed_both",
    )(hidden, grad, up, down)


HALF = CLIP // 2
EXIT_COPIES = 8 + 1 + 18 + 9 + 24 + 12 + 6 + 14
EXIT_LOCAL = 32


class Relay:
    def __init__(self, sends, recvs, local, src, full, d, z):
        self.sends, self.recvs, self.local = sends, recvs, local
        self.src, self.full, self.d, self.z = src, full, d, z
        self.core = lax.rem(d, 2)

    def place(self, clip, first, count):
        start = pl.multiple_of(lax.rem(clip, 2) * CLIP + first * HALF, HALF)
        return self.full.at[pl.ds(start, count)]

    def copy(self, src, clip, half, way, hop):
        index = way * 6 + (hop - 1) * 2 + half
        return pltpu.make_async_remote_copy(
            src_ref=src,
            dst_ref=self.place(clip, half, HALF),
            send_sem=self.sends.at[index],
            recv_sem=self.recvs.at[index],
            device_id=(self.d - self.core + clip // 2, lax.rem(self.z + (1 if way == 0 else 3), 4)),
            device_id_type=MESH,
        )

    def more(self, way):
        return self.z < 3 if way == 0 else self.z > 0

    def own(self, way):
        part = self.src.at[pl.ds(pl.multiple_of(self.core * HALF, HALF), HALF)]
        return self.copy(part, self.z, self.core, way, 1)

    def home(self):
        return pltpu.make_async_copy(self.src, self.place(self.z, 0, CLIP), self.local)

    def first(self):
        for way in range(2):

            @pl.when(self.more(way))
            def _(way=way):
                self.own(way).start()

        @pl.when(self.z // 2 == self.core)
        def _():
            self.home().start()

    def arriving(self, way, hop):
        clip = lax.rem(self.z + (4 - hop if way == 0 else hop), 4)
        there = self.z >= hop if way == 0 else self.z + hop <= 3
        return clip, jnp.logical_and(there, clip // 2 == self.core)

    def hop(self, hop):
        for way in range(2):
            clip, here = self.arriving(way, hop)

            @pl.when(here)
            def _(way=way, clip=clip):
                for half in range(2):
                    part = self.place(clip, half, HALF)
                    self.copy(part, clip, half, way, hop).wait_recv()
                    if hop < 3:

                        @pl.when(self.more(way))
                        def _(part=part, half=half):
                            self.copy(part, clip, half, way, hop + 1).start()

    def finish(self):
        for way in range(2):

            @pl.when(self.more(way))
            def _(way=way):
                self.own(way).wait_send()

            for hop in (1, 2):
                clip, here = self.arriving(way, hop)

                @pl.when(jnp.logical_and(here, self.more(way)))
                def _(way=way, clip=clip, hop=hop):
                    for half in range(2):
                        self.copy(self.place(clip, half, HALF), clip, half, way, hop + 1).wait_send()

        @pl.when(self.z // 2 == self.core)
        def _():
            self.home().wait()


def exit_kernel(
    y_hbm,
    g_hbm,
    e_hbm,
    dy_hbm,
    br_hbm,
    x_hbm,
    h_hbm,
    qkv_hbm,
    o_hbm,
    wpack_hbm,
    wmod_hbm,
    up_hbm,
    down_hbm,
    mods_ref,
    bias_ref,
    lse_ref,
    emb_ref,
    hot_ref,
    out_all,
    in_all,
    everyone,
    dwm_out,
    table_ref,
    ys,
    gs,
    es,
    dys,
    brs,
    gp,
    ep,
    qs,
    os_,
    dos,
    win,
    wout,
    dhp,
    dattn,
    got,
    loc,
    zbuf,
    red,
    dm,
    dms,
    dmall,
    trow,
    tbuf,
    dk_ref,
    dv_ref,
    sends,
    recvs,
    strip_sends,
    strip_recvs,
    out_sends,
    out_recvs,
    in_sends,
    in_recvs,
    local_sems,
):
    d, z = lax.axis_index("dp"), lax.axis_index("mp")
    core, chip = lax.rem(d, 2), d // 2
    dk, dx, dyd = jnp.bitwise_xor(d, 1), jnp.bitwise_xor(d, 2), jnp.bitwise_xor(d, 4)
    link = Link(sends, recvs)
    locals_used = [0]

    def load(src, dst):
        copy = pltpu.make_async_copy(src, dst, local_sems.at[locals_used[0]])
        locals_used[0] += 1
        copy.start()
        return copy

    barrier = pltpu.get_barrier_semaphore()
    for step in (1, 2, 4):
        pl.semaphore_signal(barrier, inc=1, device_id=(jnp.bitwise_xor(d, step), z), device_id_type=MESH)
    for s in (1, 2, 3):
        pl.semaphore_signal(barrier, inc=1, device_id=(d, lax.rem(z + s, 4)), device_id_type=MESH)
        pl.semaphore_signal(barrier, inc=1, device_id=(dk, lax.rem(z + s, 4)), device_id_type=MESH)

    first_loads = [load(a, b) for a, b in ((g_hbm, gs), (e_hbm, es), (y_hbm, ys), (dy_hbm, dys), (br_hbm, brs))]
    loads = [load(a, b) for a, b in ((o_hbm, os_), (qkv_hbm, qs))]
    for m in range(4):
        loads.append(load(wpack_hbm.at[m, 3 * TILE : 4 * TILE], wout.at[m]))
        loads.append(load(wpack_hbm.at[m, 0 : 3 * TILE], win.at[m * 3 * TILE : (m + 1) * 3 * TILE]))
    feed_loads = []
    for g, src in enumerate((up_hbm, down_hbm)):
        feed_loads.append(load(src.at[0], loc.at[g, 0:4]))
        feed_loads.append(load(src.at[2, 0:2], loc.at[g, 4:6]))
        feed_loads.append(load(src.at[1, 2:4], loc.at[g, 6:8]))
    pl.semaphore_wait(barrier, 9)

    def strip_of(i):
        return pl.ds(pl.multiple_of(i * BLK, BLK), BLK)

    def swaps(i):
        return [
            pltpu.make_async_remote_copy(
                src_ref=src.at[strip_of(i)],
                dst_ref=dst.at[strip_of(i)],
                send_sem=strip_sends.at[2 * i + k],
                recv_sem=strip_recvs.at[2 * i + k],
                device_id=(dk, z),
                device_id_type=MESH,
            )
            for k, (src, dst) in enumerate(((g_hbm, gp), (e_hbm, ep)))
        ]

    def swap_start(i, _):
        for copy in swaps(i):
            copy.start()
        return 0

    lax.fori_loop(0, CLIP // BLK, swap_start, 0)

    plane = {}

    def plane_first(g, src):
        plane[g, 0] = link.send(src.at[3, 0:2], got.at[g, 0], dx, z)
        plane[g, 1] = link.send(src.at[3, 2:4], got.at[g, 1], dyd, z)
        plane[g, 2] = link.send(src.at[1, 0:2], got.at[g, 2], dx, z)
        plane[g, 3] = link.send(src.at[2, 2:4], got.at[g, 3], dyd, z)

    def add_into(dst, first, count, parts):
        def step(i, _):
            k = i // 4
            rows = pl.ds(pl.multiple_of(lax.rem(i, 4) * 32, 32), 32)
            total = dst[first + k, rows].astype(F32)
            for g, slot in parts:
                total = total + got[g, slot, k, rows].astype(F32)
            dst[first + k, rows] = total.astype(BF)
            return 0

        lax.fori_loop(0, count * 4, step, 0)

    def places(g):
        if g == 0:
            return (dattn.at[0], 0), (dattn.at[2], 0), (dattn.at[1], 2)
        return (loc.at[g - 1], 0), (loc.at[g - 1], 4), (loc.at[g - 1], 6)

    def plane_pass(g):
        _, (low, low_at), (high, high_at) = places(g)
        plane[g, 0].wait_recv()
        add_into(low, low_at, 2, [(g, 0)])
        plane[g, 4] = link.send(low.at[pl.ds(low_at, 2)], got.at[g, 4], dyd, z)
        plane[g, 1].wait_recv()
        add_into(high, high_at, 2, [(g, 1)])
        plane[g, 5] = link.send(high.at[pl.ds(high_at, 2)], got.at[g, 5], dx, z)

    column = {}

    def plane_final(g):
        (own, _), _, _ = places(g)
        for slot in (2, 3, 4, 5):
            plane[g, slot].wait_recv()
        add_into(own, 0, 2, [(g, 2), (g, 4)])
        add_into(own, 2, 2, [(g, 3), (g, 5)])
        for s in (1, 3, 2):
            to = lax.rem(z + s, 4)
            column[g, s] = link.send(own.at[to], zbuf.at[g, s - 1], d, to)

    spread = {}
    homes = []

    def column_final(g):
        (own, _), _, _ = places(g)
        for s in (1, 3, 2):
            column[g, s].wait_recv()

        def step(i, _):
            rows = pl.ds(pl.multiple_of(i * 32, 32), 32)
            total = own[z, rows].astype(F32)
            for s in range(3):
                total = total + zbuf[g, s, rows].astype(F32)
            red[g, rows] = total.astype(BF)
            return 0

        lax.fori_loop(0, 4, step, 0)
        rows = pl.ds(g * TILE, TILE)
        spread[g, 2] = link.send(red.at[g], everyone.at[2, rows], dx, z)
        spread[g, 4] = link.send(red.at[g], everyone.at[4, rows], dyd, z)
        spread[g, 1] = link.send(red.at[g], everyone.at[1, rows], dk, z)
        homes.append(load(red.at[g], everyone.at[0, rows]))

    def spread_on(g):
        rows = pl.ds(g * TILE, TILE)
        low, high = pl.ds(g * TILE, TILE // 2), pl.ds(g * TILE + TILE // 2, TILE // 2)
        spread[g, 2].wait_recv()
        spread[g, 6] = link.send(everyone.at[2, low], everyone.at[6, low], dyd, z)
        spread[g, 3] = link.send(everyone.at[2, rows], everyone.at[3, rows], dk, z)
        spread[g, 4].wait_recv()
        spread[g, 7] = link.send(everyone.at[4, high], everyone.at[6, high], dx, z)
        spread[g, 5] = link.send(everyone.at[4, rows], everyone.at[5, rows], dk, z)

    def spread_diag(g):
        rows = pl.ds(g * TILE, TILE)
        spread[g, 6].wait_recv()
        spread[g, 7].wait_recv()
        spread[g, 8] = link.send(everyone.at[6, rows], everyone.at[7, rows], dk, z)

    plane_first(1, up_hbm)
    plane_first(2, down_hbm)
    for copy in first_loads:
        copy.wait()

    def back_strip(i, _):
        strip, frames = strip_of(i), pl.ds(i * FBLK, FBLK)
        for copy in swaps(i):
            copy.wait_recv()
        mods = mods_ref[frames]
        mid = ys[strip]
        feed = es[strip].astype(F32) + ep[strip].astype(F32)
        dy = dys[strip].astype(F32)
        ep[strip] = (mid + flat(mods[:, 5:6] * frames_of(feed))).astype(BF)
        normed, inverse_std = norm_rows(mid)
        grad = gs[strip].astype(F32) + gp[strip].astype(F32)
        dm[frames, 3] = jnp.sum(frames_of(grad), axis=1)
        dm[frames, 4] = jnp.sum(frames_of(grad * normed), axis=1)
        dm[frames, 5] = jnp.sum(frames_of(dy * feed), axis=1)
        scaled = flat(frames_of(grad) * (1.0 + mods[:, 4:5]))
        dy1 = dy + norm_back(scaled, normed, inverse_std)
        ys[strip] = dy1
        dm[frames, 2] = jnp.sum(frames_of(dy1 * brs[strip].astype(F32)), axis=1)
        gp[strip] = flat(mods[:, 2:3] * frames_of(dy1)).astype(BF)
        return 0

    lax.fori_loop(0, CLIP // BLK, back_strip, 0)

    def swap_done(i, _):
        for copy in swaps(i):
            copy.wait_send()
        return 0

    lax.fori_loop(0, CLIP // BLK, swap_done, 0)
    x_load = load(x_hbm, gs)
    h_load = load(h_hbm, es)
    output = Relay(out_sends, out_recvs, local_sems.at[EXIT_LOCAL - 1], ep, out_all, d, z)
    output.first()
    for copy in loads:
        copy.wait()

    def project(m, _):
        dos[m] = dot(wout[m], gp[...], NT).astype(BF)
        grad = dot(os_[m], gp[...], NN).astype(BF)
        for c in range(4):
            dattn[c, m, 96:128] = grad[c * 32 : (c + 1) * 32]
        return 0

    lax.fori_loop(0, 4, project, 0)

    def attend_group(m, _):
        for head in range(2):
            lanes = slice(head * HD, (head + 1) * HD)
            keys = qs[m, :, TILE + head * HD : TILE + (head + 1) * HD]
            values = qs[m, :, 2 * TILE + head * HD : 2 * TILE + (head + 1) * HD]
            dk_ref[...] = jnp.zeros_like(dk_ref)
            dv_ref[...] = jnp.zeros_like(dv_ref)

            def step(i, _, lanes=lanes, keys=keys, values=values, head=head):
                across = pl.ds(pl.multiple_of(i * QBLK, QBLK), QBLK)
                queries = qs[m, across, lanes]
                grad = dos[m, lanes, across]
                shift = bias_ref[:, across] - lse_ref[m, head : head + 1, across]
                scores = dot(keys, queries, NT).reshape(FRAMES, FRAME_TOK, QBLK)
                soft = jnp.exp2(scores * SCALE2 + shift[:, None, :]).reshape(CLIP, QBLK)
                delta = jnp.sum(
                    grad.astype(F32) * os_[m, lanes, across].astype(F32), axis=0, keepdims=True
                )
                grad_soft = dot(values, grad, NN)
                grad_scores = (soft * (grad_soft - delta)).astype(BF)
                dv_ref[...] += dot(soft.astype(BF), grad, NT)
                dk_ref[...] += dot(grad_scores, queries, NN)
                grad_query = dot(keys, grad_scores, TN) * HD ** (-0.5)
                qs[m, across, lanes] = grad_query.T.astype(BF)
                return 0

            lax.fori_loop(0, CLIP // QBLK, step, 0)
            qs[m, :, TILE + head * HD : TILE + (head + 1) * HD] = (dk_ref[...] * HD ** (-0.5)).astype(BF)
            qs[m, :, 2 * TILE + head * HD : 2 * TILE + (head + 1) * HD] = dv_ref[...].astype(BF)
        return 0

    lax.fori_loop(0, 2, attend_group, 0)
    for copy in feed_loads:
        copy.wait()
    plane_pass(1)
    lax.fori_loop(2, 4, attend_group, 0)
    plane_pass(2)
    output.hop(1)

    def hidden_strip(i, _):
        strip = strip_of(i)
        total = dot(qs[0, strip], win[0:384], NN)
        for m in range(1, 4):
            total = total + dot(qs[m, strip], win[m * 384 : (m + 1) * 384], NN)
        brs[strip] = total.astype(BF)
        return 0

    lax.fori_loop(0, CLIP // BLK, hidden_strip, 0)
    hidden_swap = link.send(brs, dhp, dk, z)
    h_load.wait()
    x_load.wait()

    def input_weights(m, _):
        grad = dot(qs[m], es[...], TN).astype(BF)
        for role in range(3):
            for c in range(4):
                first = role * TILE + c * 32
                dattn[c, m, role * 32 : (role + 1) * 32] = grad[first : first + 32]
        return 0

    lax.fori_loop(0, 4, input_weights, 0)
    plane_first(0, dattn)
    mod_loads = [load(wmod_hbm, qs)]
    plane_final(1)
    plane_final(2)

    hidden_swap.wait_recv()

    def last_strip(i, _):
        strip, frames = strip_of(i), pl.ds(i * FBLK, FBLK)
        mods = mods_ref[frames]
        normed, inverse_std = norm_rows(gs[strip].astype(F32))
        grad = brs[strip].astype(F32) + dhp[strip].astype(F32)
        dm[frames, 0] = jnp.sum(frames_of(grad), axis=1)
        dm[frames, 1] = jnp.sum(frames_of(grad * normed), axis=1)
        scaled = flat(frames_of(grad) * (1.0 + mods[:, 1:2]))
        dys[strip] = (ys[strip] + norm_back(scaled, normed, inverse_std)).astype(BF)
        return 0

    lax.fori_loop(0, CLIP // BLK, last_strip, 0)
    for m in range(4):
        for c in range(6):
            dms[m, :, c * 256 : (c + 1) * 256] = dm[:, c, m * 256 : (m + 1) * 256].astype(BF)
    mod_column = {}
    clip = chip * 4 + z
    for s in (1, 3, 2):
        to = lax.rem(z + s, 4)
        mod_column[s] = link.send(dms.at[to], dmall.at[clip], d, to)
    dmall[clip] = dms[z]
    inner = Relay(in_sends, in_recvs, local_sems.at[EXIT_LOCAL - 2], dys, in_all, d, z)
    inner.first()
    output.hop(2)

    for s in (1, 3, 2):
        mod_column[s].wait_recv()

    def clips_of(which):
        return dmall.at[pl.ds(which * 4, 4)]

    mod_x = link.send(clips_of(chip), clips_of(chip), dx, z)
    mod_y = link.send(clips_of(chip), clips_of(chip), dyd, z)
    plane_pass(0)
    column_final(1)
    column_final(2)
    mod_x.wait_recv()
    over_x = jnp.bitwise_xor(chip, 1)
    mod_xy = link.send(clips_of(over_x), clips_of(over_x), dyd, z)
    spread_on(1)
    spread_on(2)
    plane_final(0)
    inner.hop(1)
    output.hop(3)

    mod_y.wait_recv()
    mod_xy.wait_recv()
    for copy in mod_loads:
        copy.wait()
    grads = dmall[...].reshape(256, 12 * TILE)

    level_grads = dot(hot_ref[...], grads, TN).astype(BF)
    rows = dot(level_grads[:, 0:384], qs[0], NT)
    for m in range(1, 4):
        rows = rows + dot(level_grads[:, m * 384 : (m + 1) * 384], qs[m], NT)
    trow[...] = rows.reshape(4, 32, D)
    table = {}
    for s in (1, 3, 2):
        to = lax.rem(z + s, 4)
        table[s] = link.send(trow.at[to], tbuf.at[s - 1], d, to)

    for part in range(6):
        win[part * 256 : (part + 1) * 256] = dot(
            grads[:, part * 256 : (part + 1) * 256], emb_ref[...], TN
        ).astype(BF)
    homes.append(load(win, dwm_out))
    spread_diag(1)
    spread_diag(2)
    column_final(0)
    inner.hop(2)
    spread_on(0)
    for s in (1, 3, 2):
        table[s].wait_recv()
    table_ref[...] = trow[z] + tbuf[0] + tbuf[1] + tbuf[2]
    spread_diag(0)
    inner.hop(3)
    for g in range(3):
        for slot in (1, 3, 5, 8):
            spread[g, slot].wait_recv()
    for copy in homes:
        copy.wait()
    output.finish()
    inner.finish()
    link.drain()


def exit_call(*args):
    vmem = pl.BlockSpec(memory_space=pltpu.VMEM)
    hbm = pl.BlockSpec(memory_space=pl.ANY)
    chunks = (4, 4, TILE, D)
    heads = (4, TILE, D)
    return pl.pallas_call(
        exit_kernel,
        in_specs=[hbm] * 13 + [vmem] * 5,
        out_specs=[hbm] * 4 + [vmem],
        out_shape=[
            jax.ShapeDtypeStruct((2 * CLIP, D), BF),
            jax.ShapeDtypeStruct((2 * CLIP, D), BF),
            jax.ShapeDtypeStruct((8, 3 * TILE, D), BF),
            jax.ShapeDtypeStruct((12 * TILE, D), BF),
            jax.ShapeDtypeStruct((32, D), F32),
        ],
        scratch_shapes=[
            pltpu.VMEM((CLIP, D), F32),
            pltpu.VMEM((CLIP, D), BF),
            pltpu.VMEM((CLIP, D), BF),
            pltpu.VMEM((CLIP, D), BF),
            pltpu.VMEM((CLIP, D), BF),
            pltpu.VMEM((CLIP, D), BF),
            pltpu.VMEM((CLIP, D), BF),
            pltpu.VMEM((4, CLIP, 3 * TILE), BF),
            pltpu.VMEM(heads, BF),
            pltpu.VMEM(heads, BF),
            pltpu.VMEM((12 * TILE, D), BF),
            pltpu.VMEM(heads, BF),
            pltpu.VMEM((CLIP, D), BF),
            pltpu.VMEM(chunks, BF),
            pltpu.VMEM((3, 6, 2, TILE, D), BF),
            pltpu.VMEM((2, 8, TILE, D), BF),
            pltpu.VMEM((3, 3, TILE, D), BF),
            pltpu.VMEM((3, TILE, D), BF),
            pltpu.VMEM((FRAMES, 6, D), F32),
            pltpu.VMEM((4, FRAMES, 12 * TILE), BF),
            pltpu.VMEM((16, FRAMES, 12 * TILE), BF),
            pltpu.VMEM((4, 32, D), F32),
            pltpu.VMEM((3, 32, D), F32),
            pltpu.VMEM((CLIP, HD), F32),
            pltpu.VMEM((CLIP, HD), F32),
            pltpu.SemaphoreType.DMA((EXIT_COPIES,)),
            pltpu.SemaphoreType.DMA((EXIT_COPIES,)),
            pltpu.SemaphoreType.DMA((8,)),
            pltpu.SemaphoreType.DMA((8,)),
            pltpu.SemaphoreType.DMA((12,)),
            pltpu.SemaphoreType.DMA((12,)),
            pltpu.SemaphoreType.DMA((12,)),
            pltpu.SemaphoreType.DMA((12,)),
            pltpu.SemaphoreType.DMA((EXIT_LOCAL,)),
        ],
        compiler_params=pltpu.CompilerParams(
            vmem_limit_bytes=63 * 1024 * 1024, collective_id=1, has_side_effects=True
        ),
        cost_estimate=cost(1e11, 60e6),
        name="exit",
    )(*args)


def adam_step(grad, left, right, one, two, master, rate):
    low_left, low_right = left.astype(BF), right.astype(BF)
    turned = dot(low_left, grad.astype(BF), TN)
    rotated = dot(turned.astype(BF), low_right, NN)
    new_one = BETA_ONE * one + (1.0 - BETA_ONE) * rotated
    new_two = BETA_TWO * two + (1.0 - BETA_TWO) * rotated * rotated
    direction = new_one / (jnp.sqrt(new_two) + EPS_ADAM)
    back = dot(low_left, direction.astype(BF), NN)
    back = dot(back.astype(BF), low_right, NT)
    return master - rate * (back + DECAY * master), new_one, new_two


def adam_kernel(tab_ref, rate_ref, *refs, picked, batch):
    if picked:
        red_ref, mod_ref = refs[:2]
        refs = refs[2:]
    else:
        grad_ref = refs[0]
        refs = refs[1:]
    master_ref, one_ref, two_ref, left_ref, right_ref, nm_ref, n1_ref, n2_ref, nw_ref = refs
    for slot in range(batch):
        tile = pl.program_id(0) * batch + slot
        if picked:
            col = pl.multiple_of(tab_ref[tile, 8] * TILE, TILE)
            pieces = [
                red_ref[
                    tab_ref[tile, i],
                    pl.ds(pl.multiple_of(tab_ref[tile, 4 + i] * 32, 32), 32),
                    pl.ds(col, TILE),
                ]
                for i in range(4)
            ]
            grad = jnp.concatenate(pieces, axis=0).astype(F32)
            mod_row = pl.multiple_of(tab_ref[tile, 9] * TILE, TILE)
            mod_col = pl.multiple_of(tab_ref[tile, 10] * TILE, TILE)
            mod_grad = mod_ref[pl.ds(mod_col, TILE), pl.ds(mod_row, TILE)].astype(F32)
            kind = tab_ref[tile, 11]
            grad = jnp.where(kind == 0, grad, jnp.where(kind == 2, mod_grad, grad).T)
        else:
            grad = grad_ref[slot].astype(F32)
        master, one, two = adam_step(
            grad, left_ref[slot], right_ref[slot], one_ref[slot], two_ref[slot], master_ref[slot], rate_ref[tile]
        )
        nm_ref[slot] = master
        n1_ref[slot] = one
        n2_ref[slot] = two
        nw_ref[slot] = master.astype(BF)


def pick_table(tiles, device):
    table = []
    piece = jnp.arange(4, dtype=jnp.int32)[None, :]
    t = tiles[:, None]
    is_in = t < 48
    is_out = (t >= 48) & (t < 64)
    is_up = (t >= 64) & (t < 128)
    is_down = (t >= 128) & (t < 192)
    is_mod = t >= 192
    q0, q1, q2, q3, q4 = t, t - 48, t - 64, t - 128, t - 192
    core = jnp.where(is_in, (q0 % 6) % 2, jnp.where(is_out, q1 // 8, jnp.where(is_up, (q2 % 8) // 4, (q3 // 8) // 4)))
    chip = jnp.where(is_up, q2 % 4, (q3 // 8) % 4)
    chip = jnp.where(is_in | is_out, piece, chip)
    source = jnp.where(is_mod, 0, jnp.bitwise_xor(2 * chip + core, device))
    row = jnp.where(is_in, (q0 % 6) // 2, jnp.where(is_out, 3, jnp.where(is_up, 4 + piece, 8 + piece)))
    row = jnp.where(is_mod, 0, row + jnp.zeros_like(piece))
    col = jnp.where(is_in, q0 // 6, jnp.where(is_out, q1 % 8, jnp.where(is_up, q2 // 8, q3 % 8)))
    col = jnp.where(is_mod, 0, col)
    mod_row = jnp.where(is_mod, q4 // 12, 0)
    mod_col = jnp.where(is_mod, q4 % 12, 0)
    kind = jnp.where(is_mod, 2, jnp.where(is_in | is_up, 1, 0))
    return jnp.concatenate([source, row, col, mod_row, mod_col, kind], axis=1).astype(jnp.int32)


def adam(table, rates, sources, master, one, two, left, right):
    slots = master.shape[0]
    batch = max(b for b in (4, 3, 2, 1) if slots % b == 0)
    picked = len(sources) == 2
    tiles = pl.BlockSpec((batch, TILE, TILE), lambda i, *_: (i, 0, 0))
    if picked:
        source_specs = [
            pl.BlockSpec(sources[0].shape, lambda i, *_: (0, 0, 0)),
            pl.BlockSpec(sources[1].shape, lambda i, *_: (0, 0)),
        ]
    else:
        source_specs = [tiles]
    return pl.pallas_call(
        functools.partial(adam_kernel, picked=picked, batch=batch),
        grid_spec=pltpu.PrefetchScalarGridSpec(
            num_scalar_prefetch=2,
            grid=(slots // batch,),
            in_specs=source_specs + [tiles] * 5,
            out_specs=[tiles] * 4,
        ),
        out_shape=[jax.ShapeDtypeStruct(master.shape, F32)] * 3 + [jax.ShapeDtypeStruct(master.shape, BF)],
        compiler_params=params(),
        cost_estimate=cost(slots * 8 * TILE**3, slots * TILE * TILE * 36),
        name="adam",
    )(table, rates, *sources, master, one, two, left, right)


def body(
    activations,
    cotangent,
    level_table,
    true_frames,
    group_pattern,
    noise_levels,
    context_flags,
    owner_list,
    masters,
    moment_one,
    moment_two,
    basis_left,
    basis_right,
):
    groups = lax.axis_size("mp")
    owners = lax.axis_size("dp")
    chips = owners // 2
    bits = chips.bit_length() - 1
    z = lax.axis_index("mp")
    device = lax.axis_index("dp")
    core = device % 2
    chip = device // 2
    local_clips = true_frames.shape[0]
    column_clips = 2 * local_clips
    assert column_clips == groups and chips == 1 << bits
    shapes, counts = tile_layout(groups)
    slots = masters.shape[1]
    fast = chips == 4 and groups == 4

    def swap(v, step):
        return lax.ppermute(v, "dp", [(i, i ^ step) for i in range(owners)])

    def across(v):
        return swap(v, 1)

    def plane(v, bit):
        return swap(v, 2 << bit)

    def z_get(v, s):
        return lax.ppermute(v, "mp", [((i + s) % groups, i) for i in range(groups)])

    def z_put(v, s):
        return lax.ppermute(v, "mp", [(i, (i + s) % groups) for i in range(groups)])

    def plane_double(v):
        held = v[None]
        for bit in range(bits):
            held = jnp.concatenate([held, plane(held, bit)], axis=0)
        return held

    def plane_gather(v):
        if chips != 4:
            return plane_double(v)
        half = v.shape[0] // 2
        by_x, by_y = plane(v, 0), plane(v, 1)
        low, high = plane(by_x[:half], 1), plane(by_y[half:], 0)
        return jnp.stack([v, by_x, by_y, jnp.concatenate([low, high], axis=0)])

    def add(a, b):
        return (a.astype(F32) + b.astype(F32)).astype(BF)

    def plane_reduce(v):
        if chips != 4:
            held = v
            for bit in reversed(range(bits)):
                half = 1 << bit
                held = add(held[:half], plane(held[half:], bit))
            return held[0]
        half = v.shape[1] // 2
        got_low = [plane(v[1, :half], 0), plane(v[3, :half], 0)]
        got_high = [plane(v[2, half:], 1), plane(v[3, half:], 1)]
        pass_low = plane(add(v[2, :half], got_low[1]), 1)
        pass_high = plane(add(v[1, half:], got_high[1]), 0)
        low = v[0, :half].astype(F32) + got_low[0].astype(F32) + pass_low.astype(F32)
        high = v[0, half:].astype(F32) + got_high[0].astype(F32) + pass_high.astype(F32)
        return jnp.concatenate([low, high], axis=0).astype(BF)

    def z_gather(v):
        return jnp.stack([v] + [z_get(v, s) for s in range(1, groups)])

    def z_reduce(v):
        total = v[0].astype(F32)
        for s in range(1, groups):
            total = total + z_put(v[s], s).astype(F32)
        return total

    frame_index = jnp.arange(FRAMES, dtype=jnp.int32)

    def mask_rows(flagged, lengths):
        valid = frame_index[None, :] < lengths[:, None]
        in_context = flagged & valid
        visible = valid[:, :, None] & (
            jnp.logical_not(in_context)[:, None, :] | in_context[:, :, None]
        )
        return jnp.repeat(jnp.where(visible, 0.0, -1e30).astype(F32), FRAME_TOK, axis=2)

    def level_rows(flagged, patterns):
        pattern_hot = (patterns[:, None] == jnp.arange(PATTERNS, dtype=jnp.int32)[None, :]).astype(
            jnp.int32
        )
        return jnp.where(
            flagged, 0, jnp.sum(pattern_hot[:, :, None] * noise_levels[None, :, :], axis=1)
        )

    rows = TILE // chips
    level_ids = jnp.arange(LEVELS, dtype=jnp.int32)[None, :]
    if fast:
        with jax.named_scope("front"):
            flagged = context_flags == 1
            (
                _, w_mod, x, dy, h1, w_pack, qkv, o_rows, branch, y1, e_part, dh2_part, d_up, d_down,
                mods, bias, lse, all_embedded, own_hot,
            ) = front(
                masters[0],
                level_table,
                level_rows(flagged, group_pattern),
                mask_rows(flagged, true_frames),
                activations,
                cotangent,
                owner_list,
            )
        with jax.named_scope("exit"):
            block_output, input_grad, everyone, d_w_mod, table_grad = exit_call(
                y1, dh2_part, e_part, dy, branch, x, h1, qkv, o_rows, w_pack, w_mod,
                d_up, d_down, mods, bias, lse, all_embedded, own_hot,
            )
            input_grad = input_grad.astype(F32)
    else:
        with jax.named_scope("entry"):
            holds = (z // local_clips) == core
            local = (z % local_clips) * CLIP
            pair = jnp.stack(
                [
                    lax.dynamic_slice_in_dim(activations, local, CLIP, axis=0),
                    lax.dynamic_slice_in_dim(cotangent, local, CLIP, axis=0),
                ]
            )
            pair = jnp.where(holds, pair, across(pair))
            x, dy = pair[0], pair[1]
            facts = jnp.concatenate(
                [context_flags, true_frames[:, None], group_pattern[:, None]], axis=1
            ).astype(jnp.int32)
            other = across(facts)
            facts = jnp.where(
                core == 0, jnp.concatenate([facts, other]), jnp.concatenate([other, facts])
            )
            flagged = facts[:, :FRAMES] == 1
            levels = level_rows(flagged, facts[:, FRAMES + 1])
            bias = lax.dynamic_index_in_dim(
                mask_rows(flagged, facts[:, FRAMES]), z, axis=0, keepdims=False
            )
            all_levels = plane_double(levels)

        with jax.named_scope("owner_gather"):
            gathered = lax.all_gather(masters[0].astype(BF), "dp", axis=0, tiled=True)
            table = lax.all_gather(level_table, "dp", axis=0, tiled=True)
            position = jnp.arange(owner_list.shape[0], dtype=jnp.int32)
            inverse = jnp.sum(
                jnp.where(owner_list[None, :] == position[:, None], position[None, :], 0), axis=1
            ).astype(jnp.int32)
            chunk_attn, chunk_up, chunk_down, w_mod = pick_chunk_plain(
                gathered, inverse, chip, core, chips, shapes, counts
            )

        with jax.named_scope("weights"):
            got = plane_gather(z_gather(chunk_attn)).reshape(chips, groups, 4, rows, D)
            w_up = plane_gather(z_gather(chunk_up)).reshape(-1, D)
            w_down = plane_gather(z_gather(chunk_down)).reshape(-1, D)

        with jax.named_scope("modulation"):
            hot = (levels.reshape(-1)[:, None] == level_ids).astype(BF)
            embedded = dot(hot, table, NN).astype(BF)
            mod_part = dot(embedded, w_mod, NN).reshape(column_clips, FRAMES, -1)
            pieces = [lax.dynamic_index_in_dim(mod_part, z, axis=0, keepdims=False)]
            for s in range(1, groups):
                piece = lax.dynamic_index_in_dim(
                    mod_part, (z + groups - s) % groups, axis=0, keepdims=False
                )
                pieces.append(z_get(piece, s))
            mods = lax.dynamic_slice_in_dim(
                jnp.stack(pieces + pieces), (groups - z) % groups, groups, axis=0
            )
            mods = (
                mods.reshape(groups, FRAMES, 6, D // groups).transpose(1, 2, 0, 3).reshape(FRAMES, 6, D)
            )
            (h1,) = row_call(first_norm_kernel, "first_norm", [x], mods, [BF], [], 4 * CLIP * D)

        w_in = got[:, :, :3].transpose(1, 2, 0, 3, 4).reshape(-1, D)
        w_out = got[:, :, 3].transpose(1, 0, 2, 3).reshape(-1, D)

        mb = CLIP * D
        with jax.named_scope("attention"):
            qkv = dot(h1, w_in, NT).astype(BF)
            o_rows, lse = attend(qkv, bias)
            part = dot(o_rows, w_out, TN).astype(BF)
            y1, branch, h2, de = row_call(
                middle_kernel, "middle", [x, part, across(part), dy], mods, [F32, BF, BF, BF], [], 18 * mb
            )

        with jax.named_scope("feed"):
            e_part, dh2_part, d_up, d_down = feed_both(h2, de, w_up, w_down)

        with jax.named_scope("feed_back"):
            out, dy1, da, dm_mid = row_call(
                back_kernel,
                "back",
                [y1, dh2_part, across(dh2_part), dy, branch, e_part, across(e_part)],
                mods,
                [BF, F32, BF],
                [4],
                24 * mb,
            )
            shape = (chips, groups, -1, D)
            red_up = z_reduce(plane_reduce(d_up.reshape(shape))).astype(BF)
            red_down = z_reduce(plane_reduce(d_down.reshape(shape))).astype(BF)

        def to_column(rows_here):
            half = CLIP // 2
            mine = lax.dynamic_slice_in_dim(rows_here, core * half, half, axis=0)
            by_clip = [mine] + [z_get(mine, s) for s in range(1, groups)]
            by_clip = lax.dynamic_slice_in_dim(jnp.stack(by_clip + by_clip), (groups - z) % groups, groups, axis=0)
            keep = lax.dynamic_slice_in_dim(by_clip, core * local_clips, local_clips, axis=0)
            send = lax.dynamic_slice_in_dim(by_clip, (1 - core) * local_clips, local_clips, axis=0)
            got_half = across(send)
            both = jnp.where(
                core == 0, jnp.stack([keep, got_half], axis=1), jnp.stack([got_half, keep], axis=1)
            )
            return both.reshape(local_clips * CLIP, D)

        with jax.named_scope("block_output"):
            block_output = to_column(out)

        with jax.named_scope("attention_back"):
            do_rows = dot(w_out, da, NT).astype(BF)
            d_out = dot(o_rows, da, NN).astype(BF)
            d_qkv = attend_back(qkv, o_rows, do_rows, lse, bias)
            dh1_part = dot(d_qkv, w_in, NN).astype(BF)
            d_in = dot(d_qkv, h1, TN).astype(BF)
            in_grad, dm_last = row_call(
                last_kernel, "last", [x, dh1_part, across(dh1_part), dy1], mods, [BF], [2], 12 * mb
            )
            d_in = d_in.reshape(groups, 3, chips, rows, D).transpose(2, 0, 1, 3, 4)
            d_out = d_out.reshape(groups, 1, chips, rows, D).transpose(2, 0, 1, 3, 4)
            d_attn = jnp.concatenate([d_in, d_out], axis=2).reshape(chips, groups, 4 * rows, D)
            red_attn = z_reduce(plane_reduce(d_attn)).astype(BF)

        with jax.named_scope("input_grad"):
            input_grad = to_column(in_grad).astype(F32)

        with jax.named_scope("modulation_back"):
            d_mod = jnp.stack(
                [dm_last[:, 0], dm_last[:, 1], dm_mid[:, 2], dm_mid[:, 0], dm_mid[:, 1], dm_mid[:, 3]], axis=1
            ).astype(BF)
            d_mod = (
                d_mod.reshape(FRAMES, 6, groups, D // groups).transpose(2, 0, 1, 3).reshape(groups, FRAMES, -1)
            )
            pieces = [lax.dynamic_index_in_dim(d_mod, z, axis=0, keepdims=False)]
            for s in range(1, groups):
                pieces.append(z_put(lax.dynamic_index_in_dim(d_mod, (z + s) % groups, axis=0, keepdims=False), s))
            d_mod = jnp.stack(pieces)
            d_mod = plane_double(d_mod).reshape(chips * groups * FRAMES, -1)
            back_clip = (z + groups - jnp.arange(groups, dtype=jnp.int32)) % groups
            clip_hot = (back_clip[:, None] == jnp.arange(groups, dtype=jnp.int32)[None, :]).astype(
                jnp.int32
            )
            order = jnp.sum(clip_hot[None, :, :, None] * all_levels[:, None, :, :], axis=2).reshape(-1)
            all_embedded = dot((order[:, None] == level_ids).astype(BF), table, NN).astype(BF)
            own_levels = level_table.shape[0]
            own_ids = device * own_levels + jnp.arange(own_levels, dtype=jnp.int32)[None, :]
            own_hot = (order[:, None] == own_ids).astype(BF)
            d_w_mod = dot(all_embedded, d_mod, TN).astype(BF)
            own_levels = level_table.shape[0]
            own_rows = dot(dot(own_hot, d_mod, TN).astype(BF), w_mod, NT)
            own_rows = own_rows.reshape(groups, own_levels // groups, D)
            table_grad = lax.dynamic_index_in_dim(own_rows, z, axis=0, keepdims=False)
            for s in range(1, groups):
                table_grad = table_grad + z_put(
                    lax.dynamic_index_in_dim(own_rows, (z + s) % groups, axis=0, keepdims=False), s
                )

    with jax.named_scope("owners"):
        if not fast:
            reduced = jnp.concatenate([red_attn, red_up, red_down], axis=0)
            if chips == 4:
                height = reduced.shape[0]
                plane_parts = plane_gather(reduced.reshape(2, height // 2, D)).reshape(chips, height, D)
            else:
                plane_parts = plane_double(reduced)
            everyone = jnp.stack([plane_parts, across(plane_parts)], axis=1).reshape(owners, -1, D)
        tile_ids = lax.dynamic_slice_in_dim(owner_list, device * slots, slots)
        rates = kind_rates(tile_ids, counts)
        if fast:
            picks = pick_table(tile_ids, device)
            sources = [everyone, d_w_mod]
        else:
            picks = jnp.zeros((slots, 12), jnp.int32)
            absolute = jnp.take(
                everyone, jnp.bitwise_xor(jnp.arange(owners, dtype=jnp.int32), device), axis=0
            ).reshape(chips, 2, -1, D)
            attn = absolute[:, :, : 4 * rows].reshape(chips, 2, 4, rows, D)
            attn = attn.transpose(2, 1, 0, 3, 4).reshape(4, -1, D)
            ffn_rows = (absolute.shape[2] - 4 * rows) // 2
            up = absolute[:, :, 4 * rows : 4 * rows + ffn_rows].transpose(1, 0, 2, 3).reshape(-1, D)
            down = absolute[:, :, 4 * rows + ffn_rows :].transpose(1, 0, 2, 3).reshape(-1, D)
            g_in = jnp.concatenate([attn[0].T, attn[1].T, attn[2].T], axis=1)
            packed = pack([g_in, attn[3], up.T, down, d_w_mod])
            sources = [jnp.take(packed, tile_ids, axis=0)]
        new_masters, new_one, new_two, new_weights = adam(
            picks, rates, sources, masters[0], moment_one[0], moment_two[0], basis_left[0], basis_right[0]
        )
    return (
        block_output,
        input_grad,
        table_grad,
        new_masters[None],
        new_one[None],
        new_two[None],
        new_weights[None],
    )


def solution(mesh):
    tiles = P("mp", "dp", None, None)
    in_specs = (
        P("dp", None),
        P("dp", None),
        P("dp", None),
        P("dp"),
        P("dp"),
        P(),
        P("dp", None),
        P(),
        tiles,
        tiles,
        tiles,
        tiles,
        tiles,
    )
    out_specs = (P("dp", None), P("dp", None), P(("dp", "mp"), None), tiles, tiles, tiles, tiles)
    return jax.shard_map(body, mesh=mesh, in_specs=in_specs, out_specs=out_specs, check_vma=False)
```

```python
import functools

import jax
import jax.numpy as jnp
from jax import lax
from jax.experimental import pallas as pl
from jax.experimental.pallas import tpu as pltpu
from jax.sharding import PartitionSpec as P

D = 1024
H = 16
HD = 64
FF = 4096
FRAMES = 16
FRAME_TOK = 64
LEVELS = 1024
PATTERNS = 4
TILE = 128
CLIP = FRAMES * FRAME_TOK

EPS_NORM = 1e-06
BETA_ONE = 0.5
BETA_TWO = 0.75
EPS_ADAM = 1e-08
DECAY = 0.01
LOG2E = 1.4426950408889634
GELU_A = 0.7978845608028654
GELU_B = 0.044715

BF = jnp.bfloat16
F32 = jnp.float32
VMEM_BYTES = 60 * 1024 * 1024


def params(**kw):
    return pltpu.CompilerParams(vmem_limit_bytes=VMEM_BYTES, **kw)


def cost(flops, nbytes, trans=0):
    return pl.CostEstimate(flops=int(flops), bytes_accessed=int(nbytes), transcendentals=int(trans))


def dot(left, right, dims):
    return lax.dot_general(left, right, (dims, ((), ())), preferred_element_type=F32)


NN = ((1,), (0,))
NT = ((1,), (1,))
TN = ((0,), (0,))


def tile_layout(groups):
    local_width = H // groups * HD
    shapes = [
        (D, 3 * local_width),
        (local_width, D),
        (D, FF // groups),
        (FF // groups, D),
        (D, 6 * D // groups),
    ]
    counts = [height // TILE * (breadth // TILE) for height, breadth in shapes]
    return (shapes, counts)


def kind_rates(tile_ids, counts):
    scales = [
        0.35 * D ** (-0.5),
        1.5 * (H * HD) ** (-0.5),
        0.5 * D ** (-0.5),
        0.5 * FF ** (-0.5),
        0.5 * D ** (-0.5),
    ]
    tile_rates = jnp.full(tile_ids.shape, scales[0], F32)
    boundary = 0
    for category in range(1, 5):
        boundary = boundary + counts[category - 1]
        tile_rates = jnp.where(tile_ids >= boundary, jnp.float32(scales[category]), tile_rates)
    return tile_rates


def unpack(tile_stack, shapes, counts):
    matrices = []
    offset = 0
    for (height, breadth), amount in zip(shapes, counts):
        stacked = tile_stack[offset : offset + amount].reshape(
            height // TILE, breadth // TILE, TILE, TILE
        )
        matrices.append(stacked.transpose(0, 2, 1, 3).reshape(height, breadth))
        offset = offset + amount
    return matrices


def pack(matrices):
    stacked = []
    for matrix in matrices:
        height, breadth = matrix.shape
        stacked.append(
            matrix.reshape(height // TILE, TILE, breadth // TILE, TILE)
            .transpose(0, 2, 1, 3)
            .reshape(-1, TILE, TILE)
        )
    return jnp.concatenate(stacked, axis=0)


def pick_chunk_plain(gathered, inverse, chip, core, chips, shapes, counts):
    w_qkv, w_out, w_up, w_down, w_mod = unpack(jnp.take(gathered, inverse, axis=0), shapes, counts)
    width = w_out.shape[0]
    half = width // 2
    ffn = w_up.shape[1] // 2
    rows, ffn_rows = half // chips, ffn // chips
    parts = []
    for role in range(3):
        parts.append(w_qkv[:, role * width : (role + 1) * width].T)
    parts.append(w_out)
    start = core * half + chip * rows
    attn = jnp.concatenate([lax.dynamic_slice_in_dim(p, start, rows, axis=0) for p in parts], axis=0)
    ffn_start = core * ffn + chip * ffn_rows
    up = lax.dynamic_slice_in_dim(w_up.T, ffn_start, ffn_rows, axis=0)
    down = lax.dynamic_slice_in_dim(w_down, ffn_start, ffn_rows, axis=0)
    return attn, up, down, w_mod


def norm_rows(values):
    centered = values - jnp.mean(values, axis=-1, keepdims=True)
    inverse_std = lax.rsqrt(jnp.mean(centered * centered, axis=-1, keepdims=True) + EPS_NORM)
    return centered * inverse_std, inverse_std


def norm_back(grad_normed, normed, inverse_std):
    centered = grad_normed - jnp.mean(grad_normed, axis=-1, keepdims=True)
    return inverse_std * (centered - normed * jnp.mean(grad_normed * normed, axis=-1, keepdims=True))


def frames_of(rows):
    return rows.reshape(-1, FRAME_TOK, D)


def flat(framed):
    return framed.reshape(-1, D)


BLK = 256
FBLK = BLK // FRAME_TOK


def row_spec():
    return pl.BlockSpec((BLK, D), lambda i: (i, 0))


def mod_spec(parts):
    return pl.BlockSpec((FBLK, parts, D), lambda i: (i, 0, 0))


def row_call(kernel, name, row_ins, mods, row_outs, mod_outs, nbytes):
    outs = [jax.ShapeDtypeStruct((CLIP, D), t) for t in row_outs]
    outs += [jax.ShapeDtypeStruct((FRAMES, n, D), F32) for n in mod_outs]
    return pl.pallas_call(
        kernel,
        grid=(CLIP // BLK,),
        in_specs=[row_spec() for _ in row_ins] + [mod_spec(6)],
        out_specs=[row_spec() for _ in row_outs] + [mod_spec(n) for n in mod_outs],
        out_shape=outs,
        compiler_params=params(),
        cost_estimate=cost(30 * CLIP * D, nbytes),
        name=name,
    )(*row_ins, mods)


def first_norm_kernel(x_ref, mod_ref, h_ref):
    normed, _ = norm_rows(x_ref[...].astype(F32))
    mods = mod_ref[...]
    h_ref[...] = flat(
        frames_of(normed) * (1.0 + mods[:, 1:2]) + mods[:, 0:1]
    ).astype(BF)


def middle_kernel(x_ref, a_ref, b_ref, dy_ref, mod_ref, y_ref, s_ref, h_ref, de_ref):
    mods = mod_ref[...]
    branch = (a_ref[...].astype(F32) + b_ref[...].astype(F32)).astype(BF)
    s_ref[...] = branch
    mid = frames_of(x_ref[...].astype(F32)) + mods[:, 2:3] * frames_of(branch.astype(F32))
    y_ref[...] = flat(mid)
    normed, _ = norm_rows(flat(mid))
    h_ref[...] = flat(
        frames_of(normed) * (1.0 + mods[:, 4:5]) + mods[:, 3:4]
    ).astype(BF)
    de_ref[...] = flat(mods[:, 5:6] * frames_of(dy_ref[...].astype(F32))).astype(BF)


def back_kernel(y_ref, g_ref, gp_ref, dy_ref, s_ref, e_ref, ep_ref, mod_ref, out_ref, dy1_ref, da_ref, dm_ref):
    mods = mod_ref[...]
    mid = y_ref[...]
    feed = e_ref[...].astype(F32) + ep_ref[...].astype(F32)
    dy = dy_ref[...].astype(F32)
    out_ref[...] = (mid + flat(mods[:, 5:6] * frames_of(feed))).astype(BF)
    normed, inverse_std = norm_rows(mid)
    grad = g_ref[...].astype(F32) + gp_ref[...].astype(F32)
    dm_ref[:, 0] = jnp.sum(frames_of(grad), axis=1)
    dm_ref[:, 1] = jnp.sum(frames_of(grad * normed), axis=1)
    scaled = flat(frames_of(grad) * (1.0 + mods[:, 4:5]))
    dy1 = dy + norm_back(scaled, normed, inverse_std)
    dy1_ref[...] = dy1
    dm_ref[:, 2] = jnp.sum(frames_of(dy1 * s_ref[...].astype(F32)), axis=1)
    dm_ref[:, 3] = jnp.sum(frames_of(dy * feed), axis=1)
    da_ref[...] = flat(mods[:, 2:3] * frames_of(dy1)).astype(BF)


def last_kernel(x_ref, g_ref, gp_ref, dy1_ref, mod_ref, out_ref, dm_ref):
    mods = mod_ref[...]
    normed, inverse_std = norm_rows(x_ref[...].astype(F32))
    grad = g_ref[...].astype(F32) + gp_ref[...].astype(F32)
    dm_ref[:, 0] = jnp.sum(frames_of(grad), axis=1)
    dm_ref[:, 1] = jnp.sum(frames_of(grad * normed), axis=1)
    scaled = flat(frames_of(grad) * (1.0 + mods[:, 1:2]))
    out_ref[...] = (dy1_ref[...] + norm_back(scaled, normed, inverse_std)).astype(BF)


MESH = pl.DeviceIdType.MESH
HEAD_TILES = 36
TABLE_TILES = 8
PAYLOAD = 46
LEVEL_TILE = HEAD_TILES + TABLE_TILES


class Link:
    def __init__(self, sends, recvs):
        self.sends, self.recvs, self.used, self.pending = sends, recvs, 0, []

    def make(self, src, dst, dp, mp):
        copy = pltpu.make_async_remote_copy(
            src_ref=src,
            dst_ref=dst,
            send_sem=self.sends.at[self.used],
            recv_sem=self.recvs.at[self.used],
            device_id=(dp, mp),
            device_id_type=MESH,
        )
        self.used += 1
        self.pending.append(copy)
        return copy

    def send(self, src, dst, dp, mp):
        copy = self.make(src, dst, dp, mp)
        copy.start()
        return copy

    def drain(self):
        for copy in self.pending:
            copy.wait_send()
        self.pending = []


def greet(d, z):
    barrier = pltpu.get_barrier_semaphore()
    for step in (1, 2, 4):
        pl.semaphore_signal(barrier, inc=1, device_id=(jnp.bitwise_xor(d, step), z), device_id_type=MESH)
    for s in (1, 2, 3):
        pl.semaphore_signal(barrier, inc=1, device_id=(d, lax.rem(z + s, 4)), device_id_type=MESH)
    pl.semaphore_wait(barrier, 6)


QBLK = 256
ROWS = 512
SCALE2 = HD ** (-0.5) * LOG2E


ENTRY_COPIES = 8 + 45 + 3


def front_kernel(
    idx_ref,
    pay_ref,
    act_ref,
    cot_ref,
    bias_ref,
    w_ref,
    wmod_out,
    x_out,
    dy_out,
    h_out,
    wpack_out,
    qkv_out,
    o_out,
    branch_out,
    y_out,
    e_out,
    dh_out,
    dup_out,
    ddown_out,
    mods_ref,
    bias_out,
    lse_ref,
    emb_ref,
    own_hot_ref,
    gath,
    own,
    turn,
    xs,
    dys,
    bs,
    part,
    modbuf,
    hots,
    hs,
    wpack,
    qs,
    os_,
    mine,
    peer,
    e_acc,
    dh_acc,
    wfeed,
    up_stage,
    down_stage,
    up_acc,
    down_acc,
    sends,
    recvs,
    swap_sends,
    swap_recvs,
    strip_sends,
    strip_recvs,
    local_sems,
    pack_sems,
    stage_sems,
):
    d, z = lax.axis_index("dp"), lax.axis_index("mp")
    core, chip = lax.rem(d, 2), d // 2
    dk, dx, dyd = jnp.bitwise_xor(d, 1), jnp.bitwise_xor(d, 2), jnp.bitwise_xor(d, 4)
    dxy = jnp.bitwise_xor(d, 6)
    link = Link(sends, recvs)
    greet(d, z)

    def slot(owner, first=0, count=PAYLOAD):
        return gath.at[pl.ds(owner * PAYLOAD + first, count)]

    half = PAYLOAD // 2
    home = pltpu.make_async_copy(pay_ref, slot(d), local_sems.at[0])
    home.start()
    to_x = link.send(pay_ref, slot(d), dx, z)
    to_y = link.send(pay_ref, slot(d), dyd, z)
    to_k = link.send(pay_ref, slot(d), dk, z)

    holds = (z // 2) == core
    rows = pl.ds(lax.rem(z, 2) * CLIP, CLIP)
    picks = [
        (act_ref.at[rows], xs),
        (cot_ref.at[rows], dys),
        (bias_ref.at[lax.rem(z, 2)], bs),
    ]

    def swaps():
        return [
            pltpu.make_async_remote_copy(
                src_ref=src,
                dst_ref=dst,
                send_sem=swap_sends.at[i],
                recv_sem=swap_recvs.at[i],
                device_id=(dk, z),
                device_id_type=MESH,
            )
            for i, (src, dst) in enumerate(picks)
        ]

    def keeps():
        return [pltpu.make_async_copy(src, dst, local_sems.at[1 + i]) for i, (src, dst) in enumerate(picks)]

    @pl.when(holds)
    def _():
        for copy in swaps() + keeps():
            copy.start()

    to_x.wait_recv()
    x_to_y = link.send(slot(dx, 0, half), slot(dx, 0, half), dyd, z)
    x_to_k = link.send(slot(dx), slot(dx), dk, z)
    to_y.wait_recv()
    y_to_x = link.send(slot(dyd, half, half), slot(dyd, half, half), dx, z)
    y_to_k = link.send(slot(dyd), slot(dyd), dk, z)

    @pl.when(holds)
    def _():
        for copy in swaps():
            copy.wait_send()
        for copy in keeps():
            copy.wait()

    @pl.when(jnp.logical_not(holds))
    def _():
        for copy in swaps():
            copy.wait_recv()

    bias_out[...] = bs[...]
    locals_used = [7]

    def save(src, dst):
        copy = pltpu.make_async_copy(src, dst, local_sems.at[locals_used[0]])
        locals_used[0] += 1
        copy.start()
        return copy

    x_saved = save(xs, x_out)
    dy_saved = save(dys, dy_out)

    x_to_y.wait_recv()
    y_to_x.wait_recv()
    xy_to_k = link.send(slot(dxy), slot(dxy), dk, z)
    home.wait()
    to_k.wait_recv()
    x_to_k.wait_recv()
    y_to_k.wait_recv()
    xy_to_k.wait_recv()

    def tile(number):
        return gath[idx_ref[number]]

    def pick_attn(j, _):
        lanes = pl.ds(pl.multiple_of(j * TILE, TILE), TILE)
        for role in range(3):
            turn[role] = tile(j * 6 + 2 * role + core).T
        turn[3] = tile(48 + core * 8 + j)
        for role in range(4):
            own[0, role * 32 : (role + 1) * 32, lanes] = turn[role, pl.ds(pl.multiple_of(chip * 32, 32), 32), :]
        return 0

    def pick_feed(j, _):
        lanes = pl.ds(pl.multiple_of(j * TILE, TILE), TILE)
        own[1, :, lanes] = tile(64 + j * 8 + 4 * core + chip).T
        own[2, :, lanes] = tile(128 + (4 * core + chip) * 8 + j)
        return 0

    def pick_mod(j, _):
        strip = pl.ds(pl.multiple_of(j * TILE, TILE), TILE)
        for col in range(12):
            qs[col // 3, strip, (col % 3) * TILE : (col % 3 + 1) * TILE] = tile(192 + j * 12 + col)
        return 0

    along, by_x, by_y, diag = {}, {}, {}, {}
    all_groups = [(g, s) for g in range(3) for s in (0, 1, 3, 2)]

    def landing(g, p, m):
        return w_ref.at[p, m] if g == 0 else wfeed.at[g - 1, p, m]

    for g, s in all_groups:
        m = lax.rem(z + 4 - s, 4)
        if s:
            along[g, s] = link.make(own.at[g], landing(g, 0, z), d, lax.rem(z + s, 4))
        src = own.at[g] if s == 0 else landing(g, 0, m)
        by_x[g, s] = link.make(src, landing(g, 1, m), dx, z)
        by_y[g, s] = link.make(src, landing(g, 2, m), dyd, z)
        if s < 2:
            diag[g, s] = link.make(landing(g, 1, m), landing(g, 3, m), dyd, z)
        else:
            diag[g, s] = link.make(landing(g, 2, m), landing(g, 3, m), dx, z)
    homes = [pltpu.make_async_copy(own.at[g], landing(g, 0, z), local_sems.at[4 + g]) for g in range(3)]

    def send_along(g):
        for s in (1, 3, 2):
            along[g, s].start()

    def send_plane(g, s):
        if s:
            along[g, s].wait_recv()
        by_x[g, s].start()
        by_y[g, s].start()

    def send_diag(g, s):
        (by_x if s < 2 else by_y)[g, s].wait_recv()
        diag[g, s].start()

    lax.fori_loop(0, 8, pick_attn, 0)
    send_along(0)
    send_plane(0, 0)
    homes[0].start()

    lax.fori_loop(0, 8, pick_mod, 0)
    mod_saved = save(qs, wmod_out)
    places = lax.broadcasted_iota(jnp.int32, (32, LEVELS), 1).astype(F32)
    for owner in range(8):
        codes = gath[owner * PAYLOAD + LEVEL_TILE][:32].astype(F32)
        level = codes[:, 0:1] * 32.0 + codes[:, 64:65]
        hots[owner * 32 : (owner + 1) * 32] = jnp.where(level == places, 1.0, 0.0).astype(BF)
    own_hot_ref[...] = hots[:, pl.ds(pl.multiple_of(d * TILE, TILE), TILE)]
    for j in range(TABLE_TILES):
        strip = jnp.concatenate([gath[owner * PAYLOAD + HEAD_TILES + j] for owner in range(8)], axis=0)
        emb_ref[:, j * TILE : (j + 1) * TILE] = dot(hots[...], strip, NN).astype(BF)
    embedded = emb_ref[pl.ds(pl.multiple_of(chip * 64, 64), 64), :]
    for k in range(4):
        part[:, :, k * 384 : (k + 1) * 384] = dot(embedded, qs[k], NN).reshape(4, FRAMES, 384)
    modbuf[z] = part[z]
    shared = {}
    for s in (1, 3, 2):
        shared[s] = link.send(part.at[lax.rem(z + s, 4)], modbuf.at[z], d, lax.rem(z + s, 4))

    lax.fori_loop(0, 8, pick_feed, 0)
    send_along(1)
    send_along(2)
    homes[1].start()
    homes[2].start()
    for s in (1, 3, 2):
        send_plane(0, s)
    for s in (0, 1, 3, 2):
        send_diag(0, s)
    send_plane(1, 0)
    send_plane(2, 0)

    for s in (1, 3, 2):
        shared[s].wait_recv()
    for m in range(4):
        for c in range(6):
            mods_ref[:, c, m * 256 : (m + 1) * 256] = modbuf[m, :, c * 256 : (c + 1) * 256]

    def norm_strip(i, _):
        strip = pl.ds(pl.multiple_of(i * BLK, BLK), BLK)
        normed, _ = norm_rows(xs[strip].astype(F32))
        mods = mods_ref[pl.ds(i * FBLK, FBLK)]
        hs[strip] = flat(frames_of(normed) * (1.0 + mods[:, 1:2]) + mods[:, 0:1]).astype(BF)
        return 0

    lax.fori_loop(0, CLIP // BLK, norm_strip, 0)
    h_saved = save(hs, h_out)

    def late(g, p):
        for s in (0, 1, 3, 2):
            if p == 3:
                diag[g, s].wait_recv()
            elif (p == 1) == (s >= 2):
                (by_x if p == 1 else by_y)[g, s].wait_recv()

    for p in (1, 2, 3):
        late(0, p)
    homes[0].wait()

    def packs(m):
        return [
            pltpu.make_async_copy(
                w_ref.at[p, m, pl.ds(role * 32, 32)],
                wpack.at[m, pl.ds(role * TILE + p * 32, 32)],
                pack_sems.at[m * 16 + p * 4 + role],
            )
            for p in range(4)
            for role in range(4)
        ]

    def pack_start(m, _):
        for copy in packs(m):
            copy.start()
        return 0

    lax.fori_loop(0, 4, pack_start, 0)
    mod_saved.wait()

    def project_in(m, _):
        for copy in packs(m):
            copy.wait()
        qs[m] = dot(hs[...], wpack[m, 0 : 3 * TILE], NT).astype(BF)
        return 0

    lax.fori_loop(0, 4, project_in, 0)
    pack_saved = save(wpack, wpack_out)
    qkv_saved = save(qs, qkv_out)

    def attend_group(m, _):
        @pl.when(m == 0)
        def _():
            for s in (1, 3, 2):
                send_plane(1, s)

        @pl.when(m == 1)
        def _():
            send_diag(1, 0)
            send_diag(1, 1)

        @pl.when(m == 2)
        def _():
            send_plane(2, 1)
            send_plane(2, 3)
            send_diag(1, 3)

        @pl.when(m == 3)
        def _():
            send_plane(2, 2)
            send_diag(1, 2)
            send_diag(2, 0)

        for head in range(2):
            lanes = slice(head * HD, (head + 1) * HD)
            keys = qs[m, :, TILE + head * HD : TILE + (head + 1) * HD]
            values = qs[m, :, 2 * TILE + head * HD : 2 * TILE + (head + 1) * HD]

            def step(i, _, lanes=lanes, keys=keys, values=values, head=head):
                across = pl.ds(pl.multiple_of(i * QBLK, QBLK), QBLK)
                queries = qs[m, across, lanes]
                scores = dot(keys, queries, NT).reshape(FRAMES, FRAME_TOK, QBLK)
                scores = scores * SCALE2 + bs[:, across][:, None, :]
                peak = jnp.max(jnp.max(scores, axis=0), axis=0, keepdims=True)
                weights = jnp.exp2(scores - peak[None])
                total = jnp.sum(jnp.sum(weights, axis=0), axis=0, keepdims=True)
                mixed = dot(values, weights.reshape(CLIP, QBLK).astype(BF), TN)
                os_[m, lanes, across] = (mixed / total).astype(BF)
                lse_ref[m, head : head + 1, across] = peak + jnp.log2(total)
                return 0

            lax.fori_loop(0, CLIP // QBLK, step, 0)
        return 0

    lax.fori_loop(0, 4, attend_group, 0)
    o_saved = save(os_, o_out)
    send_diag(2, 1)

    def swap_strip(i):
        strip = pl.ds(pl.multiple_of(i * BLK, BLK), BLK)
        return pltpu.make_async_remote_copy(
            src_ref=mine.at[strip],
            dst_ref=peer.at[strip],
            send_sem=strip_sends.at[i],
            recv_sem=strip_recvs.at[i],
            device_id=(dk, z),
            device_id_type=MESH,
        )

    def project_out(i, _):
        strip = pl.ds(pl.multiple_of(i * BLK, BLK), BLK)
        total = dot(os_[0, :, strip], wpack[0, 3 * TILE : 4 * TILE], TN)
        for m in range(1, 4):
            total = total + dot(os_[m, :, strip], wpack[m, 3 * TILE : 4 * TILE], TN)
        mine[strip] = total.astype(BF)
        swap_strip(i).start()
        return 0

    lax.fori_loop(0, CLIP // BLK, project_out, 0)
    h_saved.wait()
    dy_saved.wait()

    def middle_strip(i, _):
        strip = pl.ds(pl.multiple_of(i * BLK, BLK), BLK)
        swap_strip(i).wait_recv()
        mods = mods_ref[pl.ds(i * FBLK, FBLK)]
        branch = (mine[strip].astype(F32) + peer[strip].astype(F32)).astype(BF)
        peer[strip] = branch
        mid = frames_of(xs[strip].astype(F32)) + mods[:, 2:3] * frames_of(branch.astype(F32))
        dh_acc[strip] = flat(mid)
        normed, _ = norm_rows(flat(mid))
        hs[strip] = flat(frames_of(normed) * (1.0 + mods[:, 4:5]) + mods[:, 3:4]).astype(BF)
        dys[strip] = flat(mods[:, 5:6] * frames_of(dys[strip].astype(F32))).astype(BF)
        return 0

    lax.fori_loop(0, CLIP // BLK, middle_strip, 0)
    y_saved = save(dh_acc, y_out)
    branch_saved = save(peer, branch_out)
    send_diag(2, 3)
    send_diag(2, 2)
    e_acc[...] = jnp.zeros_like(e_acc)
    y_saved.wait()
    dh_acc[...] = jnp.zeros_like(dh_acc)
    homes[1].wait()
    homes[2].wait()

    def stages(block):
        buf, p, first = lax.rem(block, 2), block // 2, lax.rem(block, 2) * 2
        return [
            pltpu.make_async_copy(stage.at[buf], dst.at[p, pl.ds(first, 2)], stage_sems.at[2 * buf + k])
            for k, (stage, dst) in enumerate(((up_stage, dup_out), (down_stage, ddown_out)))
        ]

    def feed_block(block, _):
        for p in (1, 2, 3):

            @pl.when(block == 2 * p)
            def _(p=p):
                late(1, p)
                late(2, p)

        buf, p, first = lax.rem(block, 2), block // 2, lax.rem(block, 2) * 2
        up = wfeed[0, p, pl.ds(first, 2)].reshape(2 * TILE, D)
        down = wfeed[1, p, pl.ds(first, 2)].reshape(2 * TILE, D)

        @pl.when(block >= 2)
        def _():
            for copy in stages(block - 2):
                copy.wait()

        for piece in range(CLIP // ROWS):
            rows = slice(piece * ROWS, (piece + 1) * ROWS)
            hidden = hs[rows]
            grad = dys[rows]
            pre = dot(hidden, up, NT)
            square = pre * pre
            tanh = jnp.tanh(GELU_A * pre * (1.0 + GELU_B * square))
            act = (0.5 * pre * (1.0 + tanh)).astype(BF)
            slope = 0.5 * (1.0 + tanh) + 0.5 * pre * (1.0 - tanh * tanh) * (
                GELU_A * (1.0 + 3.0 * GELU_B * square)
            )
            grad_act = dot(grad, down, NT).astype(BF).astype(F32)
            grad_pre = (grad_act * slope).astype(BF)
            e_acc[rows] += dot(act, down, NN)
            dh_acc[rows] += dot(grad_pre, up, NN)
            if piece == 0:
                down_acc[...] = dot(act, grad, TN)
                up_acc[...] = dot(grad_pre, hidden, TN)
            else:
                down_stage[buf] = (down_acc[...] + dot(act, grad, TN)).astype(BF).reshape(2, TILE, D)
                up_stage[buf] = (up_acc[...] + dot(grad_pre, hidden, TN)).astype(BF).reshape(2, TILE, D)
        for copy in stages(block):
            copy.start()
        return 0

    lax.fori_loop(0, 8, feed_block, 0)
    branch_saved.wait()

    def swap_done(i, _):
        swap_strip(i).wait_send()
        return 0

    lax.fori_loop(0, CLIP // BLK, swap_done, 0)

    def cast_strip(i, _):
        strip = pl.ds(pl.multiple_of(i * BLK, BLK), BLK)
        mine[strip] = e_acc[strip].astype(BF)
        peer[strip] = dh_acc[strip].astype(BF)
        return 0

    lax.fori_loop(0, CLIP // BLK, cast_strip, 0)
    ends = [save(mine, e_out), save(peer, dh_out), x_saved, pack_saved, qkv_saved, o_saved]
    for block in (6, 7):
        for copy in stages(block):
            copy.wait()
    for copy in ends:
        copy.wait()
    link.drain()


def front(masters, level_table, levels, bias_pair, activations, cotangent, owner_list):
    slots = masters.shape[0]
    codes = jnp.stack([levels.reshape(-1) // 32, levels.reshape(-1) % 32], axis=1).astype(BF)
    codes = jnp.pad(jnp.repeat(codes, 64, axis=1), ((0, TILE - codes.shape[0]), (0, 0)))
    payload = jnp.concatenate(
        [
            masters.astype(BF),
            level_table.reshape(TILE, TABLE_TILES, TILE).transpose(1, 0, 2),
            codes[None],
            jnp.zeros((1, TILE, TILE), BF),
        ]
    )
    position = jnp.arange(owner_list.shape[0], dtype=jnp.int32)
    place = (position // slots) * PAYLOAD + position % slots
    index = jnp.sum(
        jnp.where(owner_list[None, :] == position[:, None], place[None, :], 0), axis=1
    ).astype(jnp.int32)
    vmem = pl.BlockSpec(memory_space=pltpu.VMEM)
    hbm = pl.BlockSpec(memory_space=pl.ANY)
    clip = jax.ShapeDtypeStruct((CLIP, D), BF)
    chunks = jax.ShapeDtypeStruct((4, 4, TILE, D), BF)
    thirds = jax.ShapeDtypeStruct((4, CLIP, 3 * TILE), BF)
    return pl.pallas_call(
        front_kernel,
        in_specs=[pl.BlockSpec(memory_space=pltpu.SMEM), hbm, hbm, hbm, hbm],
        out_specs=[hbm] * 14 + [vmem] * 5,
        out_shape=[
            chunks,
            thirds,
            clip,
            clip,
            clip,
            jax.ShapeDtypeStruct((4, 4 * TILE, D), BF),
            thirds,
            jax.ShapeDtypeStruct((4, TILE, CLIP), BF),
            clip,
            jax.ShapeDtypeStruct((CLIP, D), F32),
            clip,
            clip,
            chunks,
            chunks,
            jax.ShapeDtypeStruct((FRAMES, 6, D), F32),
            jax.ShapeDtypeStruct((FRAMES, CLIP), F32),
            jax.ShapeDtypeStruct((4, 2, CLIP), F32),
            jax.ShapeDtypeStruct((256, D), BF),
            jax.ShapeDtypeStruct((256, TILE), BF),
        ],
        scratch_shapes=[
            pltpu.VMEM((8 * PAYLOAD, TILE, TILE), BF),
            pltpu.VMEM((3, TILE, D), BF),
            pltpu.VMEM((4, TILE, TILE), BF),
            pltpu.VMEM((CLIP, D), BF),
            pltpu.VMEM((CLIP, D), BF),
            pltpu.VMEM((FRAMES, CLIP), F32),
            pltpu.VMEM((4, FRAMES, 12 * TILE), F32),
            pltpu.VMEM((4, FRAMES, 12 * TILE), F32),
            pltpu.VMEM((256, LEVELS), BF),
            pltpu.VMEM((CLIP, D), BF),
            pltpu.VMEM((4, 4 * TILE, D), BF),
            pltpu.VMEM((4, CLIP, 3 * TILE), BF),
            pltpu.VMEM((4, TILE, CLIP), BF),
            pltpu.VMEM((CLIP, D), BF),
            pltpu.VMEM((CLIP, D), BF),
            pltpu.VMEM((CLIP, D), F32),
            pltpu.VMEM((CLIP, D), F32),
            pltpu.VMEM((2, 4, 4, TILE, D), BF),
            pltpu.VMEM((2, 2, TILE, D), BF),
            pltpu.VMEM((2, 2, TILE, D), BF),
            pltpu.VMEM((2 * TILE, D), F32),
            pltpu.VMEM((2 * TILE, D), F32),
            pltpu.SemaphoreType.DMA((ENTRY_COPIES,)),
            pltpu.SemaphoreType.DMA((ENTRY_COPIES,)),
            pltpu.SemaphoreType.DMA((3,)),
            pltpu.SemaphoreType.DMA((3,)),
            pltpu.SemaphoreType.DMA((4,)),
            pltpu.SemaphoreType.DMA((4,)),
            pltpu.SemaphoreType.DMA((24,)),
            pltpu.SemaphoreType.DMA((64,)),
            pltpu.SemaphoreType.DMA((4,)),
        ],
        compiler_params=pltpu.CompilerParams(
            vmem_limit_bytes=63 * 1024 * 1024, collective_id=0, has_side_effects=True
        ),
        cost_estimate=cost(1e11, 60e6),
        name="front",
    )(index, payload, activations, cotangent, bias_pair)


def attend_kernel(qkv_ref, bias_ref, o_ref, lse_ref):
    for head in range(2):
        lanes = slice(head * HD, (head + 1) * HD)
        keys = qkv_ref[:, TILE + head * HD : TILE + (head + 1) * HD]
        values = qkv_ref[:, 2 * TILE + head * HD : 2 * TILE + (head + 1) * HD]

        def step(i, _, lanes=lanes, keys=keys, values=values, head=head):
            start = pl.multiple_of(i * QBLK, QBLK)
            queries = qkv_ref[pl.ds(start, QBLK), lanes]
            scores = dot(keys, queries, NT).reshape(FRAMES, FRAME_TOK, QBLK)
            scores = scores * SCALE2 + bias_ref[:, pl.ds(start, QBLK)][:, None, :]
            peak = jnp.max(jnp.max(scores, axis=0), axis=0, keepdims=True)
            weights = jnp.exp2(scores - peak[None])
            total = jnp.sum(jnp.sum(weights, axis=0), axis=0, keepdims=True)
            mixed = dot(values, weights.reshape(CLIP, QBLK).astype(BF), TN)
            o_ref[lanes, pl.ds(start, QBLK)] = (mixed / total).astype(BF)
            lse_ref[0, head : head + 1, pl.ds(start, QBLK)] = peak + jnp.log2(total)
            return 0

        lax.fori_loop(0, CLIP // QBLK, step, 0)


def attend(qkv, bias):
    groups = qkv.shape[1] // (3 * TILE)
    return pl.pallas_call(
        attend_kernel,
        grid=(groups,),
        in_specs=[
            pl.BlockSpec((CLIP, 3 * TILE), lambda m: (0, m)),
            pl.BlockSpec((FRAMES, CLIP), lambda m: (0, 0)),
        ],
        out_specs=[
            pl.BlockSpec((TILE, CLIP), lambda m: (m, 0)),
            pl.BlockSpec((1, 2, CLIP), lambda m: (m, 0, 0)),
        ],
        out_shape=[
            jax.ShapeDtypeStruct((groups * TILE, CLIP), BF),
            jax.ShapeDtypeStruct((groups, 2, CLIP), F32),
        ],
        compiler_params=params(),
        cost_estimate=cost(groups * 2 * 4 * CLIP * CLIP * HD * 3, 2 * qkv.size, groups * 2 * CLIP * CLIP),
        name="attend",
    )(qkv, bias)


def attend_back_kernel(qkv_ref, o_ref, do_ref, lse_ref, bias_ref, out_ref, dk_ref, dv_ref):
    for head in range(2):
        lanes = slice(head * HD, (head + 1) * HD)
        keys = qkv_ref[:, TILE + head * HD : TILE + (head + 1) * HD]
        values = qkv_ref[:, 2 * TILE + head * HD : 2 * TILE + (head + 1) * HD]
        dk_ref[...] = jnp.zeros_like(dk_ref)
        dv_ref[...] = jnp.zeros_like(dv_ref)

        def step(i, _, lanes=lanes, keys=keys, values=values, head=head):
            start = pl.multiple_of(i * QBLK, QBLK)
            across = pl.ds(start, QBLK)
            queries = qkv_ref[across, lanes]
            grad = do_ref[lanes, across]
            shift = bias_ref[:, across] - lse_ref[0, head : head + 1, across]
            scores = dot(keys, queries, NT).reshape(FRAMES, FRAME_TOK, QBLK)
            soft = jnp.exp2(scores * SCALE2 + shift[:, None, :]).reshape(CLIP, QBLK)
            delta = jnp.sum(
                grad.astype(F32) * o_ref[lanes, across].astype(F32), axis=0, keepdims=True
            )
            grad_soft = dot(values, grad, NN)
            grad_scores = (soft * (grad_soft - delta)).astype(BF)
            dv_ref[...] += dot(soft.astype(BF), grad, NT)
            dk_ref[...] += dot(grad_scores, queries, NN)
            grad_query = dot(keys, grad_scores, TN) * HD ** (-0.5)
            out_ref[across, lanes] = grad_query.T.astype(BF)
            return 0

        lax.fori_loop(0, CLIP // QBLK, step, 0)
        out_ref[:, TILE + head * HD : TILE + (head + 1) * HD] = (dk_ref[...] * HD ** (-0.5)).astype(BF)
        out_ref[:, 2 * TILE + head * HD : 2 * TILE + (head + 1) * HD] = dv_ref[...].astype(BF)


def attend_back(qkv, o_rows, do_rows, lse, bias):
    groups = qkv.shape[1] // (3 * TILE)
    return pl.pallas_call(
        attend_back_kernel,
        grid=(groups,),
        in_specs=[
            pl.BlockSpec((CLIP, 3 * TILE), lambda m: (0, m)),
            pl.BlockSpec((TILE, CLIP), lambda m: (m, 0)),
            pl.BlockSpec((TILE, CLIP), lambda m: (m, 0)),
            pl.BlockSpec((1, 2, CLIP), lambda m: (m, 0, 0)),
            pl.BlockSpec((FRAMES, CLIP), lambda m: (0, 0)),
        ],
        out_specs=pl.BlockSpec((CLIP, 3 * TILE), lambda m: (0, m)),
        out_shape=jax.ShapeDtypeStruct(qkv.shape, BF),
        scratch_shapes=[pltpu.VMEM((CLIP, HD), F32), pltpu.VMEM((CLIP, HD), F32)],
        compiler_params=params(),
        cost_estimate=cost(groups * 2 * 10 * CLIP * CLIP * HD * 3, 4 * qkv.size, groups * 2 * CLIP * CLIP),
        name="attend_back",
    )(qkv, o_rows, do_rows, lse, bias)


UNITS = 256


def feed_kernel(h_ref, de_ref, up_ref, down_ref, e_ref, dh_ref, dup_ref, ddown_ref, e_acc, dh_acc, up_acc, down_acc):
    block = pl.program_id(0)
    last = pl.num_programs(0) - 1
    up = up_ref[...]
    down = down_ref[...]
    for part in range(CLIP // ROWS):
        rows = slice(part * ROWS, (part + 1) * ROWS)
        hidden = h_ref[rows]
        grad = de_ref[rows]
        pre = dot(hidden, up, NT)
        square = pre * pre
        tanh = jnp.tanh(GELU_A * pre * (1.0 + GELU_B * square))
        act = (0.5 * pre * (1.0 + tanh)).astype(BF)
        slope = 0.5 * (1.0 + tanh) + 0.5 * pre * (1.0 - tanh * tanh) * (
            GELU_A * (1.0 + 3.0 * GELU_B * square)
        )
        grad_act = dot(grad, down, NT).astype(BF).astype(F32)
        grad_pre = (grad_act * slope).astype(BF)
        feed = dot(act, down, NN)
        back = dot(grad_pre, up, NN)

        @pl.when(block == 0)
        def _():
            e_acc[rows] = feed
            dh_acc[rows] = back

        @pl.when(block > 0)
        def _():
            e_acc[rows] += feed
            dh_acc[rows] += back

        if part == 0:
            down_acc[...] = dot(act, grad, TN)
            up_acc[...] = dot(grad_pre, hidden, TN)
        else:
            ddown_ref[...] = (down_acc[...] + dot(act, grad, TN)).astype(BF)
            dup_ref[...] = (up_acc[...] + dot(grad_pre, hidden, TN)).astype(BF)

    @pl.when(block == last)
    def _():
        e_ref[...] = e_acc[...].astype(BF)
        dh_ref[...] = dh_acc[...].astype(BF)


def feed_both(hidden, grad, up, down):
    units = up.shape[0]
    whole = pl.BlockSpec((CLIP, D), lambda i: (0, 0))
    strip = pl.BlockSpec((UNITS, D), lambda i: (i, 0))
    return pl.pallas_call(
        feed_kernel,
        grid=(units // UNITS,),
        in_specs=[whole, whole, strip, strip],
        out_specs=[whole, whole, strip, strip],
        out_shape=[jax.ShapeDtypeStruct((CLIP, D), BF)] * 2 + [jax.ShapeDtypeStruct((units, D), BF)] * 2,
        scratch_shapes=[
            pltpu.VMEM((CLIP, D), F32),
            pltpu.VMEM((CLIP, D), F32),
            pltpu.VMEM((UNITS, D), F32),
            pltpu.VMEM((UNITS, D), F32),
        ],
        compiler_params=params(),
        cost_estimate=cost(12 * CLIP * D * units, 8 * CLIP * D + 8 * units * D, CLIP * units),
        name="feed_both",
    )(hidden, grad, up, down)


HALF = CLIP // 2
EXIT_COPIES = 8 + 1 + 18 + 9 + 24 + 12 + 6 + 14
EXIT_LOCAL = 32


class Relay:
    def __init__(self, sends, recvs, local, src, full, d, z):
        self.sends, self.recvs, self.local = sends, recvs, local
        self.src, self.full, self.d, self.z = src, full, d, z
        self.core = lax.rem(d, 2)

    def place(self, clip, first, count):
        start = pl.multiple_of(lax.rem(clip, 2) * CLIP + first * HALF, HALF)
        return self.full.at[pl.ds(start, count)]

    def copy(self, src, clip, half, way, hop):
        index = way * 6 + (hop - 1) * 2 + half
        return pltpu.make_async_remote_copy(
            src_ref=src,
            dst_ref=self.place(clip, half, HALF),
            send_sem=self.sends.at[index],
            recv_sem=self.recvs.at[index],
            device_id=(self.d - self.core + clip // 2, lax.rem(self.z + (1 if way == 0 else 3), 4)),
            device_id_type=MESH,
        )

    def more(self, way):
        return self.z < 3 if way == 0 else self.z > 0

    def own(self, way):
        part = self.src.at[pl.ds(pl.multiple_of(self.core * HALF, HALF), HALF)]
        return self.copy(part, self.z, self.core, way, 1)

    def home(self):
        return pltpu.make_async_copy(self.src, self.place(self.z, 0, CLIP), self.local)

    def first(self):
        for way in range(2):

            @pl.when(self.more(way))
            def _(way=way):
                self.own(way).start()

        @pl.when(self.z // 2 == self.core)
        def _():
            self.home().start()

    def arriving(self, way, hop):
        clip = lax.rem(self.z + (4 - hop if way == 0 else hop), 4)
        there = self.z >= hop if way == 0 else self.z + hop <= 3
        return clip, jnp.logical_and(there, clip // 2 == self.core)

    def hop(self, hop):
        for way in range(2):
            clip, here = self.arriving(way, hop)

            @pl.when(here)
            def _(way=way, clip=clip):
                for half in range(2):
                    part = self.place(clip, half, HALF)
                    self.copy(part, clip, half, way, hop).wait_recv()
                    if hop < 3:

                        @pl.when(self.more(way))
                        def _(part=part, half=half):
                            self.copy(part, clip, half, way, hop + 1).start()

    def finish(self):
        for way in range(2):

            @pl.when(self.more(way))
            def _(way=way):
                self.own(way).wait_send()

            for hop in (1, 2):
                clip, here = self.arriving(way, hop)

                @pl.when(jnp.logical_and(here, self.more(way)))
                def _(way=way, clip=clip, hop=hop):
                    for half in range(2):
                        self.copy(self.place(clip, half, HALF), clip, half, way, hop + 1).wait_send()

        @pl.when(self.z // 2 == self.core)
        def _():
            self.home().wait()


class Line:
    def __init__(self, link, own, held, z, d):
        self.own, self.held, self.z, self.d = own, held, z, d
        self.sends, self.recvs, self.base = link.sends, link.recvs, link.used
        link.used += 2

    def copy(self, way, at):
        if way == 0:
            src, count = self.own.at[at + 1 : 4], 3 - at
        else:
            src, count = self.own.at[0:at], at
        return pltpu.make_async_remote_copy(
            src_ref=src,
            dst_ref=self.held.at[way, 0:count],
            send_sem=self.sends.at[self.base + way],
            recv_sem=self.recvs.at[self.base + way],
            device_id=(self.d, at + (1 if way == 0 else -1)),
            device_id_type=MESH,
        )

    def add(self, chunk, way, slot):
        def step(i, _):
            rows = pl.ds(pl.multiple_of(i * 32, 32), 32)
            total = self.own[chunk, rows].astype(F32) + self.held[way, slot, rows].astype(F32)
            self.own[chunk, rows] = total.astype(BF)
            return 0

        lax.fori_loop(0, 4, step, 0)

    def start(self):
        @pl.when(self.z == 0)
        def _():
            self.copy(0, 0).start()

        @pl.when(self.z == 3)
        def _():
            self.copy(1, 3).start()

    def turn(self):
        @pl.when(self.z == 1)
        def _():
            self.copy(0, 0).wait_recv()
            self.add(2, 0, 1)
            self.add(3, 0, 2)
            self.copy(0, 1).start()

        @pl.when(self.z == 2)
        def _():
            self.copy(1, 3).wait_recv()
            self.add(0, 1, 0)
            self.add(1, 1, 1)
            self.copy(1, 2).start()

    def turn_again(self):
        @pl.when(self.z == 2)
        def _():
            self.copy(0, 1).wait_recv()
            self.add(3, 0, 1)
            self.copy(0, 2).start()

        @pl.when(self.z == 1)
        def _():
            self.copy(1, 2).wait_recv()
            self.add(0, 1, 0)
            self.copy(1, 1).start()

    def total(self, out):
        for at in range(4):

            @pl.when(self.z == at)
            def _(at=at):
                if at == 0:
                    self.copy(1, 1).wait_recv()
                if at == 3:
                    self.copy(0, 2).wait_recv()

                def step(i, _):
                    rows = pl.ds(pl.multiple_of(i * 32, 32), 32)
                    total = self.own[at, rows].astype(F32)
                    if at > 0:
                        total = total + self.held[0, 0, rows].astype(F32)
                    if at < 3:
                        total = total + self.held[1, at, rows].astype(F32)
                    out[rows] = total.astype(BF)
                    return 0

                lax.fori_loop(0, 4, step, 0)

    def finish(self):
        for at in range(4):

            @pl.when(self.z == at)
            def _(at=at):
                if at < 3:
                    self.copy(0, at).wait_send()
                if at > 0:
                    self.copy(1, at).wait_send()


def exit_kernel(
    y_hbm,
    g_hbm,
    e_hbm,
    dy_hbm,
    br_hbm,
    x_hbm,
    h_hbm,
    qkv_hbm,
    o_hbm,
    wpack_hbm,
    wmod_hbm,
    up_hbm,
    down_hbm,
    mods_ref,
    bias_ref,
    lse_ref,
    emb_ref,
    hot_ref,
    out_all,
    in_all,
    everyone,
    dwm_out,
    table_ref,
    ys,
    gs,
    es,
    dys,
    brs,
    gp,
    ep,
    qs,
    os_,
    dos,
    win,
    wout,
    dhp,
    dattn,
    got,
    loc,
    zbuf,
    held,
    red,
    dm,
    dms,
    dmall,
    trow,
    tbuf,
    dk_ref,
    dv_ref,
    sends,
    recvs,
    strip_sends,
    strip_recvs,
    out_sends,
    out_recvs,
    in_sends,
    in_recvs,
    local_sems,
):
    d, z = lax.axis_index("dp"), lax.axis_index("mp")
    core, chip = lax.rem(d, 2), d // 2
    dk, dx, dyd = jnp.bitwise_xor(d, 1), jnp.bitwise_xor(d, 2), jnp.bitwise_xor(d, 4)
    link = Link(sends, recvs)
    locals_used = [0]

    def load(src, dst):
        copy = pltpu.make_async_copy(src, dst, local_sems.at[locals_used[0]])
        locals_used[0] += 1
        copy.start()
        return copy

    barrier = pltpu.get_barrier_semaphore()
    for step in (1, 2, 4):
        pl.semaphore_signal(barrier, inc=1, device_id=(jnp.bitwise_xor(d, step), z), device_id_type=MESH)
    for s in (1, 2, 3):
        pl.semaphore_signal(barrier, inc=1, device_id=(d, lax.rem(z + s, 4)), device_id_type=MESH)
        pl.semaphore_signal(barrier, inc=1, device_id=(dk, lax.rem(z + s, 4)), device_id_type=MESH)

    first_loads = [load(a, b) for a, b in ((g_hbm, gs), (e_hbm, es), (y_hbm, ys), (dy_hbm, dys), (br_hbm, brs))]
    loads = [load(a, b) for a, b in ((o_hbm, os_), (qkv_hbm, qs))]
    for m in range(4):
        loads.append(load(wpack_hbm.at[m, 3 * TILE : 4 * TILE], wout.at[m]))
        loads.append(load(wpack_hbm.at[m, 0 : 3 * TILE], win.at[m * 3 * TILE : (m + 1) * 3 * TILE]))
    feed_loads = []
    for g, src in enumerate((up_hbm, down_hbm)):
        feed_loads.append(load(src.at[0], loc.at[g, 0:4]))
        feed_loads.append(load(src.at[2, 0:2], loc.at[g, 4:6]))
        feed_loads.append(load(src.at[1, 2:4], loc.at[g, 6:8]))
    pl.semaphore_wait(barrier, 9)

    def strip_of(i):
        return pl.ds(pl.multiple_of(i * BLK, BLK), BLK)

    def swaps(i):
        return [
            pltpu.make_async_remote_copy(
                src_ref=src.at[strip_of(i)],
                dst_ref=dst.at[strip_of(i)],
                send_sem=strip_sends.at[2 * i + k],
                recv_sem=strip_recvs.at[2 * i + k],
                device_id=(dk, z),
                device_id_type=MESH,
            )
            for k, (src, dst) in enumerate(((g_hbm, gp), (e_hbm, ep)))
        ]

    def swap_start(i, _):
        for copy in swaps(i):
            copy.start()
        return 0

    lax.fori_loop(0, CLIP // BLK, swap_start, 0)

    plane = {}

    def plane_first(g, src):
        plane[g, 0] = link.send(src.at[3, 0:2], got.at[g, 0], dx, z)
        plane[g, 1] = link.send(src.at[3, 2:4], got.at[g, 1], dyd, z)
        plane[g, 2] = link.send(src.at[1, 0:2], got.at[g, 2], dx, z)
        plane[g, 3] = link.send(src.at[2, 2:4], got.at[g, 3], dyd, z)

    def add_into(dst, first, count, parts):
        def step(i, _):
            k = i // 4
            rows = pl.ds(pl.multiple_of(lax.rem(i, 4) * 32, 32), 32)
            total = dst[first + k, rows].astype(F32)
            for g, slot in parts:
                total = total + got[g, slot, k, rows].astype(F32)
            dst[first + k, rows] = total.astype(BF)
            return 0

        lax.fori_loop(0, count * 4, step, 0)

    def places(g):
        if g == 0:
            return (dattn.at[0], 0), (dattn.at[2], 0), (dattn.at[1], 2)
        return (loc.at[g - 1], 0), (loc.at[g - 1], 4), (loc.at[g - 1], 6)

    def plane_pass(g):
        _, (low, low_at), (high, high_at) = places(g)
        plane[g, 0].wait_recv()
        add_into(low, low_at, 2, [(g, 0)])
        plane[g, 4] = link.send(low.at[pl.ds(low_at, 2)], got.at[g, 4], dyd, z)
        plane[g, 1].wait_recv()
        add_into(high, high_at, 2, [(g, 1)])
        plane[g, 5] = link.send(high.at[pl.ds(high_at, 2)], got.at[g, 5], dx, z)

    column, lines = {}, {}

    def plane_final(g):
        (own, _), _, _ = places(g)
        for slot in (2, 3, 4, 5):
            plane[g, slot].wait_recv()
        add_into(own, 0, 2, [(g, 2), (g, 4)])
        add_into(own, 2, 2, [(g, 3), (g, 5)])
        if g:
            lines[g] = Line(link, own, held.at[g - 1], z, d)
            lines[g].start()
            return
        for s in (1, 3, 2):
            to = lax.rem(z + s, 4)
            column[s] = link.send(own.at[to], zbuf.at[s - 1], d, to)

    spread = {}
    homes = []

    def column_final(g):
        (own, _), _, _ = places(g)

        def step(i, _):
            rows = pl.ds(pl.multiple_of(i * 32, 32), 32)
            total = own[z, rows].astype(F32)
            for s in range(3):
                total = total + zbuf[s, rows].astype(F32)
            red[g, rows] = total.astype(BF)
            return 0

        if g:
            lines[g].total(red.at[g])
        else:
            for s in (1, 3, 2):
                column[s].wait_recv()
            lax.fori_loop(0, 4, step, 0)
        rows = pl.ds(g * TILE, TILE)
        spread[g, 2] = link.send(red.at[g], everyone.at[2, rows], dx, z)
        spread[g, 4] = link.send(red.at[g], everyone.at[4, rows], dyd, z)
        spread[g, 1] = link.send(red.at[g], everyone.at[1, rows], dk, z)
        homes.append(load(red.at[g], everyone.at[0, rows]))

    def spread_on(g):
        rows = pl.ds(g * TILE, TILE)
        low, high = pl.ds(g * TILE, TILE // 2), pl.ds(g * TILE + TILE // 2, TILE // 2)
        spread[g, 2].wait_recv()
        spread[g, 6] = link.send(everyone.at[2, low], everyone.at[6, low], dyd, z)
        spread[g, 3] = link.send(everyone.at[2, rows], everyone.at[3, rows], dk, z)
        spread[g, 4].wait_recv()
        spread[g, 7] = link.send(everyone.at[4, high], everyone.at[6, high], dx, z)
        spread[g, 5] = link.send(everyone.at[4, rows], everyone.at[5, rows], dk, z)

    def spread_diag(g):
        rows = pl.ds(g * TILE, TILE)
        spread[g, 6].wait_recv()
        spread[g, 7].wait_recv()
        spread[g, 8] = link.send(everyone.at[6, rows], everyone.at[7, rows], dk, z)

    plane_first(1, up_hbm)
    plane_first(2, down_hbm)
    for copy in first_loads:
        copy.wait()

    def back_strip(i, _):
        strip, frames = strip_of(i), pl.ds(i * FBLK, FBLK)
        for copy in swaps(i):
            copy.wait_recv()
        mods = mods_ref[frames]
        mid = ys[strip]
        feed = es[strip].astype(F32) + ep[strip].astype(F32)
        dy = dys[strip].astype(F32)
        ep[strip] = (mid + flat(mods[:, 5:6] * frames_of(feed))).astype(BF)
        normed, inverse_std = norm_rows(mid)
        grad = gs[strip].astype(F32) + gp[strip].astype(F32)
        dm[frames, 3] = jnp.sum(frames_of(grad), axis=1)
        dm[frames, 4] = jnp.sum(frames_of(grad * normed), axis=1)
        dm[frames, 5] = jnp.sum(frames_of(dy * feed), axis=1)
        scaled = flat(frames_of(grad) * (1.0 + mods[:, 4:5]))
        dy1 = dy + norm_back(scaled, normed, inverse_std)
        ys[strip] = dy1
        dm[frames, 2] = jnp.sum(frames_of(dy1 * brs[strip].astype(F32)), axis=1)
        gp[strip] = flat(mods[:, 2:3] * frames_of(dy1)).astype(BF)
        return 0

    lax.fori_loop(0, CLIP // BLK, back_strip, 0)

    def swap_done(i, _):
        for copy in swaps(i):
            copy.wait_send()
        return 0

    lax.fori_loop(0, CLIP // BLK, swap_done, 0)
    x_load = load(x_hbm, gs)
    h_load = load(h_hbm, es)
    output = Relay(out_sends, out_recvs, local_sems.at[EXIT_LOCAL - 1], ep, out_all, d, z)
    output.first()
    for copy in loads:
        copy.wait()

    def project(m, _):
        dos[m] = dot(wout[m], gp[...], NT).astype(BF)
        grad = dot(os_[m], gp[...], NN).astype(BF)
        for c in range(4):
            dattn[c, m, 96:128] = grad[c * 32 : (c + 1) * 32]
        return 0

    lax.fori_loop(0, 4, project, 0)

    def attend_group(m, _):
        for head in range(2):
            lanes = slice(head * HD, (head + 1) * HD)
            keys = qs[m, :, TILE + head * HD : TILE + (head + 1) * HD]
            values = qs[m, :, 2 * TILE + head * HD : 2 * TILE + (head + 1) * HD]
            dk_ref[...] = jnp.zeros_like(dk_ref)
            dv_ref[...] = jnp.zeros_like(dv_ref)

            def step(i, _, lanes=lanes, keys=keys, values=values, head=head):
                across = pl.ds(pl.multiple_of(i * QBLK, QBLK), QBLK)
                queries = qs[m, across, lanes]
                grad = dos[m, lanes, across]
                shift = bias_ref[:, across] - lse_ref[m, head : head + 1, across]
                scores = dot(keys, queries, NT).reshape(FRAMES, FRAME_TOK, QBLK)
                soft = jnp.exp2(scores * SCALE2 + shift[:, None, :]).reshape(CLIP, QBLK)
                delta = jnp.sum(
                    grad.astype(F32) * os_[m, lanes, across].astype(F32), axis=0, keepdims=True
                )
                grad_soft = dot(values, grad, NN)
                grad_scores = (soft * (grad_soft - delta)).astype(BF)
                dv_ref[...] += dot(soft.astype(BF), grad, NT)
                dk_ref[...] += dot(grad_scores, queries, NN)
                grad_query = dot(keys, grad_scores, TN) * HD ** (-0.5)
                qs[m, across, lanes] = grad_query.T.astype(BF)
                return 0

            lax.fori_loop(0, CLIP // QBLK, step, 0)
            qs[m, :, TILE + head * HD : TILE + (head + 1) * HD] = (dk_ref[...] * HD ** (-0.5)).astype(BF)
            qs[m, :, 2 * TILE + head * HD : 2 * TILE + (head + 1) * HD] = dv_ref[...].astype(BF)
        return 0

    lax.fori_loop(0, 2, attend_group, 0)
    for copy in feed_loads:
        copy.wait()
    plane_pass(1)
    output.hop(1)
    lax.fori_loop(2, 4, attend_group, 0)
    plane_pass(2)
    plane_final(1)

    def hidden_strip(i, _):
        strip = strip_of(i)
        total = dot(qs[0, strip], win[0:384], NN)
        for m in range(1, 4):
            total = total + dot(qs[m, strip], win[m * 384 : (m + 1) * 384], NN)
        brs[strip] = total.astype(BF)
        return 0

    lax.fori_loop(0, CLIP // BLK, hidden_strip, 0)
    hidden_swap = link.send(brs, dhp, dk, z)
    output.hop(2)
    h_load.wait()
    x_load.wait()

    def input_weights(m, _):
        grad = dot(qs[m], es[...], TN).astype(BF)
        for role in range(3):
            for c in range(4):
                first = role * TILE + c * 32
                dattn[c, m, role * 32 : (role + 1) * 32] = grad[first : first + 32]
        return 0

    lax.fori_loop(0, 4, input_weights, 0)
    plane_first(0, dattn)
    mod_loads = [load(wmod_hbm, qs)]
    plane_final(2)
    lines[1].turn()

    hidden_swap.wait_recv()

    def last_strip(i, _):
        strip, frames = strip_of(i), pl.ds(i * FBLK, FBLK)
        mods = mods_ref[frames]
        normed, inverse_std = norm_rows(gs[strip].astype(F32))
        grad = brs[strip].astype(F32) + dhp[strip].astype(F32)
        dm[frames, 0] = jnp.sum(frames_of(grad), axis=1)
        dm[frames, 1] = jnp.sum(frames_of(grad * normed), axis=1)
        scaled = flat(frames_of(grad) * (1.0 + mods[:, 1:2]))
        dys[strip] = (ys[strip] + norm_back(scaled, normed, inverse_std)).astype(BF)
        return 0

    lax.fori_loop(0, CLIP // BLK, last_strip, 0)
    for m in range(4):
        for c in range(6):
            dms[m, :, c * 256 : (c + 1) * 256] = dm[:, c, m * 256 : (m + 1) * 256].astype(BF)
    mod_column = {}
    clip = chip * 4 + z
    for s in (1, 3, 2):
        to = lax.rem(z + s, 4)
        mod_column[s] = link.send(dms.at[to], dmall.at[clip], d, to)
    dmall[clip] = dms[z]
    inner = Relay(in_sends, in_recvs, local_sems.at[EXIT_LOCAL - 2], dys, in_all, d, z)
    inner.first()

    for s in (1, 3, 2):
        mod_column[s].wait_recv()

    def clips_of(which):
        return dmall.at[pl.ds(which * 4, 4)]

    mod_x = link.send(clips_of(chip), clips_of(chip), dx, z)
    mod_y = link.send(clips_of(chip), clips_of(chip), dyd, z)
    plane_pass(0)
    lines[2].turn()
    lines[1].turn_again()
    mod_x.wait_recv()
    over_x = jnp.bitwise_xor(chip, 1)
    mod_xy = link.send(clips_of(over_x), clips_of(over_x), dyd, z)
    plane_final(0)
    inner.hop(1)
    lines[2].turn_again()
    column_final(1)

    mod_y.wait_recv()
    mod_xy.wait_recv()
    for copy in mod_loads:
        copy.wait()
    grads = dmall[...].reshape(256, 12 * TILE)

    level_grads = dot(hot_ref[...], grads, TN).astype(BF)
    rows = dot(level_grads[:, 0:384], qs[0], NT)
    for m in range(1, 4):
        rows = rows + dot(level_grads[:, m * 384 : (m + 1) * 384], qs[m], NT)
    trow[...] = rows.reshape(4, 32, D)
    table = {}
    for s in (1, 3, 2):
        to = lax.rem(z + s, 4)
        table[s] = link.send(trow.at[to], tbuf.at[s - 1], d, to)

    for part in range(6):
        win[part * 256 : (part + 1) * 256] = dot(
            grads[:, part * 256 : (part + 1) * 256], emb_ref[...], TN
        ).astype(BF)
    homes.append(load(win, dwm_out))
    column_final(2)
    spread_on(1)
    inner.hop(2)
    column_final(0)
    spread_on(2)
    spread_diag(1)
    spread_diag(2)
    spread_on(0)
    for s in (1, 3, 2):
        table[s].wait_recv()
    table_ref[...] = trow[z] + tbuf[0] + tbuf[1] + tbuf[2]
    spread_diag(0)
    output.hop(3)
    inner.hop(3)
    for g in range(3):
        for slot in (1, 3, 5, 8):
            spread[g, slot].wait_recv()
    for copy in homes:
        copy.wait()
    output.finish()
    inner.finish()
    lines[1].finish()
    lines[2].finish()
    link.drain()


def exit_call(*args):
    vmem = pl.BlockSpec(memory_space=pltpu.VMEM)
    hbm = pl.BlockSpec(memory_space=pl.ANY)
    chunks = (4, 4, TILE, D)
    heads = (4, TILE, D)
    return pl.pallas_call(
        exit_kernel,
        in_specs=[hbm] * 13 + [vmem] * 5,
        out_specs=[hbm] * 4 + [vmem],
        out_shape=[
            jax.ShapeDtypeStruct((2 * CLIP, D), BF),
            jax.ShapeDtypeStruct((2 * CLIP, D), BF),
            jax.ShapeDtypeStruct((8, 3 * TILE, D), BF),
            jax.ShapeDtypeStruct((12 * TILE, D), BF),
            jax.ShapeDtypeStruct((32, D), F32),
        ],
        scratch_shapes=[
            pltpu.VMEM((CLIP, D), F32),
            pltpu.VMEM((CLIP, D), BF),
            pltpu.VMEM((CLIP, D), BF),
            pltpu.VMEM((CLIP, D), BF),
            pltpu.VMEM((CLIP, D), BF),
            pltpu.VMEM((CLIP, D), BF),
            pltpu.VMEM((CLIP, D), BF),
            pltpu.VMEM((4, CLIP, 3 * TILE), BF),
            pltpu.VMEM(heads, BF),
            pltpu.VMEM(heads, BF),
            pltpu.VMEM((12 * TILE, D), BF),
            pltpu.VMEM(heads, BF),
            pltpu.VMEM((CLIP, D), BF),
            pltpu.VMEM(chunks, BF),
            pltpu.VMEM((3, 6, 2, TILE, D), BF),
            pltpu.VMEM((2, 8, TILE, D), BF),
            pltpu.VMEM((3, TILE, D), BF),
            pltpu.VMEM((2, 2, 3, TILE, D), BF),
            pltpu.VMEM((3, TILE, D), BF),
            pltpu.VMEM((FRAMES, 6, D), F32),
            pltpu.VMEM((4, FRAMES, 12 * TILE), BF),
            pltpu.VMEM((16, FRAMES, 12 * TILE), BF),
            pltpu.VMEM((4, 32, D), F32),
            pltpu.VMEM((3, 32, D), F32),
            pltpu.VMEM((CLIP, HD), F32),
            pltpu.VMEM((CLIP, HD), F32),
            pltpu.SemaphoreType.DMA((EXIT_COPIES,)),
            pltpu.SemaphoreType.DMA((EXIT_COPIES,)),
            pltpu.SemaphoreType.DMA((8,)),
            pltpu.SemaphoreType.DMA((8,)),
            pltpu.SemaphoreType.DMA((12,)),
            pltpu.SemaphoreType.DMA((12,)),
            pltpu.SemaphoreType.DMA((12,)),
            pltpu.SemaphoreType.DMA((12,)),
            pltpu.SemaphoreType.DMA((EXIT_LOCAL,)),
        ],
        compiler_params=pltpu.CompilerParams(
            vmem_limit_bytes=63 * 1024 * 1024, collective_id=1, has_side_effects=True
        ),
        cost_estimate=cost(1e11, 60e6),
        name="exit",
    )(*args)


def adam_step(grad, left, right, one, two, master, rate):
    low_left, low_right = left.astype(BF), right.astype(BF)
    turned = dot(low_left, grad.astype(BF), TN)
    rotated = dot(turned.astype(BF), low_right, NN)
    new_one = BETA_ONE * one + (1.0 - BETA_ONE) * rotated
    new_two = BETA_TWO * two + (1.0 - BETA_TWO) * rotated * rotated
    direction = new_one / (jnp.sqrt(new_two) + EPS_ADAM)
    back = dot(low_left, direction.astype(BF), NN)
    back = dot(back.astype(BF), low_right, NT)
    return master - rate * (back + DECAY * master), new_one, new_two


def adam_kernel(tab_ref, rate_ref, *refs, picked, batch):
    if picked:
        red_ref, mod_ref, wide_ref = refs[:3]
        refs[-1][...] = wide_ref[...].astype(F32)
        refs = refs[3:-1]
    else:
        grad_ref = refs[0]
        refs = refs[1:]
    master_ref, one_ref, two_ref, left_ref, right_ref, nm_ref, n1_ref, n2_ref, nw_ref = refs
    for slot in range(batch):
        tile = pl.program_id(0) * batch + slot
        if picked:
            col = pl.multiple_of(tab_ref[tile, 8] * TILE, TILE)
            pieces = [
                red_ref[
                    tab_ref[tile, i],
                    pl.ds(pl.multiple_of(tab_ref[tile, 4 + i] * 32, 32), 32),
                    pl.ds(col, TILE),
                ]
                for i in range(4)
            ]
            grad = jnp.concatenate(pieces, axis=0).astype(F32)
            mod_row = pl.multiple_of(tab_ref[tile, 9] * TILE, TILE)
            mod_col = pl.multiple_of(tab_ref[tile, 10] * TILE, TILE)
            mod_grad = mod_ref[pl.ds(mod_col, TILE), pl.ds(mod_row, TILE)].astype(F32)
            kind = tab_ref[tile, 11]
            grad = jnp.where(kind == 0, grad, jnp.where(kind == 2, mod_grad, grad).T)
        else:
            grad = grad_ref[slot].astype(F32)
        master, one, two = adam_step(
            grad, left_ref[slot], right_ref[slot], one_ref[slot], two_ref[slot], master_ref[slot], rate_ref[tile]
        )
        nm_ref[slot] = master
        n1_ref[slot] = one
        n2_ref[slot] = two
        nw_ref[slot] = master.astype(BF)


def pick_table(tiles, device):
    table = []
    piece = jnp.arange(4, dtype=jnp.int32)[None, :]
    t = tiles[:, None]
    is_in = t < 48
    is_out = (t >= 48) & (t < 64)
    is_up = (t >= 64) & (t < 128)
    is_down = (t >= 128) & (t < 192)
    is_mod = t >= 192
    q0, q1, q2, q3, q4 = t, t - 48, t - 64, t - 128, t - 192
    core = jnp.where(is_in, (q0 % 6) % 2, jnp.where(is_out, q1 // 8, jnp.where(is_up, (q2 % 8) // 4, (q3 // 8) // 4)))
    chip = jnp.where(is_up, q2 % 4, (q3 // 8) % 4)
    chip = jnp.where(is_in | is_out, piece, chip)
    source = jnp.where(is_mod, 0, jnp.bitwise_xor(2 * chip + core, device))
    row = jnp.where(is_in, (q0 % 6) // 2, jnp.where(is_out, 3, jnp.where(is_up, 4 + piece, 8 + piece)))
    row = jnp.where(is_mod, 0, row + jnp.zeros_like(piece))
    col = jnp.where(is_in, q0 // 6, jnp.where(is_out, q1 % 8, jnp.where(is_up, q2 // 8, q3 % 8)))
    col = jnp.where(is_mod, 0, col)
    mod_row = jnp.where(is_mod, q4 // 12, 0)
    mod_col = jnp.where(is_mod, q4 % 12, 0)
    kind = jnp.where(is_mod, 2, jnp.where(is_in | is_up, 1, 0))
    return jnp.concatenate([source, row, col, mod_row, mod_col, kind], axis=1).astype(jnp.int32)


def adam(table, rates, sources, master, one, two, left, right):
    slots = master.shape[0]
    batch = max(b for b in (4, 3, 2, 1) if slots % b == 0)
    picked = len(sources) == 3
    tiles = pl.BlockSpec((batch, TILE, TILE), lambda i, *_: (i, 0, 0))
    extra = []
    if picked:
        height = 2 * TILE
        blocks = sources[2].shape[0] // height
        assert blocks <= slots // batch
        wide = pl.BlockSpec((height, D), lambda i, *_: (jnp.minimum(i, blocks - 1), 0))
        extra = [wide]
        source_specs = [
            pl.BlockSpec(sources[0].shape, lambda i, *_: (0, 0, 0)),
            pl.BlockSpec(sources[1].shape, lambda i, *_: (0, 0)),
            wide,
        ]
    else:
        source_specs = [tiles]
    return pl.pallas_call(
        functools.partial(adam_kernel, picked=picked, batch=batch),
        grid_spec=pltpu.PrefetchScalarGridSpec(
            num_scalar_prefetch=2,
            grid=(slots // batch,),
            in_specs=source_specs + [tiles] * 5,
            out_specs=[tiles] * 4 + extra,
        ),
        out_shape=[jax.ShapeDtypeStruct(master.shape, F32)] * 3
        + [jax.ShapeDtypeStruct(master.shape, BF)]
        + [jax.ShapeDtypeStruct(s.shape, F32) for s in sources[2:]],
        compiler_params=params(),
        cost_estimate=cost(slots * 8 * TILE**3, slots * TILE * TILE * 36),
        name="adam",
    )(table, rates, *sources, master, one, two, left, right)


def body(
    activations,
    cotangent,
    level_table,
    true_frames,
    group_pattern,
    noise_levels,
    context_flags,
    owner_list,
    masters,
    moment_one,
    moment_two,
    basis_left,
    basis_right,
):
    groups = lax.axis_size("mp")
    owners = lax.axis_size("dp")
    chips = owners // 2
    bits = chips.bit_length() - 1
    z = lax.axis_index("mp")
    device = lax.axis_index("dp")
    core = device % 2
    chip = device // 2
    local_clips = true_frames.shape[0]
    column_clips = 2 * local_clips
    assert column_clips == groups and chips == 1 << bits
    shapes, counts = tile_layout(groups)
    slots = masters.shape[1]
    fast = chips == 4 and groups == 4

    def swap(v, step):
        return lax.ppermute(v, "dp", [(i, i ^ step) for i in range(owners)])

    def across(v):
        return swap(v, 1)

    def plane(v, bit):
        return swap(v, 2 << bit)

    def z_get(v, s):
        return lax.ppermute(v, "mp", [((i + s) % groups, i) for i in range(groups)])

    def z_put(v, s):
        return lax.ppermute(v, "mp", [(i, (i + s) % groups) for i in range(groups)])

    def plane_double(v):
        held = v[None]
        for bit in range(bits):
            held = jnp.concatenate([held, plane(held, bit)], axis=0)
        return held

    def plane_gather(v):
        if chips != 4:
            return plane_double(v)
        half = v.shape[0] // 2
        by_x, by_y = plane(v, 0), plane(v, 1)
        low, high = plane(by_x[:half], 1), plane(by_y[half:], 0)
        return jnp.stack([v, by_x, by_y, jnp.concatenate([low, high], axis=0)])

    def add(a, b):
        return (a.astype(F32) + b.astype(F32)).astype(BF)

    def plane_reduce(v):
        if chips != 4:
            held = v
            for bit in reversed(range(bits)):
                half = 1 << bit
                held = add(held[:half], plane(held[half:], bit))
            return held[0]
        half = v.shape[1] // 2
        got_low = [plane(v[1, :half], 0), plane(v[3, :half], 0)]
        got_high = [plane(v[2, half:], 1), plane(v[3, half:], 1)]
        pass_low = plane(add(v[2, :half], got_low[1]), 1)
        pass_high = plane(add(v[1, half:], got_high[1]), 0)
        low = v[0, :half].astype(F32) + got_low[0].astype(F32) + pass_low.astype(F32)
        high = v[0, half:].astype(F32) + got_high[0].astype(F32) + pass_high.astype(F32)
        return jnp.concatenate([low, high], axis=0).astype(BF)

    def z_gather(v):
        return jnp.stack([v] + [z_get(v, s) for s in range(1, groups)])

    def z_reduce(v):
        total = v[0].astype(F32)
        for s in range(1, groups):
            total = total + z_put(v[s], s).astype(F32)
        return total

    frame_index = jnp.arange(FRAMES, dtype=jnp.int32)

    def mask_rows(flagged, lengths):
        valid = frame_index[None, :] < lengths[:, None]
        in_context = flagged & valid
        visible = valid[:, :, None] & (
            jnp.logical_not(in_context)[:, None, :] | in_context[:, :, None]
        )
        return jnp.repeat(jnp.where(visible, 0.0, -1e30).astype(F32), FRAME_TOK, axis=2)

    def level_rows(flagged, patterns):
        pattern_hot = (patterns[:, None] == jnp.arange(PATTERNS, dtype=jnp.int32)[None, :]).astype(
            jnp.int32
        )
        return jnp.where(
            flagged, 0, jnp.sum(pattern_hot[:, :, None] * noise_levels[None, :, :], axis=1)
        )

    rows = TILE // chips
    level_ids = jnp.arange(LEVELS, dtype=jnp.int32)[None, :]
    if fast:
        with jax.named_scope("front"):
            flagged = context_flags == 1
            (
                _, w_mod, x, dy, h1, w_pack, qkv, o_rows, branch, y1, e_part, dh2_part, d_up, d_down,
                mods, bias, lse, all_embedded, own_hot,
            ) = front(
                masters[0],
                level_table,
                level_rows(flagged, group_pattern),
                mask_rows(flagged, true_frames),
                activations,
                cotangent,
                owner_list,
            )
        with jax.named_scope("exit"):
            block_output, input_grad, everyone, d_w_mod, table_grad = exit_call(
                y1, dh2_part, e_part, dy, branch, x, h1, qkv, o_rows, w_pack, w_mod,
                d_up, d_down, mods, bias, lse, all_embedded, own_hot,
            )
    else:
        with jax.named_scope("entry"):
            holds = (z // local_clips) == core
            local = (z % local_clips) * CLIP
            pair = jnp.stack(
                [
                    lax.dynamic_slice_in_dim(activations, local, CLIP, axis=0),
                    lax.dynamic_slice_in_dim(cotangent, local, CLIP, axis=0),
                ]
            )
            pair = jnp.where(holds, pair, across(pair))
            x, dy = pair[0], pair[1]
            facts = jnp.concatenate(
                [context_flags, true_frames[:, None], group_pattern[:, None]], axis=1
            ).astype(jnp.int32)
            other = across(facts)
            facts = jnp.where(
                core == 0, jnp.concatenate([facts, other]), jnp.concatenate([other, facts])
            )
            flagged = facts[:, :FRAMES] == 1
            levels = level_rows(flagged, facts[:, FRAMES + 1])
            bias = lax.dynamic_index_in_dim(
                mask_rows(flagged, facts[:, FRAMES]), z, axis=0, keepdims=False
            )
            all_levels = plane_double(levels)

        with jax.named_scope("owner_gather"):
            gathered = lax.all_gather(masters[0].astype(BF), "dp", axis=0, tiled=True)
            table = lax.all_gather(level_table, "dp", axis=0, tiled=True)
            position = jnp.arange(owner_list.shape[0], dtype=jnp.int32)
            inverse = jnp.sum(
                jnp.where(owner_list[None, :] == position[:, None], position[None, :], 0), axis=1
            ).astype(jnp.int32)
            chunk_attn, chunk_up, chunk_down, w_mod = pick_chunk_plain(
                gathered, inverse, chip, core, chips, shapes, counts
            )

        with jax.named_scope("weights"):
            got = plane_gather(z_gather(chunk_attn)).reshape(chips, groups, 4, rows, D)
            w_up = plane_gather(z_gather(chunk_up)).reshape(-1, D)
            w_down = plane_gather(z_gather(chunk_down)).reshape(-1, D)

        with jax.named_scope("modulation"):
            hot = (levels.reshape(-1)[:, None] == level_ids).astype(BF)
            embedded = dot(hot, table, NN).astype(BF)
            mod_part = dot(embedded, w_mod, NN).reshape(column_clips, FRAMES, -1)
            pieces = [lax.dynamic_index_in_dim(mod_part, z, axis=0, keepdims=False)]
            for s in range(1, groups):
                piece = lax.dynamic_index_in_dim(
                    mod_part, (z + groups - s) % groups, axis=0, keepdims=False
                )
                pieces.append(z_get(piece, s))
            mods = lax.dynamic_slice_in_dim(
                jnp.stack(pieces + pieces), (groups - z) % groups, groups, axis=0
            )
            mods = (
                mods.reshape(groups, FRAMES, 6, D // groups).transpose(1, 2, 0, 3).reshape(FRAMES, 6, D)
            )
            (h1,) = row_call(first_norm_kernel, "first_norm", [x], mods, [BF], [], 4 * CLIP * D)

        w_in = got[:, :, :3].transpose(1, 2, 0, 3, 4).reshape(-1, D)
        w_out = got[:, :, 3].transpose(1, 0, 2, 3).reshape(-1, D)

        mb = CLIP * D
        with jax.named_scope("attention"):
            qkv = dot(h1, w_in, NT).astype(BF)
            o_rows, lse = attend(qkv, bias)
            part = dot(o_rows, w_out, TN).astype(BF)
            y1, branch, h2, de = row_call(
                middle_kernel, "middle", [x, part, across(part), dy], mods, [F32, BF, BF, BF], [], 18 * mb
            )

        with jax.named_scope("feed"):
            e_part, dh2_part, d_up, d_down = feed_both(h2, de, w_up, w_down)

        with jax.named_scope("feed_back"):
            out, dy1, da, dm_mid = row_call(
                back_kernel,
                "back",
                [y1, dh2_part, across(dh2_part), dy, branch, e_part, across(e_part)],
                mods,
                [BF, F32, BF],
                [4],
                24 * mb,
            )
            shape = (chips, groups, -1, D)
            red_up = z_reduce(plane_reduce(d_up.reshape(shape))).astype(BF)
            red_down = z_reduce(plane_reduce(d_down.reshape(shape))).astype(BF)

        def to_column(rows_here):
            half = CLIP // 2
            mine = lax.dynamic_slice_in_dim(rows_here, core * half, half, axis=0)
            by_clip = [mine] + [z_get(mine, s) for s in range(1, groups)]
            by_clip = lax.dynamic_slice_in_dim(jnp.stack(by_clip + by_clip), (groups - z) % groups, groups, axis=0)
            keep = lax.dynamic_slice_in_dim(by_clip, core * local_clips, local_clips, axis=0)
            send = lax.dynamic_slice_in_dim(by_clip, (1 - core) * local_clips, local_clips, axis=0)
            got_half = across(send)
            both = jnp.where(
                core == 0, jnp.stack([keep, got_half], axis=1), jnp.stack([got_half, keep], axis=1)
            )
            return both.reshape(local_clips * CLIP, D)

        with jax.named_scope("block_output"):
            block_output = to_column(out)

        with jax.named_scope("attention_back"):
            do_rows = dot(w_out, da, NT).astype(BF)
            d_out = dot(o_rows, da, NN).astype(BF)
            d_qkv = attend_back(qkv, o_rows, do_rows, lse, bias)
            dh1_part = dot(d_qkv, w_in, NN).astype(BF)
            d_in = dot(d_qkv, h1, TN).astype(BF)
            in_grad, dm_last = row_call(
                last_kernel, "last", [x, dh1_part, across(dh1_part), dy1], mods, [BF], [2], 12 * mb
            )
            d_in = d_in.reshape(groups, 3, chips, rows, D).transpose(2, 0, 1, 3, 4)
            d_out = d_out.reshape(groups, 1, chips, rows, D).transpose(2, 0, 1, 3, 4)
            d_attn = jnp.concatenate([d_in, d_out], axis=2).reshape(chips, groups, 4 * rows, D)
            red_attn = z_reduce(plane_reduce(d_attn)).astype(BF)

        with jax.named_scope("input_grad"):
            input_grad = to_column(in_grad).astype(F32)

        with jax.named_scope("modulation_back"):
            d_mod = jnp.stack(
                [dm_last[:, 0], dm_last[:, 1], dm_mid[:, 2], dm_mid[:, 0], dm_mid[:, 1], dm_mid[:, 3]], axis=1
            ).astype(BF)
            d_mod = (
                d_mod.reshape(FRAMES, 6, groups, D // groups).transpose(2, 0, 1, 3).reshape(groups, FRAMES, -1)
            )
            pieces = [lax.dynamic_index_in_dim(d_mod, z, axis=0, keepdims=False)]
            for s in range(1, groups):
                pieces.append(z_put(lax.dynamic_index_in_dim(d_mod, (z + s) % groups, axis=0, keepdims=False), s))
            d_mod = jnp.stack(pieces)
            d_mod = plane_double(d_mod).reshape(chips * groups * FRAMES, -1)
            back_clip = (z + groups - jnp.arange(groups, dtype=jnp.int32)) % groups
            clip_hot = (back_clip[:, None] == jnp.arange(groups, dtype=jnp.int32)[None, :]).astype(
                jnp.int32
            )
            order = jnp.sum(clip_hot[None, :, :, None] * all_levels[:, None, :, :], axis=2).reshape(-1)
            all_embedded = dot((order[:, None] == level_ids).astype(BF), table, NN).astype(BF)
            own_levels = level_table.shape[0]
            own_ids = device * own_levels + jnp.arange(own_levels, dtype=jnp.int32)[None, :]
            own_hot = (order[:, None] == own_ids).astype(BF)
            d_w_mod = dot(all_embedded, d_mod, TN).astype(BF)
            own_levels = level_table.shape[0]
            own_rows = dot(dot(own_hot, d_mod, TN).astype(BF), w_mod, NT)
            own_rows = own_rows.reshape(groups, own_levels // groups, D)
            table_grad = lax.dynamic_index_in_dim(own_rows, z, axis=0, keepdims=False)
            for s in range(1, groups):
                table_grad = table_grad + z_put(
                    lax.dynamic_index_in_dim(own_rows, (z + s) % groups, axis=0, keepdims=False), s
                )

    with jax.named_scope("owners"):
        if not fast:
            reduced = jnp.concatenate([red_attn, red_up, red_down], axis=0)
            if chips == 4:
                height = reduced.shape[0]
                plane_parts = plane_gather(reduced.reshape(2, height // 2, D)).reshape(chips, height, D)
            else:
                plane_parts = plane_double(reduced)
            everyone = jnp.stack([plane_parts, across(plane_parts)], axis=1).reshape(owners, -1, D)
        tile_ids = lax.dynamic_slice_in_dim(owner_list, device * slots, slots)
        rates = kind_rates(tile_ids, counts)
        if fast:
            picks = pick_table(tile_ids, device)
            sources = [everyone, d_w_mod, input_grad]
        else:
            picks = jnp.zeros((slots, 12), jnp.int32)
            absolute = jnp.take(
                everyone, jnp.bitwise_xor(jnp.arange(owners, dtype=jnp.int32), device), axis=0
            ).reshape(chips, 2, -1, D)
            attn = absolute[:, :, : 4 * rows].reshape(chips, 2, 4, rows, D)
            attn = attn.transpose(2, 1, 0, 3, 4).reshape(4, -1, D)
            ffn_rows = (absolute.shape[2] - 4 * rows) // 2
            up = absolute[:, :, 4 * rows : 4 * rows + ffn_rows].transpose(1, 0, 2, 3).reshape(-1, D)
            down = absolute[:, :, 4 * rows + ffn_rows :].transpose(1, 0, 2, 3).reshape(-1, D)
            g_in = jnp.concatenate([attn[0].T, attn[1].T, attn[2].T], axis=1)
            packed = pack([g_in, attn[3], up.T, down, d_w_mod])
            sources = [jnp.take(packed, tile_ids, axis=0)]
        new_masters, new_one, new_two, new_weights, *wide = adam(
            picks, rates, sources, masters[0], moment_one[0], moment_two[0], basis_left[0], basis_right[0]
        )
    return (
        block_output,
        wide[0] if fast else input_grad,
        table_grad,
        new_masters[None],
        new_one[None],
        new_two[None],
        new_weights[None],
    )


def solution(mesh):
    tiles = P("mp", "dp", None, None)
    in_specs = (
        P("dp", None),
        P("dp", None),
        P("dp", None),
        P("dp"),
        P("dp"),
        P(),
        P("dp", None),
        P(),
        tiles,
        tiles,
        tiles,
        tiles,
        tiles,
    )
    out_specs = (P("dp", None), P("dp", None), P(("dp", "mp"), None), tiles, tiles, tiles, tiles)
    return jax.shard_map(body, mesh=mesh, in_specs=in_specs, out_specs=out_specs, check_vma=False)
```

```python
import functools

import jax
import jax.numpy as jnp
from jax import lax
from jax.experimental import pallas as pl
from jax.experimental.pallas import tpu as pltpu
from jax.sharding import PartitionSpec as P

D = 1024
H = 16
HD = 64
FF = 4096
FRAMES = 16
FRAME_TOK = 64
LEVELS = 1024
PATTERNS = 4
TILE = 128
CLIP = FRAMES * FRAME_TOK

EPS_NORM = 1e-06
BETA_ONE = 0.5
BETA_TWO = 0.75
EPS_ADAM = 1e-08
DECAY = 0.01
LOG2E = 1.4426950408889634
GELU_A = 0.7978845608028654
GELU_B = 0.044715

BF = jnp.bfloat16
F32 = jnp.float32
VMEM_BYTES = 60 * 1024 * 1024


def params(**kw):
    return pltpu.CompilerParams(vmem_limit_bytes=VMEM_BYTES, **kw)


def cost(flops, nbytes, trans=0):
    return pl.CostEstimate(flops=int(flops), bytes_accessed=int(nbytes), transcendentals=int(trans))


def dot(left, right, dims):
    return lax.dot_general(left, right, (dims, ((), ())), preferred_element_type=F32)


NN = ((1,), (0,))
NT = ((1,), (1,))
TN = ((0,), (0,))


def tile_layout(groups):
    local_width = H // groups * HD
    shapes = [
        (D, 3 * local_width),
        (local_width, D),
        (D, FF // groups),
        (FF // groups, D),
        (D, 6 * D // groups),
    ]
    counts = [height // TILE * (breadth // TILE) for height, breadth in shapes]
    return (shapes, counts)


def kind_rates(tile_ids, counts):
    scales = [
        0.35 * D ** (-0.5),
        1.5 * (H * HD) ** (-0.5),
        0.5 * D ** (-0.5),
        0.5 * FF ** (-0.5),
        0.5 * D ** (-0.5),
    ]
    tile_rates = jnp.full(tile_ids.shape, scales[0], F32)
    boundary = 0
    for category in range(1, 5):
        boundary = boundary + counts[category - 1]
        tile_rates = jnp.where(tile_ids >= boundary, jnp.float32(scales[category]), tile_rates)
    return tile_rates


def unpack(tile_stack, shapes, counts):
    matrices = []
    offset = 0
    for (height, breadth), amount in zip(shapes, counts):
        stacked = tile_stack[offset : offset + amount].reshape(
            height // TILE, breadth // TILE, TILE, TILE
        )
        matrices.append(stacked.transpose(0, 2, 1, 3).reshape(height, breadth))
        offset = offset + amount
    return matrices


def pack(matrices):
    stacked = []
    for matrix in matrices:
        height, breadth = matrix.shape
        stacked.append(
            matrix.reshape(height // TILE, TILE, breadth // TILE, TILE)
            .transpose(0, 2, 1, 3)
            .reshape(-1, TILE, TILE)
        )
    return jnp.concatenate(stacked, axis=0)


def pick_chunk_plain(gathered, inverse, chip, core, chips, shapes, counts):
    w_qkv, w_out, w_up, w_down, w_mod = unpack(jnp.take(gathered, inverse, axis=0), shapes, counts)
    width = w_out.shape[0]
    half = width // 2
    ffn = w_up.shape[1] // 2
    rows, ffn_rows = half // chips, ffn // chips
    parts = []
    for role in range(3):
        parts.append(w_qkv[:, role * width : (role + 1) * width].T)
    parts.append(w_out)
    start = core * half + chip * rows
    attn = jnp.concatenate([lax.dynamic_slice_in_dim(p, start, rows, axis=0) for p in parts], axis=0)
    ffn_start = core * ffn + chip * ffn_rows
    up = lax.dynamic_slice_in_dim(w_up.T, ffn_start, ffn_rows, axis=0)
    down = lax.dynamic_slice_in_dim(w_down, ffn_start, ffn_rows, axis=0)
    return attn, up, down, w_mod


def norm_rows(values):
    centered = values - jnp.mean(values, axis=-1, keepdims=True)
    inverse_std = lax.rsqrt(jnp.mean(centered * centered, axis=-1, keepdims=True) + EPS_NORM)
    return centered * inverse_std, inverse_std


def norm_back(grad_normed, normed, inverse_std):
    centered = grad_normed - jnp.mean(grad_normed, axis=-1, keepdims=True)
    return inverse_std * (centered - normed * jnp.mean(grad_normed * normed, axis=-1, keepdims=True))


def frames_of(rows):
    return rows.reshape(-1, FRAME_TOK, D)


def flat(framed):
    return framed.reshape(-1, D)


BLK = 256
FBLK = BLK // FRAME_TOK


def row_spec():
    return pl.BlockSpec((BLK, D), lambda i: (i, 0))


def mod_spec(parts):
    return pl.BlockSpec((FBLK, parts, D), lambda i: (i, 0, 0))


def row_call(kernel, name, row_ins, mods, row_outs, mod_outs, nbytes):
    outs = [jax.ShapeDtypeStruct((CLIP, D), t) for t in row_outs]
    outs += [jax.ShapeDtypeStruct((FRAMES, n, D), F32) for n in mod_outs]
    return pl.pallas_call(
        kernel,
        grid=(CLIP // BLK,),
        in_specs=[row_spec() for _ in row_ins] + [mod_spec(6)],
        out_specs=[row_spec() for _ in row_outs] + [mod_spec(n) for n in mod_outs],
        out_shape=outs,
        compiler_params=params(),
        cost_estimate=cost(30 * CLIP * D, nbytes),
        name=name,
    )(*row_ins, mods)


def first_norm_kernel(x_ref, mod_ref, h_ref):
    normed, _ = norm_rows(x_ref[...].astype(F32))
    mods = mod_ref[...]
    h_ref[...] = flat(
        frames_of(normed) * (1.0 + mods[:, 1:2]) + mods[:, 0:1]
    ).astype(BF)


def middle_kernel(x_ref, a_ref, b_ref, dy_ref, mod_ref, y_ref, s_ref, h_ref, de_ref):
    mods = mod_ref[...]
    branch = (a_ref[...].astype(F32) + b_ref[...].astype(F32)).astype(BF)
    s_ref[...] = branch
    mid = frames_of(x_ref[...].astype(F32)) + mods[:, 2:3] * frames_of(branch.astype(F32))
    y_ref[...] = flat(mid)
    normed, _ = norm_rows(flat(mid))
    h_ref[...] = flat(
        frames_of(normed) * (1.0 + mods[:, 4:5]) + mods[:, 3:4]
    ).astype(BF)
    de_ref[...] = flat(mods[:, 5:6] * frames_of(dy_ref[...].astype(F32))).astype(BF)


def back_kernel(y_ref, g_ref, gp_ref, dy_ref, s_ref, e_ref, ep_ref, mod_ref, out_ref, dy1_ref, da_ref, dm_ref):
    mods = mod_ref[...]
    mid = y_ref[...]
    feed = e_ref[...].astype(F32) + ep_ref[...].astype(F32)
    dy = dy_ref[...].astype(F32)
    out_ref[...] = (mid + flat(mods[:, 5:6] * frames_of(feed))).astype(BF)
    normed, inverse_std = norm_rows(mid)
    grad = g_ref[...].astype(F32) + gp_ref[...].astype(F32)
    dm_ref[:, 0] = jnp.sum(frames_of(grad), axis=1)
    dm_ref[:, 1] = jnp.sum(frames_of(grad * normed), axis=1)
    scaled = flat(frames_of(grad) * (1.0 + mods[:, 4:5]))
    dy1 = dy + norm_back(scaled, normed, inverse_std)
    dy1_ref[...] = dy1
    dm_ref[:, 2] = jnp.sum(frames_of(dy1 * s_ref[...].astype(F32)), axis=1)
    dm_ref[:, 3] = jnp.sum(frames_of(dy * feed), axis=1)
    da_ref[...] = flat(mods[:, 2:3] * frames_of(dy1)).astype(BF)


def last_kernel(x_ref, g_ref, gp_ref, dy1_ref, mod_ref, out_ref, dm_ref):
    mods = mod_ref[...]
    normed, inverse_std = norm_rows(x_ref[...].astype(F32))
    grad = g_ref[...].astype(F32) + gp_ref[...].astype(F32)
    dm_ref[:, 0] = jnp.sum(frames_of(grad), axis=1)
    dm_ref[:, 1] = jnp.sum(frames_of(grad * normed), axis=1)
    scaled = flat(frames_of(grad) * (1.0 + mods[:, 1:2]))
    out_ref[...] = (dy1_ref[...] + norm_back(scaled, normed, inverse_std)).astype(BF)


MESH = pl.DeviceIdType.MESH
HEAD_TILES = 36
TABLE_TILES = 8
PAYLOAD = 46
LEVEL_TILE = HEAD_TILES + TABLE_TILES


class Link:
    def __init__(self, sends, recvs):
        self.sends, self.recvs, self.used, self.pending = sends, recvs, 0, []

    def make(self, src, dst, dp, mp):
        copy = pltpu.make_async_remote_copy(
            src_ref=src,
            dst_ref=dst,
            send_sem=self.sends.at[self.used],
            recv_sem=self.recvs.at[self.used],
            device_id=(dp, mp),
            device_id_type=MESH,
        )
        self.used += 1
        self.pending.append(copy)
        return copy

    def send(self, src, dst, dp, mp):
        copy = self.make(src, dst, dp, mp)
        copy.start()
        return copy

    def drain(self):
        for copy in self.pending:
            copy.wait_send()
        self.pending = []


def greet(d, z):
    barrier = pltpu.get_barrier_semaphore()
    for step in (1, 2, 4):
        pl.semaphore_signal(barrier, inc=1, device_id=(jnp.bitwise_xor(d, step), z), device_id_type=MESH)
    for s in (1, 2, 3):
        pl.semaphore_signal(barrier, inc=1, device_id=(d, lax.rem(z + s, 4)), device_id_type=MESH)
    pl.semaphore_wait(barrier, 6)


QBLK = 256
ROWS = 512
SCALE2 = HD ** (-0.5) * LOG2E


ENTRY_COPIES = 8 + 45 + 3


def front_kernel(
    idx_ref,
    pay_ref,
    act_ref,
    cot_ref,
    bias_ref,
    w_ref,
    wmod_out,
    x_out,
    dy_out,
    h_out,
    wpack_out,
    qkv_out,
    o_out,
    branch_out,
    y_out,
    e_out,
    dh_out,
    dup_out,
    ddown_out,
    mods_ref,
    bias_out,
    lse_ref,
    emb_ref,
    own_hot_ref,
    gath,
    own,
    turn,
    xs,
    dys,
    bs,
    part,
    modbuf,
    hots,
    hs,
    wpack,
    qs,
    os_,
    mine,
    peer,
    e_acc,
    dh_acc,
    wfeed,
    up_stage,
    down_stage,
    up_acc,
    down_acc,
    sends,
    recvs,
    swap_sends,
    swap_recvs,
    strip_sends,
    strip_recvs,
    local_sems,
    pack_sems,
    stage_sems,
):
    d, z = lax.axis_index("dp"), lax.axis_index("mp")
    core, chip = lax.rem(d, 2), d // 2
    dk, dx, dyd = jnp.bitwise_xor(d, 1), jnp.bitwise_xor(d, 2), jnp.bitwise_xor(d, 4)
    dxy = jnp.bitwise_xor(d, 6)
    link = Link(sends, recvs)
    greet(d, z)

    def slot(owner, first=0, count=PAYLOAD):
        return gath.at[pl.ds(owner * PAYLOAD + first, count)]

    half = PAYLOAD // 2
    home = pltpu.make_async_copy(pay_ref, slot(d), local_sems.at[0])
    home.start()
    to_x = link.send(pay_ref, slot(d), dx, z)
    to_y = link.send(pay_ref, slot(d), dyd, z)
    to_k = link.send(pay_ref, slot(d), dk, z)

    holds = (z // 2) == core
    rows = pl.ds(lax.rem(z, 2) * CLIP, CLIP)
    picks = [
        (act_ref.at[rows], xs),
        (cot_ref.at[rows], dys),
        (bias_ref.at[lax.rem(z, 2)], bs),
    ]

    def swaps():
        return [
            pltpu.make_async_remote_copy(
                src_ref=src,
                dst_ref=dst,
                send_sem=swap_sends.at[i],
                recv_sem=swap_recvs.at[i],
                device_id=(dk, z),
                device_id_type=MESH,
            )
            for i, (src, dst) in enumerate(picks)
        ]

    def keeps():
        return [pltpu.make_async_copy(src, dst, local_sems.at[1 + i]) for i, (src, dst) in enumerate(picks)]

    @pl.when(holds)
    def _():
        for copy in swaps() + keeps():
            copy.start()

    to_x.wait_recv()
    x_to_y = link.send(slot(dx, 0, half), slot(dx, 0, half), dyd, z)
    x_to_k = link.send(slot(dx), slot(dx), dk, z)
    to_y.wait_recv()
    y_to_x = link.send(slot(dyd, half, half), slot(dyd, half, half), dx, z)
    y_to_k = link.send(slot(dyd), slot(dyd), dk, z)

    @pl.when(holds)
    def _():
        for copy in swaps():
            copy.wait_send()
        for copy in keeps():
            copy.wait()

    @pl.when(jnp.logical_not(holds))
    def _():
        for copy in swaps():
            copy.wait_recv()

    bias_out[...] = bs[...]
    locals_used = [7]

    def save(src, dst):
        copy = pltpu.make_async_copy(src, dst, local_sems.at[locals_used[0]])
        locals_used[0] += 1
        copy.start()
        return copy

    x_saved = save(xs, x_out)
    dy_saved = save(dys, dy_out)

    x_to_y.wait_recv()
    y_to_x.wait_recv()
    xy_to_k = link.send(slot(dxy), slot(dxy), dk, z)
    home.wait()
    to_k.wait_recv()
    x_to_k.wait_recv()
    y_to_k.wait_recv()
    xy_to_k.wait_recv()

    def tile(number):
        return gath[idx_ref[number]]

    def pick_attn(j, _):
        lanes = pl.ds(pl.multiple_of(j * TILE, TILE), TILE)
        for role in range(3):
            turn[role] = tile(j * 6 + 2 * role + core).T
        turn[3] = tile(48 + core * 8 + j)
        for role in range(4):
            own[0, role * 32 : (role + 1) * 32, lanes] = turn[role, pl.ds(pl.multiple_of(chip * 32, 32), 32), :]
        return 0

    def pick_feed(j, _):
        lanes = pl.ds(pl.multiple_of(j * TILE, TILE), TILE)
        own[1, :, lanes] = tile(64 + j * 8 + 4 * core + chip).T
        own[2, :, lanes] = tile(128 + (4 * core + chip) * 8 + j)
        return 0

    def pick_mod(j, _):
        strip = pl.ds(pl.multiple_of(j * TILE, TILE), TILE)
        for col in range(12):
            qs[col // 3, strip, (col % 3) * TILE : (col % 3 + 1) * TILE] = tile(192 + j * 12 + col)
        return 0

    along, by_x, by_y, diag = {}, {}, {}, {}
    all_groups = [(g, s) for g in range(3) for s in (0, 1, 3, 2)]

    def landing(g, p, m):
        return w_ref.at[p, m] if g == 0 else wfeed.at[g - 1, p, m]

    for g, s in all_groups:
        m = lax.rem(z + 4 - s, 4)
        if s:
            along[g, s] = link.make(own.at[g], landing(g, 0, z), d, lax.rem(z + s, 4))
        src = own.at[g] if s == 0 else landing(g, 0, m)
        by_x[g, s] = link.make(src, landing(g, 1, m), dx, z)
        by_y[g, s] = link.make(src, landing(g, 2, m), dyd, z)
        if s < 2:
            diag[g, s] = link.make(landing(g, 1, m), landing(g, 3, m), dyd, z)
        else:
            diag[g, s] = link.make(landing(g, 2, m), landing(g, 3, m), dx, z)
    homes = [pltpu.make_async_copy(own.at[g], landing(g, 0, z), local_sems.at[4 + g]) for g in range(3)]

    def send_along(g):
        for s in (1, 3, 2):
            along[g, s].start()

    def send_plane(g, s):
        if s:
            along[g, s].wait_recv()
        by_x[g, s].start()
        by_y[g, s].start()

    def send_diag(g, s):
        (by_x if s < 2 else by_y)[g, s].wait_recv()
        diag[g, s].start()

    lax.fori_loop(0, 8, pick_attn, 0)
    send_along(0)
    send_plane(0, 0)
    homes[0].start()

    lax.fori_loop(0, 8, pick_mod, 0)
    mod_saved = save(qs, wmod_out)
    places = lax.broadcasted_iota(jnp.int32, (32, LEVELS), 1).astype(F32)
    for owner in range(8):
        codes = gath[owner * PAYLOAD + LEVEL_TILE][:32].astype(F32)
        level = codes[:, 0:1] * 32.0 + codes[:, 64:65]
        hots[owner * 32 : (owner + 1) * 32] = jnp.where(level == places, 1.0, 0.0).astype(BF)
    own_hot_ref[...] = hots[:, pl.ds(pl.multiple_of(d * TILE, TILE), TILE)]
    for j in range(TABLE_TILES):
        strip = jnp.concatenate([gath[owner * PAYLOAD + HEAD_TILES + j] for owner in range(8)], axis=0)
        emb_ref[:, j * TILE : (j + 1) * TILE] = dot(hots[...], strip, NN).astype(BF)
    embedded = emb_ref[pl.ds(pl.multiple_of(chip * 64, 64), 64), :]
    for k in range(4):
        part[:, :, k * 384 : (k + 1) * 384] = dot(embedded, qs[k], NN).reshape(4, FRAMES, 384)
    modbuf[z] = part[z]
    shared = {}
    for s in (1, 3, 2):
        shared[s] = link.send(part.at[lax.rem(z + s, 4)], modbuf.at[z], d, lax.rem(z + s, 4))

    lax.fori_loop(0, 8, pick_feed, 0)
    send_along(1)
    send_along(2)
    homes[1].start()
    homes[2].start()
    for s in (1, 3, 2):
        send_plane(0, s)
    for s in (0, 1, 3, 2):
        send_diag(0, s)
    send_plane(1, 0)
    send_plane(2, 0)

    for s in (1, 3, 2):
        shared[s].wait_recv()
    for m in range(4):
        for c in range(6):
            mods_ref[:, c, m * 256 : (m + 1) * 256] = modbuf[m, :, c * 256 : (c + 1) * 256]

    def norm_strip(i, _):
        strip = pl.ds(pl.multiple_of(i * BLK, BLK), BLK)
        normed, _ = norm_rows(xs[strip].astype(F32))
        mods = mods_ref[pl.ds(i * FBLK, FBLK)]
        hs[strip] = flat(frames_of(normed) * (1.0 + mods[:, 1:2]) + mods[:, 0:1]).astype(BF)
        return 0

    lax.fori_loop(0, CLIP // BLK, norm_strip, 0)
    h_saved = save(hs, h_out)

    def late(g, p):
        for s in (0, 1, 3, 2):
            if p == 3:
                diag[g, s].wait_recv()
            elif (p == 1) == (s >= 2):
                (by_x if p == 1 else by_y)[g, s].wait_recv()

    for p in (1, 2, 3):
        late(0, p)
    homes[0].wait()

    def packs(m):
        return [
            pltpu.make_async_copy(
                w_ref.at[p, m, pl.ds(role * 32, 32)],
                wpack.at[m, pl.ds(role * TILE + p * 32, 32)],
                pack_sems.at[m * 16 + p * 4 + role],
            )
            for p in range(4)
            for role in range(4)
        ]

    def pack_start(m, _):
        for copy in packs(m):
            copy.start()
        return 0

    lax.fori_loop(0, 4, pack_start, 0)
    mod_saved.wait()

    def project_in(m, _):
        for copy in packs(m):
            copy.wait()
        qs[m] = dot(hs[...], wpack[m, 0 : 3 * TILE], NT).astype(BF)
        return 0

    lax.fori_loop(0, 4, project_in, 0)
    pack_saved = save(wpack, wpack_out)
    qkv_saved = save(qs, qkv_out)

    def attend_group(m, _):
        @pl.when(m == 0)
        def _():
            for s in (1, 3, 2):
                send_plane(1, s)

        @pl.when(m == 1)
        def _():
            send_diag(1, 0)
            send_diag(1, 1)

        @pl.when(m == 2)
        def _():
            send_plane(2, 1)
            send_plane(2, 3)
            send_diag(1, 3)

        @pl.when(m == 3)
        def _():
            send_plane(2, 2)
            send_diag(1, 2)
            send_diag(2, 0)

        def step(i, _):
            across = pl.ds(pl.multiple_of(i * QBLK, QBLK), QBLK)
            for head in range(2):
                lanes = slice(head * HD, (head + 1) * HD)
                keys = qs[m, :, TILE + head * HD : TILE + (head + 1) * HD]
                values = qs[m, :, 2 * TILE + head * HD : 2 * TILE + (head + 1) * HD]
                queries = qs[m, across, lanes]
                scores = dot(keys, queries, NT).reshape(FRAMES, FRAME_TOK, QBLK)
                scores = scores * SCALE2 + bs[:, across][:, None, :]
                peak = jnp.max(jnp.max(scores, axis=0), axis=0, keepdims=True)
                weights = jnp.exp2(scores - peak[None])
                total = jnp.sum(jnp.sum(weights, axis=0), axis=0, keepdims=True)
                mixed = dot(values, weights.reshape(CLIP, QBLK).astype(BF), TN)
                os_[m, lanes, across] = (mixed / total).astype(BF)
                lse_ref[m, head : head + 1, across] = peak + jnp.log2(total)
            return 0

        lax.fori_loop(0, CLIP // QBLK, step, 0)
        return 0

    lax.fori_loop(0, 4, attend_group, 0)
    o_saved = save(os_, o_out)
    send_diag(2, 1)

    def swap_strip(i):
        strip = pl.ds(pl.multiple_of(i * BLK, BLK), BLK)
        return pltpu.make_async_remote_copy(
            src_ref=mine.at[strip],
            dst_ref=peer.at[strip],
            send_sem=strip_sends.at[i],
            recv_sem=strip_recvs.at[i],
            device_id=(dk, z),
            device_id_type=MESH,
        )

    def project_out(i, _):
        strip = pl.ds(pl.multiple_of(i * BLK, BLK), BLK)
        total = dot(os_[0, :, strip], wpack[0, 3 * TILE : 4 * TILE], TN)
        for m in range(1, 4):
            total = total + dot(os_[m, :, strip], wpack[m, 3 * TILE : 4 * TILE], TN)
        mine[strip] = total.astype(BF)
        swap_strip(i).start()
        return 0

    lax.fori_loop(0, CLIP // BLK, project_out, 0)
    h_saved.wait()
    dy_saved.wait()

    def middle_strip(i, _):
        strip = pl.ds(pl.multiple_of(i * BLK, BLK), BLK)
        swap_strip(i).wait_recv()
        mods = mods_ref[pl.ds(i * FBLK, FBLK)]
        branch = (mine[strip].astype(F32) + peer[strip].astype(F32)).astype(BF)
        peer[strip] = branch
        mid = frames_of(xs[strip].astype(F32)) + mods[:, 2:3] * frames_of(branch.astype(F32))
        dh_acc[strip] = flat(mid)
        normed, _ = norm_rows(flat(mid))
        hs[strip] = flat(frames_of(normed) * (1.0 + mods[:, 4:5]) + mods[:, 3:4]).astype(BF)
        dys[strip] = flat(mods[:, 5:6] * frames_of(dys[strip].astype(F32))).astype(BF)
        return 0

    lax.fori_loop(0, CLIP // BLK, middle_strip, 0)
    y_saved = save(dh_acc, y_out)
    branch_saved = save(peer, branch_out)
    send_diag(2, 3)
    send_diag(2, 2)
    e_acc[...] = jnp.zeros_like(e_acc)
    y_saved.wait()
    dh_acc[...] = jnp.zeros_like(dh_acc)
    homes[1].wait()
    homes[2].wait()

    def stages(block):
        buf, p, first = lax.rem(block, 2), block // 2, lax.rem(block, 2) * 2
        return [
            pltpu.make_async_copy(stage.at[buf], dst.at[p, pl.ds(first, 2)], stage_sems.at[2 * buf + k])
            for k, (stage, dst) in enumerate(((up_stage, dup_out), (down_stage, ddown_out)))
        ]

    def feed_block(block, _):
        for p in (1, 2, 3):

            @pl.when(block == 2 * p)
            def _(p=p):
                late(1, p)
                late(2, p)

        buf, p, first = lax.rem(block, 2), block // 2, lax.rem(block, 2) * 2
        up = wfeed[0, p, pl.ds(first, 2)].reshape(2 * TILE, D)
        down = wfeed[1, p, pl.ds(first, 2)].reshape(2 * TILE, D)

        @pl.when(block >= 2)
        def _():
            for copy in stages(block - 2):
                copy.wait()

        for piece in range(CLIP // ROWS):
            rows = slice(piece * ROWS, (piece + 1) * ROWS)
            hidden = hs[rows]
            grad = dys[rows]
            pre = dot(hidden, up, NT)
            square = pre * pre
            tanh = jnp.tanh(GELU_A * pre * (1.0 + GELU_B * square))
            act = (0.5 * pre * (1.0 + tanh)).astype(BF)
            slope = 0.5 * (1.0 + tanh) + 0.5 * pre * (1.0 - tanh * tanh) * (
                GELU_A * (1.0 + 3.0 * GELU_B * square)
            )
            grad_act = dot(grad, down, NT).astype(BF).astype(F32)
            grad_pre = (grad_act * slope).astype(BF)
            e_acc[rows] += dot(act, down, NN)
            dh_acc[rows] += dot(grad_pre, up, NN)
            if piece == 0:
                down_acc[...] = dot(act, grad, TN)
                up_acc[...] = dot(grad_pre, hidden, TN)
            else:
                down_stage[buf] = (down_acc[...] + dot(act, grad, TN)).astype(BF).reshape(2, TILE, D)
                up_stage[buf] = (up_acc[...] + dot(grad_pre, hidden, TN)).astype(BF).reshape(2, TILE, D)
        for copy in stages(block):
            copy.start()
        return 0

    lax.fori_loop(0, 8, feed_block, 0)
    branch_saved.wait()

    def swap_done(i, _):
        swap_strip(i).wait_send()
        return 0

    lax.fori_loop(0, CLIP // BLK, swap_done, 0)

    def cast_strip(i, _):
        strip = pl.ds(pl.multiple_of(i * BLK, BLK), BLK)
        mine[strip] = e_acc[strip].astype(BF)
        peer[strip] = dh_acc[strip].astype(BF)
        return 0

    lax.fori_loop(0, CLIP // BLK, cast_strip, 0)
    ends = [save(mine, e_out), save(peer, dh_out), x_saved, pack_saved, qkv_saved, o_saved]
    for block in (6, 7):
        for copy in stages(block):
            copy.wait()
    for copy in ends:
        copy.wait()
    link.drain()


def front(masters, level_table, levels, bias_pair, activations, cotangent, owner_list):
    slots = masters.shape[0]
    codes = jnp.stack([levels.reshape(-1) // 32, levels.reshape(-1) % 32], axis=1).astype(BF)
    codes = jnp.pad(jnp.repeat(codes, 64, axis=1), ((0, TILE - codes.shape[0]), (0, 0)))
    payload = jnp.concatenate(
        [
            masters.astype(BF),
            level_table.reshape(TILE, TABLE_TILES, TILE).transpose(1, 0, 2),
            codes[None],
            jnp.zeros((1, TILE, TILE), BF),
        ]
    )
    position = jnp.arange(owner_list.shape[0], dtype=jnp.int32)
    place = (position // slots) * PAYLOAD + position % slots
    index = jnp.sum(
        jnp.where(owner_list[None, :] == position[:, None], place[None, :], 0), axis=1
    ).astype(jnp.int32)
    vmem = pl.BlockSpec(memory_space=pltpu.VMEM)
    hbm = pl.BlockSpec(memory_space=pl.ANY)
    clip = jax.ShapeDtypeStruct((CLIP, D), BF)
    chunks = jax.ShapeDtypeStruct((4, 4, TILE, D), BF)
    thirds = jax.ShapeDtypeStruct((4, CLIP, 3 * TILE), BF)
    return pl.pallas_call(
        front_kernel,
        in_specs=[pl.BlockSpec(memory_space=pltpu.SMEM), hbm, hbm, hbm, hbm],
        out_specs=[hbm] * 14 + [vmem] * 5,
        out_shape=[
            chunks,
            thirds,
            clip,
            clip,
            clip,
            jax.ShapeDtypeStruct((4, 4 * TILE, D), BF),
            thirds,
            jax.ShapeDtypeStruct((4, TILE, CLIP), BF),
            clip,
            jax.ShapeDtypeStruct((CLIP, D), F32),
            clip,
            clip,
            chunks,
            chunks,
            jax.ShapeDtypeStruct((FRAMES, 6, D), F32),
            jax.ShapeDtypeStruct((FRAMES, CLIP), F32),
            jax.ShapeDtypeStruct((4, 2, CLIP), F32),
            jax.ShapeDtypeStruct((256, D), BF),
            jax.ShapeDtypeStruct((256, TILE), BF),
        ],
        scratch_shapes=[
            pltpu.VMEM((8 * PAYLOAD, TILE, TILE), BF),
            pltpu.VMEM((3, TILE, D), BF),
            pltpu.VMEM((4, TILE, TILE), BF),
            pltpu.VMEM((CLIP, D), BF),
            pltpu.VMEM((CLIP, D), BF),
            pltpu.VMEM((FRAMES, CLIP), F32),
            pltpu.VMEM((4, FRAMES, 12 * TILE), F32),
            pltpu.VMEM((4, FRAMES, 12 * TILE), F32),
            pltpu.VMEM((256, LEVELS), BF),
            pltpu.VMEM((CLIP, D), BF),
            pltpu.VMEM((4, 4 * TILE, D), BF),
            pltpu.VMEM((4, CLIP, 3 * TILE), BF),
            pltpu.VMEM((4, TILE, CLIP), BF),
            pltpu.VMEM((CLIP, D), BF),
            pltpu.VMEM((CLIP, D), BF),
            pltpu.VMEM((CLIP, D), F32),
            pltpu.VMEM((CLIP, D), F32),
            pltpu.VMEM((2, 4, 4, TILE, D), BF),
            pltpu.VMEM((2, 2, TILE, D), BF),
            pltpu.VMEM((2, 2, TILE, D), BF),
            pltpu.VMEM((2 * TILE, D), F32),
            pltpu.VMEM((2 * TILE, D), F32),
            pltpu.SemaphoreType.DMA((ENTRY_COPIES,)),
            pltpu.SemaphoreType.DMA((ENTRY_COPIES,)),
            pltpu.SemaphoreType.DMA((3,)),
            pltpu.SemaphoreType.DMA((3,)),
            pltpu.SemaphoreType.DMA((4,)),
            pltpu.SemaphoreType.DMA((4,)),
            pltpu.SemaphoreType.DMA((24,)),
            pltpu.SemaphoreType.DMA((64,)),
            pltpu.SemaphoreType.DMA((4,)),
        ],
        compiler_params=pltpu.CompilerParams(
            vmem_limit_bytes=63 * 1024 * 1024, collective_id=0, has_side_effects=True
        ),
        cost_estimate=cost(1e11, 60e6),
        name="front",
    )(index, payload, activations, cotangent, bias_pair)


def attend_kernel(qkv_ref, bias_ref, o_ref, lse_ref):
    for head in range(2):
        lanes = slice(head * HD, (head + 1) * HD)
        keys = qkv_ref[:, TILE + head * HD : TILE + (head + 1) * HD]
        values = qkv_ref[:, 2 * TILE + head * HD : 2 * TILE + (head + 1) * HD]

        def step(i, _, lanes=lanes, keys=keys, values=values, head=head):
            start = pl.multiple_of(i * QBLK, QBLK)
            queries = qkv_ref[pl.ds(start, QBLK), lanes]
            scores = dot(keys, queries, NT).reshape(FRAMES, FRAME_TOK, QBLK)
            scores = scores * SCALE2 + bias_ref[:, pl.ds(start, QBLK)][:, None, :]
            peak = jnp.max(jnp.max(scores, axis=0), axis=0, keepdims=True)
            weights = jnp.exp2(scores - peak[None])
            total = jnp.sum(jnp.sum(weights, axis=0), axis=0, keepdims=True)
            mixed = dot(values, weights.reshape(CLIP, QBLK).astype(BF), TN)
            o_ref[lanes, pl.ds(start, QBLK)] = (mixed / total).astype(BF)
            lse_ref[0, head : head + 1, pl.ds(start, QBLK)] = peak + jnp.log2(total)
            return 0

        lax.fori_loop(0, CLIP // QBLK, step, 0)


def attend(qkv, bias):
    groups = qkv.shape[1] // (3 * TILE)
    return pl.pallas_call(
        attend_kernel,
        grid=(groups,),
        in_specs=[
            pl.BlockSpec((CLIP, 3 * TILE), lambda m: (0, m)),
            pl.BlockSpec((FRAMES, CLIP), lambda m: (0, 0)),
        ],
        out_specs=[
            pl.BlockSpec((TILE, CLIP), lambda m: (m, 0)),
            pl.BlockSpec((1, 2, CLIP), lambda m: (m, 0, 0)),
        ],
        out_shape=[
            jax.ShapeDtypeStruct((groups * TILE, CLIP), BF),
            jax.ShapeDtypeStruct((groups, 2, CLIP), F32),
        ],
        compiler_params=params(),
        cost_estimate=cost(groups * 2 * 4 * CLIP * CLIP * HD * 3, 2 * qkv.size, groups * 2 * CLIP * CLIP),
        name="attend",
    )(qkv, bias)


def attend_back_kernel(qkv_ref, o_ref, do_ref, lse_ref, bias_ref, out_ref, dk_ref, dv_ref):
    for head in range(2):
        lanes = slice(head * HD, (head + 1) * HD)
        keys = qkv_ref[:, TILE + head * HD : TILE + (head + 1) * HD]
        values = qkv_ref[:, 2 * TILE + head * HD : 2 * TILE + (head + 1) * HD]
        dk_ref[...] = jnp.zeros_like(dk_ref)
        dv_ref[...] = jnp.zeros_like(dv_ref)

        def step(i, _, lanes=lanes, keys=keys, values=values, head=head):
            start = pl.multiple_of(i * QBLK, QBLK)
            across = pl.ds(start, QBLK)
            queries = qkv_ref[across, lanes]
            grad = do_ref[lanes, across]
            shift = bias_ref[:, across] - lse_ref[0, head : head + 1, across]
            scores = dot(keys, queries, NT).reshape(FRAMES, FRAME_TOK, QBLK)
            soft = jnp.exp2(scores * SCALE2 + shift[:, None, :]).reshape(CLIP, QBLK)
            delta = jnp.sum(
                grad.astype(F32) * o_ref[lanes, across].astype(F32), axis=0, keepdims=True
            )
            grad_soft = dot(values, grad, NN)
            grad_scores = (soft * (grad_soft - delta)).astype(BF)
            dv_ref[...] += dot(soft.astype(BF), grad, NT)
            dk_ref[...] += dot(grad_scores, queries, NN)
            grad_query = dot(keys, grad_scores, TN) * HD ** (-0.5)
            out_ref[across, lanes] = grad_query.T.astype(BF)
            return 0

        lax.fori_loop(0, CLIP // QBLK, step, 0)
        out_ref[:, TILE + head * HD : TILE + (head + 1) * HD] = (dk_ref[...] * HD ** (-0.5)).astype(BF)
        out_ref[:, 2 * TILE + head * HD : 2 * TILE + (head + 1) * HD] = dv_ref[...].astype(BF)


def attend_back(qkv, o_rows, do_rows, lse, bias):
    groups = qkv.shape[1] // (3 * TILE)
    return pl.pallas_call(
        attend_back_kernel,
        grid=(groups,),
        in_specs=[
            pl.BlockSpec((CLIP, 3 * TILE), lambda m: (0, m)),
            pl.BlockSpec((TILE, CLIP), lambda m: (m, 0)),
            pl.BlockSpec((TILE, CLIP), lambda m: (m, 0)),
            pl.BlockSpec((1, 2, CLIP), lambda m: (m, 0, 0)),
            pl.BlockSpec((FRAMES, CLIP), lambda m: (0, 0)),
        ],
        out_specs=pl.BlockSpec((CLIP, 3 * TILE), lambda m: (0, m)),
        out_shape=jax.ShapeDtypeStruct(qkv.shape, BF),
        scratch_shapes=[pltpu.VMEM((CLIP, HD), F32), pltpu.VMEM((CLIP, HD), F32)],
        compiler_params=params(),
        cost_estimate=cost(groups * 2 * 10 * CLIP * CLIP * HD * 3, 4 * qkv.size, groups * 2 * CLIP * CLIP),
        name="attend_back",
    )(qkv, o_rows, do_rows, lse, bias)


UNITS = 256


def feed_kernel(h_ref, de_ref, up_ref, down_ref, e_ref, dh_ref, dup_ref, ddown_ref, e_acc, dh_acc, up_acc, down_acc):
    block = pl.program_id(0)
    last = pl.num_programs(0) - 1
    up = up_ref[...]
    down = down_ref[...]
    for part in range(CLIP // ROWS):
        rows = slice(part * ROWS, (part + 1) * ROWS)
        hidden = h_ref[rows]
        grad = de_ref[rows]
        pre = dot(hidden, up, NT)
        square = pre * pre
        tanh = jnp.tanh(GELU_A * pre * (1.0 + GELU_B * square))
        act = (0.5 * pre * (1.0 + tanh)).astype(BF)
        slope = 0.5 * (1.0 + tanh) + 0.5 * pre * (1.0 - tanh * tanh) * (
            GELU_A * (1.0 + 3.0 * GELU_B * square)
        )
        grad_act = dot(grad, down, NT).astype(BF).astype(F32)
        grad_pre = (grad_act * slope).astype(BF)
        feed = dot(act, down, NN)
        back = dot(grad_pre, up, NN)

        @pl.when(block == 0)
        def _():
            e_acc[rows] = feed
            dh_acc[rows] = back

        @pl.when(block > 0)
        def _():
            e_acc[rows] += feed
            dh_acc[rows] += back

        if part == 0:
            down_acc[...] = dot(act, grad, TN)
            up_acc[...] = dot(grad_pre, hidden, TN)
        else:
            ddown_ref[...] = (down_acc[...] + dot(act, grad, TN)).astype(BF)
            dup_ref[...] = (up_acc[...] + dot(grad_pre, hidden, TN)).astype(BF)

    @pl.when(block == last)
    def _():
        e_ref[...] = e_acc[...].astype(BF)
        dh_ref[...] = dh_acc[...].astype(BF)


def feed_both(hidden, grad, up, down):
    units = up.shape[0]
    whole = pl.BlockSpec((CLIP, D), lambda i: (0, 0))
    strip = pl.BlockSpec((UNITS, D), lambda i: (i, 0))
    return pl.pallas_call(
        feed_kernel,
        grid=(units // UNITS,),
        in_specs=[whole, whole, strip, strip],
        out_specs=[whole, whole, strip, strip],
        out_shape=[jax.ShapeDtypeStruct((CLIP, D), BF)] * 2 + [jax.ShapeDtypeStruct((units, D), BF)] * 2,
        scratch_shapes=[
            pltpu.VMEM((CLIP, D), F32),
            pltpu.VMEM((CLIP, D), F32),
            pltpu.VMEM((UNITS, D), F32),
            pltpu.VMEM((UNITS, D), F32),
        ],
        compiler_params=params(),
        cost_estimate=cost(12 * CLIP * D * units, 8 * CLIP * D + 8 * units * D, CLIP * units),
        name="feed_both",
    )(hidden, grad, up, down)


HALF = CLIP // 2
EXIT_COPIES = 8 + 1 + 18 + 9 + 24 + 12 + 6 + 14
EXIT_LOCAL = 32


class Relay:
    def __init__(self, sends, recvs, local, src, full, d, z):
        self.sends, self.recvs, self.local = sends, recvs, local
        self.src, self.full, self.d, self.z = src, full, d, z
        self.core = lax.rem(d, 2)

    def place(self, clip, first, count):
        start = pl.multiple_of(lax.rem(clip, 2) * CLIP + first * HALF, HALF)
        return self.full.at[pl.ds(start, count)]

    def copy(self, src, clip, half, way, hop):
        index = way * 6 + (hop - 1) * 2 + half
        return pltpu.make_async_remote_copy(
            src_ref=src,
            dst_ref=self.place(clip, half, HALF),
            send_sem=self.sends.at[index],
            recv_sem=self.recvs.at[index],
            device_id=(self.d - self.core + clip // 2, lax.rem(self.z + (1 if way == 0 else 3), 4)),
            device_id_type=MESH,
        )

    def more(self, way):
        return self.z < 3 if way == 0 else self.z > 0

    def own(self, way):
        part = self.src.at[pl.ds(pl.multiple_of(self.core * HALF, HALF), HALF)]
        return self.copy(part, self.z, self.core, way, 1)

    def home(self):
        return pltpu.make_async_copy(self.src, self.place(self.z, 0, CLIP), self.local)

    def first(self):
        for way in range(2):

            @pl.when(self.more(way))
            def _(way=way):
                self.own(way).start()

        @pl.when(self.z // 2 == self.core)
        def _():
            self.home().start()

    def arriving(self, way, hop):
        clip = lax.rem(self.z + (4 - hop if way == 0 else hop), 4)
        there = self.z >= hop if way == 0 else self.z + hop <= 3
        return clip, jnp.logical_and(there, clip // 2 == self.core)

    def hop(self, hop):
        for way in range(2):
            clip, here = self.arriving(way, hop)

            @pl.when(here)
            def _(way=way, clip=clip):
                for half in range(2):
                    part = self.place(clip, half, HALF)
                    self.copy(part, clip, half, way, hop).wait_recv()
                    if hop < 3:

                        @pl.when(self.more(way))
                        def _(part=part, half=half):
                            self.copy(part, clip, half, way, hop + 1).start()

    def finish(self):
        for way in range(2):

            @pl.when(self.more(way))
            def _(way=way):
                self.own(way).wait_send()

            for hop in (1, 2):
                clip, here = self.arriving(way, hop)

                @pl.when(jnp.logical_and(here, self.more(way)))
                def _(way=way, clip=clip, hop=hop):
                    for half in range(2):
                        self.copy(self.place(clip, half, HALF), clip, half, way, hop + 1).wait_send()

        @pl.when(self.z // 2 == self.core)
        def _():
            self.home().wait()


class Line:
    def __init__(self, link, own, held, z, d):
        self.own, self.held, self.z, self.d = own, held, z, d
        self.sends, self.recvs, self.base = link.sends, link.recvs, link.used
        link.used += 2

    def copy(self, way, at):
        if way == 0:
            src, count = self.own.at[at + 1 : 4], 3 - at
        else:
            src, count = self.own.at[0:at], at
        return pltpu.make_async_remote_copy(
            src_ref=src,
            dst_ref=self.held.at[way, 0:count],
            send_sem=self.sends.at[self.base + way],
            recv_sem=self.recvs.at[self.base + way],
            device_id=(self.d, at + (1 if way == 0 else -1)),
            device_id_type=MESH,
        )

    def add(self, chunk, way, slot):
        def step(i, _):
            rows = pl.ds(pl.multiple_of(i * 32, 32), 32)
            total = self.own[chunk, rows].astype(F32) + self.held[way, slot, rows].astype(F32)
            self.own[chunk, rows] = total.astype(BF)
            return 0

        lax.fori_loop(0, 4, step, 0)

    def start(self):
        @pl.when(self.z == 0)
        def _():
            self.copy(0, 0).start()

        @pl.when(self.z == 3)
        def _():
            self.copy(1, 3).start()

    def turn(self):
        @pl.when(self.z == 1)
        def _():
            self.copy(0, 0).wait_recv()
            self.add(2, 0, 1)
            self.add(3, 0, 2)
            self.copy(0, 1).start()

        @pl.when(self.z == 2)
        def _():
            self.copy(1, 3).wait_recv()
            self.add(0, 1, 0)
            self.add(1, 1, 1)
            self.copy(1, 2).start()

    def turn_again(self):
        @pl.when(self.z == 2)
        def _():
            self.copy(0, 1).wait_recv()
            self.add(3, 0, 1)
            self.copy(0, 2).start()

        @pl.when(self.z == 1)
        def _():
            self.copy(1, 2).wait_recv()
            self.add(0, 1, 0)
            self.copy(1, 1).start()

    def total(self, out):
        for at in range(4):

            @pl.when(self.z == at)
            def _(at=at):
                if at == 0:
                    self.copy(1, 1).wait_recv()
                if at == 3:
                    self.copy(0, 2).wait_recv()

                def step(i, _):
                    rows = pl.ds(pl.multiple_of(i * 32, 32), 32)
                    total = self.own[at, rows].astype(F32)
                    if at > 0:
                        total = total + self.held[0, 0, rows].astype(F32)
                    if at < 3:
                        total = total + self.held[1, at, rows].astype(F32)
                    out[rows] = total.astype(BF)
                    return 0

                lax.fori_loop(0, 4, step, 0)

    def finish(self):
        for at in range(4):

            @pl.when(self.z == at)
            def _(at=at):
                if at < 3:
                    self.copy(0, at).wait_send()
                if at > 0:
                    self.copy(1, at).wait_send()


def exit_kernel(
    y_hbm,
    g_hbm,
    e_hbm,
    dy_hbm,
    br_hbm,
    x_hbm,
    h_hbm,
    qkv_hbm,
    o_hbm,
    wpack_hbm,
    wmod_hbm,
    up_hbm,
    down_hbm,
    mods_ref,
    bias_ref,
    lse_ref,
    emb_ref,
    hot_ref,
    out_all,
    in_all,
    everyone,
    dwm_out,
    table_ref,
    ys,
    gs,
    es,
    dys,
    brs,
    gp,
    ep,
    qs,
    os_,
    dos,
    win,
    wout,
    dhp,
    dattn,
    got,
    loc,
    zbuf,
    held,
    red,
    dm,
    dms,
    dmall,
    trow,
    tbuf,
    dk_ref,
    dv_ref,
    sends,
    recvs,
    strip_sends,
    strip_recvs,
    out_sends,
    out_recvs,
    in_sends,
    in_recvs,
    local_sems,
):
    d, z = lax.axis_index("dp"), lax.axis_index("mp")
    core, chip = lax.rem(d, 2), d // 2
    dk, dx, dyd = jnp.bitwise_xor(d, 1), jnp.bitwise_xor(d, 2), jnp.bitwise_xor(d, 4)
    link = Link(sends, recvs)
    locals_used = [0]

    def load(src, dst):
        copy = pltpu.make_async_copy(src, dst, local_sems.at[locals_used[0]])
        locals_used[0] += 1
        copy.start()
        return copy

    barrier = pltpu.get_barrier_semaphore()
    for step in (1, 2, 4):
        pl.semaphore_signal(barrier, inc=1, device_id=(jnp.bitwise_xor(d, step), z), device_id_type=MESH)
    for s in (1, 2, 3):
        pl.semaphore_signal(barrier, inc=1, device_id=(d, lax.rem(z + s, 4)), device_id_type=MESH)
        pl.semaphore_signal(barrier, inc=1, device_id=(dk, lax.rem(z + s, 4)), device_id_type=MESH)

    first_loads = [load(a, b) for a, b in ((g_hbm, gs), (e_hbm, es), (y_hbm, ys), (dy_hbm, dys), (br_hbm, brs))]
    loads = [load(a, b) for a, b in ((o_hbm, os_), (qkv_hbm, qs))]
    for m in range(4):
        loads.append(load(wpack_hbm.at[m, 3 * TILE : 4 * TILE], wout.at[m]))
        loads.append(load(wpack_hbm.at[m, 0 : 3 * TILE], win.at[m * 3 * TILE : (m + 1) * 3 * TILE]))
    feed_loads = []
    for g, src in enumerate((up_hbm, down_hbm)):
        feed_loads.append(load(src.at[0], loc.at[g, 0:4]))
        feed_loads.append(load(src.at[2, 0:2], loc.at[g, 4:6]))
        feed_loads.append(load(src.at[1, 2:4], loc.at[g, 6:8]))
    pl.semaphore_wait(barrier, 9)

    def strip_of(i):
        return pl.ds(pl.multiple_of(i * BLK, BLK), BLK)

    def swap(i, k):
        src, dst = ((g_hbm, gp), (e_hbm, ep))[k]
        return pltpu.make_async_remote_copy(
            src_ref=src.at[strip_of(i)],
            dst_ref=dst.at[strip_of(i)],
            send_sem=strip_sends.at[2 * i + k],
            recv_sem=strip_recvs.at[2 * i + k],
            device_id=(dk, z),
            device_id_type=MESH,
        )

    for k in (1, 0):

        def swap_start(i, _, k=k):
            swap(i, k).start()
            return 0

        lax.fori_loop(0, CLIP // BLK, swap_start, 0)

    plane = {}

    def plane_first(g, src):
        plane[g, 0] = link.send(src.at[3, 0:2], got.at[g, 0], dx, z)
        plane[g, 1] = link.send(src.at[3, 2:4], got.at[g, 1], dyd, z)
        plane[g, 2] = link.send(src.at[1, 0:2], got.at[g, 2], dx, z)
        plane[g, 3] = link.send(src.at[2, 2:4], got.at[g, 3], dyd, z)

    def add_into(dst, first, count, parts):
        def step(i, _):
            k = i // 4
            rows = pl.ds(pl.multiple_of(lax.rem(i, 4) * 32, 32), 32)
            total = dst[first + k, rows].astype(F32)
            for g, slot in parts:
                total = total + got[g, slot, k, rows].astype(F32)
            dst[first + k, rows] = total.astype(BF)
            return 0

        lax.fori_loop(0, count * 4, step, 0)

    def places(g):
        if g == 0:
            return (dattn.at[0], 0), (dattn.at[2], 0), (dattn.at[1], 2)
        return (loc.at[g - 1], 0), (loc.at[g - 1], 4), (loc.at[g - 1], 6)

    def plane_pass(g):
        _, (low, low_at), (high, high_at) = places(g)
        plane[g, 0].wait_recv()
        add_into(low, low_at, 2, [(g, 0)])
        plane[g, 4] = link.send(low.at[pl.ds(low_at, 2)], got.at[g, 4], dyd, z)
        plane[g, 1].wait_recv()
        add_into(high, high_at, 2, [(g, 1)])
        plane[g, 5] = link.send(high.at[pl.ds(high_at, 2)], got.at[g, 5], dx, z)

    column, lines = {}, {}

    def plane_final(g):
        (own, _), _, _ = places(g)
        for slot in (2, 3, 4, 5):
            plane[g, slot].wait_recv()
        add_into(own, 0, 2, [(g, 2), (g, 4)])
        add_into(own, 2, 2, [(g, 3), (g, 5)])
        if g:
            lines[g] = Line(link, own, held.at[g - 1], z, d)
            lines[g].start()
            return
        for s in (1, 3, 2):
            to = lax.rem(z + s, 4)
            column[s] = link.send(own.at[to], zbuf.at[s - 1], d, to)

    spread = {}
    homes = []

    def column_final(g):
        (own, _), _, _ = places(g)

        def step(i, _):
            rows = pl.ds(pl.multiple_of(i * 32, 32), 32)
            total = own[z, rows].astype(F32)
            for s in range(3):
                total = total + zbuf[s, rows].astype(F32)
            red[g, rows] = total.astype(BF)
            return 0

        if g:
            lines[g].total(red.at[g])
        else:
            for s in (1, 3, 2):
                column[s].wait_recv()
            lax.fori_loop(0, 4, step, 0)
        rows = pl.ds(g * TILE, TILE)
        spread[g, 2] = link.send(red.at[g], everyone.at[2, rows], dx, z)
        spread[g, 4] = link.send(red.at[g], everyone.at[4, rows], dyd, z)
        spread[g, 1] = link.send(red.at[g], everyone.at[1, rows], dk, z)
        homes.append(load(red.at[g], everyone.at[0, rows]))

    def spread_on(g):
        rows = pl.ds(g * TILE, TILE)
        low, high = pl.ds(g * TILE, TILE // 2), pl.ds(g * TILE + TILE // 2, TILE // 2)
        spread[g, 2].wait_recv()
        spread[g, 6] = link.send(everyone.at[2, low], everyone.at[6, low], dyd, z)
        spread[g, 3] = link.send(everyone.at[2, rows], everyone.at[3, rows], dk, z)
        spread[g, 4].wait_recv()
        spread[g, 7] = link.send(everyone.at[4, high], everyone.at[6, high], dx, z)
        spread[g, 5] = link.send(everyone.at[4, rows], everyone.at[5, rows], dk, z)

    def spread_diag(g):
        rows = pl.ds(g * TILE, TILE)
        spread[g, 6].wait_recv()
        spread[g, 7].wait_recv()
        spread[g, 8] = link.send(everyone.at[6, rows], everyone.at[7, rows], dk, z)

    plane_first(1, up_hbm)
    plane_first(2, down_hbm)
    for copy in first_loads:
        copy.wait()

    def out_strip(i, _):
        strip, frames = strip_of(i), pl.ds(i * FBLK, FBLK)
        swap(i, 1).wait_recv()
        mods = mods_ref[frames]
        feed = es[strip].astype(F32) + ep[strip].astype(F32)
        dm[frames, 5] = jnp.sum(frames_of(dys[strip].astype(F32) * feed), axis=1)
        ep[strip] = (ys[strip] + flat(mods[:, 5:6] * frames_of(feed))).astype(BF)
        return 0

    lax.fori_loop(0, CLIP // BLK, out_strip, 0)
    output = Relay(out_sends, out_recvs, local_sems.at[EXIT_LOCAL - 1], ep, out_all, d, z)
    output.first()

    def back_strip(i, _):
        strip, frames = strip_of(i), pl.ds(i * FBLK, FBLK)
        swap(i, 0).wait_recv()
        mods = mods_ref[frames]
        mid = ys[strip]
        dy = dys[strip].astype(F32)
        normed, inverse_std = norm_rows(mid)
        grad = gs[strip].astype(F32) + gp[strip].astype(F32)
        dm[frames, 3] = jnp.sum(frames_of(grad), axis=1)
        dm[frames, 4] = jnp.sum(frames_of(grad * normed), axis=1)
        scaled = flat(frames_of(grad) * (1.0 + mods[:, 4:5]))
        dy1 = dy + norm_back(scaled, normed, inverse_std)
        ys[strip] = dy1
        dm[frames, 2] = jnp.sum(frames_of(dy1 * brs[strip].astype(F32)), axis=1)
        gp[strip] = flat(mods[:, 2:3] * frames_of(dy1)).astype(BF)
        return 0

    lax.fori_loop(0, CLIP // BLK, back_strip, 0)

    def swap_done(i, _):
        for k in range(2):
            swap(i, k).wait_send()
        return 0

    lax.fori_loop(0, CLIP // BLK, swap_done, 0)
    x_load = load(x_hbm, gs)
    h_load = load(h_hbm, es)
    for copy in loads:
        copy.wait()

    def project(m, _):
        dos[m] = dot(wout[m], gp[...], NT).astype(BF)
        grad = dot(os_[m], gp[...], NN).astype(BF)
        for c in range(4):
            dattn[c, m, 96:128] = grad[c * 32 : (c + 1) * 32]
        return 0

    lax.fori_loop(0, 4, project, 0)

    def attend_group(m, _):
        for head in range(2):
            lanes = slice(head * HD, (head + 1) * HD)
            keys = qs[m, :, TILE + head * HD : TILE + (head + 1) * HD]
            values = qs[m, :, 2 * TILE + head * HD : 2 * TILE + (head + 1) * HD]
            dk_ref[...] = jnp.zeros_like(dk_ref)
            dv_ref[...] = jnp.zeros_like(dv_ref)

            def step(i, _, lanes=lanes, keys=keys, values=values, head=head):
                across = pl.ds(pl.multiple_of(i * QBLK, QBLK), QBLK)
                queries = qs[m, across, lanes]
                grad = dos[m, lanes, across]
                shift = bias_ref[:, across] - lse_ref[m, head : head + 1, across]
                scores = dot(keys, queries, NT).reshape(FRAMES, FRAME_TOK, QBLK)
                soft = jnp.exp2(scores * SCALE2 + shift[:, None, :]).reshape(CLIP, QBLK)
                delta = jnp.sum(
                    grad.astype(F32) * os_[m, lanes, across].astype(F32), axis=0, keepdims=True
                )
                grad_soft = dot(values, grad, NN)
                grad_scores = (soft * (grad_soft - delta)).astype(BF)
                dv_ref[...] += dot(soft.astype(BF), grad, NT)
                dk_ref[...] += dot(grad_scores, queries, NN)
                grad_query = dot(keys, grad_scores, TN) * HD ** (-0.5)
                qs[m, across, lanes] = grad_query.T.astype(BF)
                return 0

            lax.fori_loop(0, CLIP // QBLK, step, 0)
            qs[m, :, TILE + head * HD : TILE + (head + 1) * HD] = (dk_ref[...] * HD ** (-0.5)).astype(BF)
            qs[m, :, 2 * TILE + head * HD : 2 * TILE + (head + 1) * HD] = dv_ref[...].astype(BF)
        return 0

    lax.fori_loop(0, 2, attend_group, 0)
    for copy in feed_loads:
        copy.wait()
    plane_pass(1)
    output.hop(1)
    lax.fori_loop(2, 4, attend_group, 0)
    plane_pass(2)
    plane_final(1)

    def hidden_strip(i, _):
        strip = strip_of(i)
        total = dot(qs[0, strip], win[0:384], NN)
        for m in range(1, 4):
            total = total + dot(qs[m, strip], win[m * 384 : (m + 1) * 384], NN)
        brs[strip] = total.astype(BF)
        return 0

    lax.fori_loop(0, CLIP // BLK, hidden_strip, 0)
    hidden_swap = link.send(brs, dhp, dk, z)
    output.hop(2)
    h_load.wait()
    x_load.wait()

    def input_weights(m, _):
        grad = dot(qs[m], es[...], TN).astype(BF)
        for role in range(3):
            for c in range(4):
                first = role * TILE + c * 32
                dattn[c, m, role * 32 : (role + 1) * 32] = grad[first : first + 32]
        return 0

    lax.fori_loop(0, 4, input_weights, 0)
    plane_first(0, dattn)
    mod_loads = [load(wmod_hbm, qs)]
    plane_final(2)
    lines[1].turn()

    hidden_swap.wait_recv()

    def last_strip(i, _):
        strip, frames = strip_of(i), pl.ds(i * FBLK, FBLK)
        mods = mods_ref[frames]
        normed, inverse_std = norm_rows(gs[strip].astype(F32))
        grad = brs[strip].astype(F32) + dhp[strip].astype(F32)
        dm[frames, 0] = jnp.sum(frames_of(grad), axis=1)
        dm[frames, 1] = jnp.sum(frames_of(grad * normed), axis=1)
        scaled = flat(frames_of(grad) * (1.0 + mods[:, 1:2]))
        dys[strip] = (ys[strip] + norm_back(scaled, normed, inverse_std)).astype(BF)
        return 0

    lax.fori_loop(0, CLIP // BLK, last_strip, 0)
    for m in range(4):
        for c in range(6):
            dms[m, :, c * 256 : (c + 1) * 256] = dm[:, c, m * 256 : (m + 1) * 256].astype(BF)
    mod_column = {}
    clip = chip * 4 + z
    for s in (1, 3, 2):
        to = lax.rem(z + s, 4)
        mod_column[s] = link.send(dms.at[to], dmall.at[clip], d, to)
    dmall[clip] = dms[z]
    inner = Relay(in_sends, in_recvs, local_sems.at[EXIT_LOCAL - 2], dys, in_all, d, z)
    inner.first()

    for s in (1, 3, 2):
        mod_column[s].wait_recv()

    def clips_of(which):
        return dmall.at[pl.ds(which * 4, 4)]

    mod_x = link.send(clips_of(chip), clips_of(chip), dx, z)
    mod_y = link.send(clips_of(chip), clips_of(chip), dyd, z)
    plane_pass(0)
    lines[2].turn()
    lines[1].turn_again()
    mod_x.wait_recv()
    over_x = jnp.bitwise_xor(chip, 1)
    mod_xy = link.send(clips_of(over_x), clips_of(over_x), dyd, z)
    plane_final(0)
    inner.hop(1)
    lines[2].turn_again()
    column_final(1)

    mod_y.wait_recv()
    mod_xy.wait_recv()
    for copy in mod_loads:
        copy.wait()
    grads = dmall[...].reshape(256, 12 * TILE)

    level_grads = dot(hot_ref[...], grads, TN).astype(BF)
    rows = dot(level_grads[:, 0:384], qs[0], NT)
    for m in range(1, 4):
        rows = rows + dot(level_grads[:, m * 384 : (m + 1) * 384], qs[m], NT)
    trow[...] = rows.reshape(4, 32, D)
    table = {}
    for s in (1, 3, 2):
        to = lax.rem(z + s, 4)
        table[s] = link.send(trow.at[to], tbuf.at[s - 1], d, to)

    for part in range(6):
        win[part * 256 : (part + 1) * 256] = dot(
            grads[:, part * 256 : (part + 1) * 256], emb_ref[...], TN
        ).astype(BF)
    homes.append(load(win, dwm_out))
    column_final(2)
    spread_on(1)
    inner.hop(2)
    column_final(0)
    spread_on(2)
    spread_diag(1)
    spread_diag(2)
    spread_on(0)
    for s in (1, 3, 2):
        table[s].wait_recv()
    table_ref[...] = trow[z] + tbuf[0] + tbuf[1] + tbuf[2]
    spread_diag(0)
    output.hop(3)
    inner.hop(3)
    for g in range(3):
        for slot in (1, 3, 5, 8):
            spread[g, slot].wait_recv()
    for copy in homes:
        copy.wait()
    output.finish()
    inner.finish()
    lines[1].finish()
    lines[2].finish()
    link.drain()


def exit_call(*args):
    vmem = pl.BlockSpec(memory_space=pltpu.VMEM)
    hbm = pl.BlockSpec(memory_space=pl.ANY)
    chunks = (4, 4, TILE, D)
    heads = (4, TILE, D)
    return pl.pallas_call(
        exit_kernel,
        in_specs=[hbm] * 13 + [vmem] * 5,
        out_specs=[hbm] * 4 + [vmem],
        out_shape=[
            jax.ShapeDtypeStruct((2 * CLIP, D), BF),
            jax.ShapeDtypeStruct((2 * CLIP, D), BF),
            jax.ShapeDtypeStruct((8, 3 * TILE, D), BF),
            jax.ShapeDtypeStruct((12 * TILE, D), BF),
            jax.ShapeDtypeStruct((32, D), F32),
        ],
        scratch_shapes=[
            pltpu.VMEM((CLIP, D), F32),
            pltpu.VMEM((CLIP, D), BF),
            pltpu.VMEM((CLIP, D), BF),
            pltpu.VMEM((CLIP, D), BF),
            pltpu.VMEM((CLIP, D), BF),
            pltpu.VMEM((CLIP, D), BF),
            pltpu.VMEM((CLIP, D), BF),
            pltpu.VMEM((4, CLIP, 3 * TILE), BF),
            pltpu.VMEM(heads, BF),
            pltpu.VMEM(heads, BF),
            pltpu.VMEM((12 * TILE, D), BF),
            pltpu.VMEM(heads, BF),
            pltpu.VMEM((CLIP, D), BF),
            pltpu.VMEM(chunks, BF),
            pltpu.VMEM((3, 6, 2, TILE, D), BF),
            pltpu.VMEM((2, 8, TILE, D), BF),
            pltpu.VMEM((3, TILE, D), BF),
            pltpu.VMEM((2, 2, 3, TILE, D), BF),
            pltpu.VMEM((3, TILE, D), BF),
            pltpu.VMEM((FRAMES, 6, D), F32),
            pltpu.VMEM((4, FRAMES, 12 * TILE), BF),
            pltpu.VMEM((16, FRAMES, 12 * TILE), BF),
            pltpu.VMEM((4, 32, D), F32),
            pltpu.VMEM((3, 32, D), F32),
            pltpu.VMEM((CLIP, HD), F32),
            pltpu.VMEM((CLIP, HD), F32),
            pltpu.SemaphoreType.DMA((EXIT_COPIES,)),
            pltpu.SemaphoreType.DMA((EXIT_COPIES,)),
            pltpu.SemaphoreType.DMA((8,)),
            pltpu.SemaphoreType.DMA((8,)),
            pltpu.SemaphoreType.DMA((12,)),
            pltpu.SemaphoreType.DMA((12,)),
            pltpu.SemaphoreType.DMA((12,)),
            pltpu.SemaphoreType.DMA((12,)),
            pltpu.SemaphoreType.DMA((EXIT_LOCAL,)),
        ],
        compiler_params=pltpu.CompilerParams(
            vmem_limit_bytes=63 * 1024 * 1024, collective_id=1, has_side_effects=True
        ),
        cost_estimate=cost(1e11, 60e6),
        name="exit",
    )(*args)


def adam_steps(grads, lefts, rights, ones, twos, masters, rates):
    lefts = [left.astype(BF) for left in lefts]
    rights = [right.astype(BF) for right in rights]
    turned = [dot(left, grad.astype(BF), TN).astype(BF) for left, grad in zip(lefts, grads)]
    rotated = [dot(turn, right, NN) for turn, right in zip(turned, rights)]
    new_ones = [BETA_ONE * one + (1.0 - BETA_ONE) * r for one, r in zip(ones, rotated)]
    new_twos = [BETA_TWO * two + (1.0 - BETA_TWO) * r * r for two, r in zip(twos, rotated)]
    ways = [(one / (jnp.sqrt(two) + EPS_ADAM)).astype(BF) for one, two in zip(new_ones, new_twos)]
    backs = [dot(left, way, NN).astype(BF) for left, way in zip(lefts, ways)]
    backs = [dot(back, right, NT) for back, right in zip(backs, rights)]
    return (
        [m - rate * (back + DECAY * m) for m, back, rate in zip(masters, backs, rates)],
        new_ones,
        new_twos,
    )


def adam_kernel(tab_ref, rate_ref, *refs, picked, batch):
    if picked:
        red_ref, mod_ref, wide_ref, same_ref = refs[:4]
        refs[-2][...] = wide_ref[...].astype(F32)
        refs[-1][...] = same_ref[...]
        refs = refs[4:-2]
    else:
        grad_ref = refs[0]
        refs = refs[1:]
    master_ref, one_ref, two_ref, left_ref, right_ref, nm_ref, n1_ref, n2_ref, nw_ref = refs
    grads, rates = [], []
    for slot in range(batch):
        tile = pl.program_id(0) * batch + slot
        rates.append(rate_ref[tile])
        if picked:
            col = pl.multiple_of(tab_ref[tile, 8] * TILE, TILE)
            pieces = [
                red_ref[
                    tab_ref[tile, i],
                    pl.ds(pl.multiple_of(tab_ref[tile, 4 + i] * 32, 32), 32),
                    pl.ds(col, TILE),
                ]
                for i in range(4)
            ]
            grad = jnp.concatenate(pieces, axis=0)
            mod_row = pl.multiple_of(tab_ref[tile, 9] * TILE, TILE)
            mod_col = pl.multiple_of(tab_ref[tile, 10] * TILE, TILE)
            mod_grad = mod_ref[pl.ds(mod_col, TILE), pl.ds(mod_row, TILE)]
            kind = tab_ref[tile, 11]
            grads.append(jnp.where(kind == 0, grad, jnp.where(kind == 2, mod_grad, grad).T))
        else:
            grads.append(grad_ref[slot])
    slots = range(batch)
    new_masters, new_ones, new_twos = adam_steps(
        grads,
        [left_ref[slot] for slot in slots],
        [right_ref[slot] for slot in slots],
        [one_ref[slot] for slot in slots],
        [two_ref[slot] for slot in slots],
        [master_ref[slot] for slot in slots],
        rates,
    )
    for slot in slots:
        nm_ref[slot] = new_masters[slot]
        n1_ref[slot] = new_ones[slot]
        n2_ref[slot] = new_twos[slot]
        nw_ref[slot] = new_masters[slot].astype(BF)


def pick_table(tiles, device):
    table = []
    piece = jnp.arange(4, dtype=jnp.int32)[None, :]
    t = tiles[:, None]
    is_in = t < 48
    is_out = (t >= 48) & (t < 64)
    is_up = (t >= 64) & (t < 128)
    is_down = (t >= 128) & (t < 192)
    is_mod = t >= 192
    q0, q1, q2, q3, q4 = t, t - 48, t - 64, t - 128, t - 192
    core = jnp.where(is_in, (q0 % 6) % 2, jnp.where(is_out, q1 // 8, jnp.where(is_up, (q2 % 8) // 4, (q3 // 8) // 4)))
    chip = jnp.where(is_up, q2 % 4, (q3 // 8) % 4)
    chip = jnp.where(is_in | is_out, piece, chip)
    source = jnp.where(is_mod, 0, jnp.bitwise_xor(2 * chip + core, device))
    row = jnp.where(is_in, (q0 % 6) // 2, jnp.where(is_out, 3, jnp.where(is_up, 4 + piece, 8 + piece)))
    row = jnp.where(is_mod, 0, row + jnp.zeros_like(piece))
    col = jnp.where(is_in, q0 // 6, jnp.where(is_out, q1 % 8, jnp.where(is_up, q2 // 8, q3 % 8)))
    col = jnp.where(is_mod, 0, col)
    mod_row = jnp.where(is_mod, q4 // 12, 0)
    mod_col = jnp.where(is_mod, q4 % 12, 0)
    kind = jnp.where(is_mod, 2, jnp.where(is_in | is_up, 1, 0))
    return jnp.concatenate([source, row, col, mod_row, mod_col, kind], axis=1).astype(jnp.int32)


def adam(table, rates, sources, master, one, two, left, right):
    slots = master.shape[0]
    batch = max(b for b in (6, 4, 3, 2, 1) if slots % b == 0)
    picked = len(sources) == 4
    tiles = pl.BlockSpec((batch, TILE, TILE), lambda i, *_: (i, 0, 0))
    extra = []
    if picked:
        height = 4 * TILE
        blocks = sources[2].shape[0] // height
        assert blocks <= slots // batch
        wide = pl.BlockSpec((height, D), lambda i, *_: (jnp.minimum(i, blocks - 1), 0))
        extra = [wide, wide]
        source_specs = [
            pl.BlockSpec(sources[0].shape, lambda i, *_: (0, 0, 0)),
            pl.BlockSpec(sources[1].shape, lambda i, *_: (0, 0)),
            wide,
            wide,
        ]
    else:
        source_specs = [tiles]
    return pl.pallas_call(
        functools.partial(adam_kernel, picked=picked, batch=batch),
        grid_spec=pltpu.PrefetchScalarGridSpec(
            num_scalar_prefetch=2,
            grid=(slots // batch,),
            in_specs=source_specs + [tiles] * 5,
            out_specs=[tiles] * 4 + extra,
        ),
        out_shape=[jax.ShapeDtypeStruct(master.shape, F32)] * 3
        + [jax.ShapeDtypeStruct(master.shape, BF)]
        + [jax.ShapeDtypeStruct(s.shape, t) for s, t in zip(sources[2:], (F32, BF))],
        compiler_params=params(),
        cost_estimate=cost(slots * 8 * TILE**3, slots * TILE * TILE * 36),
        name="adam",
    )(table, rates, *sources, master, one, two, left, right)


def body(
    activations,
    cotangent,
    level_table,
    true_frames,
    group_pattern,
    noise_levels,
    context_flags,
    owner_list,
    masters,
    moment_one,
    moment_two,
    basis_left,
    basis_right,
):
    groups = lax.axis_size("mp")
    owners = lax.axis_size("dp")
    chips = owners // 2
    bits = chips.bit_length() - 1
    z = lax.axis_index("mp")
    device = lax.axis_index("dp")
    core = device % 2
    chip = device // 2
    local_clips = true_frames.shape[0]
    column_clips = 2 * local_clips
    assert column_clips == groups and chips == 1 << bits
    shapes, counts = tile_layout(groups)
    slots = masters.shape[1]
    fast = chips == 4 and groups == 4

    def swap(v, step):
        return lax.ppermute(v, "dp", [(i, i ^ step) for i in range(owners)])

    def across(v):
        return swap(v, 1)

    def plane(v, bit):
        return swap(v, 2 << bit)

    def z_get(v, s):
        return lax.ppermute(v, "mp", [((i + s) % groups, i) for i in range(groups)])

    def z_put(v, s):
        return lax.ppermute(v, "mp", [(i, (i + s) % groups) for i in range(groups)])

    def plane_double(v):
        held = v[None]
        for bit in range(bits):
            held = jnp.concatenate([held, plane(held, bit)], axis=0)
        return held

    def plane_gather(v):
        if chips != 4:
            return plane_double(v)
        half = v.shape[0] // 2
        by_x, by_y = plane(v, 0), plane(v, 1)
        low, high = plane(by_x[:half], 1), plane(by_y[half:], 0)
        return jnp.stack([v, by_x, by_y, jnp.concatenate([low, high], axis=0)])

    def add(a, b):
        return (a.astype(F32) + b.astype(F32)).astype(BF)

    def plane_reduce(v):
        if chips != 4:
            held = v
            for bit in reversed(range(bits)):
                half = 1 << bit
                held = add(held[:half], plane(held[half:], bit))
            return held[0]
        half = v.shape[1] // 2
        got_low = [plane(v[1, :half], 0), plane(v[3, :half], 0)]
        got_high = [plane(v[2, half:], 1), plane(v[3, half:], 1)]
        pass_low = plane(add(v[2, :half], got_low[1]), 1)
        pass_high = plane(add(v[1, half:], got_high[1]), 0)
        low = v[0, :half].astype(F32) + got_low[0].astype(F32) + pass_low.astype(F32)
        high = v[0, half:].astype(F32) + got_high[0].astype(F32) + pass_high.astype(F32)
        return jnp.concatenate([low, high], axis=0).astype(BF)

    def z_gather(v):
        return jnp.stack([v] + [z_get(v, s) for s in range(1, groups)])

    def z_reduce(v):
        total = v[0].astype(F32)
        for s in range(1, groups):
            total = total + z_put(v[s], s).astype(F32)
        return total

    frame_index = jnp.arange(FRAMES, dtype=jnp.int32)

    def mask_rows(flagged, lengths):
        valid = frame_index[None, :] < lengths[:, None]
        in_context = flagged & valid
        visible = valid[:, :, None] & (
            jnp.logical_not(in_context)[:, None, :] | in_context[:, :, None]
        )
        return jnp.repeat(jnp.where(visible, 0.0, -1e30).astype(F32), FRAME_TOK, axis=2)

    def level_rows(flagged, patterns):
        pattern_hot = (patterns[:, None] == jnp.arange(PATTERNS, dtype=jnp.int32)[None, :]).astype(
            jnp.int32
        )
        return jnp.where(
            flagged, 0, jnp.sum(pattern_hot[:, :, None] * noise_levels[None, :, :], axis=1)
        )

    rows = TILE // chips
    level_ids = jnp.arange(LEVELS, dtype=jnp.int32)[None, :]
    if fast:
        with jax.named_scope("front"):
            flagged = context_flags == 1
            (
                _, w_mod, x, dy, h1, w_pack, qkv, o_rows, branch, y1, e_part, dh2_part, d_up, d_down,
                mods, bias, lse, all_embedded, own_hot,
            ) = front(
                masters[0],
                level_table,
                level_rows(flagged, group_pattern),
                mask_rows(flagged, true_frames),
                activations,
                cotangent,
                owner_list,
            )
        with jax.named_scope("exit"):
            block_output, input_grad, everyone, d_w_mod, table_grad = exit_call(
                y1, dh2_part, e_part, dy, branch, x, h1, qkv, o_rows, w_pack, w_mod,
                d_up, d_down, mods, bias, lse, all_embedded, own_hot,
            )
    else:
        with jax.named_scope("entry"):
            holds = (z // local_clips) == core
            local = (z % local_clips) * CLIP
            pair = jnp.stack(
                [
                    lax.dynamic_slice_in_dim(activations, local, CLIP, axis=0),
                    lax.dynamic_slice_in_dim(cotangent, local, CLIP, axis=0),
                ]
            )
            pair = jnp.where(holds, pair, across(pair))
            x, dy = pair[0], pair[1]
            facts = jnp.concatenate(
                [context_flags, true_frames[:, None], group_pattern[:, None]], axis=1
            ).astype(jnp.int32)
            other = across(facts)
            facts = jnp.where(
                core == 0, jnp.concatenate([facts, other]), jnp.concatenate([other, facts])
            )
            flagged = facts[:, :FRAMES] == 1
            levels = level_rows(flagged, facts[:, FRAMES + 1])
            bias = lax.dynamic_index_in_dim(
                mask_rows(flagged, facts[:, FRAMES]), z, axis=0, keepdims=False
            )
            all_levels = plane_double(levels)

        with jax.named_scope("owner_gather"):
            gathered = lax.all_gather(masters[0].astype(BF), "dp", axis=0, tiled=True)
            table = lax.all_gather(level_table, "dp", axis=0, tiled=True)
            position = jnp.arange(owner_list.shape[0], dtype=jnp.int32)
            inverse = jnp.sum(
                jnp.where(owner_list[None, :] == position[:, None], position[None, :], 0), axis=1
            ).astype(jnp.int32)
            chunk_attn, chunk_up, chunk_down, w_mod = pick_chunk_plain(
                gathered, inverse, chip, core, chips, shapes, counts
            )

        with jax.named_scope("weights"):
            got = plane_gather(z_gather(chunk_attn)).reshape(chips, groups, 4, rows, D)
            w_up = plane_gather(z_gather(chunk_up)).reshape(-1, D)
            w_down = plane_gather(z_gather(chunk_down)).reshape(-1, D)

        with jax.named_scope("modulation"):
            hot = (levels.reshape(-1)[:, None] == level_ids).astype(BF)
            embedded = dot(hot, table, NN).astype(BF)
            mod_part = dot(embedded, w_mod, NN).reshape(column_clips, FRAMES, -1)
            pieces = [lax.dynamic_index_in_dim(mod_part, z, axis=0, keepdims=False)]
            for s in range(1, groups):
                piece = lax.dynamic_index_in_dim(
                    mod_part, (z + groups - s) % groups, axis=0, keepdims=False
                )
                pieces.append(z_get(piece, s))
            mods = lax.dynamic_slice_in_dim(
                jnp.stack(pieces + pieces), (groups - z) % groups, groups, axis=0
            )
            mods = (
                mods.reshape(groups, FRAMES, 6, D // groups).transpose(1, 2, 0, 3).reshape(FRAMES, 6, D)
            )
            (h1,) = row_call(first_norm_kernel, "first_norm", [x], mods, [BF], [], 4 * CLIP * D)

        w_in = got[:, :, :3].transpose(1, 2, 0, 3, 4).reshape(-1, D)
        w_out = got[:, :, 3].transpose(1, 0, 2, 3).reshape(-1, D)

        mb = CLIP * D
        with jax.named_scope("attention"):
            qkv = dot(h1, w_in, NT).astype(BF)
            o_rows, lse = attend(qkv, bias)
            part = dot(o_rows, w_out, TN).astype(BF)
            y1, branch, h2, de = row_call(
                middle_kernel, "middle", [x, part, across(part), dy], mods, [F32, BF, BF, BF], [], 18 * mb
            )

        with jax.named_scope("feed"):
            e_part, dh2_part, d_up, d_down = feed_both(h2, de, w_up, w_down)

        with jax.named_scope("feed_back"):
            out, dy1, da, dm_mid = row_call(
                back_kernel,
                "back",
                [y1, dh2_part, across(dh2_part), dy, branch, e_part, across(e_part)],
                mods,
                [BF, F32, BF],
                [4],
                24 * mb,
            )
            shape = (chips, groups, -1, D)
            red_up = z_reduce(plane_reduce(d_up.reshape(shape))).astype(BF)
            red_down = z_reduce(plane_reduce(d_down.reshape(shape))).astype(BF)

        def to_column(rows_here):
            half = CLIP // 2
            mine = lax.dynamic_slice_in_dim(rows_here, core * half, half, axis=0)
            by_clip = [mine] + [z_get(mine, s) for s in range(1, groups)]
            by_clip = lax.dynamic_slice_in_dim(jnp.stack(by_clip + by_clip), (groups - z) % groups, groups, axis=0)
            keep = lax.dynamic_slice_in_dim(by_clip, core * local_clips, local_clips, axis=0)
            send = lax.dynamic_slice_in_dim(by_clip, (1 - core) * local_clips, local_clips, axis=0)
            got_half = across(send)
            both = jnp.where(
                core == 0, jnp.stack([keep, got_half], axis=1), jnp.stack([got_half, keep], axis=1)
            )
            return both.reshape(local_clips * CLIP, D)

        with jax.named_scope("block_output"):
            block_output = to_column(out)

        with jax.named_scope("attention_back"):
            do_rows = dot(w_out, da, NT).astype(BF)
            d_out = dot(o_rows, da, NN).astype(BF)
            d_qkv = attend_back(qkv, o_rows, do_rows, lse, bias)
            dh1_part = dot(d_qkv, w_in, NN).astype(BF)
            d_in = dot(d_qkv, h1, TN).astype(BF)
            in_grad, dm_last = row_call(
                last_kernel, "last", [x, dh1_part, across(dh1_part), dy1], mods, [BF], [2], 12 * mb
            )
            d_in = d_in.reshape(groups, 3, chips, rows, D).transpose(2, 0, 1, 3, 4)
            d_out = d_out.reshape(groups, 1, chips, rows, D).transpose(2, 0, 1, 3, 4)
            d_attn = jnp.concatenate([d_in, d_out], axis=2).reshape(chips, groups, 4 * rows, D)
            red_attn = z_reduce(plane_reduce(d_attn)).astype(BF)

        with jax.named_scope("input_grad"):
            input_grad = to_column(in_grad).astype(F32)

        with jax.named_scope("modulation_back"):
            d_mod = jnp.stack(
                [dm_last[:, 0], dm_last[:, 1], dm_mid[:, 2], dm_mid[:, 0], dm_mid[:, 1], dm_mid[:, 3]], axis=1
            ).astype(BF)
            d_mod = (
                d_mod.reshape(FRAMES, 6, groups, D // groups).transpose(2, 0, 1, 3).reshape(groups, FRAMES, -1)
            )
            pieces = [lax.dynamic_index_in_dim(d_mod, z, axis=0, keepdims=False)]
            for s in range(1, groups):
                pieces.append(z_put(lax.dynamic_index_in_dim(d_mod, (z + s) % groups, axis=0, keepdims=False), s))
            d_mod = jnp.stack(pieces)
            d_mod = plane_double(d_mod).reshape(chips * groups * FRAMES, -1)
            back_clip = (z + groups - jnp.arange(groups, dtype=jnp.int32)) % groups
            clip_hot = (back_clip[:, None] == jnp.arange(groups, dtype=jnp.int32)[None, :]).astype(
                jnp.int32
            )
            order = jnp.sum(clip_hot[None, :, :, None] * all_levels[:, None, :, :], axis=2).reshape(-1)
            all_embedded = dot((order[:, None] == level_ids).astype(BF), table, NN).astype(BF)
            own_levels = level_table.shape[0]
            own_ids = device * own_levels + jnp.arange(own_levels, dtype=jnp.int32)[None, :]
            own_hot = (order[:, None] == own_ids).astype(BF)
            d_w_mod = dot(all_embedded, d_mod, TN).astype(BF)
            own_levels = level_table.shape[0]
            own_rows = dot(dot(own_hot, d_mod, TN).astype(BF), w_mod, NT)
            own_rows = own_rows.reshape(groups, own_levels // groups, D)
            table_grad = lax.dynamic_index_in_dim(own_rows, z, axis=0, keepdims=False)
            for s in range(1, groups):
                table_grad = table_grad + z_put(
                    lax.dynamic_index_in_dim(own_rows, (z + s) % groups, axis=0, keepdims=False), s
                )

    with jax.named_scope("owners"):
        if not fast:
            reduced = jnp.concatenate([red_attn, red_up, red_down], axis=0)
            if chips == 4:
                height = reduced.shape[0]
                plane_parts = plane_gather(reduced.reshape(2, height // 2, D)).reshape(chips, height, D)
            else:
                plane_parts = plane_double(reduced)
            everyone = jnp.stack([plane_parts, across(plane_parts)], axis=1).reshape(owners, -1, D)
        tile_ids = lax.dynamic_slice_in_dim(owner_list, device * slots, slots)
        rates = kind_rates(tile_ids, counts)
        if fast:
            picks = pick_table(tile_ids, device)
            sources = [everyone, d_w_mod, input_grad, block_output]
        else:
            picks = jnp.zeros((slots, 12), jnp.int32)
            absolute = jnp.take(
                everyone, jnp.bitwise_xor(jnp.arange(owners, dtype=jnp.int32), device), axis=0
            ).reshape(chips, 2, -1, D)
            attn = absolute[:, :, : 4 * rows].reshape(chips, 2, 4, rows, D)
            attn = attn.transpose(2, 1, 0, 3, 4).reshape(4, -1, D)
            ffn_rows = (absolute.shape[2] - 4 * rows) // 2
            up = absolute[:, :, 4 * rows : 4 * rows + ffn_rows].transpose(1, 0, 2, 3).reshape(-1, D)
            down = absolute[:, :, 4 * rows + ffn_rows :].transpose(1, 0, 2, 3).reshape(-1, D)
            g_in = jnp.concatenate([attn[0].T, attn[1].T, attn[2].T], axis=1)
            packed = pack([g_in, attn[3], up.T, down, d_w_mod])
            sources = [jnp.take(packed, tile_ids, axis=0)]
        new_masters, new_one, new_two, new_weights, *wide = adam(
            picks, rates, sources, masters[0], moment_one[0], moment_two[0], basis_left[0], basis_right[0]
        )
    return (
        wide[1] if fast else block_output,
        wide[0] if fast else input_grad,
        table_grad,
        new_masters[None],
        new_one[None],
        new_two[None],
        new_weights[None],
    )


def solution(mesh):
    tiles = P("mp", "dp", None, None)
    in_specs = (
        P("dp", None),
        P("dp", None),
        P("dp", None),
        P("dp"),
        P("dp"),
        P(),
        P("dp", None),
        P(),
        tiles,
        tiles,
        tiles,
        tiles,
        tiles,
    )
    out_specs = (P("dp", None), P("dp", None), P(("dp", "mp"), None), tiles, tiles, tiles, tiles)
    return jax.shard_map(body, mesh=mesh, in_specs=in_specs, out_specs=out_specs, check_vma=False)
```

```python
import functools

import jax
import jax.numpy as jnp
from jax import lax
from jax.experimental import pallas as pl
from jax.experimental.pallas import tpu as pltpu
from jax.sharding import PartitionSpec as P

D = 1024
H = 16
HD = 64
FF = 4096
FRAMES = 16
FRAME_TOK = 64
LEVELS = 1024
PATTERNS = 4
TILE = 128
CLIP = FRAMES * FRAME_TOK

EPS_NORM = 1e-06
BETA_ONE = 0.5
BETA_TWO = 0.75
EPS_ADAM = 1e-08
DECAY = 0.01
LOG2E = 1.4426950408889634
GELU_A = 0.7978845608028654
GELU_B = 0.044715

BF = jnp.bfloat16
F32 = jnp.float32
VMEM_BYTES = 60 * 1024 * 1024


def params(**kw):
    return pltpu.CompilerParams(vmem_limit_bytes=VMEM_BYTES, **kw)


def cost(flops, nbytes, trans=0):
    return pl.CostEstimate(flops=int(flops), bytes_accessed=int(nbytes), transcendentals=int(trans))


def dot(left, right, dims):
    return lax.dot_general(left, right, (dims, ((), ())), preferred_element_type=F32)


NN = ((1,), (0,))
NT = ((1,), (1,))
TN = ((0,), (0,))


def tile_layout(groups):
    local_width = H // groups * HD
    shapes = [
        (D, 3 * local_width),
        (local_width, D),
        (D, FF // groups),
        (FF // groups, D),
        (D, 6 * D // groups),
    ]
    counts = [height // TILE * (breadth // TILE) for height, breadth in shapes]
    return (shapes, counts)


def kind_rates(tile_ids, counts):
    scales = [
        0.35 * D ** (-0.5),
        1.5 * (H * HD) ** (-0.5),
        0.5 * D ** (-0.5),
        0.5 * FF ** (-0.5),
        0.5 * D ** (-0.5),
    ]
    tile_rates = jnp.full(tile_ids.shape, scales[0], F32)
    boundary = 0
    for category in range(1, 5):
        boundary = boundary + counts[category - 1]
        tile_rates = jnp.where(tile_ids >= boundary, jnp.float32(scales[category]), tile_rates)
    return tile_rates


def unpack(tile_stack, shapes, counts):
    matrices = []
    offset = 0
    for (height, breadth), amount in zip(shapes, counts):
        stacked = tile_stack[offset : offset + amount].reshape(
            height // TILE, breadth // TILE, TILE, TILE
        )
        matrices.append(stacked.transpose(0, 2, 1, 3).reshape(height, breadth))
        offset = offset + amount
    return matrices


def pack(matrices):
    stacked = []
    for matrix in matrices:
        height, breadth = matrix.shape
        stacked.append(
            matrix.reshape(height // TILE, TILE, breadth // TILE, TILE)
            .transpose(0, 2, 1, 3)
            .reshape(-1, TILE, TILE)
        )
    return jnp.concatenate(stacked, axis=0)


def pick_chunk_plain(gathered, inverse, chip, core, chips, shapes, counts):
    w_qkv, w_out, w_up, w_down, w_mod = unpack(jnp.take(gathered, inverse, axis=0), shapes, counts)
    width = w_out.shape[0]
    half = width // 2
    ffn = w_up.shape[1] // 2
    rows, ffn_rows = half // chips, ffn // chips
    parts = []
    for role in range(3):
        parts.append(w_qkv[:, role * width : (role + 1) * width].T)
    parts.append(w_out)
    start = core * half + chip * rows
    attn = jnp.concatenate([lax.dynamic_slice_in_dim(p, start, rows, axis=0) for p in parts], axis=0)
    ffn_start = core * ffn + chip * ffn_rows
    up = lax.dynamic_slice_in_dim(w_up.T, ffn_start, ffn_rows, axis=0)
    down = lax.dynamic_slice_in_dim(w_down, ffn_start, ffn_rows, axis=0)
    return attn, up, down, w_mod


def norm_rows(values):
    centered = values - jnp.mean(values, axis=-1, keepdims=True)
    inverse_std = lax.rsqrt(jnp.mean(centered * centered, axis=-1, keepdims=True) + EPS_NORM)
    return centered * inverse_std, inverse_std


def norm_back(grad_normed, normed, inverse_std):
    centered = grad_normed - jnp.mean(grad_normed, axis=-1, keepdims=True)
    return inverse_std * (centered - normed * jnp.mean(grad_normed * normed, axis=-1, keepdims=True))


def frames_of(rows):
    return rows.reshape(-1, FRAME_TOK, D)


def flat(framed):
    return framed.reshape(-1, D)


BLK = 256
FBLK = BLK // FRAME_TOK


def row_spec():
    return pl.BlockSpec((BLK, D), lambda i: (i, 0))


def mod_spec(parts):
    return pl.BlockSpec((FBLK, parts, D), lambda i: (i, 0, 0))


def row_call(kernel, name, row_ins, mods, row_outs, mod_outs, nbytes):
    outs = [jax.ShapeDtypeStruct((CLIP, D), t) for t in row_outs]
    outs += [jax.ShapeDtypeStruct((FRAMES, n, D), F32) for n in mod_outs]
    return pl.pallas_call(
        kernel,
        grid=(CLIP // BLK,),
        in_specs=[row_spec() for _ in row_ins] + [mod_spec(6)],
        out_specs=[row_spec() for _ in row_outs] + [mod_spec(n) for n in mod_outs],
        out_shape=outs,
        compiler_params=params(),
        cost_estimate=cost(30 * CLIP * D, nbytes),
        name=name,
    )(*row_ins, mods)


def first_norm_kernel(x_ref, mod_ref, h_ref):
    normed, _ = norm_rows(x_ref[...].astype(F32))
    mods = mod_ref[...]
    h_ref[...] = flat(
        frames_of(normed) * (1.0 + mods[:, 1:2]) + mods[:, 0:1]
    ).astype(BF)


def middle_kernel(x_ref, a_ref, b_ref, dy_ref, mod_ref, y_ref, s_ref, h_ref, de_ref):
    mods = mod_ref[...]
    branch = (a_ref[...].astype(F32) + b_ref[...].astype(F32)).astype(BF)
    s_ref[...] = branch
    mid = frames_of(x_ref[...].astype(F32)) + mods[:, 2:3] * frames_of(branch.astype(F32))
    y_ref[...] = flat(mid)
    normed, _ = norm_rows(flat(mid))
    h_ref[...] = flat(
        frames_of(normed) * (1.0 + mods[:, 4:5]) + mods[:, 3:4]
    ).astype(BF)
    de_ref[...] = flat(mods[:, 5:6] * frames_of(dy_ref[...].astype(F32))).astype(BF)


def back_kernel(y_ref, g_ref, gp_ref, dy_ref, s_ref, e_ref, ep_ref, mod_ref, out_ref, dy1_ref, da_ref, dm_ref):
    mods = mod_ref[...]
    mid = y_ref[...]
    feed = e_ref[...].astype(F32) + ep_ref[...].astype(F32)
    dy = dy_ref[...].astype(F32)
    out_ref[...] = (mid + flat(mods[:, 5:6] * frames_of(feed))).astype(BF)
    normed, inverse_std = norm_rows(mid)
    grad = g_ref[...].astype(F32) + gp_ref[...].astype(F32)
    dm_ref[:, 0] = jnp.sum(frames_of(grad), axis=1)
    dm_ref[:, 1] = jnp.sum(frames_of(grad * normed), axis=1)
    scaled = flat(frames_of(grad) * (1.0 + mods[:, 4:5]))
    dy1 = dy + norm_back(scaled, normed, inverse_std)
    dy1_ref[...] = dy1
    dm_ref[:, 2] = jnp.sum(frames_of(dy1 * s_ref[...].astype(F32)), axis=1)
    dm_ref[:, 3] = jnp.sum(frames_of(dy * feed), axis=1)
    da_ref[...] = flat(mods[:, 2:3] * frames_of(dy1)).astype(BF)


def last_kernel(x_ref, g_ref, gp_ref, dy1_ref, mod_ref, out_ref, dm_ref):
    mods = mod_ref[...]
    normed, inverse_std = norm_rows(x_ref[...].astype(F32))
    grad = g_ref[...].astype(F32) + gp_ref[...].astype(F32)
    dm_ref[:, 0] = jnp.sum(frames_of(grad), axis=1)
    dm_ref[:, 1] = jnp.sum(frames_of(grad * normed), axis=1)
    scaled = flat(frames_of(grad) * (1.0 + mods[:, 1:2]))
    out_ref[...] = (dy1_ref[...] + norm_back(scaled, normed, inverse_std)).astype(BF)


MESH = pl.DeviceIdType.MESH
HEAD_TILES = 36
TABLE_TILES = 8
PAYLOAD = 46
LEVEL_TILE = HEAD_TILES + TABLE_TILES


class Link:
    def __init__(self, sends, recvs):
        self.sends, self.recvs, self.used, self.pending = sends, recvs, 0, []

    def make(self, src, dst, dp, mp):
        copy = pltpu.make_async_remote_copy(
            src_ref=src,
            dst_ref=dst,
            send_sem=self.sends.at[self.used],
            recv_sem=self.recvs.at[self.used],
            device_id=(dp, mp),
            device_id_type=MESH,
        )
        self.used += 1
        self.pending.append(copy)
        return copy

    def send(self, src, dst, dp, mp):
        copy = self.make(src, dst, dp, mp)
        copy.start()
        return copy

    def drain(self):
        for copy in self.pending:
            copy.wait_send()
        self.pending = []


def greet(d, z):
    barrier = pltpu.get_barrier_semaphore()
    for step in (1, 2, 4):
        pl.semaphore_signal(barrier, inc=1, device_id=(jnp.bitwise_xor(d, step), z), device_id_type=MESH)
    for s in (1, 2, 3):
        pl.semaphore_signal(barrier, inc=1, device_id=(d, lax.rem(z + s, 4)), device_id_type=MESH)
    pl.semaphore_wait(barrier, 6)


QBLK = 256
ROWS = 512
SCALE2 = HD ** (-0.5) * LOG2E


ENTRY_COPIES = 8 + 45 + 3


def front_kernel(
    idx_ref,
    pay_ref,
    act_ref,
    cot_ref,
    bias_ref,
    w_ref,
    wmod_out,
    x_out,
    dy_out,
    h_out,
    wpack_out,
    qkv_out,
    o_out,
    branch_out,
    y_out,
    e_out,
    dh_out,
    dup_out,
    ddown_out,
    mods_ref,
    bias_out,
    lse_ref,
    emb_ref,
    own_hot_ref,
    gath,
    own,
    turn,
    xs,
    dys,
    bs,
    part,
    modbuf,
    hots,
    hs,
    wpack,
    qs,
    os_,
    mine,
    peer,
    e_acc,
    dh_acc,
    wfeed,
    up_stage,
    down_stage,
    up_acc,
    down_acc,
    sends,
    recvs,
    swap_sends,
    swap_recvs,
    strip_sends,
    strip_recvs,
    local_sems,
    pack_sems,
    stage_sems,
):
    d, z = lax.axis_index("dp"), lax.axis_index("mp")
    core, chip = lax.rem(d, 2), d // 2
    dk, dx, dyd = jnp.bitwise_xor(d, 1), jnp.bitwise_xor(d, 2), jnp.bitwise_xor(d, 4)
    dxy = jnp.bitwise_xor(d, 6)
    link = Link(sends, recvs)
    greet(d, z)

    def slot(owner, first=0, count=PAYLOAD):
        return gath.at[pl.ds(owner * PAYLOAD + first, count)]

    half = PAYLOAD // 2
    home = pltpu.make_async_copy(pay_ref, slot(d), local_sems.at[0])
    home.start()
    to_x = link.send(pay_ref, slot(d), dx, z)
    to_y = link.send(pay_ref, slot(d), dyd, z)
    to_k = link.send(pay_ref, slot(d), dk, z)

    holds = (z // 2) == core
    rows = pl.ds(lax.rem(z, 2) * CLIP, CLIP)
    picks = [
        (act_ref.at[rows], xs),
        (cot_ref.at[rows], dys),
        (bias_ref.at[lax.rem(z, 2)], bs),
    ]

    def swaps():
        return [
            pltpu.make_async_remote_copy(
                src_ref=src,
                dst_ref=dst,
                send_sem=swap_sends.at[i],
                recv_sem=swap_recvs.at[i],
                device_id=(dk, z),
                device_id_type=MESH,
            )
            for i, (src, dst) in enumerate(picks)
        ]

    def keeps():
        return [pltpu.make_async_copy(src, dst, local_sems.at[1 + i]) for i, (src, dst) in enumerate(picks)]

    @pl.when(holds)
    def _():
        for copy in swaps() + keeps():
            copy.start()

    to_x.wait_recv()
    x_to_y = link.send(slot(dx, 0, half), slot(dx, 0, half), dyd, z)
    x_to_k = link.send(slot(dx), slot(dx), dk, z)
    to_y.wait_recv()
    y_to_x = link.send(slot(dyd, half, half), slot(dyd, half, half), dx, z)
    y_to_k = link.send(slot(dyd), slot(dyd), dk, z)

    @pl.when(holds)
    def _():
        for copy in swaps():
            copy.wait_send()
        for copy in keeps():
            copy.wait()

    @pl.when(jnp.logical_not(holds))
    def _():
        for copy in swaps():
            copy.wait_recv()

    bias_out[...] = bs[...]
    locals_used = [7]

    def save(src, dst):
        copy = pltpu.make_async_copy(src, dst, local_sems.at[locals_used[0]])
        locals_used[0] += 1
        copy.start()
        return copy

    x_saved = save(xs, x_out)
    dy_saved = save(dys, dy_out)

    x_to_y.wait_recv()
    y_to_x.wait_recv()
    xy_to_k = link.send(slot(dxy), slot(dxy), dk, z)
    home.wait()
    to_k.wait_recv()
    x_to_k.wait_recv()
    y_to_k.wait_recv()
    xy_to_k.wait_recv()

    def tile(number):
        return gath[idx_ref[number]]

    def pick_attn(j, _):
        lanes = pl.ds(pl.multiple_of(j * TILE, TILE), TILE)
        for role in range(3):
            turn[role] = tile(j * 6 + 2 * role + core).T
        turn[3] = tile(48 + core * 8 + j)
        for role in range(4):
            own[0, role * 32 : (role + 1) * 32, lanes] = turn[role, pl.ds(pl.multiple_of(chip * 32, 32), 32), :]
        return 0

    def pick_feed(j, _):
        lanes = pl.ds(pl.multiple_of(j * TILE, TILE), TILE)
        own[1, :, lanes] = tile(64 + j * 8 + 4 * core + chip).T
        own[2, :, lanes] = tile(128 + (4 * core + chip) * 8 + j)
        return 0

    def pick_mod(j, _):
        strip = pl.ds(pl.multiple_of(j * TILE, TILE), TILE)
        for col in range(12):
            qs[col // 3, strip, (col % 3) * TILE : (col % 3 + 1) * TILE] = tile(192 + j * 12 + col)
        return 0

    along, by_x, by_y, diag = {}, {}, {}, {}
    all_groups = [(g, s) for g in range(3) for s in (0, 1, 3, 2)]

    def landing(g, p, m):
        return w_ref.at[p, m] if g == 0 else wfeed.at[g - 1, p, m]

    for g, s in all_groups:
        m = lax.rem(z + 4 - s, 4)
        if s:
            along[g, s] = link.make(own.at[g], landing(g, 0, z), d, lax.rem(z + s, 4))
        src = own.at[g] if s == 0 else landing(g, 0, m)
        by_x[g, s] = link.make(src, landing(g, 1, m), dx, z)
        by_y[g, s] = link.make(src, landing(g, 2, m), dyd, z)
        if s < 2:
            diag[g, s] = link.make(landing(g, 1, m), landing(g, 3, m), dyd, z)
        else:
            diag[g, s] = link.make(landing(g, 2, m), landing(g, 3, m), dx, z)
    homes = [pltpu.make_async_copy(own.at[g], landing(g, 0, z), local_sems.at[4 + g]) for g in range(3)]

    def send_along(g):
        for s in (1, 3, 2):
            along[g, s].start()

    def send_plane(g, s):
        if s:
            along[g, s].wait_recv()
        by_x[g, s].start()
        by_y[g, s].start()

    def send_diag(g, s):
        (by_x if s < 2 else by_y)[g, s].wait_recv()
        diag[g, s].start()

    lax.fori_loop(0, 8, pick_attn, 0)
    send_along(0)
    send_plane(0, 0)
    homes[0].start()

    lax.fori_loop(0, 8, pick_mod, 0)
    mod_saved = save(qs, wmod_out)
    places = lax.broadcasted_iota(jnp.int32, (32, LEVELS), 1).astype(F32)
    for owner in range(8):
        codes = gath[owner * PAYLOAD + LEVEL_TILE][:32].astype(F32)
        level = codes[:, 0:1] * 32.0 + codes[:, 64:65]
        hots[owner * 32 : (owner + 1) * 32] = jnp.where(level == places, 1.0, 0.0).astype(BF)
    own_hot_ref[...] = hots[:, pl.ds(pl.multiple_of(d * TILE, TILE), TILE)]
    for j in range(TABLE_TILES):
        strip = jnp.concatenate([gath[owner * PAYLOAD + HEAD_TILES + j] for owner in range(8)], axis=0)
        emb_ref[:, j * TILE : (j + 1) * TILE] = dot(hots[...], strip, NN).astype(BF)
    embedded = emb_ref[pl.ds(pl.multiple_of(chip * 64, 64), 64), :]
    for k in range(4):
        part[:, :, k * 384 : (k + 1) * 384] = dot(embedded, qs[k], NN).reshape(4, FRAMES, 384)
    modbuf[z] = part[z]
    shared = {}
    for s in (1, 3, 2):
        shared[s] = link.send(part.at[lax.rem(z + s, 4)], modbuf.at[z], d, lax.rem(z + s, 4))

    lax.fori_loop(0, 8, pick_feed, 0)
    send_along(1)
    send_along(2)
    homes[1].start()
    homes[2].start()
    for s in (1, 3, 2):
        send_plane(0, s)
    for s in (0, 1, 3, 2):
        send_diag(0, s)
    send_plane(1, 0)
    send_plane(2, 0)

    for s in (1, 3, 2):
        shared[s].wait_recv()
    for m in range(4):
        for c in range(6):
            mods_ref[:, c, m * 256 : (m + 1) * 256] = modbuf[m, :, c * 256 : (c + 1) * 256]

    def norm_strip(i, _):
        strip = pl.ds(pl.multiple_of(i * BLK, BLK), BLK)
        normed, _ = norm_rows(xs[strip].astype(F32))
        mods = mods_ref[pl.ds(i * FBLK, FBLK)]
        hs[strip] = flat(frames_of(normed) * (1.0 + mods[:, 1:2]) + mods[:, 0:1]).astype(BF)
        return 0

    lax.fori_loop(0, CLIP // BLK, norm_strip, 0)
    h_saved = save(hs, h_out)
    e_acc[...] = jnp.zeros_like(e_acc)

    def late(g, p):
        for s in (0, 1, 3, 2):
            if p == 3:
                diag[g, s].wait_recv()
            elif (p == 1) == (s >= 2):
                (by_x if p == 1 else by_y)[g, s].wait_recv()

    for p in (1, 2, 3):
        late(0, p)
    homes[0].wait()

    def packs(m):
        return [
            pltpu.make_async_copy(
                w_ref.at[p, m, pl.ds(role * 32, 32)],
                wpack.at[m, pl.ds(role * TILE + p * 32, 32)],
                pack_sems.at[m * 16 + p * 4 + role],
            )
            for p in range(4)
            for role in range(4)
        ]

    def pack_start(m, _):
        for copy in packs(m):
            copy.start()
        return 0

    lax.fori_loop(0, 4, pack_start, 0)
    mod_saved.wait()

    def project_in(m, _):
        for copy in packs(m):
            copy.wait()
        qs[m] = dot(hs[...], wpack[m, 0 : 3 * TILE], NT).astype(BF)
        return 0

    lax.fori_loop(0, 4, project_in, 0)
    pack_saved = save(wpack, wpack_out)
    qkv_saved = save(qs, qkv_out)

    def attend_group(m, _):
        @pl.when(m == 0)
        def _():
            for s in (1, 3, 2):
                send_plane(1, s)

        @pl.when(m == 1)
        def _():
            send_diag(1, 0)
            send_diag(1, 1)

        @pl.when(m == 2)
        def _():
            send_plane(2, 1)
            send_plane(2, 3)
            send_diag(1, 3)

        @pl.when(m == 3)
        def _():
            send_plane(2, 2)
            send_diag(1, 2)
            send_diag(2, 0)

        def step(i, _):
            across = pl.ds(pl.multiple_of(i * QBLK, QBLK), QBLK)
            for head in range(2):
                lanes = slice(head * HD, (head + 1) * HD)
                keys = qs[m, :, TILE + head * HD : TILE + (head + 1) * HD]
                values = qs[m, :, 2 * TILE + head * HD : 2 * TILE + (head + 1) * HD]
                queries = qs[m, across, lanes]
                scores = dot(keys, queries, NT).reshape(FRAMES, FRAME_TOK, QBLK)
                scores = scores * SCALE2 + bs[:, across][:, None, :]
                peak = jnp.max(jnp.max(scores, axis=0), axis=0, keepdims=True)
                weights = jnp.exp2(scores - peak[None])
                total = jnp.sum(jnp.sum(weights, axis=0), axis=0, keepdims=True)
                mixed = dot(values, weights.reshape(CLIP, QBLK).astype(BF), TN)
                os_[m, lanes, across] = (mixed / total).astype(BF)
                lse_ref[m, head : head + 1, across] = peak + jnp.log2(total)
            return 0

        lax.fori_loop(0, CLIP // QBLK, step, 0)
        return 0

    lax.fori_loop(0, 4, attend_group, 0)
    o_saved = save(os_, o_out)
    send_diag(2, 1)

    def swap_strip(i):
        strip = pl.ds(pl.multiple_of(i * BLK, BLK), BLK)
        return pltpu.make_async_remote_copy(
            src_ref=mine.at[strip],
            dst_ref=peer.at[strip],
            send_sem=strip_sends.at[i],
            recv_sem=strip_recvs.at[i],
            device_id=(dk, z),
            device_id_type=MESH,
        )

    def project_out(i, _):
        strip = pl.ds(pl.multiple_of(i * BLK, BLK), BLK)
        total = dot(os_[0, :, strip], wpack[0, 3 * TILE : 4 * TILE], TN)
        for m in range(1, 4):
            total = total + dot(os_[m, :, strip], wpack[m, 3 * TILE : 4 * TILE], TN)
        mine[strip] = total.astype(BF)
        swap_strip(i).start()
        return 0

    lax.fori_loop(0, CLIP // BLK, project_out, 0)
    h_saved.wait()
    dy_saved.wait()

    def middle_strip(i, _):
        strip = pl.ds(pl.multiple_of(i * BLK, BLK), BLK)
        swap_strip(i).wait_recv()
        mods = mods_ref[pl.ds(i * FBLK, FBLK)]
        branch = (mine[strip].astype(F32) + peer[strip].astype(F32)).astype(BF)
        peer[strip] = branch
        mid = frames_of(xs[strip].astype(F32)) + mods[:, 2:3] * frames_of(branch.astype(F32))
        dh_acc[strip] = flat(mid)
        normed, _ = norm_rows(flat(mid))
        hs[strip] = flat(frames_of(normed) * (1.0 + mods[:, 4:5]) + mods[:, 3:4]).astype(BF)
        dys[strip] = flat(mods[:, 5:6] * frames_of(dys[strip].astype(F32))).astype(BF)
        return 0

    lax.fori_loop(0, CLIP // BLK, middle_strip, 0)
    y_saved = save(dh_acc, y_out)
    branch_saved = save(peer, branch_out)
    send_diag(2, 3)
    send_diag(2, 2)
    y_saved.wait()
    dh_acc[...] = jnp.zeros_like(dh_acc)
    homes[1].wait()
    homes[2].wait()

    def stages(block):
        buf, p, first = lax.rem(block, 2), block // 2, lax.rem(block, 2) * 2
        return [
            pltpu.make_async_copy(stage.at[buf], dst.at[p, pl.ds(first, 2)], stage_sems.at[2 * buf + k])
            for k, (stage, dst) in enumerate(((up_stage, dup_out), (down_stage, ddown_out)))
        ]

    def feed_block(block, _):
        for p in (1, 2, 3):

            @pl.when(block == 2 * p)
            def _(p=p):
                late(1, p)
                late(2, p)

        buf, p, first = lax.rem(block, 2), block // 2, lax.rem(block, 2) * 2
        up = wfeed[0, p, pl.ds(first, 2)].reshape(2 * TILE, D)
        down = wfeed[1, p, pl.ds(first, 2)].reshape(2 * TILE, D)

        @pl.when(block >= 2)
        def _():
            for copy in stages(block - 2):
                copy.wait()

        for piece in range(CLIP // ROWS):
            rows = slice(piece * ROWS, (piece + 1) * ROWS)
            hidden = hs[rows]
            grad = dys[rows]
            pre = dot(hidden, up, NT)
            square = pre * pre
            tanh = jnp.tanh(GELU_A * pre * (1.0 + GELU_B * square))
            act = (0.5 * pre * (1.0 + tanh)).astype(BF)
            slope = 0.5 * (1.0 + tanh) + 0.5 * pre * (1.0 - tanh * tanh) * (
                GELU_A * (1.0 + 3.0 * GELU_B * square)
            )
            grad_act = dot(grad, down, NT).astype(BF).astype(F32)
            grad_pre = (grad_act * slope).astype(BF)
            e_acc[rows] += dot(act, down, NN)
            dh_acc[rows] += dot(grad_pre, up, NN)
            if piece == 0:
                down_acc[...] = dot(act, grad, TN)
                up_acc[...] = dot(grad_pre, hidden, TN)
            else:
                down_stage[buf] = (down_acc[...] + dot(act, grad, TN)).astype(BF).reshape(2, TILE, D)
                up_stage[buf] = (up_acc[...] + dot(grad_pre, hidden, TN)).astype(BF).reshape(2, TILE, D)
        for copy in stages(block):
            copy.start()
        return 0

    lax.fori_loop(0, 8, feed_block, 0)
    branch_saved.wait()

    def swap_done(i, _):
        swap_strip(i).wait_send()
        return 0

    lax.fori_loop(0, CLIP // BLK, swap_done, 0)

    def cast_strip(i, _):
        strip = pl.ds(pl.multiple_of(i * BLK, BLK), BLK)
        mine[strip] = e_acc[strip].astype(BF)
        peer[strip] = dh_acc[strip].astype(BF)
        return 0

    lax.fori_loop(0, CLIP // BLK, cast_strip, 0)
    ends = [save(mine, e_out), save(peer, dh_out), x_saved, pack_saved, qkv_saved, o_saved]
    for block in (6, 7):
        for copy in stages(block):
            copy.wait()
    for copy in ends:
        copy.wait()
    link.drain()


def front(masters, level_table, levels, bias_pair, activations, cotangent, owner_list):
    slots = masters.shape[0]
    codes = jnp.stack([levels.reshape(-1) // 32, levels.reshape(-1) % 32], axis=1).astype(BF)
    codes = jnp.pad(jnp.repeat(codes, 64, axis=1), ((0, TILE - codes.shape[0]), (0, 0)))
    payload = jnp.concatenate(
        [
            masters.astype(BF),
            level_table.reshape(TILE, TABLE_TILES, TILE).transpose(1, 0, 2),
            codes[None],
            jnp.zeros((1, TILE, TILE), BF),
        ]
    )
    position = jnp.arange(owner_list.shape[0], dtype=jnp.int32)
    place = (position // slots) * PAYLOAD + position % slots
    index = jnp.sum(
        jnp.where(owner_list[None, :] == position[:, None], place[None, :], 0), axis=1
    ).astype(jnp.int32)
    vmem = pl.BlockSpec(memory_space=pltpu.VMEM)
    hbm = pl.BlockSpec(memory_space=pl.ANY)
    clip = jax.ShapeDtypeStruct((CLIP, D), BF)
    chunks = jax.ShapeDtypeStruct((4, 4, TILE, D), BF)
    thirds = jax.ShapeDtypeStruct((4, CLIP, 3 * TILE), BF)
    return pl.pallas_call(
        front_kernel,
        in_specs=[pl.BlockSpec(memory_space=pltpu.SMEM), hbm, hbm, hbm, hbm],
        out_specs=[hbm] * 14 + [vmem] * 5,
        out_shape=[
            chunks,
            thirds,
            clip,
            clip,
            clip,
            jax.ShapeDtypeStruct((4, 4 * TILE, D), BF),
            thirds,
            jax.ShapeDtypeStruct((4, TILE, CLIP), BF),
            clip,
            jax.ShapeDtypeStruct((CLIP, D), F32),
            clip,
            clip,
            chunks,
            chunks,
            jax.ShapeDtypeStruct((FRAMES, 6, D), F32),
            jax.ShapeDtypeStruct((FRAMES, CLIP), F32),
            jax.ShapeDtypeStruct((4, 2, CLIP), F32),
            jax.ShapeDtypeStruct((256, D), BF),
            jax.ShapeDtypeStruct((256, TILE), BF),
        ],
        scratch_shapes=[
            pltpu.VMEM((8 * PAYLOAD, TILE, TILE), BF),
            pltpu.VMEM((3, TILE, D), BF),
            pltpu.VMEM((4, TILE, TILE), BF),
            pltpu.VMEM((CLIP, D), BF),
            pltpu.VMEM((CLIP, D), BF),
            pltpu.VMEM((FRAMES, CLIP), F32),
            pltpu.VMEM((4, FRAMES, 12 * TILE), F32),
            pltpu.VMEM((4, FRAMES, 12 * TILE), F32),
            pltpu.VMEM((256, LEVELS), BF),
            pltpu.VMEM((CLIP, D), BF),
            pltpu.VMEM((4, 4 * TILE, D), BF),
            pltpu.VMEM((4, CLIP, 3 * TILE), BF),
            pltpu.VMEM((4, TILE, CLIP), BF),
            pltpu.VMEM((CLIP, D), BF),
            pltpu.VMEM((CLIP, D), BF),
            pltpu.VMEM((CLIP, D), F32),
            pltpu.VMEM((CLIP, D), F32),
            pltpu.VMEM((2, 4, 4, TILE, D), BF),
            pltpu.VMEM((2, 2, TILE, D), BF),
            pltpu.VMEM((2, 2, TILE, D), BF),
            pltpu.VMEM((2 * TILE, D), F32),
            pltpu.VMEM((2 * TILE, D), F32),
            pltpu.SemaphoreType.DMA((ENTRY_COPIES,)),
            pltpu.SemaphoreType.DMA((ENTRY_COPIES,)),
            pltpu.SemaphoreType.DMA((3,)),
            pltpu.SemaphoreType.DMA((3,)),
            pltpu.SemaphoreType.DMA((4,)),
            pltpu.SemaphoreType.DMA((4,)),
            pltpu.SemaphoreType.DMA((24,)),
            pltpu.SemaphoreType.DMA((64,)),
            pltpu.SemaphoreType.DMA((4,)),
        ],
        compiler_params=pltpu.CompilerParams(
            vmem_limit_bytes=63 * 1024 * 1024, collective_id=0, has_side_effects=True
        ),
        cost_estimate=cost(1e11, 60e6),
        name="front",
    )(index, payload, activations, cotangent, bias_pair)


def attend_kernel(qkv_ref, bias_ref, o_ref, lse_ref):
    for head in range(2):
        lanes = slice(head * HD, (head + 1) * HD)
        keys = qkv_ref[:, TILE + head * HD : TILE + (head + 1) * HD]
        values = qkv_ref[:, 2 * TILE + head * HD : 2 * TILE + (head + 1) * HD]

        def step(i, _, lanes=lanes, keys=keys, values=values, head=head):
            start = pl.multiple_of(i * QBLK, QBLK)
            queries = qkv_ref[pl.ds(start, QBLK), lanes]
            scores = dot(keys, queries, NT).reshape(FRAMES, FRAME_TOK, QBLK)
            scores = scores * SCALE2 + bias_ref[:, pl.ds(start, QBLK)][:, None, :]
            peak = jnp.max(jnp.max(scores, axis=0), axis=0, keepdims=True)
            weights = jnp.exp2(scores - peak[None])
            total = jnp.sum(jnp.sum(weights, axis=0), axis=0, keepdims=True)
            mixed = dot(values, weights.reshape(CLIP, QBLK).astype(BF), TN)
            o_ref[lanes, pl.ds(start, QBLK)] = (mixed / total).astype(BF)
            lse_ref[0, head : head + 1, pl.ds(start, QBLK)] = peak + jnp.log2(total)
            return 0

        lax.fori_loop(0, CLIP // QBLK, step, 0)


def attend(qkv, bias):
    groups = qkv.shape[1] // (3 * TILE)
    return pl.pallas_call(
        attend_kernel,
        grid=(groups,),
        in_specs=[
            pl.BlockSpec((CLIP, 3 * TILE), lambda m: (0, m)),
            pl.BlockSpec((FRAMES, CLIP), lambda m: (0, 0)),
        ],
        out_specs=[
            pl.BlockSpec((TILE, CLIP), lambda m: (m, 0)),
            pl.BlockSpec((1, 2, CLIP), lambda m: (m, 0, 0)),
        ],
        out_shape=[
            jax.ShapeDtypeStruct((groups * TILE, CLIP), BF),
            jax.ShapeDtypeStruct((groups, 2, CLIP), F32),
        ],
        compiler_params=params(),
        cost_estimate=cost(groups * 2 * 4 * CLIP * CLIP * HD * 3, 2 * qkv.size, groups * 2 * CLIP * CLIP),
        name="attend",
    )(qkv, bias)


def attend_back_kernel(qkv_ref, o_ref, do_ref, lse_ref, bias_ref, out_ref, dk_ref, dv_ref):
    for head in range(2):
        lanes = slice(head * HD, (head + 1) * HD)
        keys = qkv_ref[:, TILE + head * HD : TILE + (head + 1) * HD]
        values = qkv_ref[:, 2 * TILE + head * HD : 2 * TILE + (head + 1) * HD]
        dk_ref[...] = jnp.zeros_like(dk_ref)
        dv_ref[...] = jnp.zeros_like(dv_ref)

        def step(i, _, lanes=lanes, keys=keys, values=values, head=head):
            start = pl.multiple_of(i * QBLK, QBLK)
            across = pl.ds(start, QBLK)
            queries = qkv_ref[across, lanes]
            grad = do_ref[lanes, across]
            shift = bias_ref[:, across] - lse_ref[0, head : head + 1, across]
            scores = dot(keys, queries, NT).reshape(FRAMES, FRAME_TOK, QBLK)
            soft = jnp.exp2(scores * SCALE2 + shift[:, None, :]).reshape(CLIP, QBLK)
            delta = jnp.sum(
                grad.astype(F32) * o_ref[lanes, across].astype(F32), axis=0, keepdims=True
            )
            grad_soft = dot(values, grad, NN)
            grad_scores = (soft * (grad_soft - delta)).astype(BF)
            dv_ref[...] += dot(soft.astype(BF), grad, NT)
            dk_ref[...] += dot(grad_scores, queries, NN)
            grad_query = dot(keys, grad_scores, TN) * HD ** (-0.5)
            out_ref[across, lanes] = grad_query.T.astype(BF)
            return 0

        lax.fori_loop(0, CLIP // QBLK, step, 0)
        out_ref[:, TILE + head * HD : TILE + (head + 1) * HD] = (dk_ref[...] * HD ** (-0.5)).astype(BF)
        out_ref[:, 2 * TILE + head * HD : 2 * TILE + (head + 1) * HD] = dv_ref[...].astype(BF)


def attend_back(qkv, o_rows, do_rows, lse, bias):
    groups = qkv.shape[1] // (3 * TILE)
    return pl.pallas_call(
        attend_back_kernel,
        grid=(groups,),
        in_specs=[
            pl.BlockSpec((CLIP, 3 * TILE), lambda m: (0, m)),
            pl.BlockSpec((TILE, CLIP), lambda m: (m, 0)),
            pl.BlockSpec((TILE, CLIP), lambda m: (m, 0)),
            pl.BlockSpec((1, 2, CLIP), lambda m: (m, 0, 0)),
            pl.BlockSpec((FRAMES, CLIP), lambda m: (0, 0)),
        ],
        out_specs=pl.BlockSpec((CLIP, 3 * TILE), lambda m: (0, m)),
        out_shape=jax.ShapeDtypeStruct(qkv.shape, BF),
        scratch_shapes=[pltpu.VMEM((CLIP, HD), F32), pltpu.VMEM((CLIP, HD), F32)],
        compiler_params=params(),
        cost_estimate=cost(groups * 2 * 10 * CLIP * CLIP * HD * 3, 4 * qkv.size, groups * 2 * CLIP * CLIP),
        name="attend_back",
    )(qkv, o_rows, do_rows, lse, bias)


UNITS = 256


def feed_kernel(h_ref, de_ref, up_ref, down_ref, e_ref, dh_ref, dup_ref, ddown_ref, e_acc, dh_acc, up_acc, down_acc):
    block = pl.program_id(0)
    last = pl.num_programs(0) - 1
    up = up_ref[...]
    down = down_ref[...]
    for part in range(CLIP // ROWS):
        rows = slice(part * ROWS, (part + 1) * ROWS)
        hidden = h_ref[rows]
        grad = de_ref[rows]
        pre = dot(hidden, up, NT)
        square = pre * pre
        tanh = jnp.tanh(GELU_A * pre * (1.0 + GELU_B * square))
        act = (0.5 * pre * (1.0 + tanh)).astype(BF)
        slope = 0.5 * (1.0 + tanh) + 0.5 * pre * (1.0 - tanh * tanh) * (
            GELU_A * (1.0 + 3.0 * GELU_B * square)
        )
        grad_act = dot(grad, down, NT).astype(BF).astype(F32)
        grad_pre = (grad_act * slope).astype(BF)
        feed = dot(act, down, NN)
        back = dot(grad_pre, up, NN)

        @pl.when(block == 0)
        def _():
            e_acc[rows] = feed
            dh_acc[rows] = back

        @pl.when(block > 0)
        def _():
            e_acc[rows] += feed
            dh_acc[rows] += back

        if part == 0:
            down_acc[...] = dot(act, grad, TN)
            up_acc[...] = dot(grad_pre, hidden, TN)
        else:
            ddown_ref[...] = (down_acc[...] + dot(act, grad, TN)).astype(BF)
            dup_ref[...] = (up_acc[...] + dot(grad_pre, hidden, TN)).astype(BF)

    @pl.when(block == last)
    def _():
        e_ref[...] = e_acc[...].astype(BF)
        dh_ref[...] = dh_acc[...].astype(BF)


def feed_both(hidden, grad, up, down):
    units = up.shape[0]
    whole = pl.BlockSpec((CLIP, D), lambda i: (0, 0))
    strip = pl.BlockSpec((UNITS, D), lambda i: (i, 0))
    return pl.pallas_call(
        feed_kernel,
        grid=(units // UNITS,),
        in_specs=[whole, whole, strip, strip],
        out_specs=[whole, whole, strip, strip],
        out_shape=[jax.ShapeDtypeStruct((CLIP, D), BF)] * 2 + [jax.ShapeDtypeStruct((units, D), BF)] * 2,
        scratch_shapes=[
            pltpu.VMEM((CLIP, D), F32),
            pltpu.VMEM((CLIP, D), F32),
            pltpu.VMEM((UNITS, D), F32),
            pltpu.VMEM((UNITS, D), F32),
        ],
        compiler_params=params(),
        cost_estimate=cost(12 * CLIP * D * units, 8 * CLIP * D + 8 * units * D, CLIP * units),
        name="feed_both",
    )(hidden, grad, up, down)


HALF = CLIP // 2
EXIT_COPIES = 8 + 1 + 18 + 9 + 24 + 12 + 6 + 14
EXIT_LOCAL = 32


class Relay:
    def __init__(self, sends, recvs, local, src, full, d, z):
        self.sends, self.recvs, self.local = sends, recvs, local
        self.src, self.full, self.d, self.z = src, full, d, z
        self.core = lax.rem(d, 2)

    def place(self, clip, first, count):
        start = pl.multiple_of(lax.rem(clip, 2) * CLIP + first * HALF, HALF)
        return self.full.at[pl.ds(start, count)]

    def copy(self, src, clip, half, way, hop):
        index = way * 6 + (hop - 1) * 2 + half
        return pltpu.make_async_remote_copy(
            src_ref=src,
            dst_ref=self.place(clip, half, HALF),
            send_sem=self.sends.at[index],
            recv_sem=self.recvs.at[index],
            device_id=(self.d - self.core + clip // 2, lax.rem(self.z + (1 if way == 0 else 3), 4)),
            device_id_type=MESH,
        )

    def more(self, way):
        return self.z < 3 if way == 0 else self.z > 0

    def own(self, way):
        part = self.src.at[pl.ds(pl.multiple_of(self.core * HALF, HALF), HALF)]
        return self.copy(part, self.z, self.core, way, 1)

    def home(self):
        return pltpu.make_async_copy(self.src, self.place(self.z, 0, CLIP), self.local)

    def first(self):
        for way in range(2):

            @pl.when(self.more(way))
            def _(way=way):
                self.own(way).start()

        @pl.when(self.z // 2 == self.core)
        def _():
            self.home().start()

    def arriving(self, way, hop):
        clip = lax.rem(self.z + (4 - hop if way == 0 else hop), 4)
        there = self.z >= hop if way == 0 else self.z + hop <= 3
        return clip, jnp.logical_and(there, clip // 2 == self.core)

    def hop(self, hop):
        for way in range(2):
            clip, here = self.arriving(way, hop)

            @pl.when(here)
            def _(way=way, clip=clip):
                for half in range(2):
                    part = self.place(clip, half, HALF)
                    self.copy(part, clip, half, way, hop).wait_recv()
                    if hop < 3:

                        @pl.when(self.more(way))
                        def _(part=part, half=half):
                            self.copy(part, clip, half, way, hop + 1).start()

    def finish(self):
        for way in range(2):

            @pl.when(self.more(way))
            def _(way=way):
                self.own(way).wait_send()

            for hop in (1, 2):
                clip, here = self.arriving(way, hop)

                @pl.when(jnp.logical_and(here, self.more(way)))
                def _(way=way, clip=clip, hop=hop):
                    for half in range(2):
                        self.copy(self.place(clip, half, HALF), clip, half, way, hop + 1).wait_send()

        @pl.when(self.z // 2 == self.core)
        def _():
            self.home().wait()


class Line:
    def __init__(self, link, own, held, z, d):
        self.own, self.held, self.z, self.d = own, held, z, d
        self.sends, self.recvs, self.base = link.sends, link.recvs, link.used
        link.used += 2

    def copy(self, way, at):
        if way == 0:
            src, count = self.own.at[at + 1 : 4], 3 - at
        else:
            src, count = self.own.at[0:at], at
        return pltpu.make_async_remote_copy(
            src_ref=src,
            dst_ref=self.held.at[way, 0:count],
            send_sem=self.sends.at[self.base + way],
            recv_sem=self.recvs.at[self.base + way],
            device_id=(self.d, at + (1 if way == 0 else -1)),
            device_id_type=MESH,
        )

    def add(self, chunk, way, slot):
        def step(i, _):
            rows = pl.ds(pl.multiple_of(i * 32, 32), 32)
            total = self.own[chunk, rows].astype(F32) + self.held[way, slot, rows].astype(F32)
            self.own[chunk, rows] = total.astype(BF)
            return 0

        lax.fori_loop(0, 4, step, 0)

    def start(self):
        @pl.when(self.z == 0)
        def _():
            self.copy(0, 0).start()

        @pl.when(self.z == 3)
        def _():
            self.copy(1, 3).start()

    def turn(self):
        @pl.when(self.z == 1)
        def _():
            self.copy(0, 0).wait_recv()
            self.add(2, 0, 1)
            self.add(3, 0, 2)
            self.copy(0, 1).start()

        @pl.when(self.z == 2)
        def _():
            self.copy(1, 3).wait_recv()
            self.add(0, 1, 0)
            self.add(1, 1, 1)
            self.copy(1, 2).start()

    def turn_again(self):
        @pl.when(self.z == 2)
        def _():
            self.copy(0, 1).wait_recv()
            self.add(3, 0, 1)
            self.copy(0, 2).start()

        @pl.when(self.z == 1)
        def _():
            self.copy(1, 2).wait_recv()
            self.add(0, 1, 0)
            self.copy(1, 1).start()

    def total(self, out):
        for at in range(4):

            @pl.when(self.z == at)
            def _(at=at):
                if at == 0:
                    self.copy(1, 1).wait_recv()
                if at == 3:
                    self.copy(0, 2).wait_recv()

                def step(i, _):
                    rows = pl.ds(pl.multiple_of(i * 32, 32), 32)
                    total = self.own[at, rows].astype(F32)
                    if at > 0:
                        total = total + self.held[0, 0, rows].astype(F32)
                    if at < 3:
                        total = total + self.held[1, at, rows].astype(F32)
                    out[rows] = total.astype(BF)
                    return 0

                lax.fori_loop(0, 4, step, 0)

    def finish(self):
        for at in range(4):

            @pl.when(self.z == at)
            def _(at=at):
                if at < 3:
                    self.copy(0, at).wait_send()
                if at > 0:
                    self.copy(1, at).wait_send()


def exit_kernel(
    y_hbm,
    g_hbm,
    e_hbm,
    dy_hbm,
    br_hbm,
    x_hbm,
    h_hbm,
    qkv_hbm,
    o_hbm,
    wpack_hbm,
    wmod_hbm,
    up_hbm,
    down_hbm,
    mods_ref,
    bias_ref,
    lse_ref,
    emb_ref,
    hot_ref,
    out_all,
    in_all,
    everyone,
    dwm_out,
    table_ref,
    ys,
    gs,
    es,
    dys,
    brs,
    gp,
    ep,
    qs,
    os_,
    dos,
    win,
    wout,
    dhp,
    dattn,
    got,
    loc,
    zbuf,
    held,
    red,
    dm,
    dms,
    dmall,
    trow,
    tbuf,
    dk_ref,
    dv_ref,
    sends,
    recvs,
    strip_sends,
    strip_recvs,
    out_sends,
    out_recvs,
    in_sends,
    in_recvs,
    local_sems,
):
    d, z = lax.axis_index("dp"), lax.axis_index("mp")
    core, chip = lax.rem(d, 2), d // 2
    dk, dx, dyd = jnp.bitwise_xor(d, 1), jnp.bitwise_xor(d, 2), jnp.bitwise_xor(d, 4)
    link = Link(sends, recvs)
    locals_used = [0]

    def load(src, dst):
        copy = pltpu.make_async_copy(src, dst, local_sems.at[locals_used[0]])
        locals_used[0] += 1
        copy.start()
        return copy

    barrier = pltpu.get_barrier_semaphore()
    for step in (1, 2, 4):
        pl.semaphore_signal(barrier, inc=1, device_id=(jnp.bitwise_xor(d, step), z), device_id_type=MESH)
    for s in (1, 2, 3):
        pl.semaphore_signal(barrier, inc=1, device_id=(d, lax.rem(z + s, 4)), device_id_type=MESH)
        pl.semaphore_signal(barrier, inc=1, device_id=(dk, lax.rem(z + s, 4)), device_id_type=MESH)

    first_loads = [load(a, b) for a, b in ((g_hbm, gs), (e_hbm, es), (y_hbm, ys), (dy_hbm, dys), (br_hbm, brs))]
    loads = [load(a, b) for a, b in ((o_hbm, os_), (qkv_hbm, qs))]
    for m in range(4):
        loads.append(load(wpack_hbm.at[m, 3 * TILE : 4 * TILE], wout.at[m]))
        loads.append(load(wpack_hbm.at[m, 0 : 3 * TILE], win.at[m * 3 * TILE : (m + 1) * 3 * TILE]))
    feed_loads = []
    for g, src in enumerate((up_hbm, down_hbm)):
        feed_loads.append(load(src.at[0], loc.at[g, 0:4]))
        feed_loads.append(load(src.at[2, 0:2], loc.at[g, 4:6]))
        feed_loads.append(load(src.at[1, 2:4], loc.at[g, 6:8]))
    pl.semaphore_wait(barrier, 9)

    def strip_of(i):
        return pl.ds(pl.multiple_of(i * BLK, BLK), BLK)

    def swap(i, k):
        src, dst = ((g_hbm, gp), (e_hbm, ep))[k]
        return pltpu.make_async_remote_copy(
            src_ref=src.at[strip_of(i)],
            dst_ref=dst.at[strip_of(i)],
            send_sem=strip_sends.at[2 * i + k],
            recv_sem=strip_recvs.at[2 * i + k],
            device_id=(dk, z),
            device_id_type=MESH,
        )

    for k in (1, 0):

        def swap_start(i, _, k=k):
            swap(i, k).start()
            return 0

        lax.fori_loop(0, CLIP // BLK, swap_start, 0)

    plane = {}

    def plane_first(g, src):
        plane[g, 0] = link.send(src.at[3, 0:2], got.at[g, 0], dx, z)
        plane[g, 1] = link.send(src.at[3, 2:4], got.at[g, 1], dyd, z)
        plane[g, 2] = link.send(src.at[1, 0:2], got.at[g, 2], dx, z)
        plane[g, 3] = link.send(src.at[2, 2:4], got.at[g, 3], dyd, z)

    def add_into(dst, first, count, parts):
        def step(i, _):
            k = i // 4
            rows = pl.ds(pl.multiple_of(lax.rem(i, 4) * 32, 32), 32)
            total = dst[first + k, rows].astype(F32)
            for g, slot in parts:
                total = total + got[g, slot, k, rows].astype(F32)
            dst[first + k, rows] = total.astype(BF)
            return 0

        lax.fori_loop(0, count * 4, step, 0)

    def places(g):
        if g == 0:
            return (dattn.at[0], 0), (dattn.at[2], 0), (dattn.at[1], 2)
        return (loc.at[g - 1], 0), (loc.at[g - 1], 4), (loc.at[g - 1], 6)

    def plane_pass(g):
        _, (low, low_at), (high, high_at) = places(g)
        plane[g, 0].wait_recv()
        add_into(low, low_at, 2, [(g, 0)])
        plane[g, 4] = link.send(low.at[pl.ds(low_at, 2)], got.at[g, 4], dyd, z)
        plane[g, 1].wait_recv()
        add_into(high, high_at, 2, [(g, 1)])
        plane[g, 5] = link.send(high.at[pl.ds(high_at, 2)], got.at[g, 5], dx, z)

    column, lines = {}, {}

    def plane_final(g):
        (own, _), _, _ = places(g)
        for slot in (2, 3, 4, 5):
            plane[g, slot].wait_recv()
        add_into(own, 0, 2, [(g, 2), (g, 4)])
        add_into(own, 2, 2, [(g, 3), (g, 5)])
        if g:
            lines[g] = Line(link, own, held.at[g - 1], z, d)
            lines[g].start()
            return
        for s in (1, 3, 2):
            to = lax.rem(z + s, 4)
            column[s] = link.send(own.at[to], zbuf.at[s - 1], d, to)

    spread = {}
    homes = []

    def column_final(g):
        (own, _), _, _ = places(g)

        def step(i, _):
            rows = pl.ds(pl.multiple_of(i * 32, 32), 32)
            total = own[z, rows].astype(F32)
            for s in range(3):
                total = total + zbuf[s, rows].astype(F32)
            red[g, rows] = total.astype(BF)
            return 0

        if g:
            lines[g].total(red.at[g])
        else:
            for s in (1, 3, 2):
                column[s].wait_recv()
            lax.fori_loop(0, 4, step, 0)
        rows = pl.ds(g * TILE, TILE)
        spread[g, 2] = link.send(red.at[g], everyone.at[2, rows], dx, z)
        spread[g, 4] = link.send(red.at[g], everyone.at[4, rows], dyd, z)
        spread[g, 1] = link.send(red.at[g], everyone.at[1, rows], dk, z)
        homes.append(load(red.at[g], everyone.at[0, rows]))

    def spread_on(g):
        rows = pl.ds(g * TILE, TILE)
        low, high = pl.ds(g * TILE, TILE // 2), pl.ds(g * TILE + TILE // 2, TILE // 2)
        spread[g, 2].wait_recv()
        spread[g, 6] = link.send(everyone.at[2, low], everyone.at[6, low], dyd, z)
        spread[g, 3] = link.send(everyone.at[2, rows], everyone.at[3, rows], dk, z)
        spread[g, 4].wait_recv()
        spread[g, 7] = link.send(everyone.at[4, high], everyone.at[6, high], dx, z)
        spread[g, 5] = link.send(everyone.at[4, rows], everyone.at[5, rows], dk, z)

    def spread_diag(g):
        rows = pl.ds(g * TILE, TILE)
        spread[g, 6].wait_recv()
        spread[g, 7].wait_recv()
        spread[g, 8] = link.send(everyone.at[6, rows], everyone.at[7, rows], dk, z)

    plane_first(1, up_hbm)
    plane_first(2, down_hbm)
    for copy in first_loads:
        copy.wait()

    def out_strip(i, _):
        strip, frames = strip_of(i), pl.ds(i * FBLK, FBLK)
        swap(i, 1).wait_recv()
        mods = mods_ref[frames]
        feed = es[strip].astype(F32) + ep[strip].astype(F32)
        dm[frames, 5] = jnp.sum(frames_of(dys[strip].astype(F32) * feed), axis=1)
        ep[strip] = (ys[strip] + flat(mods[:, 5:6] * frames_of(feed))).astype(BF)
        return 0

    lax.fori_loop(0, CLIP // BLK, out_strip, 0)
    output = Relay(out_sends, out_recvs, local_sems.at[EXIT_LOCAL - 1], ep, out_all, d, z)
    output.first()

    def back_strip(i, _):
        strip, frames = strip_of(i), pl.ds(i * FBLK, FBLK)
        swap(i, 0).wait_recv()
        mods = mods_ref[frames]
        mid = ys[strip]
        dy = dys[strip].astype(F32)
        normed, inverse_std = norm_rows(mid)
        grad = gs[strip].astype(F32) + gp[strip].astype(F32)
        dm[frames, 3] = jnp.sum(frames_of(grad), axis=1)
        dm[frames, 4] = jnp.sum(frames_of(grad * normed), axis=1)
        scaled = flat(frames_of(grad) * (1.0 + mods[:, 4:5]))
        dy1 = dy + norm_back(scaled, normed, inverse_std)
        ys[strip] = dy1
        dm[frames, 2] = jnp.sum(frames_of(dy1 * brs[strip].astype(F32)), axis=1)
        gp[strip] = flat(mods[:, 2:3] * frames_of(dy1)).astype(BF)
        return 0

    lax.fori_loop(0, CLIP // BLK, back_strip, 0)

    def swap_done(i, _):
        for k in range(2):
            swap(i, k).wait_send()
        return 0

    lax.fori_loop(0, CLIP // BLK, swap_done, 0)
    x_load = load(x_hbm, gs)
    h_load = load(h_hbm, es)
    for copy in loads:
        copy.wait()

    def project(m, _):
        dos[m] = dot(wout[m], gp[...], NT).astype(BF)
        grad = dot(os_[m], gp[...], NN).astype(BF)
        for c in range(4):
            dattn[c, m, 96:128] = grad[c * 32 : (c + 1) * 32]
        return 0

    lax.fori_loop(0, 4, project, 0)

    def attend_group(m, _):
        @pl.when(m == 1)
        def _():
            output.hop(1)

        for head in range(2):
            lanes = slice(head * HD, (head + 1) * HD)
            keys = qs[m, :, TILE + head * HD : TILE + (head + 1) * HD]
            values = qs[m, :, 2 * TILE + head * HD : 2 * TILE + (head + 1) * HD]
            dk_ref[...] = jnp.zeros_like(dk_ref)
            dv_ref[...] = jnp.zeros_like(dv_ref)

            def step(i, _, lanes=lanes, keys=keys, values=values, head=head):
                across = pl.ds(pl.multiple_of(i * QBLK, QBLK), QBLK)
                queries = qs[m, across, lanes]
                grad = dos[m, lanes, across]
                shift = bias_ref[:, across] - lse_ref[m, head : head + 1, across]
                scores = dot(keys, queries, NT).reshape(FRAMES, FRAME_TOK, QBLK)
                soft = jnp.exp2(scores * SCALE2 + shift[:, None, :]).reshape(CLIP, QBLK)
                delta = jnp.sum(
                    grad.astype(F32) * os_[m, lanes, across].astype(F32), axis=0, keepdims=True
                )
                grad_soft = dot(values, grad, NN)
                grad_scores = (soft * (grad_soft - delta)).astype(BF)
                dv_ref[...] += dot(soft.astype(BF), grad, NT)
                dk_ref[...] += dot(grad_scores, queries, NN)
                grad_query = dot(keys, grad_scores, TN) * HD ** (-0.5)
                qs[m, across, lanes] = grad_query.T.astype(BF)
                return 0

            lax.fori_loop(0, CLIP // QBLK, step, 0)
            qs[m, :, TILE + head * HD : TILE + (head + 1) * HD] = (dk_ref[...] * HD ** (-0.5)).astype(BF)
            qs[m, :, 2 * TILE + head * HD : 2 * TILE + (head + 1) * HD] = dv_ref[...].astype(BF)
        return 0

    lax.fori_loop(0, 2, attend_group, 0)
    for copy in feed_loads:
        copy.wait()
    plane_pass(1)
    lax.fori_loop(2, 4, attend_group, 0)
    plane_pass(2)
    plane_final(1)
    output.hop(2)

    def hidden_strip(i, _):
        strip = strip_of(i)
        total = dot(qs[0, strip], win[0:384], NN)
        for m in range(1, 4):
            total = total + dot(qs[m, strip], win[m * 384 : (m + 1) * 384], NN)
        brs[strip] = total.astype(BF)
        return 0

    lax.fori_loop(0, CLIP // BLK, hidden_strip, 0)
    hidden_swap = link.send(brs, dhp, dk, z)
    h_load.wait()
    x_load.wait()

    def input_weights(m, _):
        grad = dot(qs[m], es[...], TN).astype(BF)
        for role in range(3):
            for c in range(4):
                first = role * TILE + c * 32
                dattn[c, m, role * 32 : (role + 1) * 32] = grad[first : first + 32]
        return 0

    lax.fori_loop(0, 4, input_weights, 0)
    plane_first(0, dattn)
    mod_loads = [load(wmod_hbm, qs)]
    plane_final(2)
    lines[1].turn()

    hidden_swap.wait_recv()

    def last_strip(i, _):
        strip, frames = strip_of(i), pl.ds(i * FBLK, FBLK)
        mods = mods_ref[frames]
        normed, inverse_std = norm_rows(gs[strip].astype(F32))
        grad = brs[strip].astype(F32) + dhp[strip].astype(F32)
        dm[frames, 0] = jnp.sum(frames_of(grad), axis=1)
        dm[frames, 1] = jnp.sum(frames_of(grad * normed), axis=1)
        scaled = flat(frames_of(grad) * (1.0 + mods[:, 1:2]))
        dys[strip] = (ys[strip] + norm_back(scaled, normed, inverse_std)).astype(BF)
        return 0

    lax.fori_loop(0, CLIP // BLK, last_strip, 0)
    for m in range(4):
        for c in range(6):
            dms[m, :, c * 256 : (c + 1) * 256] = dm[:, c, m * 256 : (m + 1) * 256].astype(BF)
    mod_column = {}
    clip = chip * 4 + z
    for s in (1, 3, 2):
        to = lax.rem(z + s, 4)
        mod_column[s] = link.send(dms.at[to], dmall.at[clip], d, to)
    dmall[clip] = dms[z]
    inner = Relay(in_sends, in_recvs, local_sems.at[EXIT_LOCAL - 2], dys, in_all, d, z)
    inner.first()

    for s in (1, 3, 2):
        mod_column[s].wait_recv()

    def clips_of(which):
        return dmall.at[pl.ds(which * 4, 4)]

    mod_x = link.send(clips_of(chip), clips_of(chip), dx, z)
    mod_y = link.send(clips_of(chip), clips_of(chip), dyd, z)
    plane_pass(0)
    lines[2].turn()
    lines[1].turn_again()
    mod_x.wait_recv()
    over_x = jnp.bitwise_xor(chip, 1)
    mod_xy = link.send(clips_of(over_x), clips_of(over_x), dyd, z)
    plane_final(0)
    inner.hop(1)
    lines[2].turn_again()
    column_final(1)

    mod_y.wait_recv()
    mod_xy.wait_recv()
    for copy in mod_loads:
        copy.wait()
    grads = dmall[...].reshape(256, 12 * TILE)

    level_grads = dot(hot_ref[...], grads, TN).astype(BF)
    rows = dot(level_grads[:, 0:384], qs[0], NT)
    for m in range(1, 4):
        rows = rows + dot(level_grads[:, m * 384 : (m + 1) * 384], qs[m], NT)
    trow[...] = rows.reshape(4, 32, D)
    table = {}
    for s in (1, 3, 2):
        to = lax.rem(z + s, 4)
        table[s] = link.send(trow.at[to], tbuf.at[s - 1], d, to)

    for part in range(6):
        win[part * 256 : (part + 1) * 256] = dot(
            grads[:, part * 256 : (part + 1) * 256], emb_ref[...], TN
        ).astype(BF)
    homes.append(load(win, dwm_out))
    column_final(2)
    spread_on(1)
    inner.hop(2)
    column_final(0)
    spread_on(2)
    spread_diag(1)
    spread_diag(2)
    spread_on(0)
    for s in (1, 3, 2):
        table[s].wait_recv()
    table_ref[...] = trow[z] + tbuf[0] + tbuf[1] + tbuf[2]
    spread_diag(0)
    output.hop(3)
    inner.hop(3)
    for g in range(3):
        for slot in (1, 3, 5, 8):
            spread[g, slot].wait_recv()
    for copy in homes:
        copy.wait()
    output.finish()
    inner.finish()
    lines[1].finish()
    lines[2].finish()
    link.drain()


def exit_call(*args):
    vmem = pl.BlockSpec(memory_space=pltpu.VMEM)
    hbm = pl.BlockSpec(memory_space=pl.ANY)
    chunks = (4, 4, TILE, D)
    heads = (4, TILE, D)
    return pl.pallas_call(
        exit_kernel,
        in_specs=[hbm] * 13 + [vmem] * 5,
        out_specs=[hbm] * 4 + [vmem],
        out_shape=[
            jax.ShapeDtypeStruct((2 * CLIP, D), BF),
            jax.ShapeDtypeStruct((2 * CLIP, D), BF),
            jax.ShapeDtypeStruct((8, 3 * TILE, D), BF),
            jax.ShapeDtypeStruct((12 * TILE, D), BF),
            jax.ShapeDtypeStruct((32, D), F32),
        ],
        scratch_shapes=[
            pltpu.VMEM((CLIP, D), F32),
            pltpu.VMEM((CLIP, D), BF),
            pltpu.VMEM((CLIP, D), BF),
            pltpu.VMEM((CLIP, D), BF),
            pltpu.VMEM((CLIP, D), BF),
            pltpu.VMEM((CLIP, D), BF),
            pltpu.VMEM((CLIP, D), BF),
            pltpu.VMEM((4, CLIP, 3 * TILE), BF),
            pltpu.VMEM(heads, BF),
            pltpu.VMEM(heads, BF),
            pltpu.VMEM((12 * TILE, D), BF),
            pltpu.VMEM(heads, BF),
            pltpu.VMEM((CLIP, D), BF),
            pltpu.VMEM(chunks, BF),
            pltpu.VMEM((3, 6, 2, TILE, D), BF),
            pltpu.VMEM((2, 8, TILE, D), BF),
            pltpu.VMEM((3, TILE, D), BF),
            pltpu.VMEM((2, 2, 3, TILE, D), BF),
            pltpu.VMEM((3, TILE, D), BF),
            pltpu.VMEM((FRAMES, 6, D), F32),
            pltpu.VMEM((4, FRAMES, 12 * TILE), BF),
            pltpu.VMEM((16, FRAMES, 12 * TILE), BF),
            pltpu.VMEM((4, 32, D), F32),
            pltpu.VMEM((3, 32, D), F32),
            pltpu.VMEM((CLIP, HD), F32),
            pltpu.VMEM((CLIP, HD), F32),
            pltpu.SemaphoreType.DMA((EXIT_COPIES,)),
            pltpu.SemaphoreType.DMA((EXIT_COPIES,)),
            pltpu.SemaphoreType.DMA((8,)),
            pltpu.SemaphoreType.DMA((8,)),
            pltpu.SemaphoreType.DMA((12,)),
            pltpu.SemaphoreType.DMA((12,)),
            pltpu.SemaphoreType.DMA((12,)),
            pltpu.SemaphoreType.DMA((12,)),
            pltpu.SemaphoreType.DMA((EXIT_LOCAL,)),
        ],
        compiler_params=pltpu.CompilerParams(
            vmem_limit_bytes=63 * 1024 * 1024, collective_id=1, has_side_effects=True
        ),
        cost_estimate=cost(1e11, 60e6),
        name="exit",
    )(*args)


def adam_steps(grads, lefts, rights, ones, twos, masters, rates):
    lefts = [left.astype(BF) for left in lefts]
    rights = [right.astype(BF) for right in rights]
    turned = [dot(left, grad.astype(BF), TN).astype(BF) for left, grad in zip(lefts, grads)]
    rotated = [dot(turn, right, NN) for turn, right in zip(turned, rights)]
    new_ones = [BETA_ONE * one + (1.0 - BETA_ONE) * r for one, r in zip(ones, rotated)]
    new_twos = [BETA_TWO * two + (1.0 - BETA_TWO) * r * r for two, r in zip(twos, rotated)]
    ways = [(one / (jnp.sqrt(two) + EPS_ADAM)).astype(BF) for one, two in zip(new_ones, new_twos)]
    backs = [dot(left, way, NN).astype(BF) for left, way in zip(lefts, ways)]
    backs = [dot(back, right, NT) for back, right in zip(backs, rights)]
    return (
        [m - rate * (back + DECAY * m) for m, back, rate in zip(masters, backs, rates)],
        new_ones,
        new_twos,
    )


def adam_kernel(tab_ref, rate_ref, *refs, picked, batch):
    if picked:
        red_ref, mod_ref, wide_ref, same_ref = refs[:4]
        refs[-2][...] = wide_ref[...].astype(F32)
        refs[-1][...] = same_ref[...]
        refs = refs[4:-2]
    else:
        grad_ref = refs[0]
        refs = refs[1:]
    master_ref, one_ref, two_ref, left_ref, right_ref, nm_ref, n1_ref, n2_ref, nw_ref = refs
    grads, rates = [], []
    for slot in range(batch):
        tile = pl.program_id(0) * batch + slot
        rates.append(rate_ref[tile])
        if picked:
            col = pl.multiple_of(tab_ref[tile, 8] * TILE, TILE)
            pieces = [
                red_ref[
                    tab_ref[tile, i],
                    pl.ds(pl.multiple_of(tab_ref[tile, 4 + i] * 32, 32), 32),
                    pl.ds(col, TILE),
                ]
                for i in range(4)
            ]
            grad = jnp.concatenate(pieces, axis=0)
            mod_row = pl.multiple_of(tab_ref[tile, 9] * TILE, TILE)
            mod_col = pl.multiple_of(tab_ref[tile, 10] * TILE, TILE)
            mod_grad = mod_ref[pl.ds(mod_col, TILE), pl.ds(mod_row, TILE)]
            kind = tab_ref[tile, 11]
            grads.append(jnp.where(kind == 0, grad, jnp.where(kind == 2, mod_grad, grad).T))
        else:
            grads.append(grad_ref[slot])
    slots = range(batch)
    new_masters, new_ones, new_twos = adam_steps(
        grads,
        [left_ref[slot] for slot in slots],
        [right_ref[slot] for slot in slots],
        [one_ref[slot] for slot in slots],
        [two_ref[slot] for slot in slots],
        [master_ref[slot] for slot in slots],
        rates,
    )
    for slot in slots:
        nm_ref[slot] = new_masters[slot]
        n1_ref[slot] = new_ones[slot]
        n2_ref[slot] = new_twos[slot]
        nw_ref[slot] = new_masters[slot].astype(BF)


def pick_table(tiles, device):
    table = []
    piece = jnp.arange(4, dtype=jnp.int32)[None, :]
    t = tiles[:, None]
    is_in = t < 48
    is_out = (t >= 48) & (t < 64)
    is_up = (t >= 64) & (t < 128)
    is_down = (t >= 128) & (t < 192)
    is_mod = t >= 192
    q0, q1, q2, q3, q4 = t, t - 48, t - 64, t - 128, t - 192
    core = jnp.where(is_in, (q0 % 6) % 2, jnp.where(is_out, q1 // 8, jnp.where(is_up, (q2 % 8) // 4, (q3 // 8) // 4)))
    chip = jnp.where(is_up, q2 % 4, (q3 // 8) % 4)
    chip = jnp.where(is_in | is_out, piece, chip)
    source = jnp.where(is_mod, 0, jnp.bitwise_xor(2 * chip + core, device))
    row = jnp.where(is_in, (q0 % 6) // 2, jnp.where(is_out, 3, jnp.where(is_up, 4 + piece, 8 + piece)))
    row = jnp.where(is_mod, 0, row + jnp.zeros_like(piece))
    col = jnp.where(is_in, q0 // 6, jnp.where(is_out, q1 % 8, jnp.where(is_up, q2 // 8, q3 % 8)))
    col = jnp.where(is_mod, 0, col)
    mod_row = jnp.where(is_mod, q4 // 12, 0)
    mod_col = jnp.where(is_mod, q4 % 12, 0)
    kind = jnp.where(is_mod, 2, jnp.where(is_in | is_up, 1, 0))
    return jnp.concatenate([source, row, col, mod_row, mod_col, kind], axis=1).astype(jnp.int32)


def adam(table, rates, sources, master, one, two, left, right):
    slots = master.shape[0]
    batch = max(b for b in (9, 6, 4, 3, 2, 1) if slots % b == 0)
    picked = len(sources) == 4
    tiles = pl.BlockSpec((batch, TILE, TILE), lambda i, *_: (i, 0, 0))
    extra = []
    if picked:
        height = 4 * TILE
        blocks = sources[2].shape[0] // height
        assert blocks <= slots // batch
        wide = pl.BlockSpec((height, D), lambda i, *_: (jnp.minimum(i, blocks - 1), 0))
        extra = [wide, wide]
        source_specs = [
            pl.BlockSpec(sources[0].shape, lambda i, *_: (0, 0, 0)),
            pl.BlockSpec(sources[1].shape, lambda i, *_: (0, 0)),
            wide,
            wide,
        ]
    else:
        source_specs = [tiles]
    return pl.pallas_call(
        functools.partial(adam_kernel, picked=picked, batch=batch),
        grid_spec=pltpu.PrefetchScalarGridSpec(
            num_scalar_prefetch=2,
            grid=(slots // batch,),
            in_specs=source_specs + [tiles] * 5,
            out_specs=[tiles] * 4 + extra,
        ),
        out_shape=[jax.ShapeDtypeStruct(master.shape, F32)] * 3
        + [jax.ShapeDtypeStruct(master.shape, BF)]
        + [jax.ShapeDtypeStruct(s.shape, t) for s, t in zip(sources[2:], (F32, BF))],
        compiler_params=params(),
        cost_estimate=cost(slots * 8 * TILE**3, slots * TILE * TILE * 36),
        name="adam",
    )(table, rates, *sources, master, one, two, left, right)


def body(
    activations,
    cotangent,
    level_table,
    true_frames,
    group_pattern,
    noise_levels,
    context_flags,
    owner_list,
    masters,
    moment_one,
    moment_two,
    basis_left,
    basis_right,
):
    groups = lax.axis_size("mp")
    owners = lax.axis_size("dp")
    chips = owners // 2
    bits = chips.bit_length() - 1
    z = lax.axis_index("mp")
    device = lax.axis_index("dp")
    core = device % 2
    chip = device // 2
    local_clips = true_frames.shape[0]
    column_clips = 2 * local_clips
    assert column_clips == groups and chips == 1 << bits
    shapes, counts = tile_layout(groups)
    slots = masters.shape[1]
    fast = chips == 4 and groups == 4

    def swap(v, step):
        return lax.ppermute(v, "dp", [(i, i ^ step) for i in range(owners)])

    def across(v):
        return swap(v, 1)

    def plane(v, bit):
        return swap(v, 2 << bit)

    def z_get(v, s):
        return lax.ppermute(v, "mp", [((i + s) % groups, i) for i in range(groups)])

    def z_put(v, s):
        return lax.ppermute(v, "mp", [(i, (i + s) % groups) for i in range(groups)])

    def plane_double(v):
        held = v[None]
        for bit in range(bits):
            held = jnp.concatenate([held, plane(held, bit)], axis=0)
        return held

    def plane_gather(v):
        if chips != 4:
            return plane_double(v)
        half = v.shape[0] // 2
        by_x, by_y = plane(v, 0), plane(v, 1)
        low, high = plane(by_x[:half], 1), plane(by_y[half:], 0)
        return jnp.stack([v, by_x, by_y, jnp.concatenate([low, high], axis=0)])

    def add(a, b):
        return (a.astype(F32) + b.astype(F32)).astype(BF)

    def plane_reduce(v):
        if chips != 4:
            held = v
            for bit in reversed(range(bits)):
                half = 1 << bit
                held = add(held[:half], plane(held[half:], bit))
            return held[0]
        half = v.shape[1] // 2
        got_low = [plane(v[1, :half], 0), plane(v[3, :half], 0)]
        got_high = [plane(v[2, half:], 1), plane(v[3, half:], 1)]
        pass_low = plane(add(v[2, :half], got_low[1]), 1)
        pass_high = plane(add(v[1, half:], got_high[1]), 0)
        low = v[0, :half].astype(F32) + got_low[0].astype(F32) + pass_low.astype(F32)
        high = v[0, half:].astype(F32) + got_high[0].astype(F32) + pass_high.astype(F32)
        return jnp.concatenate([low, high], axis=0).astype(BF)

    def z_gather(v):
        return jnp.stack([v] + [z_get(v, s) for s in range(1, groups)])

    def z_reduce(v):
        total = v[0].astype(F32)
        for s in range(1, groups):
            total = total + z_put(v[s], s).astype(F32)
        return total

    frame_index = jnp.arange(FRAMES, dtype=jnp.int32)

    def mask_rows(flagged, lengths):
        valid = frame_index[None, :] < lengths[:, None]
        in_context = flagged & valid
        visible = valid[:, :, None] & (
            jnp.logical_not(in_context)[:, None, :] | in_context[:, :, None]
        )
        return jnp.repeat(jnp.where(visible, 0.0, -1e30).astype(F32), FRAME_TOK, axis=2)

    def level_rows(flagged, patterns):
        pattern_hot = (patterns[:, None] == jnp.arange(PATTERNS, dtype=jnp.int32)[None, :]).astype(
            jnp.int32
        )
        return jnp.where(
            flagged, 0, jnp.sum(pattern_hot[:, :, None] * noise_levels[None, :, :], axis=1)
        )

    rows = TILE // chips
    level_ids = jnp.arange(LEVELS, dtype=jnp.int32)[None, :]
    if fast:
        with jax.named_scope("front"):
            flagged = context_flags == 1
            (
                _, w_mod, x, dy, h1, w_pack, qkv, o_rows, branch, y1, e_part, dh2_part, d_up, d_down,
                mods, bias, lse, all_embedded, own_hot,
            ) = front(
                masters[0],
                level_table,
                level_rows(flagged, group_pattern),
                mask_rows(flagged, true_frames),
                activations,
                cotangent,
                owner_list,
            )
        with jax.named_scope("exit"):
            block_output, input_grad, everyone, d_w_mod, table_grad = exit_call(
                y1, dh2_part, e_part, dy, branch, x, h1, qkv, o_rows, w_pack, w_mod,
                d_up, d_down, mods, bias, lse, all_embedded, own_hot,
            )
    else:
        with jax.named_scope("entry"):
            holds = (z // local_clips) == core
            local = (z % local_clips) * CLIP
            pair = jnp.stack(
                [
                    lax.dynamic_slice_in_dim(activations, local, CLIP, axis=0),
                    lax.dynamic_slice_in_dim(cotangent, local, CLIP, axis=0),
                ]
            )
            pair = jnp.where(holds, pair, across(pair))
            x, dy = pair[0], pair[1]
            facts = jnp.concatenate(
                [context_flags, true_frames[:, None], group_pattern[:, None]], axis=1
            ).astype(jnp.int32)
            other = across(facts)
            facts = jnp.where(
                core == 0, jnp.concatenate([facts, other]), jnp.concatenate([other, facts])
            )
            flagged = facts[:, :FRAMES] == 1
            levels = level_rows(flagged, facts[:, FRAMES + 1])
            bias = lax.dynamic_index_in_dim(
                mask_rows(flagged, facts[:, FRAMES]), z, axis=0, keepdims=False
            )
            all_levels = plane_double(levels)

        with jax.named_scope("owner_gather"):
            gathered = lax.all_gather(masters[0].astype(BF), "dp", axis=0, tiled=True)
            table = lax.all_gather(level_table, "dp", axis=0, tiled=True)
            position = jnp.arange(owner_list.shape[0], dtype=jnp.int32)
            inverse = jnp.sum(
                jnp.where(owner_list[None, :] == position[:, None], position[None, :], 0), axis=1
            ).astype(jnp.int32)
            chunk_attn, chunk_up, chunk_down, w_mod = pick_chunk_plain(
                gathered, inverse, chip, core, chips, shapes, counts
            )

        with jax.named_scope("weights"):
            got = plane_gather(z_gather(chunk_attn)).reshape(chips, groups, 4, rows, D)
            w_up = plane_gather(z_gather(chunk_up)).reshape(-1, D)
            w_down = plane_gather(z_gather(chunk_down)).reshape(-1, D)

        with jax.named_scope("modulation"):
            hot = (levels.reshape(-1)[:, None] == level_ids).astype(BF)
            embedded = dot(hot, table, NN).astype(BF)
            mod_part = dot(embedded, w_mod, NN).reshape(column_clips, FRAMES, -1)
            pieces = [lax.dynamic_index_in_dim(mod_part, z, axis=0, keepdims=False)]
            for s in range(1, groups):
                piece = lax.dynamic_index_in_dim(
                    mod_part, (z + groups - s) % groups, axis=0, keepdims=False
                )
                pieces.append(z_get(piece, s))
            mods = lax.dynamic_slice_in_dim(
                jnp.stack(pieces + pieces), (groups - z) % groups, groups, axis=0
            )
            mods = (
                mods.reshape(groups, FRAMES, 6, D // groups).transpose(1, 2, 0, 3).reshape(FRAMES, 6, D)
            )
            (h1,) = row_call(first_norm_kernel, "first_norm", [x], mods, [BF], [], 4 * CLIP * D)

        w_in = got[:, :, :3].transpose(1, 2, 0, 3, 4).reshape(-1, D)
        w_out = got[:, :, 3].transpose(1, 0, 2, 3).reshape(-1, D)

        mb = CLIP * D
        with jax.named_scope("attention"):
            qkv = dot(h1, w_in, NT).astype(BF)
            o_rows, lse = attend(qkv, bias)
            part = dot(o_rows, w_out, TN).astype(BF)
            y1, branch, h2, de = row_call(
                middle_kernel, "middle", [x, part, across(part), dy], mods, [F32, BF, BF, BF], [], 18 * mb
            )

        with jax.named_scope("feed"):
            e_part, dh2_part, d_up, d_down = feed_both(h2, de, w_up, w_down)

        with jax.named_scope("feed_back"):
            out, dy1, da, dm_mid = row_call(
                back_kernel,
                "back",
                [y1, dh2_part, across(dh2_part), dy, branch, e_part, across(e_part)],
                mods,
                [BF, F32, BF],
                [4],
                24 * mb,
            )
            shape = (chips, groups, -1, D)
            red_up = z_reduce(plane_reduce(d_up.reshape(shape))).astype(BF)
            red_down = z_reduce(plane_reduce(d_down.reshape(shape))).astype(BF)

        def to_column(rows_here):
            half = CLIP // 2
            mine = lax.dynamic_slice_in_dim(rows_here, core * half, half, axis=0)
            by_clip = [mine] + [z_get(mine, s) for s in range(1, groups)]
            by_clip = lax.dynamic_slice_in_dim(jnp.stack(by_clip + by_clip), (groups - z) % groups, groups, axis=0)
            keep = lax.dynamic_slice_in_dim(by_clip, core * local_clips, local_clips, axis=0)
            send = lax.dynamic_slice_in_dim(by_clip, (1 - core) * local_clips, local_clips, axis=0)
            got_half = across(send)
            both = jnp.where(
                core == 0, jnp.stack([keep, got_half], axis=1), jnp.stack([got_half, keep], axis=1)
            )
            return both.reshape(local_clips * CLIP, D)

        with jax.named_scope("block_output"):
            block_output = to_column(out)

        with jax.named_scope("attention_back"):
            do_rows = dot(w_out, da, NT).astype(BF)
            d_out = dot(o_rows, da, NN).astype(BF)
            d_qkv = attend_back(qkv, o_rows, do_rows, lse, bias)
            dh1_part = dot(d_qkv, w_in, NN).astype(BF)
            d_in = dot(d_qkv, h1, TN).astype(BF)
            in_grad, dm_last = row_call(
                last_kernel, "last", [x, dh1_part, across(dh1_part), dy1], mods, [BF], [2], 12 * mb
            )
            d_in = d_in.reshape(groups, 3, chips, rows, D).transpose(2, 0, 1, 3, 4)
            d_out = d_out.reshape(groups, 1, chips, rows, D).transpose(2, 0, 1, 3, 4)
            d_attn = jnp.concatenate([d_in, d_out], axis=2).reshape(chips, groups, 4 * rows, D)
            red_attn = z_reduce(plane_reduce(d_attn)).astype(BF)

        with jax.named_scope("input_grad"):
            input_grad = to_column(in_grad).astype(F32)

        with jax.named_scope("modulation_back"):
            d_mod = jnp.stack(
                [dm_last[:, 0], dm_last[:, 1], dm_mid[:, 2], dm_mid[:, 0], dm_mid[:, 1], dm_mid[:, 3]], axis=1
            ).astype(BF)
            d_mod = (
                d_mod.reshape(FRAMES, 6, groups, D // groups).transpose(2, 0, 1, 3).reshape(groups, FRAMES, -1)
            )
            pieces = [lax.dynamic_index_in_dim(d_mod, z, axis=0, keepdims=False)]
            for s in range(1, groups):
                pieces.append(z_put(lax.dynamic_index_in_dim(d_mod, (z + s) % groups, axis=0, keepdims=False), s))
            d_mod = jnp.stack(pieces)
            d_mod = plane_double(d_mod).reshape(chips * groups * FRAMES, -1)
            back_clip = (z + groups - jnp.arange(groups, dtype=jnp.int32)) % groups
            clip_hot = (back_clip[:, None] == jnp.arange(groups, dtype=jnp.int32)[None, :]).astype(
                jnp.int32
            )
            order = jnp.sum(clip_hot[None, :, :, None] * all_levels[:, None, :, :], axis=2).reshape(-1)
            all_embedded = dot((order[:, None] == level_ids).astype(BF), table, NN).astype(BF)
            own_levels = level_table.shape[0]
            own_ids = device * own_levels + jnp.arange(own_levels, dtype=jnp.int32)[None, :]
            own_hot = (order[:, None] == own_ids).astype(BF)
            d_w_mod = dot(all_embedded, d_mod, TN).astype(BF)
            own_levels = level_table.shape[0]
            own_rows = dot(dot(own_hot, d_mod, TN).astype(BF), w_mod, NT)
            own_rows = own_rows.reshape(groups, own_levels // groups, D)
            table_grad = lax.dynamic_index_in_dim(own_rows, z, axis=0, keepdims=False)
            for s in range(1, groups):
                table_grad = table_grad + z_put(
                    lax.dynamic_index_in_dim(own_rows, (z + s) % groups, axis=0, keepdims=False), s
                )

    with jax.named_scope("owners"):
        if not fast:
            reduced = jnp.concatenate([red_attn, red_up, red_down], axis=0)
            if chips == 4:
                height = reduced.shape[0]
                plane_parts = plane_gather(reduced.reshape(2, height // 2, D)).reshape(chips, height, D)
            else:
                plane_parts = plane_double(reduced)
            everyone = jnp.stack([plane_parts, across(plane_parts)], axis=1).reshape(owners, -1, D)
        tile_ids = lax.dynamic_slice_in_dim(owner_list, device * slots, slots)
        rates = kind_rates(tile_ids, counts)
        if fast:
            picks = pick_table(tile_ids, device)
            sources = [everyone, d_w_mod, input_grad, block_output]
        else:
            picks = jnp.zeros((slots, 12), jnp.int32)
            absolute = jnp.take(
                everyone, jnp.bitwise_xor(jnp.arange(owners, dtype=jnp.int32), device), axis=0
            ).reshape(chips, 2, -1, D)
            attn = absolute[:, :, : 4 * rows].reshape(chips, 2, 4, rows, D)
            attn = attn.transpose(2, 1, 0, 3, 4).reshape(4, -1, D)
            ffn_rows = (absolute.shape[2] - 4 * rows) // 2
            up = absolute[:, :, 4 * rows : 4 * rows + ffn_rows].transpose(1, 0, 2, 3).reshape(-1, D)
            down = absolute[:, :, 4 * rows + ffn_rows :].transpose(1, 0, 2, 3).reshape(-1, D)
            g_in = jnp.concatenate([attn[0].T, attn[1].T, attn[2].T], axis=1)
            packed = pack([g_in, attn[3], up.T, down, d_w_mod])
            sources = [jnp.take(packed, tile_ids, axis=0)]
        new_masters, new_one, new_two, new_weights, *wide = adam(
            picks, rates, sources, masters[0], moment_one[0], moment_two[0], basis_left[0], basis_right[0]
        )
    return (
        wide[1] if fast else block_output,
        wide[0] if fast else input_grad,
        table_grad,
        new_masters[None],
        new_one[None],
        new_two[None],
        new_weights[None],
    )


def solution(mesh):
    tiles = P("mp", "dp", None, None)
    in_specs = (
        P("dp", None),
        P("dp", None),
        P("dp", None),
        P("dp"),
        P("dp"),
        P(),
        P("dp", None),
        P(),
        tiles,
        tiles,
        tiles,
        tiles,
        tiles,
    )
    out_specs = (P("dp", None), P("dp", None), P(("dp", "mp"), None), tiles, tiles, tiles, tiles)
    return jax.shard_map(body, mesh=mesh, in_specs=in_specs, out_specs=out_specs, check_vma=False)
```
